32 devices in a mesh: rep: 8 (over z, core), shard: 4 (over y, x).
Axes of the slice: x: 2, y: 2, z: 4, core: 2. Of those that a mesh axis runs over, the one named last changes fastest.
Arguments:
- tokens: bfloat16 [32, 256, 2048], P(('rep', 'shard')), may hold values from -6 to 6
- segment_ids: int32 [32, 256], P(('rep', 'shard')), may hold values from 0 to 2, as said below
- attn_gain: bfloat16 [2048], P('shard'), may hold values from 0.5 to 1.5
- w_query: bfloat16 [2048, 2048], P('shard'), may hold values from -0.125 to 0.125
- w_key: bfloat16 [2048, 1024], P('shard'), may hold values from -0.125 to 0.125
- w_value: bfloat16 [2048, 1024], P('shard'), may hold values from -0.125 to 0.125
- w_out: bfloat16 [2048, 2048], P('shard'), may hold values from -0.5 to 0.5
- mlp_gain: bfloat16 [2048], P('shard'), may hold values from 0.5 to 1.5
- w_gate: bfloat16 [2048, 8192], P('shard'), may hold values from -0.125 to 0.125
- w_up: bfloat16 [2048, 8192], P('shard'), may hold values from -0.125 to 0.125
- w_down: bfloat16 [8192, 2048], P('shard'), may hold values from -0.0625 to 0.0625
- cotangent: bfloat16 [32, 256, 2048], P(('rep', 'shard')), may hold values from -6 to 6
Outputs:
- output: bfloat16 [32, 256, 2048], P(('rep', 'shard'))
- input_grad: bfloat16 [32, 256, 2048], P(('rep', 'shard'))
- attn_gain_grad: float32 [2048], P('shard')
- w_query_grad: float32 [2048, 2048], P('shard')
- w_key_grad: float32 [2048, 1024], P('shard')
- w_value_grad: float32 [2048, 1024], P('shard')
- w_out_grad: float32 [2048, 2048], P('shard')
- mlp_gain_grad: float32 [2048], P('shard')
- w_gate_grad: float32 [2048, 8192], P('shard')
- w_up_grad: float32 [2048, 8192], P('shard')
- w_down_grad: float32 [8192, 2048], P('shard')
The draws below stay inside these ranges and needn't reach their ends.
Inputs may be any that keep to these rules, and one draw needn't show every extreme that they name: `segment_ids`: each sequence holds 3 documents, ids never falling; each document has 60 to 128 tokens and one has exactly 128.
All inputs are finite; a program needn't handle non-finite values.
Results may differ from the reference program's by a relative error of at most 0.02.
Values may be sent and summed in bfloat16 or wider, within the bound.
A program may use at most 576 MiB of HBM per device.

```python
import math
import jax
import jax.numpy as jnp
from jax import lax

D = 2048
HEADS = 8
KV_HEADS = 4
HEAD_DIM = 256
FF = 8192
TOK_DEV = 256
Q_WIDTH = 2048
KV_WIDTH = 1024
SEQS = 32
DOC_MOST = 128
DOC_LEAST = 60


def draw_segment_ids(key, part):
    rest = TOK_DEV - DOC_MOST
    key_small, key_where = jax.random.split(jax.random.fold_in(key, 7))
    small = jax.random.randint(key_small, (SEQS,), DOC_LEAST, rest - DOC_LEAST + 1).astype(jnp.int32)
    other = (rest - small).astype(jnp.int32)
    where_most = jax.random.randint(key_where, (SEQS,), 0, 3).astype(jnp.int32)
    first_len = jnp.where(where_most == 0, DOC_MOST, small).astype(jnp.int32)
    second_len = jnp.where(where_most == 1, DOC_MOST, jnp.where(where_most == 0, small, other)).astype(jnp.int32)
    iota = jnp.arange(TOK_DEV, dtype=jnp.int32)[None, :]
    bound_one = first_len[:, None]
    bound_two = (first_len + second_len)[:, None]
    return ((iota >= bound_one).astype(jnp.int32) + (iota >= bound_two).astype(jnp.int32)).astype(jnp.int32)


def steps_of(stream_key, shape, shards, smallest, largest):
    level = 1.0
    for dim, blocks in shards:
        heights = jax.random.uniform(jax.random.fold_in(jax.random.fold_in(stream_key, 6), dim), (blocks,), jnp.float32, smallest / len(shards), largest / len(shards))
        level = level * jnp.repeat(jnp.exp(heights), shape[dim] // blocks).reshape((-1,) + (1,) * (len(shape) - 1 - dim))
    return level


def noise(stream_key, dims, scale, reach, shards=(), kind=jnp.bfloat16):
    array = jax.random.normal(stream_key, dims, jnp.float32) * scale
    if len(shards) > 0:
        array = steps_of(stream_key, dims, shards, -0.22, 0.18) * array
    return jnp.clip(array, min=-reach, max=reach).astype(kind)


def setup_inputs(seed: int = 0) -> dict:
    splits = jax.random.split(jax.random.key(seed), 13)
    tokens = noise(splits[0], (SEQS, TOK_DEV, D), 1.0, 6.0, ((0, 32),))
    segment_ids = draw_segment_ids(jax.random.fold_in(splits[12], 71), 0)
    attn_gain = jnp.clip(1.0 + 0.1 * jax.random.normal(splits[2], (D,), jnp.float32), 0.5, 1.5).astype(jnp.bfloat16)
    w_query = noise(splits[3], (D, Q_WIDTH), D ** -0.5, 0.125, ((0, 4),))
    w_key = noise(splits[4], (D, KV_WIDTH), D ** -0.5, 0.125, ((0, 4),))
    w_value = noise(splits[5], (D, KV_WIDTH), D ** -0.5, 0.125, ((0, 4),))
    w_out = noise(splits[6], (Q_WIDTH, D), (Q_WIDTH // 16) ** -0.5, 0.5, ((0, 4),))
    mlp_gain = jnp.clip(1.0 + 0.1 * jax.random.normal(splits[7], (D,), jnp.float32), 0.5, 1.5).astype(jnp.bfloat16)
    w_gate = noise(splits[8], (D, FF), D ** -0.5, 0.125, ((0, 4),))
    w_up = noise(splits[9], (D, FF), D ** -0.5, 0.125, ((0, 4),))
    w_down = noise(splits[10], (FF, D), FF ** -0.5, 0.0625, ((0, 4),))
    cotangent = noise(splits[11], (SEQS, TOK_DEV, D), 1.0, 6.0, ((0, 32),))
    return {"tokens": tokens, "segment_ids": segment_ids, "attn_gain": attn_gain, "w_query": w_query, "w_key": w_key, "w_value": w_value, "w_out": w_out, "mlp_gain": mlp_gain, "w_gate": w_gate, "w_up": w_up, "w_down": w_down, "cotangent": cotangent}


@jax.custom_vjp
def low(v):
    return lax.optimization_barrier(v.astype(jnp.bfloat16)).astype(jnp.float32)

@jax.custom_vjp
def low_back(v):
    return v

def low_keep(v):
    return (low(v), None)

def low_pass(kept, grad):
    return (grad,)

def back_keep(v):
    return (v, None)

def back_low(kept, grad):
    return (low(grad),)
low.defvjp(low_keep, low_pass)
low_back.defvjp(back_keep, back_low)
rope_base = 1000042.0
norm_eps = 1e-06
mask_fill = -1e+30
precise_mode = lax.Precision.HIGHEST

def matmul_high(left, right):
    return jnp.einsum('...d,de->...e', left, right, precision=precise_mode)

def rotate(values, cosine, sine):
    half = values.shape[-1] // 2
    first = values[..., :half]
    second = values[..., half:]
    return jnp.concatenate([first * cosine - second * sine, second * cosine + first * sine], -1)

def normalize(values):
    return values * lax.rsqrt(lax.optimization_barrier(jnp.mean(values * values, axis=-1, keepdims=True)) + norm_eps)

def layer(layer_input_rows, allowed, cosine, sine, attn_gain, w_query, w_key, w_value, w_out, mlp_gain, w_gate, w_up, w_down):
    batch, length, width = layer_input_rows.shape
    groups = HEADS // KV_HEADS
    normalized_rows = low(normalize(layer_input_rows) * attn_gain)
    queries = low_back(matmul_high(normalized_rows, w_query)).reshape(batch, length, KV_HEADS, groups, HEAD_DIM)
    queries = low(rotate(queries, cosine[:, :, None, None, :], sine[:, :, None, None, :]))
    keys = low_back(matmul_high(normalized_rows, w_key)).reshape(batch, length, KV_HEADS, HEAD_DIM)
    keys = low(rotate(keys, cosine[:, :, None, :], sine[:, :, None, :]))
    values = low(low_back(matmul_high(normalized_rows, w_value))).reshape(batch, length, KV_HEADS, HEAD_DIM)
    scores = jnp.einsum('blgrd,bmgd->bgrlm', queries, keys, precision=precise_mode) * HEAD_DIM ** (-0.5)
    scores = low_back(jnp.where(allowed[:, None, None], scores, mask_fill))
    weights = low(jax.nn.softmax(scores, axis=-1))
    mixed = jnp.einsum('bgrlm,bmgd->blgrd', weights, values, precision=precise_mode)
    mixed = low(low_back(mixed.reshape(batch, length, HEADS * HEAD_DIM)))
    residual_hidden_state = layer_input_rows + low_back(matmul_high(mixed, w_out))
    normed_two = low(normalize(residual_hidden_state) * mlp_gain)
    gate = low_back(matmul_high(normed_two, w_gate))
    up_value = low_back(matmul_high(normed_two, w_up))
    inner = low(jax.nn.silu(gate) * up_value)
    return residual_hidden_state + low_back(matmul_high(inner, w_down))

def reference(tokens, segment_ids, attn_gain, w_query, w_key, w_value, w_out, mlp_gain, w_gate, w_up, w_down, cotangent):
    count, length, width = tokens.shape
    group = math.gcd(count, max(1, 4096 // length))
    turns = count // group
    params = tuple((w.astype(jnp.float32) for w in (attn_gain, w_query, w_key, w_value, w_out, mlp_gain, w_gate, w_up, w_down)))
    half = HEAD_DIM // 2
    inv_freq = rope_base ** (-(jnp.arange(half, dtype=jnp.float32) * 2.0 / HEAD_DIM))

    def one_group(totals, batch_in):
        layer_input_rows, segments, grads_out = batch_in
        iota = jnp.arange(length, dtype=jnp.int32)
        change = jnp.concatenate([jnp.ones((group, 1), dtype=bool), segments[:, 1:] != segments[:, :-1]], axis=1)
        starts = lax.cummax(jnp.where(change, iota[None, :], 0).astype(jnp.int32), axis=1)
        positions = (iota[None, :] - starts).astype(jnp.float32)
        allowed = (segments[:, :, None] == segments[:, None, :]) & (iota[:, None] >= iota[None, :])[None]
        angles = positions[..., None] * inv_freq
        cosine = jnp.cos(angles)
        sine = jnp.sin(angles)

        def forward(x_value, *weights_in):
            return layer(x_value, allowed, cosine, sine, *weights_in)
        result, pull = jax.vjp(forward, layer_input_rows.astype(jnp.float32), *params)
        grads = pull(grads_out.astype(jnp.float32))
        totals = tuple((a + b for a, b in zip(totals, grads[1:])))
        return (totals, (result.astype(jnp.bfloat16), grads[0].astype(jnp.bfloat16)))
    zeros = tuple((jnp.zeros(p.shape, jnp.float32) for p in params))
    stacked = (tokens.reshape(turns, group, length, width), segment_ids.reshape(turns, group, length), cotangent.reshape(turns, group, length, width))
    totals, (outputs, in_grads) = lax.scan(one_group, zeros, stacked)
    return (outputs.reshape(count, length, width), in_grads.reshape(count, length, width), totals[0], totals[1], totals[2], totals[3], totals[4], totals[5], totals[6], totals[7], totals[8])
```

```python
import jax
import jax.numpy as jnp
import numpy as np
from jax import lax
from jax.sharding import Mesh
from jax.sharding import PartitionSpec as P

HEADS = 8
KV_HEADS = 4
HEAD_DIM = 256
FF = 8192

rope_base = 1000042.0
norm_eps = 1e-06
mask_fill = -1e30

BF = jnp.bfloat16
F32 = jnp.float32


def mm(a, b):
    return jnp.dot(a, b, preferred_element_type=F32)


def mm_tn(a, b):
    return lax.dot_general(a, b, (((0,), (0,)), ((), ())), preferred_element_type=F32)


def mm_nt(a, b):
    return lax.dot_general(a, b, (((1,), (1,)), ((), ())), preferred_element_type=F32)


def rotate(values, cosine, sine):
    half = values.shape[-1] // 2
    first = values[..., :half]
    second = values[..., half:]
    return jnp.concatenate([first * cosine - second * sine, second * cosine + first * sine], -1)


def norm_backward_step(grad_hat, normalized_rows, factor):
    return factor * (
        grad_hat - normalized_rows * jnp.mean(grad_hat * normalized_rows, axis=1, keepdims=True)
    )


def gather_plane(v):
    return lax.all_gather(lax.all_gather(v, "shard", axis=0, tiled=True), "core", axis=0, tiled=True)


def scatter_plane(v):
    v = lax.psum_scatter(v, "core", scatter_dimension=0, tiled=True)
    return lax.psum_scatter(v, "shard", scatter_dimension=0, tiled=True)


def pieces(
    tokens,
    segment_ids,
    attn_gain,
    w_query,
    w_key,
    w_value,
    w_out,
    mlp_gain,
    w_gate,
    w_up,
    w_down,
    cotangent,
):
    rows, width = tokens.shape[1], tokens.shape[2]
    core = lax.axis_index("core")
    nz, nc, ns = lax.axis_size("z"), lax.axis_size("core"), lax.axis_size("shard")
    hd = HEAD_DIM
    ff = w_gate.shape[1]
    fb = ff // (nc * ns)
    part = width // ns

    x = tokens.reshape(rows, width)
    g = cotangent.reshape(rows, width)
    x_all = gather_plane(x)
    g_all = gather_plane(g)
    seg = gather_plane(segment_ids)
    gains = lax.all_gather(jnp.stack([attn_gain, mlp_gain]), "shard", axis=1, tiled=True)
    gains = gains.astype(F32)
    gain1, gain2 = gains[0:1], gains[1:2]
    nseq = seg.shape[0]

    def blocks(w, cols):
        v = w.reshape(w.shape[0], ns, nc, cols)
        return lax.dynamic_index_in_dim(v, core, 2, keepdims=False)

    wq_b = blocks(w_query, hd)
    wkv = jnp.where(core == 0, w_key, w_value).reshape(part, ns, hd)
    wqkv = lax.all_to_all(jnp.concatenate([wq_b, wkv], -1), "shard", 1, 0, tiled=True)
    wqkv = wqkv.reshape(width, 2 * hd)
    wgu = lax.all_to_all(
        jnp.concatenate([blocks(w_gate, fb), blocks(w_up, fb)], -1), "shard", 1, 0, tiled=True
    ).reshape(width, 2 * fb)
    wo = lax.dynamic_slice_in_dim(w_out, core * hd, hd, 0)
    wd = lax.dynamic_slice_in_dim(w_down, core * fb, fb, 0)

    iota = jnp.arange(rows, dtype=jnp.int32)
    same = seg[:, :, None] == seg[:, None, :]
    allowed = same & (iota[:, None] >= iota[None, :])[None]
    starts = jnp.sum((seg[:, None, :] < seg[:, :, None]).astype(jnp.int32), axis=2)
    positions = (iota[None, :] - starts).astype(F32)
    half = hd // 2
    inv_freq = rope_base ** (-(jnp.arange(half, dtype=F32) * 2.0 / hd))
    angles = positions[..., None] * inv_freq
    cosine, sine = jnp.cos(angles), jnp.sin(angles)

    xf_all = x_all.astype(F32)
    f1_all = lax.rsqrt(jnp.mean(xf_all * xf_all, axis=1, keepdims=True) + norm_eps)
    xn1 = (xf_all * f1_all * gain1).astype(BF)
    qkv = mm(xn1, wqkv).reshape(nseq, rows, 2 * hd)
    q = rotate(qkv[..., :hd], cosine, sine).astype(BF)
    kv_lin = qkv[..., hd:]
    kv_mine = jnp.where(core == 0, rotate(kv_lin, cosine, sine), kv_lin).astype(BF)
    kv = lax.all_gather(kv_mine, "core", axis=0)
    k, v = kv[0], kv[1]
    scale = hd ** (-0.5)
    scores = jnp.einsum("bqd,bkd->bqk", q, k, preferred_element_type=F32) * scale
    scores = jnp.where(allowed, scores, mask_fill)
    top = jnp.max(scores, axis=-1, keepdims=True)
    ex = jnp.exp(scores - top)
    probs = ex / jnp.sum(ex, axis=-1, keepdims=True)
    pb = probs.astype(BF)
    attn = jnp.einsum("bqk,bkd->bqd", pb, v, preferred_element_type=F32).astype(BF)
    attn = attn.reshape(nseq * rows, hd)
    o_sum = scatter_plane(mm(attn, wo).astype(BF))
    xf = x.astype(F32)
    h = xf + o_sum.astype(F32)
    f2 = lax.rsqrt(jnp.mean(h * h, axis=1, keepdims=True) + norm_eps)
    xhat2 = h * f2
    xn2 = gather_plane((xhat2 * gain2).astype(BF))
    gu = mm(xn2, wgu)
    gate, up = gu[:, :fb], gu[:, fb:]
    sigma = jax.nn.sigmoid(gate)
    swish = gate * sigma
    hid = (swish * up).astype(BF)
    d_sum = scatter_plane(mm(hid, wd).astype(BF))
    output = (h + d_sum.astype(F32)).astype(BF).reshape(1, rows, width)

    g_down = mm_tn(hid, g_all).astype(BF)
    dhid = mm_nt(g_all, wd)
    dgate = (dhid * up * sigma * (1.0 + gate * (1.0 - sigma))).astype(BF)
    dup = (dhid * swish).astype(BF)
    dgu = jnp.concatenate([dgate, dup], 1)
    g_gu = mm_tn(xn2, dgu).astype(BF)
    dxn2 = scatter_plane(mm_nt(dgu, wgu).astype(BF)).astype(F32)
    gain2_g = jnp.sum(dxn2 * xhat2, axis=0)
    dh = g.astype(F32) + norm_backward_step(dxn2 * gain2, xhat2, f2)
    dhb = gather_plane(dh.astype(BF))
    g_out = mm_tn(attn, dhb).astype(BF)
    dattn = mm_nt(dhb, wo).astype(BF).reshape(nseq, rows, hd)
    dp = jnp.einsum("bqd,bkd->bqk", dattn, v, preferred_element_type=F32)
    dv = jnp.einsum("bqk,bqd->bkd", pb, dattn, preferred_element_type=F32)
    ds = (probs * (dp - jnp.sum(dp * probs, axis=-1, keepdims=True))).astype(BF)
    dq = jnp.einsum("bqk,bkd->bqd", ds, k, preferred_element_type=F32) * scale
    dk = jnp.einsum("bqk,bqd->bkd", ds, q, preferred_element_type=F32) * scale
    dq = rotate(dq, cosine, -sine).astype(BF)
    dk = rotate(dk, cosine, -sine)
    mine = jnp.where(core == 0, dk, dv)
    other = jnp.where(core == 0, dv, dk).astype(BF)
    swap = [(i, nc - 1 - i) for i in range(nc)]
    dkv = (mine + lax.ppermute(other, "core", swap).astype(F32)).astype(BF)
    dqkv = jnp.concatenate([dq, dkv], -1).reshape(nseq * rows, 2 * hd)
    g_qkv = mm_tn(xn1, dqkv).astype(BF)
    dxn1 = scatter_plane(mm_nt(dqkv, wqkv).astype(BF)).astype(F32)
    f1 = lax.rsqrt(jnp.mean(xf * xf, axis=1, keepdims=True) + norm_eps)
    xhat1 = xf * f1
    gain1_g = jnp.sum(dxn1 * xhat1, axis=0)
    input_grad = (dh + norm_backward_step(dxn1 * gain1, xhat1, f1)).astype(BF)
    input_grad = input_grad.reshape(1, rows, width)

    gain_g = lax.psum(jnp.stack([gain1_g, gain2_g]), ("z", "core", "shard"))
    mine_s = lax.axis_index("shard") * part
    gain_g = lax.dynamic_slice_in_dim(gain_g, mine_s, part, 1)

    def row_grad(v):
        v = lax.psum(v, "z")
        return lax.all_gather(v, "core", axis=0, tiled=True).astype(F32)

    def col_grad(v):
        n = v.shape[1]
        v = v.reshape(ns, nz, part // nz, n)
        v = lax.psum_scatter(v, "z", scatter_dimension=1, tiled=True)
        v = v.reshape(ns, part // nz, n)
        v = lax.all_to_all(v, "shard", 0, 0, tiled=True)
        v = lax.all_gather(v, "z", axis=0)
        v = lax.all_gather(v, "core", axis=0)
        return v

    qkv_g = col_grad(g_qkv)
    gu_g = col_grad(g_gu)
    wq_g = qkv_g[..., :hd].transpose(1, 3, 2, 0, 4).reshape(part, ns * nc * hd).astype(F32)
    wk_g = qkv_g[0, ..., hd:].transpose(0, 2, 1, 3).reshape(part, ns * hd).astype(F32)
    wv_g = qkv_g[1, ..., hd:].transpose(0, 2, 1, 3).reshape(part, ns * hd).astype(F32)
    gate_g = gu_g[..., :fb].transpose(1, 3, 2, 0, 4).reshape(part, ff).astype(F32)
    up_g = gu_g[..., fb:].transpose(1, 3, 2, 0, 4).reshape(part, ff).astype(F32)
    return (
        output,
        input_grad,
        gain_g[0],
        wq_g,
        wk_g,
        wv_g,
        row_grad(g_out),
        gain_g[1],
        gate_g,
        up_g,
        row_grad(g_down),
    )


def contract_rows(left, right):
    return lax.dot_general(
        left, right, (((0,), (0,)), ((), ())), preferred_element_type=jnp.float32
    )


def contract_cols(left, right):
    return lax.dot_general(
        left, right, (((1,), (1,)), ((), ())), preferred_element_type=jnp.float32
    )


def scores_of(queries, keys, allowed):
    raw = jnp.einsum(
        "qgrd,kgd->grqk", queries, keys, preferred_element_type=jnp.float32
    ) * HEAD_DIM ** (-0.5)
    return jnp.where(allowed, raw, mask_fill)


def general(
    tokens,
    segment_ids,
    attn_gain,
    w_query,
    w_key,
    w_value,
    w_out,
    mlp_gain,
    w_gate,
    w_up,
    w_down,
    cotangent,
):
    rows = tokens.shape[1]
    width = tokens.shape[2]
    groups = HEADS // KV_HEADS
    q_cols = HEADS * HEAD_DIM
    kv_cols = KV_HEADS * HEAD_DIM
    layer_input_rows = tokens.reshape(rows, width).astype(jnp.float32)
    segments = segment_ids.reshape(rows)
    iota = jnp.arange(rows, dtype=jnp.int32)
    starts = jnp.sum((segments[None, :] < segments[:, None]).astype(jnp.int32), axis=1)
    positions = (iota - starts).astype(jnp.float32)
    allowed = (segments[:, None] == segments[None, :]) & (iota[:, None] >= iota[None, :])
    half = HEAD_DIM // 2
    inv_freq = rope_base ** (-(jnp.arange(half, dtype=jnp.float32) * 2.0 / HEAD_DIM))
    angles = positions[:, None] * inv_freq
    cosine = jnp.cos(angles)
    sine = jnp.sin(angles)
    first_norm_factor = lax.rsqrt(
        jnp.mean(layer_input_rows * layer_input_rows, axis=1, keepdims=True) + norm_eps
    )
    first_standardized = layer_input_rows * first_norm_factor
    gain_fragment = lax.all_gather(attn_gain, "shard", axis=0, tiled=True)
    query_piece = lax.all_gather(w_query, "shard", axis=0, tiled=True)
    key_piece = lax.all_gather(w_key, "shard", axis=0, tiled=True)
    value_piece = lax.all_gather(w_value, "shard", axis=0, tiled=True)
    normalized_rows = (first_standardized * gain_fragment.astype(jnp.float32)).astype(jnp.bfloat16)
    joined = jnp.concatenate([query_piece, key_piece, value_piece], 1)
    result = (
        jnp.dot(normalized_rows, joined, preferred_element_type=jnp.float32),
        normalized_rows,
        gain_fragment.astype(jnp.float32),
    )
    folded = result
    projected, normed_one, first_norm_gain = (folded[0], folded[1], folded[2])
    queries = rotate(
        projected[:, :q_cols].reshape(rows, KV_HEADS, groups, HEAD_DIM),
        cosine[:, None, None, :],
        sine[:, None, None, :],
    ).astype(jnp.bfloat16)
    keys = rotate(
        projected[:, q_cols : q_cols + kv_cols].reshape(rows, KV_HEADS, HEAD_DIM),
        cosine[:, None, :],
        sine[:, None, :],
    ).astype(jnp.bfloat16)
    values = projected[:, q_cols + kv_cols :].reshape(rows, KV_HEADS, HEAD_DIM).astype(jnp.bfloat16)
    scores = scores_of(queries, keys, allowed)
    top = jnp.max(scores, axis=-1, keepdims=True)
    log_total = top + jnp.log(jnp.sum(jnp.exp(scores - top), axis=-1, keepdims=True))
    probs = jnp.exp(scores - log_total)
    probs_low = probs.astype(jnp.bfloat16)
    attn = (
        jnp.einsum("grqk,kgd->qgrd", probs_low, values, preferred_element_type=jnp.float32)
        .reshape(rows, q_cols)
        .astype(jnp.bfloat16)
    )
    part = attn
    result = (
        jnp.dot(
            part,
            lax.all_gather(w_out, "shard", axis=0, tiled=True),
            preferred_element_type=jnp.float32,
        ),
    )
    folded_out = result
    residual_hidden_state = layer_input_rows + folded_out[0]
    second_norm_factor = lax.rsqrt(
        jnp.mean(residual_hidden_state * residual_hidden_state, axis=1, keepdims=True) + norm_eps
    )
    second_standardized = residual_hidden_state * second_norm_factor
    gain_fragment = lax.all_gather(mlp_gain, "shard", axis=0, tiled=True)
    gate_piece = lax.all_gather(w_gate, "shard", axis=0, tiled=True)
    up_piece = lax.all_gather(w_up, "shard", axis=0, tiled=True)
    normalized_rows = (second_standardized * gain_fragment.astype(jnp.float32)).astype(jnp.bfloat16)
    joined = jnp.concatenate([gate_piece, up_piece], 1)
    result = (
        jnp.dot(normalized_rows, joined, preferred_element_type=jnp.float32),
        normalized_rows,
        gain_fragment.astype(jnp.float32),
    )
    folded_mlp = result
    gate = folded_mlp[0][:, :FF]
    up_value = folded_mlp[0][:, FF:]
    normed_two = folded_mlp[1]
    second_norm_gain = folded_mlp[2]
    sigma = jax.nn.sigmoid(gate)
    swish = gate * sigma
    inner = (swish * up_value).astype(jnp.bfloat16)
    part = inner
    result = (
        jnp.dot(
            part,
            lax.all_gather(w_down, "shard", axis=0, tiled=True),
            preferred_element_type=jnp.float32,
        ),
    )
    output = (residual_hidden_state + result[0]).astype(jnp.bfloat16).reshape(1, rows, width)
    grad_out = cotangent.reshape(rows, width)
    grad_down = lax.psum_scatter(
        contract_rows(inner, grad_out).astype(jnp.bfloat16),
        "shard",
        scatter_dimension=0,
        tiled=True,
    )
    down_full, gate_full, up_full = (
        lax.all_gather(w_down, "shard", axis=0, tiled=True),
        lax.all_gather(w_gate, "shard", axis=0, tiled=True),
        lax.all_gather(w_up, "shard", axis=0, tiled=True),
    )
    grad_inner = contract_cols(grad_out, down_full)
    grad_gate = (grad_inner * up_value * sigma * (1.0 + gate * (1.0 - sigma))).astype(jnp.bfloat16)
    grad_up = (grad_inner * swish).astype(jnp.bfloat16)
    grad_mlp = jnp.concatenate([grad_gate, grad_up], 1)
    mlp_shards = lax.psum_scatter(
        contract_rows(normed_two, grad_mlp).astype(jnp.bfloat16),
        "shard",
        scatter_dimension=0,
        tiled=True,
    ).astype(jnp.float32)
    second_norm_gradient = contract_cols(grad_gate, gate_full) + contract_cols(grad_up, up_full)
    second_gain_products = jnp.sum(second_norm_gradient * second_standardized, axis=0)
    hidden_gradient = grad_out.astype(jnp.float32) + norm_backward_step(
        second_norm_gradient * second_norm_gain, second_standardized, second_norm_factor
    )
    grad_hidden_low = hidden_gradient.astype(jnp.bfloat16)
    grad_out_proj = lax.psum_scatter(
        contract_rows(attn, grad_hidden_low).astype(jnp.bfloat16),
        "shard",
        scatter_dimension=0,
        tiled=True,
    )
    grad_attn = contract_cols(grad_hidden_low, lax.all_gather(w_out, "shard", axis=0, tiled=True))
    grad_attn = grad_attn.astype(jnp.bfloat16).reshape(rows, KV_HEADS, groups, HEAD_DIM)
    scores_again = scores_of(queries, keys, allowed)
    probs_again = jnp.exp(scores_again - log_total)
    probs_again_low = probs_again.astype(jnp.bfloat16)
    grad_probs = jnp.einsum("qgrd,kgd->grqk", grad_attn, values, preferred_element_type=jnp.float32)
    grad_values = jnp.einsum(
        "grqk,qgrd->kgd", probs_again_low, grad_attn, preferred_element_type=jnp.float32
    )
    grad_scores = (
        probs_again * (grad_probs - jnp.sum(grad_probs * probs_again, axis=-1, keepdims=True))
    ).astype(jnp.bfloat16)
    grad_queries = jnp.einsum(
        "grqk,kgd->qgrd", grad_scores, keys, preferred_element_type=jnp.float32
    ) * HEAD_DIM ** (-0.5)
    grad_keys = jnp.einsum(
        "grqk,qgrd->kgd", grad_scores, queries, preferred_element_type=jnp.float32
    ) * HEAD_DIM ** (-0.5)
    grad_queries = rotate(grad_queries, cosine[:, None, None, :], -sine[:, None, None, :]).reshape(
        rows, q_cols
    )
    grad_keys = rotate(grad_keys, cosine[:, None, :], -sine[:, None, :]).reshape(rows, kv_cols)
    grad_joined = jnp.concatenate(
        [
            grad_queries.astype(jnp.bfloat16),
            grad_keys.astype(jnp.bfloat16),
            grad_values.reshape(rows, kv_cols).astype(jnp.bfloat16),
        ],
        1,
    )
    qkv_shards = lax.psum_scatter(
        contract_rows(normed_one, grad_joined).astype(jnp.bfloat16),
        "shard",
        scatter_dimension=0,
        tiled=True,
    ).astype(jnp.float32)
    local_qkv = jnp.concatenate([w_query, w_key, w_value], 1)
    first_norm_gradient = contract_cols(
        grad_joined, lax.all_gather(local_qkv, "shard", axis=0, tiled=True)
    )
    first_gain_products = jnp.sum(first_norm_gradient * first_standardized, axis=0)
    input_gradient_rows = hidden_gradient + norm_backward_step(
        first_norm_gradient * first_norm_gain, first_standardized, first_norm_factor
    )
    input_grad = input_gradient_rows.astype(jnp.bfloat16).reshape(1, rows, width)
    gain_one_grad, gain_two_grad = (
        lax.psum_scatter(first_gain_products, "shard", scatter_dimension=0, tiled=True),
        lax.psum_scatter(second_gain_products, "shard", scatter_dimension=0, tiled=True),
    )
    summed = (
        lax.psum(gain_one_grad.astype(jnp.bfloat16), "rep").astype(jnp.float32),
        lax.psum(qkv_shards[:, :q_cols].astype(jnp.bfloat16), "rep").astype(jnp.float32),
        lax.psum(qkv_shards[:, q_cols : q_cols + kv_cols].astype(jnp.bfloat16), "rep").astype(
            jnp.float32
        ),
        lax.psum(qkv_shards[:, q_cols + kv_cols :].astype(jnp.bfloat16), "rep").astype(jnp.float32),
        lax.psum(grad_out_proj, "rep").astype(jnp.float32),
        lax.psum(gain_two_grad.astype(jnp.bfloat16), "rep").astype(jnp.float32),
        lax.psum(mlp_shards[:, :FF].astype(jnp.bfloat16), "rep").astype(jnp.float32),
        lax.psum(mlp_shards[:, FF:].astype(jnp.bfloat16), "rep").astype(jnp.float32),
        lax.psum(grad_down, "rep").astype(jnp.float32),
    )
    return (
        output,
        input_grad,
        summed[0],
        summed[1],
        summed[2],
        summed[3],
        summed[4],
        summed[5],
        summed[6],
        summed[7],
        summed[8],
    )


def solution(mesh):
    rep, shard = mesh.devices.shape
    if shard == KV_HEADS and rep % 2 == 0:
        fine = Mesh(np.asarray(mesh.devices).reshape(rep // 2, 2, shard), ("z", "core", "shard"))
        body, every = pieces, ("z", "core", "shard")
    else:
        fine, body, every = mesh, general, ("rep", "shard")
    seqs, vec, mat = P(every, None, None), P("shard"), P("shard", None)
    in_specs = (seqs, P(every, None), vec, mat, mat, mat, mat, vec, mat, mat, mat, seqs)
    out_specs = (seqs, seqs, vec, mat, mat, mat, mat, vec, mat, mat, mat)
    return jax.shard_map(body, mesh=fine, in_specs=in_specs, out_specs=out_specs, check_vma=False)
```

```python
import functools

import jax
import jax.numpy as jnp
import numpy as np
from jax import lax
from jax.experimental import pallas as pl
from jax.experimental.pallas import tpu as pltpu
from jax.sharding import Mesh
from jax.sharding import PartitionSpec as P

HEADS = 8
KV_HEADS = 4
HEAD_DIM = 256
FF = 8192

rope_base = 1000042.0
norm_eps = 1e-06
mask_fill = -1e30

BF = jnp.bfloat16
F32 = jnp.float32
MESH = pl.DeviceIdType.MESH
ANY = pl.BlockSpec(memory_space=pl.ANY)
VM = pl.BlockSpec(memory_space=pltpu.VMEM)
DMA = pltpu.SemaphoreType.DMA


def mm(a, b):
    return jnp.dot(a, b, preferred_element_type=F32)


def mm_tn(a, b):
    return lax.dot_general(a, b, (((0,), (0,)), ((), ())), preferred_element_type=F32)


def mm_nt(a, b):
    return lax.dot_general(a, b, (((1,), (1,)), ((), ())), preferred_element_type=F32)


def rotate(values, cosine, sine):
    half = values.shape[-1] // 2
    first = values[..., :half]
    second = values[..., half:]
    return jnp.concatenate([first * cosine - second * sine, second * cosine + first * sine], -1)


def norm_backward_step(grad_hat, normalized_rows, factor):
    return factor * (
        grad_hat - normalized_rows * jnp.mean(grad_hat * normalized_rows, axis=1, keepdims=True)
    )


class Place:
    def __init__(self):
        self.z = lax.axis_index("z")
        self.c = lax.axis_index("core")
        self.s = lax.axis_index("shard")

    def shard(self, d):
        s = self.s
        if d == 0:
            return s
        if d == 1:
            return s + 1 - 2 * lax.rem(s, 2)
        if d == 2:
            return lax.rem(s + 2, 4)
        return 3 - s

    def to(self, d):
        return {"shard": self.shard(d)}

    def sibling(self):
        return {"core": 1 - self.c}


def greet(ids):
    barrier = pltpu.get_barrier_semaphore()
    for d in ids:
        pl.semaphore_signal(barrier, inc=1, device_id=d, device_id_type=MESH)
    pl.semaphore_wait(barrier, len(ids))


def rcopy(src, dst, send, recv, dev):
    return pltpu.make_async_remote_copy(
        src_ref=src, dst_ref=dst, send_sem=send, recv_sem=recv, device_id=dev, device_id_type=MESH
    )


GATHER_SEMS = [DMA((6,)), DMA((6,)), DMA((7,)), DMA((7,)), DMA((1,))]


class Gather:
    def __init__(self, p, src, out, sems):
        self.p, self.src, self.out = p, src, out
        self.send, self.recv, self.csend, self.crecv, self.lsem = sems
        self.rows = src.shape[0]
        self.half = self.rows // 2

    def at(self, d, h, core=None):
        core = self.p.c if core is None else core
        row = (core * 4 + self.p.shard(d)) * self.rows
        if h is None:
            return self.out.at[pl.ds(row, self.rows)]
        return self.out.at[pl.ds(row + h * self.half, self.half)]

    def move(self, k):
        d, h, to = [(0, 0, 1), (0, 1, 2), (0, 1, 1), (0, 0, 2), (1, 0, 2), (2, 1, 1)][k]
        dst = self.at(d, h)
        src = self.src.at[pl.ds(h * self.half, self.half)] if d == 0 else dst
        return rcopy(src, dst, self.send.at[k], self.recv.at[k], self.p.to(to))

    def landed(self, k):
        d, h = [(1, 0), (2, 1), (1, 1), (2, 0), (3, 0), (3, 1)][k]
        return self.at(d, h)

    def pass_on(self, k):
        here = self.src if k == 6 else self.landed(k)
        there = self.at(0, None) if k == 6 else self.landed(k)
        return rcopy(here, there, self.csend.at[k], self.crecv.at[k], self.p.sibling())

    def arrived(self, k):
        ref = self.landed(k)
        rcopy(ref, ref, self.send.at[k], self.recv.at[k], self.p.to(1)).wait_recv()
        self.pass_on(k).start()

    def start(self):
        for k in range(4):
            self.move(k).start()
        self.pass_on(6).start()
        pltpu.make_async_copy(self.src, self.at(0, None), self.lsem.at[0]).start()

    def relay(self):
        for k in (0, 1):
            self.arrived(k)
            self.move(4 + k).start()

    def finish(self):
        for k in (2, 3, 4, 5):
            self.arrived(k)
        for k in range(6):
            self.move(k).wait_send()
        for k in range(7):
            self.pass_on(k).wait()
        pltpu.make_async_copy(self.src, self.at(0, None), self.lsem.at[0]).wait()


SCATTER_SEMS = [DMA((4,)), DMA((4,)), DMA((4,)), DMA((6,)), DMA((6,))]
ORDER = (3, 1, 2, 0)


def scatter_scratch(rows, width):
    half = rows // 2
    return [
        pltpu.VMEM((4, rows, width), BF),
        pltpu.VMEM((4, rows, width), BF),
        pltpu.VMEM((6, half, width), BF),
    ] + SCATTER_SEMS


class Scatter:
    def __init__(self, p, part, scratch):
        self.p, self.part = p, part
        self.own, self.got, self.slot, self.lsem, self.csend, self.crecv, self.send, self.recv = scratch
        self.rows = self.own.shape[1]
        self.half = self.rows // 2

    def block(self, core, d):
        return self.part.at[pl.ds((core * 4 + self.p.shard(d)) * self.rows, self.rows)]

    def local(self, d):
        return pltpu.make_async_copy(self.block(self.p.c, d), self.own.at[d], self.lsem.at[d])

    def swap(self, d):
        src = self.block(1 - self.p.c, d)
        return rcopy(src, self.got.at[d], self.csend.at[d], self.crecv.at[d], self.p.sibling())

    def rowsof(self, h):
        return pl.ds(h * self.half, self.half)

    def move(self, k):
        d, h, to = [(3, 0, 1), (3, 1, 2), (1, 0, 1), (2, 1, 2), (2, 0, 2), (1, 1, 1)][k]
        return rcopy(
            self.own.at[d, self.rowsof(h)], self.slot.at[k], self.send.at[k], self.recv.at[k], self.p.to(to)
        )

    def start(self):
        for d in ORDER:
            self.swap(d).start()
            self.local(d).start()

    def pair(self, d):
        self.swap(d).wait_recv()
        self.local(d).wait()
        self.own[d] = (self.own[d].astype(F32) + self.got[d].astype(F32)).astype(BF)

    def first(self):
        self.pair(3)
        self.move(0).start()
        self.move(1).start()
        self.pair(1)
        self.move(2).start()
        self.pair(2)
        self.move(3).start()
        self.pair(0)

    def relay(self):
        for k, d, h in ((0, 2, 0), (1, 1, 1)):
            self.move(k).wait_recv()
            r = self.rowsof(h)
            self.own[d, r] = (self.own[d, r].astype(F32) + self.slot[k].astype(F32)).astype(BF)
            self.move(4 + k).start()

    def total(self, h):
        near, far = (2, 4) if h == 0 else (3, 5)
        self.move(near).wait_recv()
        self.move(far).wait_recv()
        return (
            self.own[0, self.rowsof(h)].astype(F32)
            + self.slot[near].astype(F32)
            + self.slot[far].astype(F32)
        )

    def drain(self):
        for k in range(6):
            self.move(k).wait_send()
        for d in range(4):
            self.swap(d).wait_send()


def params(cid, mb):
    return pltpu.CompilerParams(
        collective_id=cid, has_side_effects=True, vmem_limit_bytes=mb * 2**20
    )


def plane_ids(p):
    return [p.to(1), p.to(2), p.to(3), p.sibling()]


class Columns:
    def __init__(self, p, sems):
        self.p = p
        self.send, self.recv, self.lsem = sems

    def cols(self, j, d, src, width):
        return src.at[:, pl.ds(pl.multiple_of(j * width, width), width)]

    def copy(self, k, d, src, dst):
        if d == 0:
            return pltpu.make_async_copy(src, dst, self.lsem.at[k])
        return rcopy(src, dst, self.send.at[k, d - 1], self.recv.at[k, d - 1], self.p.to(d))


def rows_at(ref, r, n, c0, width):
    return ref.at[pl.ds(r, n), pl.ds(c0, width)]


def enter_kernel(x_ref, wq_ref, wk_ref, wv_ref, xa_ref, wqkv_ref, *sems):
    p = Place()
    greet(plane_ids(p))
    ga = Gather(p, x_ref, xa_ref, sems[:5])
    co = Columns(p, sems[5:8])
    ga.start()
    part = wq_ref.shape[0]
    hd = HEAD_DIM

    def q_copy(d):
        src = co.cols(p.shard(d) * 2 + p.c, d, wq_ref, hd)
        return co.copy(0, d, src, rows_at(wqkv_ref, p.s * part, part, 0, hd))

    def kv_copy(d, w):
        src = co.cols(p.shard(d), d, w, hd)
        return co.copy(1, d, src, rows_at(wqkv_ref, p.s * part, part, hd, hd))

    for d in (3, 1, 2, 0):
        q_copy(d).start()

        @pl.when(p.c == 0)
        def _():
            kv_copy(d, wk_ref).start()

        @pl.when(p.c != 0)
        def _():
            kv_copy(d, wv_ref).start()

    ga.relay()
    ga.finish()
    for d in (3, 1, 2, 0):
        q_copy(d).wait()
        kv_copy(d, wk_ref).wait()


def enter(x, wq, wk, wv):
    rows, width = x.shape
    return pl.pallas_call(
        enter_kernel,
        out_shape=(
            jax.ShapeDtypeStruct((8 * rows, width), BF),
            jax.ShapeDtypeStruct((width, 2 * HEAD_DIM), BF),
        ),
        in_specs=[VM, ANY, ANY, ANY],
        out_specs=(ANY, ANY),
        scratch_shapes=GATHER_SEMS + [DMA((2, 3)), DMA((2, 3)), DMA((2,))],
        compiler_params=params(0, 16),
        name="enter",
    )(x, wq, wk, wv)


def middle_kernel(part_ref, x_ref, gain_ref, g_ref, wg_ref, wu_ref, h_ref, xn_ref, ga_ref, wgu_ref, xnb, *scr):
    p = Place()
    greet(plane_ids(p))
    sc = Scatter(p, part_ref, scr[:8])
    gx = Gather(p, xnb, xn_ref, scr[8:13])
    gg = Gather(p, g_ref, ga_ref, scr[13:18])
    co = Columns(p, scr[18:21])
    fb = wgu_ref.shape[1] // 2
    part = wg_ref.shape[0]
    sc.start()
    sc.first()

    def w_copy(k, d):
        w = wg_ref if k == 0 else wu_ref
        src = co.cols(p.shard(d) * 2 + p.c, d, w, fb)
        return co.copy(k, d, src, rows_at(wgu_ref, p.s * part, part, k * fb, fb))

    gg.start()
    sc.relay()
    gg.relay()
    for d in (3, 1, 2, 0):
        for k in (0, 1):
            w_copy(k, d).start()
    half = sc.half
    for h in (0, 1):
        r = pl.ds(h * half, half)
        res = x_ref[r].astype(F32) + sc.total(h)
        h_ref[r] = res
        f = lax.rsqrt(jnp.mean(res * res, axis=1, keepdims=True) + norm_eps)
        xnb[r] = (res * f * gain_ref[...]).astype(BF)
    gx.start()
    gx.relay()
    gg.finish()
    gx.finish()
    for d in (3, 1, 2, 0):
        for k in (0, 1):
            w_copy(k, d).wait()
    sc.drain()


def middle(part, x, gain2, g, wg, wu):
    rows, width = x.shape
    fb = wg.shape[1] // 8
    return pl.pallas_call(
        middle_kernel,
        out_shape=(
            jax.ShapeDtypeStruct((rows, width), F32),
            jax.ShapeDtypeStruct((8 * rows, width), BF),
            jax.ShapeDtypeStruct((8 * rows, width), BF),
            jax.ShapeDtypeStruct((width, 2 * fb), BF),
        ),
        in_specs=[ANY, VM, VM, VM, ANY, ANY],
        out_specs=(VM, ANY, ANY, ANY),
        scratch_shapes=[pltpu.VMEM((rows, width), BF)]
        + scatter_scratch(rows, width)
        + GATHER_SEMS * 2
        + [DMA((2, 3)), DMA((2, 3)), DMA((2,))],
        compiler_params=params(1, 48),
        name="middle",
    )(part, x, gain2, g, wg, wu)


def scatter_kernel(part_ref, out_ref, *scr):
    p = Place()
    greet(plane_ids(p)[:2] + [p.sibling()])
    sc = Scatter(p, part_ref, scr)
    sc.start()
    sc.first()
    sc.relay()
    for h in (0, 1):
        out_ref[pl.ds(h * sc.half, sc.half)] = sc.total(h)
    sc.drain()


def scatter(part, cid):
    rows, width = part.shape[0] // 8, part.shape[1]
    return pl.pallas_call(
        scatter_kernel,
        out_shape=jax.ShapeDtypeStruct((rows, width), F32),
        in_specs=[ANY],
        out_specs=VM,
        scratch_shapes=scatter_scratch(rows, width),
        compiler_params=params(cid, 32),
        name="scatter",
    )(part)


def gather_kernel(src_ref, out_ref, *sems):
    p = Place()
    greet(plane_ids(p)[:2] + [p.sibling()])
    ga = Gather(p, src_ref, out_ref, sems)
    ga.start()
    ga.relay()
    ga.finish()


def gather(src, cid):
    rows, width = src.shape
    return pl.pallas_call(
        gather_kernel,
        out_shape=jax.ShapeDtypeStruct((8 * rows, width), BF),
        in_specs=[VM],
        out_specs=ANY,
        scratch_shapes=GATHER_SEMS,
        compiler_params=params(cid, 16),
        name="gather",
    )(src)


CH = 64
DOWN, GU, OUT, QKV = range(4)


class Chain:
    def __init__(self, p, h, ins, outs, bufs, sems):
        self.p, self.h = p, h
        self.ins = ins
        self.gate, self.up, self.down, self.out, self.wq, self.wk, self.wv = outs
        self.buf, self.bufq = bufs
        self.rs_send, self.rs_recv, self.ag_send, self.ag_recv, self.cp_send, self.cp_recv, self.tsend = sems
        nz = lax.axis_size("z")
        self.nz = nz
        self.pos = nz - 1 - p.z if h == 0 else p.z
        self.step = -1 if h == 0 else 1

    def dev(self, by):
        return {"z": self.p.z + by}

    BASE = {DOWN: 0, GU: 8, OUT: 24, QKV: 26}

    def tick(self, kind, t):
        return self.BASE[kind] + t

    def shard_of(self, t):
        s, d = self.p.s, lax.rem(t, 4)
        one = s + 1 - 2 * lax.rem(s, 2)
        two = lax.rem(s + 2, 4)
        return jnp.where(d == 0, s, jnp.where(d == 1, one, jnp.where(d == 2, two, 3 - s)))

    def mine(self, kind, t):
        h = self.h
        if kind == DOWN:
            return self.ins[DOWN].at[pl.ds(h * 512 + t * CH, CH)]
        if kind == OUT:
            return self.ins[OUT].at[pl.ds(h * 128 + t * CH, CH)]
        row = self.shard_of(t) * 512 + h * 256
        if kind == QKV:
            return self.ins[QKV].at[pl.ds(row, 256)]
        return self.ins[GU].at[pl.ds(row + (t // 4) * CH, CH)]

    def slot(self, kind, t):
        return self.bufq.at[t] if kind == QKV else self.buf.at[self.tick(kind, t)]

    def rs_copy(self, kind, t, src):
        k = self.tick(kind, t)
        return rcopy(
            src, self.slot(kind, t), self.rs_send.at[k], self.rs_recv.at[k], self.dev(self.step)
        )

    def reduce(self, kind, t):
        first, last = self.pos == 0, self.pos == self.nz - 1

        @pl.when(first)
        def _():
            self.rs_copy(kind, t, self.mine(kind, t)).start()

        @pl.when(jnp.logical_not(first))
        def _():
            slot = self.slot(kind, t)
            self.rs_copy(kind, t, slot).wait_recv()
            slot[...] = (slot[...].astype(F32) + self.mine(kind, t)[...].astype(F32)).astype(BF)

        @pl.when(jnp.logical_and(jnp.logical_not(first), jnp.logical_not(last)))
        def _():
            self.rs_copy(kind, t, self.slot(kind, t)).start()

        @pl.when(last)
        def _():
            self.turn(kind, t)

    def pieces(self, kind, t, s, d_shard):
        h, c = self.h, self.p.c
        if kind == DOWN:
            return [(None, self.down.at[pl.ds(c * 1024 + h * 512 + t * CH, CH)])]
        if kind == OUT:
            return [(None, self.out.at[pl.ds(c * 256 + h * 128 + t * CH, CH)])]
        if kind == GU:
            r = h * 256 + (t // 4) * CH
            c0 = pl.multiple_of((s * 2 + c) * 1024, 1024)
            return [
                ((0, 1024), self.gate.at[pl.ds(r, CH), pl.ds(c0, 1024)]),
                ((1024, 1024), self.up.at[pl.ds(r, CH), pl.ds(c0, 1024)]),
            ]
        r = h * 256
        cq = pl.multiple_of((s * 2 + c) * 256, 256)
        return [((0, 256), self.wq.at[pl.ds(r, 256), pl.ds(cq, 256)])]

    def kv_piece(self, s, w):
        return w.at[pl.ds(self.h * 256, 256), pl.ds(pl.multiple_of(s * 256, 256), 256)]

    def turn(self, kind, t):
        slot = self.slot(kind, t)
        k = self.tick(kind, t)
        to = self.p.s if kind in (DOWN, OUT) else self.shard_of(t)

        def send(i, src, dst):
            if kind in (DOWN, OUT):
                pltpu.make_async_copy(src, dst, self.ag_recv.at[i, k]).start()
                return

            @pl.when(lax.rem(t, 4) == 0)
            def _():
                pltpu.make_async_copy(src, dst, self.ag_recv.at[i, k]).start()

            @pl.when(lax.rem(t, 4) != 0)
            def _():
                rcopy(src, dst, self.tsend.at[i, k], self.ag_recv.at[i, k], {"shard": to}).start()

        for i, (cols, dst) in enumerate(self.pieces(kind, t, self.p.s, to)):
            send(i, slot if cols is None else slot.at[:, pl.ds(*cols)], dst)
        if kind == QKV:
            src = slot.at[:, pl.ds(256, 256)]

            @pl.when(self.p.c == 0)
            def _():
                send(1, src, self.kv_piece(self.p.s, self.wk))

            @pl.when(self.p.c != 0)
            def _():
                send(1, src, self.kv_piece(self.p.s, self.wv))

    def spread_copy(self, i, k, ref):
        return rcopy(ref, ref, self.ag_send.at[i, k], self.ag_recv.at[i, k], self.dev(-self.step))

    def spread(self, kind, t):
        k = self.tick(kind, t)
        s = self.p.s if kind in (DOWN, OUT) else self.shard_of(t)

        def go(i, ref, wait=True):
            if wait:
                self.spread_copy(i, k, ref).wait_recv()

            @pl.when(self.pos > 0)
            def _():
                self.spread_copy(i, k, ref).start()

            rcopy(ref, ref, self.cp_send.at[i, k], self.cp_recv.at[i, k], self.p.sibling()).start()

        for i, (_, ref) in enumerate(self.pieces(kind, t, s, None)):
            go(i, ref)
        if kind == QKV:
            self.spread_copy(1, k, self.kv_piece(s, self.wk)).wait_recv()

            @pl.when(self.p.c == 0)
            def _():
                go(1, self.kv_piece(s, self.wk), False)

            @pl.when(self.p.c != 0)
            def _():
                go(1, self.kv_piece(s, self.wv), False)

    def drain_reduce(self, kind, t):
        k = self.tick(kind, t)

        @pl.when(self.pos < self.nz - 1)
        def _():
            self.rs_copy(kind, t, self.slot(kind, t)).wait_send()

        if kind in (GU, QKV):

            @pl.when(jnp.logical_and(self.pos == self.nz - 1, lax.rem(t, 4) != 0))
            def _():
                for i, (cols, dst) in enumerate(self.pieces(kind, t, self.p.s, None)):
                    src = self.slot(kind, t).at[:, pl.ds(*cols)]
                    rcopy(src, dst, self.tsend.at[i, k], self.ag_recv.at[i, k], self.p.to(1)).wait_send()
                if kind == QKV:
                    src = self.slot(kind, t).at[:, pl.ds(256, 256)]
                    dst = self.kv_piece(self.p.s, self.wk)
                    rcopy(src, dst, self.tsend.at[1, k], self.ag_recv.at[1, k], self.p.to(1)).wait_send()

    def drain_spread(self, kind, t):
        k = self.tick(kind, t)
        s = self.p.s if kind in (DOWN, OUT) else self.shard_of(t)
        refs = [ref for _, ref in self.pieces(kind, t, s, None)]
        if kind == QKV:
            refs.append(self.kv_piece(s, self.wk))
        for i, ref in enumerate(refs):

            @pl.when(self.pos > 0)
            def _():
                self.spread_copy(i, k, ref).wait_send()

            rcopy(ref, ref, self.cp_send.at[i, k], self.cp_recv.at[i, k], self.p.sibling()).wait()


N_TICKS = 30
CHAIN_SEMS = [
    DMA((N_TICKS,)),
    DMA((N_TICKS,)),
    DMA((2, N_TICKS)),
    DMA((2, N_TICKS)),
    DMA((2, N_TICKS)),
    DMA((2, N_TICKS)),
    DMA((2, N_TICKS)),
]


def z_neighbours_enter(p):
    barrier = pltpu.get_barrier_semaphore()
    nz = lax.axis_size("z")
    for d in plane_ids(p):
        pl.semaphore_signal(barrier, inc=1, device_id=d, device_id_type=MESH)

    @pl.when(p.z > 0)
    def _():
        pl.semaphore_signal(barrier, inc=1, device_id={"z": p.z - 1}, device_id_type=MESH)

    @pl.when(p.z < nz - 1)
    def _():
        pl.semaphore_signal(barrier, inc=1, device_id={"z": p.z + 1}, device_id_type=MESH)

    ends = jnp.logical_or(p.z == 0, p.z == nz - 1)
    pl.semaphore_wait(barrier, jnp.where(ends, 5, 6))


def loop(lo, hi, body):
    def step(t, _):
        body(t)
        return 0

    lax.fori_loop(lo, hi, step, 0)


COUNT = {DOWN: 8, GU: 16, OUT: 2, QKV: 4}


def sums_kernel(gd_ref, ggu_ref, go_ref, gqkv_ref, gate, up, down, out, wq, wk, wv, bufa, bufb, qa, qb, *sems):
    p = Place()
    z_neighbours_enter(p)
    ins = (gd_ref, ggu_ref, go_ref, gqkv_ref)
    outs = (gate, up, down, out, wq, wk, wv)
    both = [
        Chain(p, 0, ins, outs, (bufa, qa), sems[:7]),
        Chain(p, 1, ins, outs, (bufb, qb), sems[7:]),
    ]

    def run(n, red, spr):
        def body(t):
            for ch in both:
                if red:
                    ch.reduce(red[0], red[1] + t)
            for ch in both:
                if spr:
                    ch.spread(spr[0], spr[1] + t)

        loop(0, n, body)

    run(8, (DOWN, 0), None)
    run(8, (GU, 0), (DOWN, 0))
    run(8, (GU, 8), (GU, 0))
    run(2, (OUT, 0), (GU, 8))
    run(4, (QKV, 0), (GU, 10))
    run(2, None, (GU, 14))
    run(2, None, (OUT, 0))
    run(4, None, (QKV, 0))
    for kind, n in COUNT.items():

        def body(t):
            for ch in both:
                ch.drain_reduce(kind, t)
                ch.drain_spread(kind, t)

        loop(0, n, body)


def sums(g_down, g_gu, g_out, g_qkv, part, ff):
    width = g_down.shape[1]
    shapes = [(part, ff), (part, ff), (ff // 4, width), (part, width), (part, width), (part, 1024), (part, 1024)]
    return pl.pallas_call(
        sums_kernel,
        out_shape=tuple(jax.ShapeDtypeStruct(s, BF) for s in shapes),
        in_specs=[VM] * 4,
        out_specs=(ANY,) * 7,
        scratch_shapes=[
            pltpu.VMEM((26, CH, width), BF),
            pltpu.VMEM((26, CH, width), BF),
            pltpu.VMEM((4, 256, 512), BF),
            pltpu.VMEM((4, 256, 512), BF),
        ]
        + CHAIN_SEMS * 2,
        compiler_params=params(9, 56),
        name="sums",
    )(g_down, g_gu, g_out, g_qkv)


def pieces(
    tokens,
    segment_ids,
    attn_gain,
    w_query,
    w_key,
    w_value,
    w_out,
    mlp_gain,
    w_gate,
    w_up,
    w_down,
    cotangent,
):
    rows, width = tokens.shape[1], tokens.shape[2]
    core = lax.axis_index("core")
    nc, ns = lax.axis_size("core"), lax.axis_size("shard")
    hd = HEAD_DIM
    ff = w_gate.shape[1]
    fb = ff // (nc * ns)
    part = width // ns

    x = tokens.reshape(rows, width)
    g = cotangent.reshape(rows, width)
    seg = lax.all_gather(segment_ids, ("core", "shard"), axis=0, tiled=True)
    gains = lax.all_gather(jnp.stack([attn_gain, mlp_gain]), "shard", axis=1, tiled=True)
    gains = gains.astype(F32)
    gain1, gain2 = gains[0:1], gains[1:2]
    nseq = seg.shape[0]
    wo = lax.dynamic_slice_in_dim(w_out, core * hd, hd, 0)
    wd = lax.dynamic_slice_in_dim(w_down, core * fb, fb, 0)

    x_all, wqkv = enter(x, w_query, w_key, w_value)

    iota = jnp.arange(rows, dtype=jnp.int32)
    same = seg[:, :, None] == seg[:, None, :]
    allowed = same & (iota[:, None] >= iota[None, :])[None]
    starts = jnp.sum((seg[:, None, :] < seg[:, :, None]).astype(jnp.int32), axis=2)
    positions = (iota[None, :] - starts).astype(F32)
    half = hd // 2
    inv_freq = rope_base ** (-(jnp.arange(half, dtype=F32) * 2.0 / hd))
    angles = positions[..., None] * inv_freq
    cosine, sine = jnp.cos(angles), jnp.sin(angles)

    xf_all = x_all.astype(F32)
    f1_all = lax.rsqrt(jnp.mean(xf_all * xf_all, axis=1, keepdims=True) + norm_eps)
    xn1 = (xf_all * f1_all * gain1).astype(BF)
    qkv = mm(xn1, wqkv).reshape(nseq, rows, 2 * hd)
    q = rotate(qkv[..., :hd], cosine, sine).astype(BF)
    kv_lin = qkv[..., hd:]
    kv_mine = jnp.where(core == 0, rotate(kv_lin, cosine, sine), kv_lin).astype(BF)
    swap = [(i, nc - 1 - i) for i in range(nc)]
    kv_other = lax.ppermute(kv_mine, "core", swap)
    k = jnp.where(core == 0, kv_mine, kv_other)
    v = jnp.where(core == 0, kv_other, kv_mine)
    scale = hd ** (-0.5)
    scores = jnp.einsum("bqd,bkd->bqk", q, k, preferred_element_type=F32) * scale
    scores = jnp.where(allowed, scores, mask_fill)
    top = jnp.max(scores, axis=-1, keepdims=True)
    ex = jnp.exp(scores - top)
    probs = ex / jnp.sum(ex, axis=-1, keepdims=True)
    pb = probs.astype(BF)
    attn = jnp.einsum("bqk,bkd->bqd", pb, v, preferred_element_type=F32).astype(BF)
    attn = attn.reshape(nseq * rows, hd)

    h, xn2, g_all, wgu = middle(mm(attn, wo).astype(BF), x, gain2, g, w_gate, w_up)

    xf = x.astype(F32)
    f2 = lax.rsqrt(jnp.mean(h * h, axis=1, keepdims=True) + norm_eps)
    xhat2 = h * f2
    gu = mm(xn2, wgu)
    gate, up = gu[:, :fb], gu[:, fb:]
    sigma = jax.nn.sigmoid(gate)
    swish = gate * sigma
    hid = (swish * up).astype(BF)
    g_down = mm_tn(hid, g_all).astype(BF)
    dhid = mm_nt(g_all, wd)
    dgate = (dhid * up * sigma * (1.0 + gate * (1.0 - sigma))).astype(BF)
    dup = (dhid * swish).astype(BF)
    dgu = jnp.concatenate([dgate, dup], 1)
    g_gu = mm_tn(xn2, dgu).astype(BF)
    dxn2 = scatter(mm_nt(dgu, wgu).astype(BF), 2)
    gain2_g = jnp.sum(dxn2 * xhat2, axis=0)
    dh = g.astype(F32) + norm_backward_step(dxn2 * gain2, xhat2, f2)
    dhb = gather(dh.astype(BF), 3)
    d_sum = scatter(mm(hid, wd).astype(BF), 4)
    output = (h + d_sum).astype(BF).reshape(1, rows, width)
    g_out = mm_tn(attn, dhb).astype(BF)
    dattn = mm_nt(dhb, wo).astype(BF).reshape(nseq, rows, hd)
    dp = jnp.einsum("bqd,bkd->bqk", dattn, v, preferred_element_type=F32)
    dv = jnp.einsum("bqk,bqd->bkd", pb, dattn, preferred_element_type=F32)
    ds = (probs * (dp - jnp.sum(dp * probs, axis=-1, keepdims=True))).astype(BF)
    dq = jnp.einsum("bqk,bkd->bqd", ds, k, preferred_element_type=F32) * scale
    dk = jnp.einsum("bqk,bqd->bkd", ds, q, preferred_element_type=F32) * scale
    dq = rotate(dq, cosine, -sine).astype(BF)
    dk = rotate(dk, cosine, -sine)
    mine = jnp.where(core == 0, dk, dv)
    other = jnp.where(core == 0, dv, dk).astype(BF)
    dkv = (mine + lax.ppermute(other, "core", swap).astype(F32)).astype(BF)
    dqkv = jnp.concatenate([dq, dkv], -1).reshape(nseq * rows, 2 * hd)
    g_qkv = mm_tn(xn1, dqkv).astype(BF)
    dxn1 = scatter(mm_nt(dqkv, wqkv).astype(BF), 5)
    f1 = lax.rsqrt(jnp.mean(xf * xf, axis=1, keepdims=True) + norm_eps)
    xhat1 = xf * f1
    gain1_g = jnp.sum(dxn1 * xhat1, axis=0)
    input_grad = (dh + norm_backward_step(dxn1 * gain1, xhat1, f1)).astype(BF)
    input_grad = input_grad.reshape(1, rows, width)

    gain_g = lax.psum(jnp.stack([gain1_g, gain2_g]), ("z", "core", "shard"))
    mine_s = lax.axis_index("shard") * part
    gain_g = lax.dynamic_slice_in_dim(gain_g, mine_s, part, 1)

    gate_g, up_g, down_g, out_g, wq_g, wk_g, wv_g = sums(g_down, g_gu, g_out, g_qkv, part, ff)
    return (
        output,
        input_grad,
        gain_g[0],
        wq_g.astype(F32),
        wk_g.astype(F32),
        wv_g.astype(F32),
        out_g.astype(F32),
        gain_g[1],
        gate_g.astype(F32),
        up_g.astype(F32),
        down_g.astype(F32),
    )


def contract_rows(left, right):
    return lax.dot_general(
        left, right, (((0,), (0,)), ((), ())), preferred_element_type=jnp.float32
    )


def contract_cols(left, right):
    return lax.dot_general(
        left, right, (((1,), (1,)), ((), ())), preferred_element_type=jnp.float32
    )


def scores_of(queries, keys, allowed):
    raw = jnp.einsum(
        "qgrd,kgd->grqk", queries, keys, preferred_element_type=jnp.float32
    ) * HEAD_DIM ** (-0.5)
    return jnp.where(allowed, raw, mask_fill)


def general(
    tokens,
    segment_ids,
    attn_gain,
    w_query,
    w_key,
    w_value,
    w_out,
    mlp_gain,
    w_gate,
    w_up,
    w_down,
    cotangent,
):
    rows = tokens.shape[1]
    width = tokens.shape[2]
    groups = HEADS // KV_HEADS
    q_cols = HEADS * HEAD_DIM
    kv_cols = KV_HEADS * HEAD_DIM
    layer_input_rows = tokens.reshape(rows, width).astype(jnp.float32)
    segments = segment_ids.reshape(rows)
    iota = jnp.arange(rows, dtype=jnp.int32)
    starts = jnp.sum((segments[None, :] < segments[:, None]).astype(jnp.int32), axis=1)
    positions = (iota - starts).astype(jnp.float32)
    allowed = (segments[:, None] == segments[None, :]) & (iota[:, None] >= iota[None, :])
    half = HEAD_DIM // 2
    inv_freq = rope_base ** (-(jnp.arange(half, dtype=jnp.float32) * 2.0 / HEAD_DIM))
    angles = positions[:, None] * inv_freq
    cosine = jnp.cos(angles)
    sine = jnp.sin(angles)
    first_norm_factor = lax.rsqrt(
        jnp.mean(layer_input_rows * layer_input_rows, axis=1, keepdims=True) + norm_eps
    )
    first_standardized = layer_input_rows * first_norm_factor
    gain_fragment = lax.all_gather(attn_gain, "shard", axis=0, tiled=True)
    query_piece = lax.all_gather(w_query, "shard", axis=0, tiled=True)
    key_piece = lax.all_gather(w_key, "shard", axis=0, tiled=True)
    value_piece = lax.all_gather(w_value, "shard", axis=0, tiled=True)
    normalized_rows = (first_standardized * gain_fragment.astype(jnp.float32)).astype(jnp.bfloat16)
    joined = jnp.concatenate([query_piece, key_piece, value_piece], 1)
    result = (
        jnp.dot(normalized_rows, joined, preferred_element_type=jnp.float32),
        normalized_rows,
        gain_fragment.astype(jnp.float32),
    )
    folded = result
    projected, normed_one, first_norm_gain = (folded[0], folded[1], folded[2])
    queries = rotate(
        projected[:, :q_cols].reshape(rows, KV_HEADS, groups, HEAD_DIM),
        cosine[:, None, None, :],
        sine[:, None, None, :],
    ).astype(jnp.bfloat16)
    keys = rotate(
        projected[:, q_cols : q_cols + kv_cols].reshape(rows, KV_HEADS, HEAD_DIM),
        cosine[:, None, :],
        sine[:, None, :],
    ).astype(jnp.bfloat16)
    values = projected[:, q_cols + kv_cols :].reshape(rows, KV_HEADS, HEAD_DIM).astype(jnp.bfloat16)
    scores = scores_of(queries, keys, allowed)
    top = jnp.max(scores, axis=-1, keepdims=True)
    log_total = top + jnp.log(jnp.sum(jnp.exp(scores - top), axis=-1, keepdims=True))
    probs = jnp.exp(scores - log_total)
    probs_low = probs.astype(jnp.bfloat16)
    attn = (
        jnp.einsum("grqk,kgd->qgrd", probs_low, values, preferred_element_type=jnp.float32)
        .reshape(rows, q_cols)
        .astype(jnp.bfloat16)
    )
    part = attn
    result = (
        jnp.dot(
            part,
            lax.all_gather(w_out, "shard", axis=0, tiled=True),
            preferred_element_type=jnp.float32,
        ),
    )
    folded_out = result
    residual_hidden_state = layer_input_rows + folded_out[0]
    second_norm_factor = lax.rsqrt(
        jnp.mean(residual_hidden_state * residual_hidden_state, axis=1, keepdims=True) + norm_eps
    )
    second_standardized = residual_hidden_state * second_norm_factor
    gain_fragment = lax.all_gather(mlp_gain, "shard", axis=0, tiled=True)
    gate_piece = lax.all_gather(w_gate, "shard", axis=0, tiled=True)
    up_piece = lax.all_gather(w_up, "shard", axis=0, tiled=True)
    normalized_rows = (second_standardized * gain_fragment.astype(jnp.float32)).astype(jnp.bfloat16)
    joined = jnp.concatenate([gate_piece, up_piece], 1)
    result = (
        jnp.dot(normalized_rows, joined, preferred_element_type=jnp.float32),
        normalized_rows,
        gain_fragment.astype(jnp.float32),
    )
    folded_mlp = result
    gate = folded_mlp[0][:, :FF]
    up_value = folded_mlp[0][:, FF:]
    normed_two = folded_mlp[1]
    second_norm_gain = folded_mlp[2]
    sigma = jax.nn.sigmoid(gate)
    swish = gate * sigma
    inner = (swish * up_value).astype(jnp.bfloat16)
    part = inner
    result = (
        jnp.dot(
            part,
            lax.all_gather(w_down, "shard", axis=0, tiled=True),
            preferred_element_type=jnp.float32,
        ),
    )
    output = (residual_hidden_state + result[0]).astype(jnp.bfloat16).reshape(1, rows, width)
    grad_out = cotangent.reshape(rows, width)
    grad_down = lax.psum_scatter(
        contract_rows(inner, grad_out).astype(jnp.bfloat16),
        "shard",
        scatter_dimension=0,
        tiled=True,
    )
    down_full, gate_full, up_full = (
        lax.all_gather(w_down, "shard", axis=0, tiled=True),
        lax.all_gather(w_gate, "shard", axis=0, tiled=True),
        lax.all_gather(w_up, "shard", axis=0, tiled=True),
    )
    grad_inner = contract_cols(grad_out, down_full)
    grad_gate = (grad_inner * up_value * sigma * (1.0 + gate * (1.0 - sigma))).astype(jnp.bfloat16)
    grad_up = (grad_inner * swish).astype(jnp.bfloat16)
    grad_mlp = jnp.concatenate([grad_gate, grad_up], 1)
    mlp_shards = lax.psum_scatter(
        contract_rows(normed_two, grad_mlp).astype(jnp.bfloat16),
        "shard",
        scatter_dimension=0,
        tiled=True,
    ).astype(jnp.float32)
    second_norm_gradient = contract_cols(grad_gate, gate_full) + contract_cols(grad_up, up_full)
    second_gain_products = jnp.sum(second_norm_gradient * second_standardized, axis=0)
    hidden_gradient = grad_out.astype(jnp.float32) + norm_backward_step(
        second_norm_gradient * second_norm_gain, second_standardized, second_norm_factor
    )
    grad_hidden_low = hidden_gradient.astype(jnp.bfloat16)
    grad_out_proj = lax.psum_scatter(
        contract_rows(attn, grad_hidden_low).astype(jnp.bfloat16),
        "shard",
        scatter_dimension=0,
        tiled=True,
    )
    grad_attn = contract_cols(grad_hidden_low, lax.all_gather(w_out, "shard", axis=0, tiled=True))
    grad_attn = grad_attn.astype(jnp.bfloat16).reshape(rows, KV_HEADS, groups, HEAD_DIM)
    scores_again = scores_of(queries, keys, allowed)
    probs_again = jnp.exp(scores_again - log_total)
    probs_again_low = probs_again.astype(jnp.bfloat16)
    grad_probs = jnp.einsum("qgrd,kgd->grqk", grad_attn, values, preferred_element_type=jnp.float32)
    grad_values = jnp.einsum(
        "grqk,qgrd->kgd", probs_again_low, grad_attn, preferred_element_type=jnp.float32
    )
    grad_scores = (
        probs_again * (grad_probs - jnp.sum(grad_probs * probs_again, axis=-1, keepdims=True))
    ).astype(jnp.bfloat16)
    grad_queries = jnp.einsum(
        "grqk,kgd->qgrd", grad_scores, keys, preferred_element_type=jnp.float32
    ) * HEAD_DIM ** (-0.5)
    grad_keys = jnp.einsum(
        "grqk,qgrd->kgd", grad_scores, queries, preferred_element_type=jnp.float32
    ) * HEAD_DIM ** (-0.5)
    grad_queries = rotate(grad_queries, cosine[:, None, None, :], -sine[:, None, None, :]).reshape(
        rows, q_cols
    )
    grad_keys = rotate(grad_keys, cosine[:, None, :], -sine[:, None, :]).reshape(rows, kv_cols)
    grad_joined = jnp.concatenate(
        [
            grad_queries.astype(jnp.bfloat16),
            grad_keys.astype(jnp.bfloat16),
            grad_values.reshape(rows, kv_cols).astype(jnp.bfloat16),
        ],
        1,
    )
    qkv_shards = lax.psum_scatter(
        contract_rows(normed_one, grad_joined).astype(jnp.bfloat16),
        "shard",
        scatter_dimension=0,
        tiled=True,
    ).astype(jnp.float32)
    local_qkv = jnp.concatenate([w_query, w_key, w_value], 1)
    first_norm_gradient = contract_cols(
        grad_joined, lax.all_gather(local_qkv, "shard", axis=0, tiled=True)
    )
    first_gain_products = jnp.sum(first_norm_gradient * first_standardized, axis=0)
    input_gradient_rows = hidden_gradient + norm_backward_step(
        first_norm_gradient * first_norm_gain, first_standardized, first_norm_factor
    )
    input_grad = input_gradient_rows.astype(jnp.bfloat16).reshape(1, rows, width)
    gain_one_grad, gain_two_grad = (
        lax.psum_scatter(first_gain_products, "shard", scatter_dimension=0, tiled=True),
        lax.psum_scatter(second_gain_products, "shard", scatter_dimension=0, tiled=True),
    )
    summed = (
        lax.psum(gain_one_grad.astype(jnp.bfloat16), "rep").astype(jnp.float32),
        lax.psum(qkv_shards[:, :q_cols].astype(jnp.bfloat16), "rep").astype(jnp.float32),
        lax.psum(qkv_shards[:, q_cols : q_cols + kv_cols].astype(jnp.bfloat16), "rep").astype(
            jnp.float32
        ),
        lax.psum(qkv_shards[:, q_cols + kv_cols :].astype(jnp.bfloat16), "rep").astype(jnp.float32),
        lax.psum(grad_out_proj, "rep").astype(jnp.float32),
        lax.psum(gain_two_grad.astype(jnp.bfloat16), "rep").astype(jnp.float32),
        lax.psum(mlp_shards[:, :FF].astype(jnp.bfloat16), "rep").astype(jnp.float32),
        lax.psum(mlp_shards[:, FF:].astype(jnp.bfloat16), "rep").astype(jnp.float32),
        lax.psum(grad_down, "rep").astype(jnp.float32),
    )
    return (
        output,
        input_grad,
        summed[0],
        summed[1],
        summed[2],
        summed[3],
        summed[4],
        summed[5],
        summed[6],
        summed[7],
        summed[8],
    )


def solution(mesh):
    rep, shard = mesh.devices.shape
    if shard == KV_HEADS and rep % 2 == 0:
        fine = Mesh(np.asarray(mesh.devices).reshape(rep // 2, 2, shard), ("z", "core", "shard"))
        body, every = pieces, ("z", "core", "shard")
    else:
        fine, body, every = mesh, general, ("rep", "shard")
    seqs, vec, mat = P(every, None, None), P("shard"), P("shard", None)
    in_specs = (seqs, P(every, None), vec, mat, mat, mat, mat, vec, mat, mat, mat, seqs)
    out_specs = (seqs, seqs, vec, mat, mat, mat, mat, vec, mat, mat, mat)
    return jax.shard_map(body, mesh=fine, in_specs=in_specs, out_specs=out_specs, check_vma=False)
```

```python
import functools

import jax
import jax.numpy as jnp
import numpy as np
from jax import lax
from jax.experimental import pallas as pl
from jax.experimental.pallas import tpu as pltpu
from jax.sharding import Mesh
from jax.sharding import PartitionSpec as P

HEADS = 8
KV_HEADS = 4
HEAD_DIM = 256
FF = 8192

rope_base = 1000042.0
norm_eps = 1e-06
mask_fill = -1e30

BF = jnp.bfloat16
F32 = jnp.float32
MESH = pl.DeviceIdType.MESH
ANY = pl.BlockSpec(memory_space=pl.ANY)
VM = pl.BlockSpec(memory_space=pltpu.VMEM)
DMA = pltpu.SemaphoreType.DMA


def mm(a, b):
    return jnp.dot(a, b, preferred_element_type=F32)


def mm_tn(a, b):
    return lax.dot_general(a, b, (((0,), (0,)), ((), ())), preferred_element_type=F32)


def mm_nt(a, b):
    return lax.dot_general(a, b, (((1,), (1,)), ((), ())), preferred_element_type=F32)


def rotate(values, cosine, sine):
    half = values.shape[-1] // 2
    first = values[..., :half]
    second = values[..., half:]
    return jnp.concatenate([first * cosine - second * sine, second * cosine + first * sine], -1)


def norm_backward_step(grad_hat, normalized_rows, factor):
    return factor * (
        grad_hat - normalized_rows * jnp.mean(grad_hat * normalized_rows, axis=1, keepdims=True)
    )


class Place:
    def __init__(self):
        self.z = lax.axis_index("z")
        self.c = lax.axis_index("core")
        self.s = lax.axis_index("shard")

    def shard(self, d):
        s = self.s
        if d == 0:
            return s
        if d == 1:
            return s + 1 - 2 * lax.rem(s, 2)
        if d == 2:
            return lax.rem(s + 2, 4)
        return 3 - s

    def to(self, d):
        return {"shard": self.shard(d)}

    def sibling(self):
        return {"core": 1 - self.c}


def greet(ids):
    barrier = pltpu.get_barrier_semaphore()
    for d in ids:
        pl.semaphore_signal(barrier, inc=1, device_id=d, device_id_type=MESH)
    pl.semaphore_wait(barrier, len(ids))


def rcopy(src, dst, send, recv, dev):
    return pltpu.make_async_remote_copy(
        src_ref=src, dst_ref=dst, send_sem=send, recv_sem=recv, device_id=dev, device_id_type=MESH
    )


GATHER_SEMS = [DMA((6,)), DMA((6,)), DMA((7,)), DMA((7,)), DMA((1,))]


class Gather:
    def __init__(self, p, src, out, sems):
        self.p, self.src, self.out = p, src, out
        self.send, self.recv, self.csend, self.crecv, self.lsem = sems
        self.rows = src.shape[0]
        self.half = self.rows // 2

    def at(self, d, h, core=None):
        core = self.p.c if core is None else core
        row = (core * 4 + self.p.shard(d)) * self.rows
        if h is None:
            return self.out.at[pl.ds(row, self.rows)]
        return self.out.at[pl.ds(row + h * self.half, self.half)]

    def move(self, k):
        d, h, to = [(0, 0, 1), (0, 1, 2), (0, 1, 1), (0, 0, 2), (1, 0, 2), (2, 1, 1)][k]
        dst = self.at(d, h)
        src = self.src.at[pl.ds(h * self.half, self.half)] if d == 0 else dst
        return rcopy(src, dst, self.send.at[k], self.recv.at[k], self.p.to(to))

    def landed(self, k):
        d, h = [(1, 0), (2, 1), (1, 1), (2, 0), (3, 0), (3, 1)][k]
        return self.at(d, h)

    def pass_on(self, k):
        here = self.src if k == 6 else self.landed(k)
        there = self.at(0, None) if k == 6 else self.landed(k)
        return rcopy(here, there, self.csend.at[k], self.crecv.at[k], self.p.sibling())

    def arrived(self, k):
        ref = self.landed(k)
        rcopy(ref, ref, self.send.at[k], self.recv.at[k], self.p.to(1)).wait_recv()
        self.pass_on(k).start()

    def start(self):
        for k in range(4):
            self.move(k).start()
        self.pass_on(6).start()
        pltpu.make_async_copy(self.src, self.at(0, None), self.lsem.at[0]).start()

    def relay(self):
        for k in (0, 1):
            self.arrived(k)
            self.move(4 + k).start()

    def finish(self):
        for k in (2, 3, 4, 5):
            self.arrived(k)
        for k in range(6):
            self.move(k).wait_send()
        for k in range(7):
            self.pass_on(k).wait()
        pltpu.make_async_copy(self.src, self.at(0, None), self.lsem.at[0]).wait()


SCATTER_SEMS = [DMA((4,)), DMA((4,)), DMA((4,)), DMA((6,)), DMA((6,))]
ORDER = (3, 1, 2, 0)


def scatter_scratch(rows, width):
    half = rows // 2
    return [
        pltpu.VMEM((4, rows, width), BF),
        pltpu.VMEM((4, rows, width), BF),
        pltpu.VMEM((6, half, width), BF),
    ] + SCATTER_SEMS


class Scatter:
    def __init__(self, p, part, scratch):
        self.p, self.part = p, part
        self.own, self.got, self.slot, self.lsem, self.csend, self.crecv, self.send, self.recv = scratch
        self.rows = self.own.shape[1]
        self.half = self.rows // 2

    def block(self, core, d):
        return self.part.at[pl.ds((core * 4 + self.p.shard(d)) * self.rows, self.rows)]

    def local(self, d):
        return pltpu.make_async_copy(self.block(self.p.c, d), self.own.at[d], self.lsem.at[d])

    def swap(self, d):
        src = self.block(1 - self.p.c, d)
        return rcopy(src, self.got.at[d], self.csend.at[d], self.crecv.at[d], self.p.sibling())

    def rowsof(self, h):
        return pl.ds(h * self.half, self.half)

    def move(self, k):
        d, h, to = [(3, 0, 1), (3, 1, 2), (1, 0, 1), (2, 1, 2), (2, 0, 2), (1, 1, 1)][k]
        return rcopy(
            self.own.at[d, self.rowsof(h)], self.slot.at[k], self.send.at[k], self.recv.at[k], self.p.to(to)
        )

    def start(self):
        for d in ORDER:
            self.swap(d).start()
            self.local(d).start()

    def pair(self, d):
        self.swap(d).wait_recv()
        self.local(d).wait()
        self.own[d] = (self.own[d].astype(F32) + self.got[d].astype(F32)).astype(BF)

    def first(self):
        self.pair(3)
        self.move(0).start()
        self.move(1).start()
        self.pair(1)
        self.move(2).start()
        self.pair(2)
        self.move(3).start()
        self.pair(0)

    def relay(self):
        for k, d, h in ((0, 2, 0), (1, 1, 1)):
            self.move(k).wait_recv()
            r = self.rowsof(h)
            self.own[d, r] = (self.own[d, r].astype(F32) + self.slot[k].astype(F32)).astype(BF)
            self.move(4 + k).start()

    def total(self, h):
        near, far = (2, 4) if h == 0 else (3, 5)
        self.move(near).wait_recv()
        self.move(far).wait_recv()
        return (
            self.own[0, self.rowsof(h)].astype(F32)
            + self.slot[near].astype(F32)
            + self.slot[far].astype(F32)
        )

    def drain(self):
        for k in range(6):
            self.move(k).wait_send()
        for d in range(4):
            self.swap(d).wait_send()


def params(cid, mb):
    return pltpu.CompilerParams(
        collective_id=cid, has_side_effects=True, vmem_limit_bytes=mb * 2**20
    )


def plane_ids(p):
    return [p.to(1), p.to(2), p.to(3), p.sibling()]


class Columns:
    def __init__(self, p, sems):
        self.p = p
        self.send, self.recv, self.lsem = sems

    def cols(self, j, d, src, width):
        return src.at[:, pl.ds(pl.multiple_of(j * width, width), width)]

    def copy(self, k, d, src, dst):
        if d == 0:
            return pltpu.make_async_copy(src, dst, self.lsem.at[k])
        return rcopy(src, dst, self.send.at[k, d - 1], self.recv.at[k, d - 1], self.p.to(d))


def rows_at(ref, r, n, c0, width):
    return ref.at[pl.ds(r, n), pl.ds(c0, width)]


def enter_kernel(x_ref, wq_ref, wk_ref, wv_ref, xa_ref, wqkv_ref, *sems):
    p = Place()
    greet(plane_ids(p))
    ga = Gather(p, x_ref, xa_ref, sems[:5])
    co = Columns(p, sems[5:8])
    ga.start()
    part = wq_ref.shape[0]
    hd = HEAD_DIM

    def q_copy(d):
        src = co.cols(p.shard(d) * 2 + p.c, d, wq_ref, hd)
        return co.copy(0, d, src, rows_at(wqkv_ref, p.s * part, part, 0, hd))

    def kv_copy(d, w):
        src = co.cols(p.shard(d), d, w, hd)
        return co.copy(1, d, src, rows_at(wqkv_ref, p.s * part, part, hd, hd))

    for d in (3, 1, 2, 0):
        q_copy(d).start()

        @pl.when(p.c == 0)
        def _():
            kv_copy(d, wk_ref).start()

        @pl.when(p.c != 0)
        def _():
            kv_copy(d, wv_ref).start()

    ga.relay()
    ga.finish()
    for d in (3, 1, 2, 0):
        q_copy(d).wait()
        kv_copy(d, wk_ref).wait()


def enter(x, wq, wk, wv):
    rows, width = x.shape
    return pl.pallas_call(
        enter_kernel,
        out_shape=(
            jax.ShapeDtypeStruct((8 * rows, width), BF),
            jax.ShapeDtypeStruct((width, 2 * HEAD_DIM), BF),
        ),
        in_specs=[VM, ANY, ANY, ANY],
        out_specs=(ANY, ANY),
        scratch_shapes=GATHER_SEMS + [DMA((2, 3)), DMA((2, 3)), DMA((2,))],
        compiler_params=params(0, 16),
        name="enter",
    )(x, wq, wk, wv)


def middle_kernel(part_ref, x_ref, gain_ref, g_ref, wg_ref, wu_ref, h_ref, xn_ref, ga_ref, wgu_ref, xnb, *scr):
    p = Place()
    greet(plane_ids(p))
    sc = Scatter(p, part_ref, scr[:8])
    gx = Gather(p, xnb, xn_ref, scr[8:13])
    gg = Gather(p, g_ref, ga_ref, scr[13:18])
    co = Columns(p, scr[18:21])
    fb = wgu_ref.shape[1] // 2
    part = wg_ref.shape[0]
    sc.start()
    sc.first()

    def w_copy(k, d):
        w = wg_ref if k == 0 else wu_ref
        src = co.cols(p.shard(d) * 2 + p.c, d, w, fb)
        return co.copy(k, d, src, rows_at(wgu_ref, p.s * part, part, k * fb, fb))

    gg.start()
    sc.relay()
    gg.relay()
    for d in (3, 1, 2, 0):
        for k in (0, 1):
            w_copy(k, d).start()
    half = sc.half
    for h in (0, 1):
        r = pl.ds(h * half, half)
        res = x_ref[r].astype(F32) + sc.total(h)
        h_ref[r] = res
        f = lax.rsqrt(jnp.mean(res * res, axis=1, keepdims=True) + norm_eps)
        xnb[r] = (res * f * gain_ref[...]).astype(BF)
    gx.start()
    gx.relay()
    gg.finish()
    gx.finish()
    for d in (3, 1, 2, 0):
        for k in (0, 1):
            w_copy(k, d).wait()
    sc.drain()


def middle(part, x, gain2, g, wg, wu):
    rows, width = x.shape
    fb = wg.shape[1] // 8
    return pl.pallas_call(
        middle_kernel,
        out_shape=(
            jax.ShapeDtypeStruct((rows, width), F32),
            jax.ShapeDtypeStruct((8 * rows, width), BF),
            jax.ShapeDtypeStruct((8 * rows, width), BF),
            jax.ShapeDtypeStruct((width, 2 * fb), BF),
        ),
        in_specs=[ANY, VM, VM, VM, ANY, ANY],
        out_specs=(VM, ANY, ANY, ANY),
        scratch_shapes=[pltpu.VMEM((rows, width), BF)]
        + scatter_scratch(rows, width)
        + GATHER_SEMS * 2
        + [DMA((2, 3)), DMA((2, 3)), DMA((2,))],
        compiler_params=params(1, 48),
        name="middle",
    )(part, x, gain2, g, wg, wu)


def scatter_kernel(part_ref, out_ref, *scr):
    p = Place()
    greet(plane_ids(p)[:2] + [p.sibling()])
    sc = Scatter(p, part_ref, scr)
    sc.start()
    sc.first()
    sc.relay()
    for h in (0, 1):
        out_ref[pl.ds(h * sc.half, sc.half)] = sc.total(h)
    sc.drain()


def scatter(part, cid):
    rows, width = part.shape[0] // 8, part.shape[1]
    return pl.pallas_call(
        scatter_kernel,
        out_shape=jax.ShapeDtypeStruct((rows, width), F32),
        in_specs=[ANY],
        out_specs=VM,
        scratch_shapes=scatter_scratch(rows, width),
        compiler_params=params(cid, 32),
        name="scatter",
    )(part)


def gather_kernel(src_ref, out_ref, *sems):
    p = Place()
    greet(plane_ids(p)[:2] + [p.sibling()])
    ga = Gather(p, src_ref, out_ref, sems)
    ga.start()
    ga.relay()
    ga.finish()


def gather(src, cid):
    rows, width = src.shape
    return pl.pallas_call(
        gather_kernel,
        out_shape=jax.ShapeDtypeStruct((8 * rows, width), BF),
        in_specs=[VM],
        out_specs=ANY,
        scratch_shapes=GATHER_SEMS,
        compiler_params=params(cid, 16),
        name="gather",
    )(src)


CH = 64
DOWN, GU, OUT, QKV = range(4)


class Chain:
    def __init__(self, p, h, ins, outs, bufs, sems):
        self.p, self.h = p, h
        self.ins = ins
        self.gate, self.up, self.down, self.out, self.wq, self.wk, self.wv = outs
        self.buf, self.bufq = bufs
        self.rs_send, self.rs_recv, self.ag_send, self.ag_recv, self.cp_send, self.cp_recv, self.tsend = sems
        nz = lax.axis_size("z")
        self.nz = nz
        self.pos = nz - 1 - p.z if h == 0 else p.z
        self.step = -1 if h == 0 else 1

    def dev(self, by):
        return {"z": self.p.z + by}

    BASE = {DOWN: 0, GU: 8, OUT: 24, QKV: 26}

    def tick(self, kind, t):
        return self.BASE[kind] + t

    def shard_of(self, t):
        s, d = self.p.s, lax.rem(t, 4)
        one = s + 1 - 2 * lax.rem(s, 2)
        two = lax.rem(s + 2, 4)
        return jnp.where(d == 0, s, jnp.where(d == 1, one, jnp.where(d == 2, two, 3 - s)))

    def mine(self, kind, t):
        h = self.h
        if kind == DOWN:
            return self.ins[DOWN].at[pl.ds(h * 512 + t * CH, CH)]
        if kind == OUT:
            return self.ins[OUT].at[pl.ds(h * 128 + t * CH, CH)]
        row = self.shard_of(t) * 512 + h * 256
        if kind == QKV:
            return self.ins[QKV].at[pl.ds(row, 256)]
        return self.ins[GU].at[pl.ds(row + (t // 4) * CH, CH)]

    def slot(self, kind, t):
        return self.bufq.at[t] if kind == QKV else self.buf.at[self.tick(kind, t)]

    def rs_copy(self, kind, t, src):
        k = self.tick(kind, t)
        return rcopy(
            src, self.slot(kind, t), self.rs_send.at[k], self.rs_recv.at[k], self.dev(self.step)
        )

    def reduce(self, kind, t):
        first, last = self.pos == 0, self.pos == self.nz - 1

        @pl.when(first)
        def _():
            self.rs_copy(kind, t, self.mine(kind, t)).start()

        @pl.when(jnp.logical_not(first))
        def _():
            slot = self.slot(kind, t)
            self.rs_copy(kind, t, slot).wait_recv()
            slot[...] = (slot[...].astype(F32) + self.mine(kind, t)[...].astype(F32)).astype(BF)

        @pl.when(jnp.logical_and(jnp.logical_not(first), jnp.logical_not(last)))
        def _():
            self.rs_copy(kind, t, self.slot(kind, t)).start()

        @pl.when(last)
        def _():
            self.turn(kind, t)

    def pieces(self, kind, t, s, d_shard):
        h, c = self.h, self.p.c
        if kind == DOWN:
            return [(None, self.down.at[pl.ds(c * 1024 + h * 512 + t * CH, CH)])]
        if kind == OUT:
            return [(None, self.out.at[pl.ds(c * 256 + h * 128 + t * CH, CH)])]
        if kind == GU:
            r = h * 256 + (t // 4) * CH
            c0 = pl.multiple_of((s * 2 + c) * 1024, 1024)
            return [
                ((0, 1024), self.gate.at[pl.ds(r, CH), pl.ds(c0, 1024)]),
                ((1024, 1024), self.up.at[pl.ds(r, CH), pl.ds(c0, 1024)]),
            ]
        r = h * 256
        cq = pl.multiple_of((s * 2 + c) * 256, 256)
        return [((0, 256), self.wq.at[pl.ds(r, 256), pl.ds(cq, 256)])]

    def kv_piece(self, s, w):
        return w.at[pl.ds(self.h * 256, 256), pl.ds(pl.multiple_of(s * 256, 256), 256)]

    def turn(self, kind, t):
        slot = self.slot(kind, t)
        k = self.tick(kind, t)
        to = self.p.s if kind in (DOWN, OUT) else self.shard_of(t)

        def send(i, src, dst):
            if kind in (DOWN, OUT):
                pltpu.make_async_copy(src, dst, self.ag_recv.at[i, k]).start()
                return

            @pl.when(lax.rem(t, 4) == 0)
            def _():
                pltpu.make_async_copy(src, dst, self.ag_recv.at[i, k]).start()

            @pl.when(lax.rem(t, 4) != 0)
            def _():
                rcopy(src, dst, self.tsend.at[i, k], self.ag_recv.at[i, k], {"shard": to}).start()

        for i, (cols, dst) in enumerate(self.pieces(kind, t, self.p.s, to)):
            send(i, slot if cols is None else slot.at[:, pl.ds(*cols)], dst)
        if kind == QKV:
            src = slot.at[:, pl.ds(256, 256)]

            @pl.when(self.p.c == 0)
            def _():
                send(1, src, self.kv_piece(self.p.s, self.wk))

            @pl.when(self.p.c != 0)
            def _():
                send(1, src, self.kv_piece(self.p.s, self.wv))

    def spread_copy(self, i, k, ref):
        return rcopy(ref, ref, self.ag_send.at[i, k], self.ag_recv.at[i, k], self.dev(-self.step))

    def spread(self, kind, t):
        k = self.tick(kind, t)
        s = self.p.s if kind in (DOWN, OUT) else self.shard_of(t)

        def go(i, ref, wait=True):
            if wait:
                self.spread_copy(i, k, ref).wait_recv()

            @pl.when(self.pos > 0)
            def _():
                self.spread_copy(i, k, ref).start()

            rcopy(ref, ref, self.cp_send.at[i, k], self.cp_recv.at[i, k], self.p.sibling()).start()

        for i, (_, ref) in enumerate(self.pieces(kind, t, s, None)):
            go(i, ref)
        if kind == QKV:
            self.spread_copy(1, k, self.kv_piece(s, self.wk)).wait_recv()

            @pl.when(self.p.c == 0)
            def _():
                go(1, self.kv_piece(s, self.wk), False)

            @pl.when(self.p.c != 0)
            def _():
                go(1, self.kv_piece(s, self.wv), False)

    def drain_reduce(self, kind, t):
        k = self.tick(kind, t)

        @pl.when(self.pos < self.nz - 1)
        def _():
            self.rs_copy(kind, t, self.slot(kind, t)).wait_send()

        if kind in (GU, QKV):

            @pl.when(jnp.logical_and(self.pos == self.nz - 1, lax.rem(t, 4) != 0))
            def _():
                for i, (cols, dst) in enumerate(self.pieces(kind, t, self.p.s, None)):
                    src = self.slot(kind, t).at[:, pl.ds(*cols)]
                    rcopy(src, dst, self.tsend.at[i, k], self.ag_recv.at[i, k], self.p.to(1)).wait_send()
                if kind == QKV:
                    src = self.slot(kind, t).at[:, pl.ds(256, 256)]
                    dst = self.kv_piece(self.p.s, self.wk)
                    rcopy(src, dst, self.tsend.at[1, k], self.ag_recv.at[1, k], self.p.to(1)).wait_send()

    def drain_spread(self, kind, t):
        k = self.tick(kind, t)
        s = self.p.s if kind in (DOWN, OUT) else self.shard_of(t)
        refs = [ref for _, ref in self.pieces(kind, t, s, None)]
        if kind == QKV:
            refs.append(self.kv_piece(s, self.wk))
        for i, ref in enumerate(refs):

            @pl.when(self.pos > 0)
            def _():
                self.spread_copy(i, k, ref).wait_send()

            rcopy(ref, ref, self.cp_send.at[i, k], self.cp_recv.at[i, k], self.p.sibling()).wait()


N_TICKS = 30
CHAIN_SEMS = [
    DMA((N_TICKS,)),
    DMA((N_TICKS,)),
    DMA((2, N_TICKS)),
    DMA((2, N_TICKS)),
    DMA((2, N_TICKS)),
    DMA((2, N_TICKS)),
    DMA((2, N_TICKS)),
]


def z_neighbours_enter(p):
    barrier = pltpu.get_barrier_semaphore()
    nz = lax.axis_size("z")
    for d in plane_ids(p):
        pl.semaphore_signal(barrier, inc=1, device_id=d, device_id_type=MESH)

    @pl.when(p.z > 0)
    def _():
        pl.semaphore_signal(barrier, inc=1, device_id={"z": p.z - 1}, device_id_type=MESH)

    @pl.when(p.z < nz - 1)
    def _():
        pl.semaphore_signal(barrier, inc=1, device_id={"z": p.z + 1}, device_id_type=MESH)

    ends = jnp.logical_or(p.z == 0, p.z == nz - 1)
    pl.semaphore_wait(barrier, jnp.where(ends, 5, 6))


def loop(lo, hi, body):
    def step(t, _):
        body(t)
        return 0

    lax.fori_loop(lo, hi, step, 0)


COUNT = {DOWN: 8, GU: 16, OUT: 2, QKV: 4}


SKEW, TURN = 2, 3


def between(i, lo, hi):
    return jnp.logical_and(i >= lo, i < hi)


class Both:
    def __init__(self, p, ins, outs, bufs, sems):
        n = len(CHAIN_SEMS)
        self.chains = [
            Chain(p, h, ins, outs, (bufs[h], bufs[2 + h]), sems[h * n : h * n + n]) for h in (0, 1)
        ]
        self.line = SKEW * (lax.axis_size("z") - 1)
        self.lag = self.line * 2 + TURN

    def each(self, i, lo, hi, act):
        for kind, n in COUNT.items():
            base = Chain.BASE[kind]
            a, b = max(lo, base), min(hi, base + n)
            if a < b:

                @pl.when(between(i, a, b))
                def _():
                    act(kind, i - base)

    def tick(self, t, red, spr):
        for ch in self.chains:
            if red[0] < red[1]:
                self.each(t - SKEW * ch.pos, *red, ch.reduce)
        for ch in self.chains:
            if spr[0] < spr[1]:
                self.each(t - self.lag + SKEW * ch.pos, *spr, ch.spread)

    def drain(self, red, spr):
        def body(i):
            for ch in self.chains:
                if red[0] < red[1]:
                    self.each(i, *red, ch.drain_reduce)
                if spr[0] < spr[1]:
                    self.each(i, *spr, ch.drain_spread)

        loop(0, N_TICKS, body)


def sums_kernel(gd_ref, ggu_ref, go_ref, gqkv_ref, gate, up, down, out, wq, wk, wv, *scr):
    p = Place()
    z_neighbours_enter(p)
    ins = (gd_ref, ggu_ref, go_ref, gqkv_ref)
    outs = (gate, up, down, out, wq, wk, wv)
    both = Both(p, ins, outs, scr[:4], scr[4:])
    every = (0, N_TICKS)
    loop(0, N_TICKS + both.lag, lambda t: both.tick(t, every, every))
    both.drain(every, every)


def sums(g_down, g_gu, g_out, g_qkv, part, ff):
    width = g_down.shape[1]
    shapes = [(part, ff), (part, ff), (ff // 4, width), (part, width), (part, width), (part, 1024), (part, 1024)]
    return pl.pallas_call(
        sums_kernel,
        out_shape=tuple(jax.ShapeDtypeStruct(s, BF) for s in shapes),
        in_specs=[VM] * 4,
        out_specs=(ANY,) * 7,
        scratch_shapes=[
            pltpu.VMEM((26, CH, width), BF),
            pltpu.VMEM((26, CH, width), BF),
            pltpu.VMEM((4, 256, 512), BF),
            pltpu.VMEM((4, 256, 512), BF),
        ]
        + CHAIN_SEMS * 2,
        compiler_params=params(9, 56),
        name="sums",
    )(g_down, g_gu, g_out, g_qkv)


def pieces(
    tokens,
    segment_ids,
    attn_gain,
    w_query,
    w_key,
    w_value,
    w_out,
    mlp_gain,
    w_gate,
    w_up,
    w_down,
    cotangent,
):
    rows, width = tokens.shape[1], tokens.shape[2]
    core = lax.axis_index("core")
    nc, ns = lax.axis_size("core"), lax.axis_size("shard")
    hd = HEAD_DIM
    ff = w_gate.shape[1]
    fb = ff // (nc * ns)
    part = width // ns

    x = tokens.reshape(rows, width)
    g = cotangent.reshape(rows, width)
    seg = lax.all_gather(segment_ids, ("core", "shard"), axis=0, tiled=True)
    gains = lax.all_gather(jnp.stack([attn_gain, mlp_gain]), "shard", axis=1, tiled=True)
    gains = gains.astype(F32)
    gain1, gain2 = gains[0:1], gains[1:2]
    nseq = seg.shape[0]
    wo = lax.dynamic_slice_in_dim(w_out, core * hd, hd, 0)
    wd = lax.dynamic_slice_in_dim(w_down, core * fb, fb, 0)

    x_all, wqkv = enter(x, w_query, w_key, w_value)

    iota = jnp.arange(rows, dtype=jnp.int32)
    same = seg[:, :, None] == seg[:, None, :]
    allowed = same & (iota[:, None] >= iota[None, :])[None]
    starts = jnp.sum((seg[:, None, :] < seg[:, :, None]).astype(jnp.int32), axis=2)
    positions = (iota[None, :] - starts).astype(F32)
    half = hd // 2
    inv_freq = rope_base ** (-(jnp.arange(half, dtype=F32) * 2.0 / hd))
    angles = positions[..., None] * inv_freq
    cosine, sine = jnp.cos(angles), jnp.sin(angles)

    xf_all = x_all.astype(F32)
    f1_all = lax.rsqrt(jnp.mean(xf_all * xf_all, axis=1, keepdims=True) + norm_eps)
    xn1 = (xf_all * f1_all * gain1).astype(BF)
    qkv = mm(xn1, wqkv).reshape(nseq, rows, 2 * hd)
    q = rotate(qkv[..., :hd], cosine, sine).astype(BF)
    kv_lin = qkv[..., hd:]
    kv_mine = jnp.where(core == 0, rotate(kv_lin, cosine, sine), kv_lin).astype(BF)
    swap = [(i, nc - 1 - i) for i in range(nc)]
    kv_other = lax.ppermute(kv_mine, "core", swap)
    k = jnp.where(core == 0, kv_mine, kv_other)
    v = jnp.where(core == 0, kv_other, kv_mine)
    scale = hd ** (-0.5)
    scores = jnp.einsum("bqd,bkd->bqk", q, k, preferred_element_type=F32) * scale
    scores = jnp.where(allowed, scores, mask_fill)
    top = jnp.max(scores, axis=-1, keepdims=True)
    ex = jnp.exp(scores - top)
    probs = ex / jnp.sum(ex, axis=-1, keepdims=True)
    pb = probs.astype(BF)
    attn = jnp.einsum("bqk,bkd->bqd", pb, v, preferred_element_type=F32).astype(BF)
    attn = attn.reshape(nseq * rows, hd)

    h, xn2, g_all, wgu = middle(mm(attn, wo).astype(BF), x, gain2, g, w_gate, w_up)

    xf = x.astype(F32)
    f2 = lax.rsqrt(jnp.mean(h * h, axis=1, keepdims=True) + norm_eps)
    xhat2 = h * f2
    gu = mm(xn2, wgu)
    gate, up = gu[:, :fb], gu[:, fb:]
    sigma = jax.nn.sigmoid(gate)
    swish = gate * sigma
    hid = (swish * up).astype(BF)
    g_down = mm_tn(hid, g_all).astype(BF)
    dhid = mm_nt(g_all, wd)
    dgate = (dhid * up * sigma * (1.0 + gate * (1.0 - sigma))).astype(BF)
    dup = (dhid * swish).astype(BF)
    dgu = jnp.concatenate([dgate, dup], 1)
    g_gu = mm_tn(xn2, dgu).astype(BF)
    dxn2 = scatter(mm_nt(dgu, wgu).astype(BF), 2)
    gain2_g = jnp.sum(dxn2 * xhat2, axis=0)
    dh = g.astype(F32) + norm_backward_step(dxn2 * gain2, xhat2, f2)
    dhb = gather(dh.astype(BF), 3)
    d_sum = scatter(mm(hid, wd).astype(BF), 4)
    output = (h + d_sum).astype(BF).reshape(1, rows, width)
    g_out = mm_tn(attn, dhb).astype(BF)
    dattn = mm_nt(dhb, wo).astype(BF).reshape(nseq, rows, hd)
    dp = jnp.einsum("bqd,bkd->bqk", dattn, v, preferred_element_type=F32)
    dv = jnp.einsum("bqk,bqd->bkd", pb, dattn, preferred_element_type=F32)
    ds = (probs * (dp - jnp.sum(dp * probs, axis=-1, keepdims=True))).astype(BF)
    dq = jnp.einsum("bqk,bkd->bqd", ds, k, preferred_element_type=F32) * scale
    dk = jnp.einsum("bqk,bqd->bkd", ds, q, preferred_element_type=F32) * scale
    dq = rotate(dq, cosine, -sine).astype(BF)
    dk = rotate(dk, cosine, -sine)
    mine = jnp.where(core == 0, dk, dv)
    other = jnp.where(core == 0, dv, dk).astype(BF)
    dkv = (mine + lax.ppermute(other, "core", swap).astype(F32)).astype(BF)
    dqkv = jnp.concatenate([dq, dkv], -1).reshape(nseq * rows, 2 * hd)
    g_qkv = mm_tn(xn1, dqkv).astype(BF)
    dxn1 = scatter(mm_nt(dqkv, wqkv).astype(BF), 5)
    f1 = lax.rsqrt(jnp.mean(xf * xf, axis=1, keepdims=True) + norm_eps)
    xhat1 = xf * f1
    gain1_g = jnp.sum(dxn1 * xhat1, axis=0)
    input_grad = (dh + norm_backward_step(dxn1 * gain1, xhat1, f1)).astype(BF)
    input_grad = input_grad.reshape(1, rows, width)

    gain_g = lax.psum(jnp.stack([gain1_g, gain2_g]), ("z", "core", "shard"))
    mine_s = lax.axis_index("shard") * part
    gain_g = lax.dynamic_slice_in_dim(gain_g, mine_s, part, 1)

    gate_g, up_g, down_g, out_g, wq_g, wk_g, wv_g = sums(g_down, g_gu, g_out, g_qkv, part, ff)
    return (
        output,
        input_grad,
        gain_g[0],
        wq_g.astype(F32),
        wk_g.astype(F32),
        wv_g.astype(F32),
        out_g.astype(F32),
        gain_g[1],
        gate_g.astype(F32),
        up_g.astype(F32),
        down_g.astype(F32),
    )


def contract_rows(left, right):
    return lax.dot_general(
        left, right, (((0,), (0,)), ((), ())), preferred_element_type=jnp.float32
    )


def contract_cols(left, right):
    return lax.dot_general(
        left, right, (((1,), (1,)), ((), ())), preferred_element_type=jnp.float32
    )


def scores_of(queries, keys, allowed):
    raw = jnp.einsum(
        "qgrd,kgd->grqk", queries, keys, preferred_element_type=jnp.float32
    ) * HEAD_DIM ** (-0.5)
    return jnp.where(allowed, raw, mask_fill)


def general(
    tokens,
    segment_ids,
    attn_gain,
    w_query,
    w_key,
    w_value,
    w_out,
    mlp_gain,
    w_gate,
    w_up,
    w_down,
    cotangent,
):
    rows = tokens.shape[1]
    width = tokens.shape[2]
    groups = HEADS // KV_HEADS
    q_cols = HEADS * HEAD_DIM
    kv_cols = KV_HEADS * HEAD_DIM
    layer_input_rows = tokens.reshape(rows, width).astype(jnp.float32)
    segments = segment_ids.reshape(rows)
    iota = jnp.arange(rows, dtype=jnp.int32)
    starts = jnp.sum((segments[None, :] < segments[:, None]).astype(jnp.int32), axis=1)
    positions = (iota - starts).astype(jnp.float32)
    allowed = (segments[:, None] == segments[None, :]) & (iota[:, None] >= iota[None, :])
    half = HEAD_DIM // 2
    inv_freq = rope_base ** (-(jnp.arange(half, dtype=jnp.float32) * 2.0 / HEAD_DIM))
    angles = positions[:, None] * inv_freq
    cosine = jnp.cos(angles)
    sine = jnp.sin(angles)
    first_norm_factor = lax.rsqrt(
        jnp.mean(layer_input_rows * layer_input_rows, axis=1, keepdims=True) + norm_eps
    )
    first_standardized = layer_input_rows * first_norm_factor
    gain_fragment = lax.all_gather(attn_gain, "shard", axis=0, tiled=True)
    query_piece = lax.all_gather(w_query, "shard", axis=0, tiled=True)
    key_piece = lax.all_gather(w_key, "shard", axis=0, tiled=True)
    value_piece = lax.all_gather(w_value, "shard", axis=0, tiled=True)
    normalized_rows = (first_standardized * gain_fragment.astype(jnp.float32)).astype(jnp.bfloat16)
    joined = jnp.concatenate([query_piece, key_piece, value_piece], 1)
    result = (
        jnp.dot(normalized_rows, joined, preferred_element_type=jnp.float32),
        normalized_rows,
        gain_fragment.astype(jnp.float32),
    )
    folded = result
    projected, normed_one, first_norm_gain = (folded[0], folded[1], folded[2])
    queries = rotate(
        projected[:, :q_cols].reshape(rows, KV_HEADS, groups, HEAD_DIM),
        cosine[:, None, None, :],
        sine[:, None, None, :],
    ).astype(jnp.bfloat16)
    keys = rotate(
        projected[:, q_cols : q_cols + kv_cols].reshape(rows, KV_HEADS, HEAD_DIM),
        cosine[:, None, :],
        sine[:, None, :],
    ).astype(jnp.bfloat16)
    values = projected[:, q_cols + kv_cols :].reshape(rows, KV_HEADS, HEAD_DIM).astype(jnp.bfloat16)
    scores = scores_of(queries, keys, allowed)
    top = jnp.max(scores, axis=-1, keepdims=True)
    log_total = top + jnp.log(jnp.sum(jnp.exp(scores - top), axis=-1, keepdims=True))
    probs = jnp.exp(scores - log_total)
    probs_low = probs.astype(jnp.bfloat16)
    attn = (
        jnp.einsum("grqk,kgd->qgrd", probs_low, values, preferred_element_type=jnp.float32)
        .reshape(rows, q_cols)
        .astype(jnp.bfloat16)
    )
    part = attn
    result = (
        jnp.dot(
            part,
            lax.all_gather(w_out, "shard", axis=0, tiled=True),
            preferred_element_type=jnp.float32,
        ),
    )
    folded_out = result
    residual_hidden_state = layer_input_rows + folded_out[0]
    second_norm_factor = lax.rsqrt(
        jnp.mean(residual_hidden_state * residual_hidden_state, axis=1, keepdims=True) + norm_eps
    )
    second_standardized = residual_hidden_state * second_norm_factor
    gain_fragment = lax.all_gather(mlp_gain, "shard", axis=0, tiled=True)
    gate_piece = lax.all_gather(w_gate, "shard", axis=0, tiled=True)
    up_piece = lax.all_gather(w_up, "shard", axis=0, tiled=True)
    normalized_rows = (second_standardized * gain_fragment.astype(jnp.float32)).astype(jnp.bfloat16)
    joined = jnp.concatenate([gate_piece, up_piece], 1)
    result = (
        jnp.dot(normalized_rows, joined, preferred_element_type=jnp.float32),
        normalized_rows,
        gain_fragment.astype(jnp.float32),
    )
    folded_mlp = result
    gate = folded_mlp[0][:, :FF]
    up_value = folded_mlp[0][:, FF:]
    normed_two = folded_mlp[1]
    second_norm_gain = folded_mlp[2]
    sigma = jax.nn.sigmoid(gate)
    swish = gate * sigma
    inner = (swish * up_value).astype(jnp.bfloat16)
    part = inner
    result = (
        jnp.dot(
            part,
            lax.all_gather(w_down, "shard", axis=0, tiled=True),
            preferred_element_type=jnp.float32,
        ),
    )
    output = (residual_hidden_state + result[0]).astype(jnp.bfloat16).reshape(1, rows, width)
    grad_out = cotangent.reshape(rows, width)
    grad_down = lax.psum_scatter(
        contract_rows(inner, grad_out).astype(jnp.bfloat16),
        "shard",
        scatter_dimension=0,
        tiled=True,
    )
    down_full, gate_full, up_full = (
        lax.all_gather(w_down, "shard", axis=0, tiled=True),
        lax.all_gather(w_gate, "shard", axis=0, tiled=True),
        lax.all_gather(w_up, "shard", axis=0, tiled=True),
    )
    grad_inner = contract_cols(grad_out, down_full)
    grad_gate = (grad_inner * up_value * sigma * (1.0 + gate * (1.0 - sigma))).astype(jnp.bfloat16)
    grad_up = (grad_inner * swish).astype(jnp.bfloat16)
    grad_mlp = jnp.concatenate([grad_gate, grad_up], 1)
    mlp_shards = lax.psum_scatter(
        contract_rows(normed_two, grad_mlp).astype(jnp.bfloat16),
        "shard",
        scatter_dimension=0,
        tiled=True,
    ).astype(jnp.float32)
    second_norm_gradient = contract_cols(grad_gate, gate_full) + contract_cols(grad_up, up_full)
    second_gain_products = jnp.sum(second_norm_gradient * second_standardized, axis=0)
    hidden_gradient = grad_out.astype(jnp.float32) + norm_backward_step(
        second_norm_gradient * second_norm_gain, second_standardized, second_norm_factor
    )
    grad_hidden_low = hidden_gradient.astype(jnp.bfloat16)
    grad_out_proj = lax.psum_scatter(
        contract_rows(attn, grad_hidden_low).astype(jnp.bfloat16),
        "shard",
        scatter_dimension=0,
        tiled=True,
    )
    grad_attn = contract_cols(grad_hidden_low, lax.all_gather(w_out, "shard", axis=0, tiled=True))
    grad_attn = grad_attn.astype(jnp.bfloat16).reshape(rows, KV_HEADS, groups, HEAD_DIM)
    scores_again = scores_of(queries, keys, allowed)
    probs_again = jnp.exp(scores_again - log_total)
    probs_again_low = probs_again.astype(jnp.bfloat16)
    grad_probs = jnp.einsum("qgrd,kgd->grqk", grad_attn, values, preferred_element_type=jnp.float32)
    grad_values = jnp.einsum(
        "grqk,qgrd->kgd", probs_again_low, grad_attn, preferred_element_type=jnp.float32
    )
    grad_scores = (
        probs_again * (grad_probs - jnp.sum(grad_probs * probs_again, axis=-1, keepdims=True))
    ).astype(jnp.bfloat16)
    grad_queries = jnp.einsum(
        "grqk,kgd->qgrd", grad_scores, keys, preferred_element_type=jnp.float32
    ) * HEAD_DIM ** (-0.5)
    grad_keys = jnp.einsum(
        "grqk,qgrd->kgd", grad_scores, queries, preferred_element_type=jnp.float32
    ) * HEAD_DIM ** (-0.5)
    grad_queries = rotate(grad_queries, cosine[:, None, None, :], -sine[:, None, None, :]).reshape(
        rows, q_cols
    )
    grad_keys = rotate(grad_keys, cosine[:, None, :], -sine[:, None, :]).reshape(rows, kv_cols)
    grad_joined = jnp.concatenate(
        [
            grad_queries.astype(jnp.bfloat16),
            grad_keys.astype(jnp.bfloat16),
            grad_values.reshape(rows, kv_cols).astype(jnp.bfloat16),
        ],
        1,
    )
    qkv_shards = lax.psum_scatter(
        contract_rows(normed_one, grad_joined).astype(jnp.bfloat16),
        "shard",
        scatter_dimension=0,
        tiled=True,
    ).astype(jnp.float32)
    local_qkv = jnp.concatenate([w_query, w_key, w_value], 1)
    first_norm_gradient = contract_cols(
        grad_joined, lax.all_gather(local_qkv, "shard", axis=0, tiled=True)
    )
    first_gain_products = jnp.sum(first_norm_gradient * first_standardized, axis=0)
    input_gradient_rows = hidden_gradient + norm_backward_step(
        first_norm_gradient * first_norm_gain, first_standardized, first_norm_factor
    )
    input_grad = input_gradient_rows.astype(jnp.bfloat16).reshape(1, rows, width)
    gain_one_grad, gain_two_grad = (
        lax.psum_scatter(first_gain_products, "shard", scatter_dimension=0, tiled=True),
        lax.psum_scatter(second_gain_products, "shard", scatter_dimension=0, tiled=True),
    )
    summed = (
        lax.psum(gain_one_grad.astype(jnp.bfloat16), "rep").astype(jnp.float32),
        lax.psum(qkv_shards[:, :q_cols].astype(jnp.bfloat16), "rep").astype(jnp.float32),
        lax.psum(qkv_shards[:, q_cols : q_cols + kv_cols].astype(jnp.bfloat16), "rep").astype(
            jnp.float32
        ),
        lax.psum(qkv_shards[:, q_cols + kv_cols :].astype(jnp.bfloat16), "rep").astype(jnp.float32),
        lax.psum(grad_out_proj, "rep").astype(jnp.float32),
        lax.psum(gain_two_grad.astype(jnp.bfloat16), "rep").astype(jnp.float32),
        lax.psum(mlp_shards[:, :FF].astype(jnp.bfloat16), "rep").astype(jnp.float32),
        lax.psum(mlp_shards[:, FF:].astype(jnp.bfloat16), "rep").astype(jnp.float32),
        lax.psum(grad_down, "rep").astype(jnp.float32),
    )
    return (
        output,
        input_grad,
        summed[0],
        summed[1],
        summed[2],
        summed[3],
        summed[4],
        summed[5],
        summed[6],
        summed[7],
        summed[8],
    )


def solution(mesh):
    rep, shard = mesh.devices.shape
    if shard == KV_HEADS and rep % 2 == 0:
        fine = Mesh(np.asarray(mesh.devices).reshape(rep // 2, 2, shard), ("z", "core", "shard"))
        body, every = pieces, ("z", "core", "shard")
    else:
        fine, body, every = mesh, general, ("rep", "shard")
    seqs, vec, mat = P(every, None, None), P("shard"), P("shard", None)
    in_specs = (seqs, P(every, None), vec, mat, mat, mat, mat, vec, mat, mat, mat, seqs)
    out_specs = (seqs, seqs, vec, mat, mat, mat, mat, vec, mat, mat, mat)
    return jax.shard_map(body, mesh=fine, in_specs=in_specs, out_specs=out_specs, check_vma=False)
```

```python
import functools

import jax
import jax.numpy as jnp
import numpy as np
from jax import lax
from jax.experimental import pallas as pl
from jax.experimental.pallas import tpu as pltpu
from jax.sharding import Mesh
from jax.sharding import PartitionSpec as P

HEADS = 8
KV_HEADS = 4
HEAD_DIM = 256
FF = 8192

rope_base = 1000042.0
norm_eps = 1e-06
mask_fill = -1e30

BF = jnp.bfloat16
F32 = jnp.float32
MESH = pl.DeviceIdType.MESH
ANY = pl.BlockSpec(memory_space=pl.ANY)
VM = pl.BlockSpec(memory_space=pltpu.VMEM)
DMA = pltpu.SemaphoreType.DMA


def mm(a, b):
    return jnp.dot(a, b, preferred_element_type=F32)


def mm_tn(a, b):
    return lax.dot_general(a, b, (((0,), (0,)), ((), ())), preferred_element_type=F32)


def mm_nt(a, b):
    return lax.dot_general(a, b, (((1,), (1,)), ((), ())), preferred_element_type=F32)


def rotate(values, cosine, sine):
    half = values.shape[-1] // 2
    first = values[..., :half]
    second = values[..., half:]
    return jnp.concatenate([first * cosine - second * sine, second * cosine + first * sine], -1)


def norm_backward_step(grad_hat, normalized_rows, factor):
    return factor * (
        grad_hat - normalized_rows * jnp.mean(grad_hat * normalized_rows, axis=1, keepdims=True)
    )


class Place:
    def __init__(self):
        self.z = lax.axis_index("z")
        self.c = lax.axis_index("core")
        self.s = lax.axis_index("shard")

    def shard(self, d):
        s = self.s
        if d == 0:
            return s
        if d == 1:
            return s + 1 - 2 * lax.rem(s, 2)
        if d == 2:
            return lax.rem(s + 2, 4)
        return 3 - s

    def to(self, d):
        return {"shard": self.shard(d)}

    def sibling(self):
        return {"core": 1 - self.c}


def greet(ids):
    barrier = pltpu.get_barrier_semaphore()
    for d in ids:
        pl.semaphore_signal(barrier, inc=1, device_id=d, device_id_type=MESH)
    pl.semaphore_wait(barrier, len(ids))


def rcopy(src, dst, send, recv, dev):
    return pltpu.make_async_remote_copy(
        src_ref=src, dst_ref=dst, send_sem=send, recv_sem=recv, device_id=dev, device_id_type=MESH
    )


GATHER_SEMS = [DMA((6,)), DMA((6,)), DMA((7,)), DMA((7,)), DMA((1,))]


class Gather:
    def __init__(self, p, src, out, sems):
        self.p, self.src, self.out = p, src, out
        self.send, self.recv, self.csend, self.crecv, self.lsem = sems
        self.rows = src.shape[0]
        self.half = self.rows // 2

    def at(self, d, h, core=None):
        core = self.p.c if core is None else core
        row = (core * 4 + self.p.shard(d)) * self.rows
        if h is None:
            return self.out.at[pl.ds(row, self.rows)]
        return self.out.at[pl.ds(row + h * self.half, self.half)]

    def move(self, k):
        d, h, to = [(0, 0, 1), (0, 1, 2), (0, 1, 1), (0, 0, 2), (1, 0, 2), (2, 1, 1)][k]
        dst = self.at(d, h)
        src = self.src.at[pl.ds(h * self.half, self.half)] if d == 0 else dst
        return rcopy(src, dst, self.send.at[k], self.recv.at[k], self.p.to(to))

    def landed(self, k):
        d, h = [(1, 0), (2, 1), (1, 1), (2, 0), (3, 0), (3, 1)][k]
        return self.at(d, h)

    def pass_on(self, k):
        here = self.src if k == 6 else self.landed(k)
        there = self.at(0, None) if k == 6 else self.landed(k)
        return rcopy(here, there, self.csend.at[k], self.crecv.at[k], self.p.sibling())

    def arrived(self, k):
        ref = self.landed(k)
        rcopy(ref, ref, self.send.at[k], self.recv.at[k], self.p.to(1)).wait_recv()
        self.pass_on(k).start()

    def start(self):
        for k in range(4):
            self.move(k).start()
        self.pass_on(6).start()
        pltpu.make_async_copy(self.src, self.at(0, None), self.lsem.at[0]).start()

    def relay(self):
        for k in (0, 1):
            self.arrived(k)
            self.move(4 + k).start()

    def finish(self):
        for k in (2, 3, 4, 5):
            self.arrived(k)
        for k in range(6):
            self.move(k).wait_send()
        for k in range(7):
            self.pass_on(k).wait()
        pltpu.make_async_copy(self.src, self.at(0, None), self.lsem.at[0]).wait()


SCATTER_SEMS = [DMA((4,)), DMA((4,)), DMA((4,)), DMA((6,)), DMA((6,))]
ORDER = (3, 1, 2, 0)


def scatter_scratch(rows, width):
    half = rows // 2
    return [
        pltpu.VMEM((4, rows, width), BF),
        pltpu.VMEM((4, rows, width), BF),
        pltpu.VMEM((6, half, width), BF),
    ] + SCATTER_SEMS


class Scatter:
    def __init__(self, p, part, scratch):
        self.p, self.part = p, part
        self.own, self.got, self.slot, self.lsem, self.csend, self.crecv, self.send, self.recv = scratch
        self.rows = self.own.shape[1]
        self.half = self.rows // 2

    def block(self, core, d):
        return self.part.at[pl.ds((core * 4 + self.p.shard(d)) * self.rows, self.rows)]

    def local(self, d):
        return pltpu.make_async_copy(self.block(self.p.c, d), self.own.at[d], self.lsem.at[d])

    def swap(self, d):
        src = self.block(1 - self.p.c, d)
        return rcopy(src, self.got.at[d], self.csend.at[d], self.crecv.at[d], self.p.sibling())

    def rowsof(self, h):
        return pl.ds(h * self.half, self.half)

    def move(self, k):
        d, h, to = [(3, 0, 1), (3, 1, 2), (1, 0, 1), (2, 1, 2), (2, 0, 2), (1, 1, 1)][k]
        return rcopy(
            self.own.at[d, self.rowsof(h)], self.slot.at[k], self.send.at[k], self.recv.at[k], self.p.to(to)
        )

    def start(self):
        for d in ORDER:
            self.swap(d).start()
            self.local(d).start()

    def pair(self, d):
        self.swap(d).wait_recv()
        self.local(d).wait()
        self.own[d] = (self.own[d].astype(F32) + self.got[d].astype(F32)).astype(BF)

    def first(self):
        self.pair(3)
        self.move(0).start()
        self.move(1).start()
        self.pair(1)
        self.move(2).start()
        self.pair(2)
        self.move(3).start()
        self.pair(0)

    def relay(self):
        for k, d, h in ((0, 2, 0), (1, 1, 1)):
            self.move(k).wait_recv()
            r = self.rowsof(h)
            self.own[d, r] = (self.own[d, r].astype(F32) + self.slot[k].astype(F32)).astype(BF)
            self.move(4 + k).start()

    def total(self, h):
        near, far = (2, 4) if h == 0 else (3, 5)
        self.move(near).wait_recv()
        self.move(far).wait_recv()
        return (
            self.own[0, self.rowsof(h)].astype(F32)
            + self.slot[near].astype(F32)
            + self.slot[far].astype(F32)
        )

    def drain(self):
        for k in range(6):
            self.move(k).wait_send()
        for d in range(4):
            self.swap(d).wait_send()


def params(cid, mb):
    return pltpu.CompilerParams(
        collective_id=cid, has_side_effects=True, vmem_limit_bytes=mb * 2**20
    )


def plane_ids(p):
    return [p.to(1), p.to(2), p.to(3), p.sibling()]


class Columns:
    def __init__(self, p, sems):
        self.p = p
        self.send, self.recv, self.lsem = sems

    def cols(self, j, d, src, width):
        return src.at[:, pl.ds(pl.multiple_of(j * width, width), width)]

    def copy(self, k, d, src, dst):
        if d == 0:
            return pltpu.make_async_copy(src, dst, self.lsem.at[k])
        return rcopy(src, dst, self.send.at[k, d - 1], self.recv.at[k, d - 1], self.p.to(d))


def rows_at(ref, r, n, c0, width):
    return ref.at[pl.ds(r, n), pl.ds(c0, width)]


def enter_kernel(x_ref, seg_ref, gain_ref, wq_ref, wk_ref, wv_ref, xa_ref, wqkv_ref, sega_ref, gaina_ref, *sems):
    p = Place()
    others = [(0, 1)] + [(d, o) for d in (1, 2, 3) for o in (0, 1)]

    def dev(d, o):
        return {"core": 1 - p.c if o else p.c, "shard": p.shard(d)}

    greet([dev(d, o) for d, o in others])
    ga = Gather(p, x_ref, xa_ref, sems[:5])
    co = Columns(p, sems[5:8])
    tsend, trecv, tlocal = sems[8:11]
    ga.start()
    part = wq_ref.shape[0]
    hd = HEAD_DIM

    def small(k):
        d, o = others[k]
        block = sega_ref.at[p.c * 4 + p.s]
        yield rcopy(seg_ref, block, tsend.at[k], trecv.at[k], dev(d, o))
        if d and not o:
            yield rcopy(gain_ref, gaina_ref.at[p.s], tsend.at[7 + d - 1], trecv.at[7 + d - 1], dev(d, o))

    smalls = [cp for k in range(7) for cp in small(k)]
    smalls_here = [
        pltpu.make_async_copy(seg_ref, sega_ref.at[p.c * 4 + p.s], tlocal.at[0]),
        pltpu.make_async_copy(gain_ref, gaina_ref.at[p.s], tlocal.at[1]),
    ]
    for cp in smalls + smalls_here:
        cp.start()

    def q_copy(d):
        src = co.cols(p.shard(d) * 2 + p.c, d, wq_ref, hd)
        return co.copy(0, d, src, rows_at(wqkv_ref, p.s * part, part, 0, hd))

    def kv_copy(d, w):
        src = co.cols(p.shard(d), d, w, hd)
        return co.copy(1, d, src, rows_at(wqkv_ref, p.s * part, part, hd, hd))

    for d in (3, 1, 2, 0):
        q_copy(d).start()

        @pl.when(p.c == 0)
        def _():
            kv_copy(d, wk_ref).start()

        @pl.when(p.c != 0)
        def _():
            kv_copy(d, wv_ref).start()

    ga.relay()
    ga.finish()
    for d in (3, 1, 2, 0):
        q_copy(d).wait()
        kv_copy(d, wk_ref).wait()
    for cp in smalls + smalls_here:
        cp.wait()


def enter(x, seg, gains, wq, wk, wv):
    rows, width = x.shape
    return pl.pallas_call(
        enter_kernel,
        out_shape=(
            jax.ShapeDtypeStruct((8 * rows, width), BF),
            jax.ShapeDtypeStruct((width, 2 * HEAD_DIM), BF),
            jax.ShapeDtypeStruct((8, *seg.shape), jnp.int32),
            jax.ShapeDtypeStruct((4, *gains.shape), F32),
        ),
        in_specs=[VM, VM, VM, ANY, ANY, ANY],
        out_specs=(ANY, ANY, VM, VM),
        scratch_shapes=GATHER_SEMS
        + [DMA((2, 3)), DMA((2, 3)), DMA((2,)), DMA((10,)), DMA((10,)), DMA((2,))],
        compiler_params=params(0, 16),
        name="enter",
    )(x, seg, gains, wq, wk, wv)


def middle_kernel(part_ref, x_ref, gain_ref, g_ref, wg_ref, wu_ref, h_ref, xn_ref, ga_ref, wgu_ref, xnb, *scr):
    p = Place()
    greet(plane_ids(p))
    sc = Scatter(p, part_ref, scr[:8])
    gx = Gather(p, xnb, xn_ref, scr[8:13])
    gg = Gather(p, g_ref, ga_ref, scr[13:18])
    co = Columns(p, scr[18:21])
    fb = wgu_ref.shape[1] // 2
    part = wg_ref.shape[0]
    sc.start()
    sc.first()

    def w_copy(k, d):
        w = wg_ref if k == 0 else wu_ref
        src = co.cols(p.shard(d) * 2 + p.c, d, w, fb)
        return co.copy(k, d, src, rows_at(wgu_ref, p.s * part, part, k * fb, fb))

    gg.start()
    sc.relay()
    gg.relay()
    for d in (3, 1, 2, 0):
        for k in (0, 1):
            w_copy(k, d).start()
    half = sc.half
    for h in (0, 1):
        r = pl.ds(h * half, half)
        res = x_ref[r].astype(F32) + sc.total(h)
        h_ref[r] = res
        f = lax.rsqrt(jnp.mean(res * res, axis=1, keepdims=True) + norm_eps)
        xnb[r] = (res * f * gain_ref[...]).astype(BF)
    gx.start()
    gx.relay()
    gg.finish()
    gx.finish()
    for d in (3, 1, 2, 0):
        for k in (0, 1):
            w_copy(k, d).wait()
    sc.drain()


def middle(part, x, gain2, g, wg, wu):
    rows, width = x.shape
    fb = wg.shape[1] // 8
    return pl.pallas_call(
        middle_kernel,
        out_shape=(
            jax.ShapeDtypeStruct((rows, width), F32),
            jax.ShapeDtypeStruct((8 * rows, width), BF),
            jax.ShapeDtypeStruct((8 * rows, width), BF),
            jax.ShapeDtypeStruct((width, 2 * fb), BF),
        ),
        in_specs=[ANY, VM, VM, VM, ANY, ANY],
        out_specs=(VM, ANY, ANY, ANY),
        scratch_shapes=[pltpu.VMEM((rows, width), BF)]
        + scatter_scratch(rows, width)
        + GATHER_SEMS * 2
        + [DMA((2, 3)), DMA((2, 3)), DMA((2,))],
        compiler_params=params(1, 48),
        name="middle",
    )(part, x, gain2, g, wg, wu)


CH = 64
DOWN, GU, OUT, QKV = range(4)


class Chain:
    def __init__(self, p, h, ins, outs, bufs, sems):
        self.p, self.h = p, h
        self.ins = ins
        if outs:
            self.gate, self.up, self.down, self.out, self.wq, self.wk, self.wv = outs
        self.pre, self.buf, self.bufq = bufs
        self.rs_send, self.rs_recv = sems[:2]
        if outs:
            self.ag_send, self.ag_recv, self.cp_send, self.cp_recv, self.tsend = sems[2:]
        nz = lax.axis_size("z")
        self.nz = nz
        self.pos = nz - 1 - p.z if h == 0 else p.z
        self.step = -1 if h == 0 else 1

    def dev(self, by):
        return {"z": self.p.z + by}

    BASE = {DOWN: 0, GU: 8, OUT: 24, QKV: 26}

    def tick(self, kind, t):
        return self.BASE[kind] + t

    def shard_of(self, t):
        s, d = self.p.s, lax.rem(t, 4)
        one = s + 1 - 2 * lax.rem(s, 2)
        two = lax.rem(s + 2, 4)
        return jnp.where(d == 0, s, jnp.where(d == 1, one, jnp.where(d == 2, two, 3 - s)))

    def mine(self, kind, t):
        h = self.h
        if kind == DOWN:
            return self.ins[DOWN].at[pl.ds(h * 512 + t * CH, CH)]
        if kind == OUT:
            return self.ins[OUT].at[pl.ds(h * 128 + t * CH, CH)]
        row = self.shard_of(t) * 512 + h * 256
        if kind == QKV:
            return self.ins[QKV].at[pl.ds(row, 256)]
        return self.ins[GU].at[pl.ds(row + (t // 4) * CH, CH)]

    def slot(self, kind, t, pre):
        if kind == QKV:
            return self.bufq.at[t]
        k = self.tick(kind, t)
        return self.pre.at[k] if pre else self.buf.at[k - PRE]

    def rs_copy(self, kind, t, src, pre):
        k = self.tick(kind, t)
        return rcopy(
            src, self.slot(kind, t, pre), self.rs_send.at[k], self.rs_recv.at[k], self.dev(self.step)
        )

    def reduce(self, kind, t, pre):
        first, last = self.pos == 0, self.pos == self.nz - 1

        @pl.when(first)
        def _():
            self.rs_copy(kind, t, self.mine(kind, t), pre).start()

        @pl.when(jnp.logical_not(first))
        def _():
            slot = self.slot(kind, t, pre)
            self.rs_copy(kind, t, slot, pre).wait_recv()
            slot[...] = (slot[...].astype(F32) + self.mine(kind, t)[...].astype(F32)).astype(BF)

        @pl.when(jnp.logical_and(jnp.logical_not(first), jnp.logical_not(last)))
        def _():
            self.rs_copy(kind, t, self.slot(kind, t, pre), pre).start()

        if not pre:

            @pl.when(last)
            def _():
                self.turn(kind, t, False)

    def turn_pre(self, kind, t, pre):
        @pl.when(self.pos == self.nz - 1)
        def _():
            self.turn(kind, t, True)

    def pieces(self, kind, t, s, d_shard):
        h, c = self.h, self.p.c
        if kind == DOWN:
            return [(None, self.down.at[pl.ds(c * 1024 + h * 512 + t * CH, CH)])]
        if kind == OUT:
            return [(None, self.out.at[pl.ds(c * 256 + h * 128 + t * CH, CH)])]
        if kind == GU:
            r = h * 256 + (t // 4) * CH
            c0 = pl.multiple_of((s * 2 + c) * 1024, 1024)
            return [
                ((0, 1024), self.gate.at[pl.ds(r, CH), pl.ds(c0, 1024)]),
                ((1024, 1024), self.up.at[pl.ds(r, CH), pl.ds(c0, 1024)]),
            ]
        r = h * 256
        cq = pl.multiple_of((s * 2 + c) * 256, 256)
        return [((0, 256), self.wq.at[pl.ds(r, 256), pl.ds(cq, 256)])]

    def kv_piece(self, s, w):
        return w.at[pl.ds(self.h * 256, 256), pl.ds(pl.multiple_of(s * 256, 256), 256)]

    def turn(self, kind, t, pre):
        slot = self.slot(kind, t, pre)
        k = self.tick(kind, t)
        to = self.p.s if kind in (DOWN, OUT) else self.shard_of(t)

        def send(i, src, dst):
            if kind in (DOWN, OUT):
                pltpu.make_async_copy(src, dst, self.ag_recv.at[i, k]).start()
                return

            @pl.when(lax.rem(t, 4) == 0)
            def _():
                pltpu.make_async_copy(src, dst, self.ag_recv.at[i, k]).start()

            @pl.when(lax.rem(t, 4) != 0)
            def _():
                rcopy(src, dst, self.tsend.at[i, k], self.ag_recv.at[i, k], {"shard": to}).start()

        for i, (cols, dst) in enumerate(self.pieces(kind, t, self.p.s, to)):
            send(i, slot if cols is None else slot.at[:, pl.ds(*cols)], dst)
        if kind == QKV:
            src = slot.at[:, pl.ds(256, 256)]

            @pl.when(self.p.c == 0)
            def _():
                send(1, src, self.kv_piece(self.p.s, self.wk))

            @pl.when(self.p.c != 0)
            def _():
                send(1, src, self.kv_piece(self.p.s, self.wv))

    def spread_copy(self, i, k, ref):
        return rcopy(ref, ref, self.ag_send.at[i, k], self.ag_recv.at[i, k], self.dev(-self.step))

    def spread(self, kind, t, pre):
        k = self.tick(kind, t)
        s = self.p.s if kind in (DOWN, OUT) else self.shard_of(t)

        def go(i, ref, wait=True):
            if wait:
                self.spread_copy(i, k, ref).wait_recv()

            @pl.when(self.pos > 0)
            def _():
                self.spread_copy(i, k, ref).start()

            rcopy(ref, ref, self.cp_send.at[i, k], self.cp_recv.at[i, k], self.p.sibling()).start()

        for i, (_, ref) in enumerate(self.pieces(kind, t, s, None)):
            go(i, ref)
        if kind == QKV:
            self.spread_copy(1, k, self.kv_piece(s, self.wk)).wait_recv()

            @pl.when(self.p.c == 0)
            def _():
                go(1, self.kv_piece(s, self.wk), False)

            @pl.when(self.p.c != 0)
            def _():
                go(1, self.kv_piece(s, self.wv), False)

    def drain_reduce(self, kind, t, pre):
        @pl.when(self.pos < self.nz - 1)
        def _():
            self.rs_copy(kind, t, self.slot(kind, t, pre), pre).wait_send()

    def drain_turn(self, kind, t, pre):
        if kind not in (GU, QKV):
            return
        k = self.tick(kind, t)

        @pl.when(jnp.logical_and(self.pos == self.nz - 1, lax.rem(t, 4) != 0))
        def _():
            slot = self.slot(kind, t, pre)
            for i, (cols, dst) in enumerate(self.pieces(kind, t, self.p.s, None)):
                src = slot.at[:, pl.ds(*cols)]
                rcopy(src, dst, self.tsend.at[i, k], self.ag_recv.at[i, k], self.p.to(1)).wait_send()
            if kind == QKV:
                src = slot.at[:, pl.ds(256, 256)]
                dst = self.kv_piece(self.p.s, self.wk)
                rcopy(src, dst, self.tsend.at[1, k], self.ag_recv.at[1, k], self.p.to(1)).wait_send()

    def drain_spread(self, kind, t, pre):
        k = self.tick(kind, t)
        s = self.p.s if kind in (DOWN, OUT) else self.shard_of(t)
        refs = [ref for _, ref in self.pieces(kind, t, s, None)]
        if kind == QKV:
            refs.append(self.kv_piece(s, self.wk))
        for i, ref in enumerate(refs):

            @pl.when(self.pos > 0)
            def _():
                self.spread_copy(i, k, ref).wait_send()

            rcopy(ref, ref, self.cp_send.at[i, k], self.cp_recv.at[i, k], self.p.sibling()).wait()


N_TICKS, PRE = 30, 12
RS_SEMS = [DMA((N_TICKS,)), DMA((N_TICKS,))]
CHAIN_SEMS = RS_SEMS + [DMA((2, N_TICKS))] * 5


def z_neighbours_enter(p):
    barrier = pltpu.get_barrier_semaphore()
    nz = lax.axis_size("z")
    for d in plane_ids(p):
        pl.semaphore_signal(barrier, inc=1, device_id=d, device_id_type=MESH)

    @pl.when(p.z > 0)
    def _():
        pl.semaphore_signal(barrier, inc=1, device_id={"z": p.z - 1}, device_id_type=MESH)

    @pl.when(p.z < nz - 1)
    def _():
        pl.semaphore_signal(barrier, inc=1, device_id={"z": p.z + 1}, device_id_type=MESH)

    ends = jnp.logical_or(p.z == 0, p.z == nz - 1)
    pl.semaphore_wait(barrier, jnp.where(ends, 5, 6))


def loop(lo, hi, body):
    def step(t, _):
        body(t)
        return 0

    lax.fori_loop(lo, hi, step, 0)


COUNT = {DOWN: 8, GU: 16, OUT: 2, QKV: 4}


SKEW, TURN = 2, 3


def between(i, lo, hi):
    return jnp.logical_and(i >= lo, i < hi)


def each(i, lo, hi, act):
    for kind, n in COUNT.items():
        base = Chain.BASE[kind]
        for pre, first, last in ((True, 0, PRE), (False, PRE, N_TICKS)):
            a, b = max(lo, base, first), min(hi, base + n, last)
            if a < b:

                @pl.when(between(i, a, b))
                def _():
                    act(kind, i - base, pre)


def at_tick(t, when, act):
    @pl.when(t == when)
    def _():
        act()


def back_kernel(
    part_ref, h_ref, g_ref, gain_ref, gd_ref, ggu_ref, dhb_ref, dh_ref, gsum_ref, prea, preb, low, *scr
):
    p = Place()
    z_neighbours_enter(p)
    sc = Scatter(p, part_ref, scr[:8])
    ga = Gather(p, low, dhb_ref, scr[8:13])
    ins = (gd_ref, ggu_ref, None, None)
    chains = [
        Chain(p, 0, ins, None, (prea, None, None), scr[13:15]),
        Chain(p, 1, ins, None, (preb, None, None), scr[15:17]),
    ]
    sc.start()
    sc.first()

    def norm():
        for h in (0, 1):
            r = pl.ds(h * sc.half, sc.half)
            dx = sc.total(h)
            res = h_ref[r]
            f = lax.rsqrt(jnp.mean(res * res, axis=1, keepdims=True) + norm_eps)
            hat = res * f
            term = jnp.sum(dx * hat, axis=0, keepdims=True)
            gsum_ref[...] = term if h == 0 else gsum_ref[...] + term
            dh = g_ref[r].astype(F32) + norm_backward_step(dx * gain_ref[...], hat, f)
            dh_ref[r] = dh
            low[r] = dh.astype(BF)
        ga.start()

    def tick(t):
        for ch in chains:
            each(t - SKEW * ch.pos, 0, PRE, ch.reduce)
        at_tick(t, 1, sc.relay)
        at_tick(t, 5, norm)
        at_tick(t, 7, ga.relay)

    loop(0, PRE + SKEW * (lax.axis_size("z") - 1), tick)
    ga.finish()
    sc.drain()

    def drain(i):
        for ch in chains:
            each(i, 0, PRE, ch.drain_reduce)

    loop(0, PRE, drain)


def back(part, h, g, gain2, g_down, g_gu):
    rows, width = h.shape
    return pl.pallas_call(
        back_kernel,
        out_shape=(
            jax.ShapeDtypeStruct((8 * rows, width), BF),
            jax.ShapeDtypeStruct((rows, width), F32),
            jax.ShapeDtypeStruct((1, width), F32),
            jax.ShapeDtypeStruct((PRE, CH, width), BF),
            jax.ShapeDtypeStruct((PRE, CH, width), BF),
        ),
        in_specs=[ANY, VM, VM, VM, VM, VM],
        out_specs=(ANY, VM, VM, VM, VM),
        scratch_shapes=[pltpu.VMEM((rows, width), BF)]
        + scatter_scratch(rows, width)
        + GATHER_SEMS
        + RS_SEMS * 2,
        compiler_params=params(2, 52),
        name="back",
    )(part, h, g, gain2, g_down, g_gu)


def last_kernel(
    part1_ref, part2_ref, x_ref, h_ref, dh_ref, gain_ref, gsum_ref, prea, preb, ggu_ref, go_ref, gqkv_ref,
    out_ref, grad_ref, gains_ref, gate, up, down, out, wq, wk, wv,
    bufa, bufb, qa, qb, tot, got, gz, gsend, grecv, *scr,
):
    p = Place()
    nz = lax.axis_size("z")
    z_all_enter(p)
    s1 = Scatter(p, part1_ref, scr[:8])
    s2 = Scatter(p, part2_ref, scr[8:16])
    ins = (None, ggu_ref, go_ref, gqkv_ref)
    outs = (gate, up, down, out, wq, wk, wv)
    n = len(CHAIN_SEMS)
    chains = [
        Chain(p, 0, ins, outs, (prea, bufa, qa), scr[16 : 16 + n]),
        Chain(p, 1, ins, outs, (preb, bufb, qb), scr[16 + n : 16 + 2 * n]),
    ]
    line = SKEW * (nz - 1)
    tot[0] = jnp.zeros_like(tot[0])
    s1.start()
    s2.start()
    s1.first()

    def gain_copy(k):
        dev = (p.sibling(), p.to(1), p.to(2))[k]
        return rcopy(tot.at[k], got.at[k], gsend.at[k], grecv.at[k], dev)

    def z_copy(k):
        return rcopy(
            tot.at[3], gz.at[p.z], gsend.at[2 + k], grecv.at[3 + p.z], {"z": lax.rem(p.z + k, nz)}
        )

    def z_landed(k):
        src = lax.rem(p.z + nz - k, nz)
        ref = gz.at[src]
        return rcopy(ref, ref, gsend.at[2 + k], grecv.at[3 + src], {"z": src})

    def finish1():
        for h in (0, 1):
            r = pl.ds(h * s1.half, s1.half)
            dx = s1.total(h)
            xf = x_ref[r].astype(F32)
            f = lax.rsqrt(jnp.mean(xf * xf, axis=1, keepdims=True) + norm_eps)
            hat = xf * f
            term = jnp.sum(dx * hat, axis=0, keepdims=True)
            tot[0, 0:1] = term if h == 0 else tot[0, 0:1] + term
            grad = dh_ref[r] + norm_backward_step(dx * gain_ref[...], hat, f)
            grad_ref[r] = grad.astype(BF)
        tot[0, 1:2] = gsum_ref[...]
        gain_copy(0).start()

    def add_gains(k):
        gain_copy(k).wait()
        tot[k + 1] = tot[k] + got[k]
        if k < 2:
            gain_copy(k + 1).start()
        else:
            for j in range(1, nz):
                z_copy(j).start()
            gz[p.z] = tot[3]

    def finish_gains():
        for j in range(1, nz):
            z_copy(j).wait_send()
            z_landed(j).wait_recv()
        total = gz[0]
        for j in range(1, nz):
            total = total + gz[j]
        gains_ref[...] = total

    def finish2():
        for h in (0, 1):
            r = pl.ds(h * s2.half, s2.half)
            out_ref[r] = (h_ref[r] + s2.total(h)).astype(BF)

    def tick(t):
        for ch in chains:
            each(t, 0, PRE, ch.turn_pre)
            each(t + PRE - SKEW * ch.pos, PRE, N_TICKS, ch.reduce)
        for ch in chains:
            each(t - TURN - line + SKEW * ch.pos, 0, N_TICKS, ch.spread)
        at_tick(t, 1, s1.relay)
        at_tick(t, 2, s2.first)
        at_tick(t, 5, finish1)
        at_tick(t, 6, s2.relay)
        for k in range(3):
            at_tick(t, 7 + 2 * k, functools.partial(add_gains, k))
        at_tick(t, 10, finish2)
        at_tick(t, 16, finish_gains)

    loop(0, N_TICKS + TURN + line, tick)
    s1.drain()
    s2.drain()

    def drain(i):
        for ch in chains:
            each(i, PRE, N_TICKS, ch.drain_reduce)
            each(i, 0, N_TICKS, ch.drain_turn)
            each(i, 0, N_TICKS, ch.drain_spread)

    loop(0, N_TICKS, drain)


def z_all_enter(p):
    barrier = pltpu.get_barrier_semaphore()
    nz = lax.axis_size("z")
    ids = plane_ids(p) + [{"z": lax.rem(p.z + k, nz)} for k in range(1, nz)]
    for d in ids:
        pl.semaphore_signal(barrier, inc=1, device_id=d, device_id_type=MESH)
    pl.semaphore_wait(barrier, len(ids))


def last(part1, part2, x, h, dh, gain1, gsum2, pre, g_gu, g_out, g_qkv, part, ff):
    rows, width = x.shape
    nz = lax.axis_size("z")
    shapes = [(part, ff), (part, ff), (ff // 4, width), (part, width), (part, width), (part, 1024), (part, 1024)]
    return pl.pallas_call(
        last_kernel,
        out_shape=(
            jax.ShapeDtypeStruct((rows, width), BF),
            jax.ShapeDtypeStruct((rows, width), BF),
            jax.ShapeDtypeStruct((8, width), F32),
        )
        + tuple(jax.ShapeDtypeStruct(s, BF) for s in shapes),
        in_specs=[ANY, ANY] + [VM] * 10,
        out_specs=(VM, VM, VM) + (ANY,) * 7,
        scratch_shapes=[
            pltpu.VMEM((26 - PRE, CH, width), BF),
            pltpu.VMEM((26 - PRE, CH, width), BF),
            pltpu.VMEM((4, 256, 512), BF),
            pltpu.VMEM((4, 256, 512), BF),
            pltpu.VMEM((4, 8, width), F32),
            pltpu.VMEM((3, 8, width), F32),
            pltpu.VMEM((nz, 8, width), F32),
            DMA((nz + 3,)),
            DMA((nz + 3,)),
        ]
        + scatter_scratch(rows, width) * 2
        + CHAIN_SEMS * 2,
        compiler_params=params(3, 62),
        name="last",
    )(part1, part2, x, h, dh, gain1, gsum2, *pre, g_gu, g_out, g_qkv)


def pieces(
    tokens,
    segment_ids,
    attn_gain,
    w_query,
    w_key,
    w_value,
    w_out,
    mlp_gain,
    w_gate,
    w_up,
    w_down,
    cotangent,
):
    rows, width = tokens.shape[1], tokens.shape[2]
    core = lax.axis_index("core")
    nc, ns = lax.axis_size("core"), lax.axis_size("shard")
    hd = HEAD_DIM
    ff = w_gate.shape[1]
    fb = ff // (nc * ns)
    part = width // ns

    x = tokens.reshape(rows, width)
    g = cotangent.reshape(rows, width)
    wo = lax.dynamic_slice_in_dim(w_out, core * hd, hd, 0)
    wd = lax.dynamic_slice_in_dim(w_down, core * fb, fb, 0)

    gains = jnp.concatenate([attn_gain[None], mlp_gain[None], jnp.zeros((6, part), BF)], 0).astype(F32)
    seg8 = jnp.broadcast_to(segment_ids, (8, rows))
    x_all, wqkv, seg, gains = enter(x, seg8, gains, w_query, w_key, w_value)
    seg = seg[:, 0]
    gain1, gain2 = gains[:, 0].reshape(1, width), gains[:, 1].reshape(1, width)
    nseq = nc * ns

    iota = jnp.arange(rows, dtype=jnp.int32)
    same = seg[:, :, None] == seg[:, None, :]
    allowed = same & (iota[:, None] >= iota[None, :])[None]
    starts = jnp.sum((seg[:, None, :] < seg[:, :, None]).astype(jnp.int32), axis=2)
    positions = (iota[None, :] - starts).astype(F32)
    half = hd // 2
    inv_freq = rope_base ** (-(jnp.arange(half, dtype=F32) * 2.0 / hd))
    angles = positions[..., None] * inv_freq
    cosine, sine = jnp.cos(angles), jnp.sin(angles)

    xf_all = x_all.astype(F32)
    f1_all = lax.rsqrt(jnp.mean(xf_all * xf_all, axis=1, keepdims=True) + norm_eps)
    xn1 = (xf_all * f1_all * gain1).astype(BF)
    qkv = mm(xn1, wqkv).reshape(nseq, rows, 2 * hd)
    q = rotate(qkv[..., :hd], cosine, sine).astype(BF)
    kv_lin = qkv[..., hd:]
    kv_mine = jnp.where(core == 0, rotate(kv_lin, cosine, sine), kv_lin).astype(BF)
    swap = [(i, nc - 1 - i) for i in range(nc)]
    kv_other = lax.ppermute(kv_mine, "core", swap)
    k = jnp.where(core == 0, kv_mine, kv_other)
    v = jnp.where(core == 0, kv_other, kv_mine)
    scale = hd ** (-0.5)
    scores = jnp.einsum("bqd,bkd->bqk", q, k, preferred_element_type=F32) * scale
    scores = jnp.where(allowed, scores, mask_fill)
    top = jnp.max(scores, axis=-1, keepdims=True)
    ex = jnp.exp(scores - top)
    probs = ex / jnp.sum(ex, axis=-1, keepdims=True)
    pb = probs.astype(BF)
    attn = jnp.einsum("bqk,bkd->bqd", pb, v, preferred_element_type=F32).astype(BF)
    attn = attn.reshape(nseq * rows, hd)

    h, xn2, g_all, wgu = middle(mm(attn, wo).astype(BF), x, gain2, g, w_gate, w_up)

    gu = mm(xn2, wgu)
    gate, up = gu[:, :fb], gu[:, fb:]
    sigma = jax.nn.sigmoid(gate)
    swish = gate * sigma
    hid = (swish * up).astype(BF)
    g_down = mm_tn(hid, g_all).astype(BF)
    dhid = mm_nt(g_all, wd)
    dgate = (dhid * up * sigma * (1.0 + gate * (1.0 - sigma))).astype(BF)
    dup = (dhid * swish).astype(BF)
    dgu = jnp.concatenate([dgate, dup], 1)
    g_gu = mm_tn(xn2, dgu).astype(BF)
    dhb, dh, gsum2, prea, preb = back(mm_nt(dgu, wgu).astype(BF), h, g, gain2, g_down, g_gu)
    g_out = mm_tn(attn, dhb).astype(BF)
    dattn = mm_nt(dhb, wo).astype(BF).reshape(nseq, rows, hd)
    dp = jnp.einsum("bqd,bkd->bqk", dattn, v, preferred_element_type=F32)
    dv = jnp.einsum("bqk,bqd->bkd", pb, dattn, preferred_element_type=F32)
    ds = (probs * (dp - jnp.sum(dp * probs, axis=-1, keepdims=True))).astype(BF)
    dq = jnp.einsum("bqk,bkd->bqd", ds, k, preferred_element_type=F32) * scale
    dk = jnp.einsum("bqk,bqd->bkd", ds, q, preferred_element_type=F32) * scale
    dq = rotate(dq, cosine, -sine).astype(BF)
    dk = rotate(dk, cosine, -sine)
    mine = jnp.where(core == 0, dk, dv)
    other = jnp.where(core == 0, dv, dk).astype(BF)
    dkv = (mine + lax.ppermute(other, "core", swap).astype(F32)).astype(BF)
    dqkv = jnp.concatenate([dq, dkv], -1).reshape(nseq * rows, 2 * hd)
    g_qkv = mm_tn(xn1, dqkv).astype(BF)
    output, input_grad, gain_g, gate_g, up_g, down_g, out_g, wq_g, wk_g, wv_g = last(
        mm_nt(dqkv, wqkv).astype(BF),
        mm(hid, wd).astype(BF),
        x,
        h,
        dh,
        gain1,
        gsum2,
        (prea, preb),
        g_gu,
        g_out,
        g_qkv,
        part,
        ff,
    )
    output = output.reshape(1, rows, width)
    input_grad = input_grad.reshape(1, rows, width)
    gain_g = lax.dynamic_slice_in_dim(gain_g, lax.axis_index("shard") * part, part, 1)
    return (
        output,
        input_grad,
        gain_g[0],
        wq_g.astype(F32),
        wk_g.astype(F32),
        wv_g.astype(F32),
        out_g.astype(F32),
        gain_g[1],
        gate_g.astype(F32),
        up_g.astype(F32),
        down_g.astype(F32),
    )


def contract_rows(left, right):
    return lax.dot_general(
        left, right, (((0,), (0,)), ((), ())), preferred_element_type=jnp.float32
    )


def contract_cols(left, right):
    return lax.dot_general(
        left, right, (((1,), (1,)), ((), ())), preferred_element_type=jnp.float32
    )


def scores_of(queries, keys, allowed):
    raw = jnp.einsum(
        "qgrd,kgd->grqk", queries, keys, preferred_element_type=jnp.float32
    ) * HEAD_DIM ** (-0.5)
    return jnp.where(allowed, raw, mask_fill)


def general(
    tokens,
    segment_ids,
    attn_gain,
    w_query,
    w_key,
    w_value,
    w_out,
    mlp_gain,
    w_gate,
    w_up,
    w_down,
    cotangent,
):
    rows = tokens.shape[1]
    width = tokens.shape[2]
    groups = HEADS // KV_HEADS
    q_cols = HEADS * HEAD_DIM
    kv_cols = KV_HEADS * HEAD_DIM
    layer_input_rows = tokens.reshape(rows, width).astype(jnp.float32)
    segments = segment_ids.reshape(rows)
    iota = jnp.arange(rows, dtype=jnp.int32)
    starts = jnp.sum((segments[None, :] < segments[:, None]).astype(jnp.int32), axis=1)
    positions = (iota - starts).astype(jnp.float32)
    allowed = (segments[:, None] == segments[None, :]) & (iota[:, None] >= iota[None, :])
    half = HEAD_DIM // 2
    inv_freq = rope_base ** (-(jnp.arange(half, dtype=jnp.float32) * 2.0 / HEAD_DIM))
    angles = positions[:, None] * inv_freq
    cosine = jnp.cos(angles)
    sine = jnp.sin(angles)
    first_norm_factor = lax.rsqrt(
        jnp.mean(layer_input_rows * layer_input_rows, axis=1, keepdims=True) + norm_eps
    )
    first_standardized = layer_input_rows * first_norm_factor
    gain_fragment = lax.all_gather(attn_gain, "shard", axis=0, tiled=True)
    query_piece = lax.all_gather(w_query, "shard", axis=0, tiled=True)
    key_piece = lax.all_gather(w_key, "shard", axis=0, tiled=True)
    value_piece = lax.all_gather(w_value, "shard", axis=0, tiled=True)
    normalized_rows = (first_standardized * gain_fragment.astype(jnp.float32)).astype(jnp.bfloat16)
    joined = jnp.concatenate([query_piece, key_piece, value_piece], 1)
    result = (
        jnp.dot(normalized_rows, joined, preferred_element_type=jnp.float32),
        normalized_rows,
        gain_fragment.astype(jnp.float32),
    )
    folded = result
    projected, normed_one, first_norm_gain = (folded[0], folded[1], folded[2])
    queries = rotate(
        projected[:, :q_cols].reshape(rows, KV_HEADS, groups, HEAD_DIM),
        cosine[:, None, None, :],
        sine[:, None, None, :],
    ).astype(jnp.bfloat16)
    keys = rotate(
        projected[:, q_cols : q_cols + kv_cols].reshape(rows, KV_HEADS, HEAD_DIM),
        cosine[:, None, :],
        sine[:, None, :],
    ).astype(jnp.bfloat16)
    values = projected[:, q_cols + kv_cols :].reshape(rows, KV_HEADS, HEAD_DIM).astype(jnp.bfloat16)
    scores = scores_of(queries, keys, allowed)
    top = jnp.max(scores, axis=-1, keepdims=True)
    log_total = top + jnp.log(jnp.sum(jnp.exp(scores - top), axis=-1, keepdims=True))
    probs = jnp.exp(scores - log_total)
    probs_low = probs.astype(jnp.bfloat16)
    attn = (
        jnp.einsum("grqk,kgd->qgrd", probs_low, values, preferred_element_type=jnp.float32)
        .reshape(rows, q_cols)
        .astype(jnp.bfloat16)
    )
    part = attn
    result = (
        jnp.dot(
            part,
            lax.all_gather(w_out, "shard", axis=0, tiled=True),
            preferred_element_type=jnp.float32,
        ),
    )
    folded_out = result
    residual_hidden_state = layer_input_rows + folded_out[0]
    second_norm_factor = lax.rsqrt(
        jnp.mean(residual_hidden_state * residual_hidden_state, axis=1, keepdims=True) + norm_eps
    )
    second_standardized = residual_hidden_state * second_norm_factor
    gain_fragment = lax.all_gather(mlp_gain, "shard", axis=0, tiled=True)
    gate_piece = lax.all_gather(w_gate, "shard", axis=0, tiled=True)
    up_piece = lax.all_gather(w_up, "shard", axis=0, tiled=True)
    normalized_rows = (second_standardized * gain_fragment.astype(jnp.float32)).astype(jnp.bfloat16)
    joined = jnp.concatenate([gate_piece, up_piece], 1)
    result = (
        jnp.dot(normalized_rows, joined, preferred_element_type=jnp.float32),
        normalized_rows,
        gain_fragment.astype(jnp.float32),
    )
    folded_mlp = result
    gate = folded_mlp[0][:, :FF]
    up_value = folded_mlp[0][:, FF:]
    normed_two = folded_mlp[1]
    second_norm_gain = folded_mlp[2]
    sigma = jax.nn.sigmoid(gate)
    swish = gate * sigma
    inner = (swish * up_value).astype(jnp.bfloat16)
    part = inner
    result = (
        jnp.dot(
            part,
            lax.all_gather(w_down, "shard", axis=0, tiled=True),
            preferred_element_type=jnp.float32,
        ),
    )
    output = (residual_hidden_state + result[0]).astype(jnp.bfloat16).reshape(1, rows, width)
    grad_out = cotangent.reshape(rows, width)
    grad_down = lax.psum_scatter(
        contract_rows(inner, grad_out).astype(jnp.bfloat16),
        "shard",
        scatter_dimension=0,
        tiled=True,
    )
    down_full, gate_full, up_full = (
        lax.all_gather(w_down, "shard", axis=0, tiled=True),
        lax.all_gather(w_gate, "shard", axis=0, tiled=True),
        lax.all_gather(w_up, "shard", axis=0, tiled=True),
    )
    grad_inner = contract_cols(grad_out, down_full)
    grad_gate = (grad_inner * up_value * sigma * (1.0 + gate * (1.0 - sigma))).astype(jnp.bfloat16)
    grad_up = (grad_inner * swish).astype(jnp.bfloat16)
    grad_mlp = jnp.concatenate([grad_gate, grad_up], 1)
    mlp_shards = lax.psum_scatter(
        contract_rows(normed_two, grad_mlp).astype(jnp.bfloat16),
        "shard",
        scatter_dimension=0,
        tiled=True,
    ).astype(jnp.float32)
    second_norm_gradient = contract_cols(grad_gate, gate_full) + contract_cols(grad_up, up_full)
    second_gain_products = jnp.sum(second_norm_gradient * second_standardized, axis=0)
    hidden_gradient = grad_out.astype(jnp.float32) + norm_backward_step(
        second_norm_gradient * second_norm_gain, second_standardized, second_norm_factor
    )
    grad_hidden_low = hidden_gradient.astype(jnp.bfloat16)
    grad_out_proj = lax.psum_scatter(
        contract_rows(attn, grad_hidden_low).astype(jnp.bfloat16),
        "shard",
        scatter_dimension=0,
        tiled=True,
    )
    grad_attn = contract_cols(grad_hidden_low, lax.all_gather(w_out, "shard", axis=0, tiled=True))
    grad_attn = grad_attn.astype(jnp.bfloat16).reshape(rows, KV_HEADS, groups, HEAD_DIM)
    scores_again = scores_of(queries, keys, allowed)
    probs_again = jnp.exp(scores_again - log_total)
    probs_again_low = probs_again.astype(jnp.bfloat16)
    grad_probs = jnp.einsum("qgrd,kgd->grqk", grad_attn, values, preferred_element_type=jnp.float32)
    grad_values = jnp.einsum(
        "grqk,qgrd->kgd", probs_again_low, grad_attn, preferred_element_type=jnp.float32
    )
    grad_scores = (
        probs_again * (grad_probs - jnp.sum(grad_probs * probs_again, axis=-1, keepdims=True))
    ).astype(jnp.bfloat16)
    grad_queries = jnp.einsum(
        "grqk,kgd->qgrd", grad_scores, keys, preferred_element_type=jnp.float32
    ) * HEAD_DIM ** (-0.5)
    grad_keys = jnp.einsum(
        "grqk,qgrd->kgd", grad_scores, queries, preferred_element_type=jnp.float32
    ) * HEAD_DIM ** (-0.5)
    grad_queries = rotate(grad_queries, cosine[:, None, None, :], -sine[:, None, None, :]).reshape(
        rows, q_cols
    )
    grad_keys = rotate(grad_keys, cosine[:, None, :], -sine[:, None, :]).reshape(rows, kv_cols)
    grad_joined = jnp.concatenate(
        [
            grad_queries.astype(jnp.bfloat16),
            grad_keys.astype(jnp.bfloat16),
            grad_values.reshape(rows, kv_cols).astype(jnp.bfloat16),
        ],
        1,
    )
    qkv_shards = lax.psum_scatter(
        contract_rows(normed_one, grad_joined).astype(jnp.bfloat16),
        "shard",
        scatter_dimension=0,
        tiled=True,
    ).astype(jnp.float32)
    local_qkv = jnp.concatenate([w_query, w_key, w_value], 1)
    first_norm_gradient = contract_cols(
        grad_joined, lax.all_gather(local_qkv, "shard", axis=0, tiled=True)
    )
    first_gain_products = jnp.sum(first_norm_gradient * first_standardized, axis=0)
    input_gradient_rows = hidden_gradient + norm_backward_step(
        first_norm_gradient * first_norm_gain, first_standardized, first_norm_factor
    )
    input_grad = input_gradient_rows.astype(jnp.bfloat16).reshape(1, rows, width)
    gain_one_grad, gain_two_grad = (
        lax.psum_scatter(first_gain_products, "shard", scatter_dimension=0, tiled=True),
        lax.psum_scatter(second_gain_products, "shard", scatter_dimension=0, tiled=True),
    )
    summed = (
        lax.psum(gain_one_grad.astype(jnp.bfloat16), "rep").astype(jnp.float32),
        lax.psum(qkv_shards[:, :q_cols].astype(jnp.bfloat16), "rep").astype(jnp.float32),
        lax.psum(qkv_shards[:, q_cols : q_cols + kv_cols].astype(jnp.bfloat16), "rep").astype(
            jnp.float32
        ),
        lax.psum(qkv_shards[:, q_cols + kv_cols :].astype(jnp.bfloat16), "rep").astype(jnp.float32),
        lax.psum(grad_out_proj, "rep").astype(jnp.float32),
        lax.psum(gain_two_grad.astype(jnp.bfloat16), "rep").astype(jnp.float32),
        lax.psum(mlp_shards[:, :FF].astype(jnp.bfloat16), "rep").astype(jnp.float32),
        lax.psum(mlp_shards[:, FF:].astype(jnp.bfloat16), "rep").astype(jnp.float32),
        lax.psum(grad_down, "rep").astype(jnp.float32),
    )
    return (
        output,
        input_grad,
        summed[0],
        summed[1],
        summed[2],
        summed[3],
        summed[4],
        summed[5],
        summed[6],
        summed[7],
        summed[8],
    )


def solution(mesh):
    rep, shard = mesh.devices.shape
    if shard == KV_HEADS and rep % 2 == 0:
        fine = Mesh(np.asarray(mesh.devices).reshape(rep // 2, 2, shard), ("z", "core", "shard"))
        body, every = pieces, ("z", "core", "shard")
    else:
        fine, body, every = mesh, general, ("rep", "shard")
    seqs, vec, mat = P(every, None, None), P("shard"), P("shard", None)
    in_specs = (seqs, P(every, None), vec, mat, mat, mat, mat, vec, mat, mat, mat, seqs)
    out_specs = (seqs, seqs, vec, mat, mat, mat, mat, vec, mat, mat, mat)
    return jax.shard_map(body, mesh=fine, in_specs=in_specs, out_specs=out_specs, check_vma=False)
```

```python
import functools

import jax
import jax.numpy as jnp
import numpy as np
from jax import lax
from jax.experimental import pallas as pl
from jax.experimental.pallas import tpu as pltpu
from jax.sharding import Mesh
from jax.sharding import PartitionSpec as P

HEADS = 8
KV_HEADS = 4
HEAD_DIM = 256
FF = 8192

rope_base = 1000042.0
norm_eps = 1e-06
mask_fill = -1e30

BF = jnp.bfloat16
F32 = jnp.float32
MESH = pl.DeviceIdType.MESH
ANY = pl.BlockSpec(memory_space=pl.ANY)
VM = pl.BlockSpec(memory_space=pltpu.VMEM)
DMA = pltpu.SemaphoreType.DMA


def mm(a, b):
    return jnp.dot(a, b, preferred_element_type=F32)


def mm_tn(a, b):
    return lax.dot_general(a, b, (((0,), (0,)), ((), ())), preferred_element_type=F32)


def mm_nt(a, b):
    return lax.dot_general(a, b, (((1,), (1,)), ((), ())), preferred_element_type=F32)


def rotate(values, cosine, sine):
    half = values.shape[-1] // 2
    first = values[..., :half]
    second = values[..., half:]
    return jnp.concatenate([first * cosine - second * sine, second * cosine + first * sine], -1)


def norm_backward_step(grad_hat, normalized_rows, factor):
    return factor * (
        grad_hat - normalized_rows * jnp.mean(grad_hat * normalized_rows, axis=1, keepdims=True)
    )


class Place:
    def __init__(self):
        self.z = lax.axis_index("z")
        self.c = lax.axis_index("core")
        self.s = lax.axis_index("shard")

    def shard(self, d):
        s = self.s
        if d == 0:
            return s
        if d == 1:
            return s + 1 - 2 * lax.rem(s, 2)
        if d == 2:
            return lax.rem(s + 2, 4)
        return 3 - s

    def to(self, d):
        return {"shard": self.shard(d)}

    def sibling(self):
        return {"core": 1 - self.c}


def greet(ids):
    barrier = pltpu.get_barrier_semaphore()
    for d in ids:
        pl.semaphore_signal(barrier, inc=1, device_id=d, device_id_type=MESH)
    pl.semaphore_wait(barrier, len(ids))


def rcopy(src, dst, send, recv, dev):
    return pltpu.make_async_remote_copy(
        src_ref=src, dst_ref=dst, send_sem=send, recv_sem=recv, device_id=dev, device_id_type=MESH
    )


GATHER_SEMS = [DMA((6,)), DMA((6,)), DMA((7,)), DMA((7,)), DMA((1,))]


class Gather:
    def __init__(self, p, src, out, sems):
        self.p, self.src, self.out = p, src, out
        self.send, self.recv, self.csend, self.crecv, self.lsem = sems
        self.rows = src.shape[0]
        self.half = self.rows // 2

    def at(self, d, h, core=None):
        core = self.p.c if core is None else core
        row = (core * 4 + self.p.shard(d)) * self.rows
        if h is None:
            return self.out.at[pl.ds(row, self.rows)]
        return self.out.at[pl.ds(row + h * self.half, self.half)]

    def move(self, k):
        d, h, to = [(0, 0, 1), (0, 1, 2), (0, 1, 1), (0, 0, 2), (1, 0, 2), (2, 1, 1)][k]
        dst = self.at(d, h)
        src = self.src.at[pl.ds(h * self.half, self.half)] if d == 0 else dst
        return rcopy(src, dst, self.send.at[k], self.recv.at[k], self.p.to(to))

    def landed(self, k):
        d, h = [(1, 0), (2, 1), (1, 1), (2, 0), (3, 0), (3, 1)][k]
        return self.at(d, h)

    def pass_on(self, k):
        here = self.src if k == 6 else self.landed(k)
        there = self.at(0, None) if k == 6 else self.landed(k)
        return rcopy(here, there, self.csend.at[k], self.crecv.at[k], self.p.sibling())

    def arrived(self, k):
        ref = self.landed(k)
        rcopy(ref, ref, self.send.at[k], self.recv.at[k], self.p.to(1)).wait_recv()
        self.pass_on(k).start()

    def start(self):
        for k in range(4):
            self.move(k).start()
        self.pass_on(6).start()
        pltpu.make_async_copy(self.src, self.at(0, None), self.lsem.at[0]).start()

    def relay(self):
        for k in (0, 1):
            self.arrived(k)
            self.move(4 + k).start()

    def early(self):
        for k in (2, 3):
            self.arrived(k)

    def finish(self, early=False):
        if not early:
            self.early()
        for k in (4, 5):
            self.arrived(k)
        for k in range(6):
            self.move(k).wait_send()
        for k in range(7):
            self.pass_on(k).wait()
        pltpu.make_async_copy(self.src, self.at(0, None), self.lsem.at[0]).wait()


SCATTER_SEMS = [DMA((4,)), DMA((4,)), DMA((4,)), DMA((6,)), DMA((6,))]
ORDER = (3, 1, 2, 0)


def scatter_scratch(rows, width):
    half = rows // 2
    return [
        pltpu.VMEM((4, rows, width), BF),
        pltpu.VMEM((4, rows, width), BF),
        pltpu.VMEM((6, half, width), BF),
    ] + SCATTER_SEMS


class Scatter:
    def __init__(self, p, part, scratch):
        self.p, self.part = p, part
        self.own, self.got, self.slot, self.lsem, self.csend, self.crecv, self.send, self.recv = scratch
        self.rows = self.own.shape[1]
        self.half = self.rows // 2

    def block(self, core, d):
        return self.part.at[pl.ds((core * 4 + self.p.shard(d)) * self.rows, self.rows)]

    def local(self, d):
        return pltpu.make_async_copy(self.block(self.p.c, d), self.own.at[d], self.lsem.at[d])

    def swap(self, d):
        src = self.block(1 - self.p.c, d)
        return rcopy(src, self.got.at[d], self.csend.at[d], self.crecv.at[d], self.p.sibling())

    def rowsof(self, h):
        return pl.ds(h * self.half, self.half)

    def move(self, k):
        d, h, to = [(3, 0, 1), (3, 1, 2), (1, 0, 1), (2, 1, 2), (2, 0, 2), (1, 1, 1)][k]
        return rcopy(
            self.own.at[d, self.rowsof(h)], self.slot.at[k], self.send.at[k], self.recv.at[k], self.p.to(to)
        )

    def start(self):
        for d in ORDER:
            self.swap(d).start()
            self.local(d).start()

    def pair(self, d):
        self.swap(d).wait_recv()
        self.local(d).wait()
        self.own[d] = (self.own[d].astype(F32) + self.got[d].astype(F32)).astype(BF)

    def first(self):
        self.pair(3)
        self.move(0).start()
        self.move(1).start()
        self.pair(1)
        self.move(2).start()
        self.pair(2)
        self.move(3).start()
        self.pair(0)

    def relay(self):
        for k, d, h in ((0, 2, 0), (1, 1, 1)):
            self.move(k).wait_recv()
            r = self.rowsof(h)
            self.own[d, r] = (self.own[d, r].astype(F32) + self.slot[k].astype(F32)).astype(BF)
            self.move(4 + k).start()

    def total(self, h):
        near, far = (2, 4) if h == 0 else (3, 5)
        self.move(near).wait_recv()
        self.move(far).wait_recv()
        return (
            self.own[0, self.rowsof(h)].astype(F32)
            + self.slot[near].astype(F32)
            + self.slot[far].astype(F32)
        )

    def drain(self):
        for k in range(6):
            self.move(k).wait_send()
        for d in range(4):
            self.swap(d).wait_send()


def params(cid, mb):
    return pltpu.CompilerParams(
        collective_id=cid, has_side_effects=True, vmem_limit_bytes=mb * 2**20
    )


def plane_ids(p):
    return [p.to(1), p.to(2), p.to(3), p.sibling()]


class Columns:
    def __init__(self, p, sems):
        self.p = p
        self.send, self.recv, self.lsem = sems

    def cols(self, j, d, src, width):
        return src.at[:, pl.ds(pl.multiple_of(j * width, width), width)]

    def copy(self, k, d, src, dst):
        if d == 0:
            return pltpu.make_async_copy(src, dst, self.lsem.at[k])
        return rcopy(src, dst, self.send.at[k, d - 1], self.recv.at[k, d - 1], self.p.to(d))


def rows_at(ref, r, n, c0, width):
    return ref.at[pl.ds(r, n), pl.ds(c0, width)]


def greet_line(p, ids):
    barrier = pltpu.get_barrier_semaphore()
    nz = lax.axis_size("z")
    for d in ids:
        pl.semaphore_signal(barrier, inc=1, device_id=d, device_id_type=MESH)

    @pl.when(p.z > 0)
    def _():
        pl.semaphore_signal(barrier, inc=1, device_id={"z": p.z - 1}, device_id_type=MESH)

    @pl.when(p.z < nz - 1)
    def _():
        pl.semaphore_signal(barrier, inc=1, device_id={"z": p.z + 1}, device_id_type=MESH)

    ends = jnp.where(p.z == 0, 1, 0) + jnp.where(p.z == nz - 1, 1, 0)
    pl.semaphore_wait(barrier, len(ids) + 2 - ends)


def relay_sems(nz):
    return [DMA((3,)), DMA((3,)), DMA((1,)), DMA((2, nz, 3)), DMA((nz, 3))]


class Relay:
    def __init__(self, p, w, dst, c0, sems):
        self.p, self.w, self.dst, self.c0 = p, w, dst, c0
        self.xs, self.xr, self.ls, self.zs, self.zr = sems
        self.nz = lax.axis_size("z")
        self.part = w.shape[0]
        self.n = self.part // self.nz
        self.fb = w.shape[1] // 8

    def cols(self, d):
        return pl.ds(pl.multiple_of((self.p.shard(d) * 2 + self.p.c) * self.fb, self.fb), self.fb)

    def rows(self, d, q):
        return self.dst.at[pl.ds(self.p.shard(d) * self.part + q * self.n, self.n), pl.ds(self.c0, self.fb)]

    def fetch(self, d):
        src = self.w.at[pl.ds(self.p.z * self.n, self.n), self.cols(d)]
        return rcopy(src, self.rows(0, self.p.z), self.xs.at[d - 1], self.xr.at[d - 1], self.p.to(d))

    def local(self):
        dst = self.dst.at[pl.ds(self.p.s * self.part, self.part), pl.ds(self.c0, self.fb)]
        return pltpu.make_async_copy(self.w.at[:, self.cols(0)], dst, self.ls.at[0])

    def along(self, way, q, d):
        ref = self.rows(d, q)
        to = {"z": self.p.z + (1 if way else -1)}
        return rcopy(ref, ref, self.zs.at[way, q, d - 1], self.zr.at[q, d - 1], to)

    def start(self):
        for d in (3, 1, 2):
            self.fetch(d).start()
        self.local().start()

    def can(self, way):
        return self.p.z < self.nz - 1 if way else self.p.z > 0

    def own(self):
        for d in (1, 2, 3):
            self.fetch(d).wait_recv()
        for way in (0, 1):

            @pl.when(self.can(way))
            def _():
                for d in (1, 2, 3):
                    self.along(way, self.p.z, d).start()

    def hop(self, k):
        for way in (0, 1):
            q = self.p.z - k if way else self.p.z + k
            there = q >= 0 if way else q < self.nz

            @pl.when(there)
            def _():
                for d in (1, 2, 3):
                    self.along(way, q, d).wait_recv()

            @pl.when(jnp.logical_and(there, self.can(way)))
            def _():
                for d in (1, 2, 3):
                    self.along(way, q, d).start()

    def finish(self):
        self.local().wait()
        for d in (1, 2, 3):
            self.fetch(d).wait_send()
        for k in range(self.nz):
            for way in (0, 1):
                q = self.p.z - k if way else self.p.z + k
                there = q >= 0 if way else q < self.nz

                @pl.when(jnp.logical_and(there, self.can(way)))
                def _():
                    for d in (1, 2, 3):
                        self.along(way, q, d).wait_send()


def enter_kernel(
    x_ref, seg_ref, gain_ref, wq_ref, wk_ref, wv_ref, wg_ref,
    xa_ref, wqkv_ref, sega_ref, gaina_ref, wgate_ref, *sems
):
    p = Place()
    others = [(0, 1)] + [(d, o) for d in (1, 2, 3) for o in (0, 1)]

    def dev(d, o):
        return {"core": 1 - p.c if o else p.c, "shard": p.shard(d)}

    greet_line(p, [dev(d, o) for d, o in others])
    ga = Gather(p, x_ref, xa_ref, sems[:5])
    co = Columns(p, sems[5:8])
    tsend, trecv, tlocal = sems[8:11]
    re = Relay(p, wg_ref, wgate_ref, 0, sems[11:16])
    re.start()
    ga.start()
    part = wq_ref.shape[0]
    hd = HEAD_DIM

    def small(k):
        d, o = others[k]
        block = sega_ref.at[p.c * 4 + p.s]
        yield rcopy(seg_ref, block, tsend.at[k], trecv.at[k], dev(d, o))
        if d and not o:
            yield rcopy(gain_ref, gaina_ref.at[p.s], tsend.at[7 + d - 1], trecv.at[7 + d - 1], dev(d, o))

    smalls = [cp for k in range(7) for cp in small(k)]
    smalls_here = [
        pltpu.make_async_copy(seg_ref, sega_ref.at[p.c * 4 + p.s], tlocal.at[0]),
        pltpu.make_async_copy(gain_ref, gaina_ref.at[p.s], tlocal.at[1]),
    ]
    for cp in smalls + smalls_here:
        cp.start()

    def q_copy(d):
        src = co.cols(p.shard(d) * 2 + p.c, d, wq_ref, hd)
        return co.copy(0, d, src, rows_at(wqkv_ref, p.s * part, part, 0, hd))

    def kv_copy(d, w):
        src = co.cols(p.shard(d), d, w, hd)
        return co.copy(1, d, src, rows_at(wqkv_ref, p.s * part, part, hd, hd))

    for d in (3, 1, 2, 0):
        q_copy(d).start()

        @pl.when(p.c == 0)
        def _():
            kv_copy(d, wk_ref).start()

        @pl.when(p.c != 0)
        def _():
            kv_copy(d, wv_ref).start()

    re.own()
    ga.relay()
    re.hop(1)
    ga.early()
    for k in range(2, lax.axis_size("z")):
        re.hop(k)
    ga.finish(early=True)
    for d in (3, 1, 2, 0):
        q_copy(d).wait()
        kv_copy(d, wk_ref).wait()
    for cp in smalls + smalls_here:
        cp.wait()
    re.finish()


def enter(x, seg, gains, wq, wk, wv, wg):
    rows, width = x.shape
    return pl.pallas_call(
        enter_kernel,
        out_shape=(
            jax.ShapeDtypeStruct((8 * rows, width), BF),
            jax.ShapeDtypeStruct((width, 2 * HEAD_DIM), BF),
            jax.ShapeDtypeStruct((8, *seg.shape), jnp.int32),
            jax.ShapeDtypeStruct((4, *gains.shape), F32),
            jax.ShapeDtypeStruct((width, wg.shape[1] // 8), BF),
        ),
        in_specs=[VM, VM, VM, ANY, ANY, ANY, ANY],
        out_specs=(ANY, ANY, VM, VM, ANY),
        scratch_shapes=GATHER_SEMS
        + [DMA((2, 3)), DMA((2, 3)), DMA((2,)), DMA((10,)), DMA((10,)), DMA((2,))]
        + relay_sems(lax.axis_size("z")),
        compiler_params=params(0, 16),
        name="enter",
    )(x, seg, gains, wq, wk, wv, wg)


def middle_kernel(part_ref, x_ref, gain_ref, g_ref, wu_ref, h_ref, xn_ref, ga_ref, wup_ref, xnb, *scr):
    p = Place()
    greet_line(p, plane_ids(p))
    sc = Scatter(p, part_ref, scr[:8])
    gx = Gather(p, xnb, xn_ref, scr[8:13])
    gg = Gather(p, g_ref, ga_ref, scr[13:18])
    re = Relay(p, wu_ref, wup_ref, 0, scr[18:23])
    sc.start()
    re.start()
    sc.first()
    re.own()
    gg.start()
    sc.relay()
    re.hop(1)
    half = sc.half
    for h in (0, 1):
        r = pl.ds(h * half, half)
        res = x_ref[r].astype(F32) + sc.total(h)
        h_ref[r] = res
        f = lax.rsqrt(jnp.mean(res * res, axis=1, keepdims=True) + norm_eps)
        xnb[r] = (res * f * gain_ref[...]).astype(BF)
    gx.start()
    gg.relay()
    for k in range(2, lax.axis_size("z")):
        re.hop(k)
    gg.early()
    gx.relay()
    gg.finish(early=True)
    gx.finish()
    sc.drain()
    re.finish()


def middle(part, x, gain2, g, wu):
    rows, width = x.shape
    return pl.pallas_call(
        middle_kernel,
        out_shape=(
            jax.ShapeDtypeStruct((rows, width), F32),
            jax.ShapeDtypeStruct((8 * rows, width), BF),
            jax.ShapeDtypeStruct((8 * rows, width), BF),
            jax.ShapeDtypeStruct((width, wu.shape[1] // 8), BF),
        ),
        in_specs=[ANY, VM, VM, VM, ANY],
        out_specs=(VM, ANY, ANY, ANY),
        scratch_shapes=[pltpu.VMEM((rows, width), BF)]
        + scatter_scratch(rows, width)
        + GATHER_SEMS * 2
        + relay_sems(lax.axis_size("z")),
        compiler_params=params(1, 48),
        name="middle",
    )(part, x, gain2, g, wu)


CH = 64
DOWN, GU, OUT, QKV = range(4)


class Chain:
    def __init__(self, p, h, ins, outs, bufs, sems):
        self.p, self.h = p, h
        self.ins = ins
        if outs:
            self.gate, self.up, self.down, self.out, self.wq, self.wk, self.wv = outs
        self.pre, self.buf, self.bufq = bufs
        self.rs_send, self.rs_recv = sems[:2]
        if outs:
            self.ag_send, self.ag_recv, self.cp_send, self.cp_recv, self.tsend = sems[2:]
        nz = lax.axis_size("z")
        self.nz = nz
        self.pos = nz - 1 - p.z if h == 0 else p.z
        self.step = -1 if h == 0 else 1

    def dev(self, by):
        return {"z": self.p.z + by}

    BASE = {DOWN: 0, GU: 8, OUT: 24, QKV: 26}

    def tick(self, kind, t):
        return self.BASE[kind] + t

    def shard_of(self, t):
        s, d = self.p.s, lax.rem(t, 4)
        one = s + 1 - 2 * lax.rem(s, 2)
        two = lax.rem(s + 2, 4)
        return jnp.where(d == 0, s, jnp.where(d == 1, one, jnp.where(d == 2, two, 3 - s)))

    def mine(self, kind, t):
        h = self.h
        if kind == DOWN:
            return self.ins[DOWN].at[pl.ds(h * 512 + t * CH, CH)]
        if kind == OUT:
            return self.ins[OUT].at[pl.ds(h * 128 + t * CH, CH)]
        row = self.shard_of(t) * 512 + h * 256
        if kind == QKV:
            return self.ins[QKV].at[pl.ds(row, 256)]
        return self.ins[GU].at[pl.ds(row + (t // 4) * CH, CH)]

    def slot(self, kind, t, pre):
        if kind == QKV:
            return self.bufq.at[t]
        k = self.tick(kind, t)
        return self.pre.at[k] if pre else self.buf.at[k - PRE]

    def rs_copy(self, kind, t, src, pre):
        k = self.tick(kind, t)
        return rcopy(
            src, self.slot(kind, t, pre), self.rs_send.at[k], self.rs_recv.at[k], self.dev(self.step)
        )

    def reduce(self, kind, t, pre):
        first, last = self.pos == 0, self.pos == self.nz - 1

        @pl.when(first)
        def _():
            self.rs_copy(kind, t, self.mine(kind, t), pre).start()

        @pl.when(jnp.logical_not(first))
        def _():
            slot = self.slot(kind, t, pre)
            self.rs_copy(kind, t, slot, pre).wait_recv()
            slot[...] = (slot[...].astype(F32) + self.mine(kind, t)[...].astype(F32)).astype(BF)

        @pl.when(jnp.logical_and(jnp.logical_not(first), jnp.logical_not(last)))
        def _():
            self.rs_copy(kind, t, self.slot(kind, t, pre), pre).start()

        if not pre:

            @pl.when(last)
            def _():
                self.turn(kind, t, False)

    def turn_pre(self, kind, t, pre):
        @pl.when(self.pos == self.nz - 1)
        def _():
            self.turn(kind, t, True)

    def pieces(self, kind, t, s, d_shard):
        h, c = self.h, self.p.c
        if kind == DOWN:
            return [(None, self.down.at[pl.ds(c * 1024 + h * 512 + t * CH, CH)])]
        if kind == OUT:
            return [(None, self.out.at[pl.ds(c * 256 + h * 128 + t * CH, CH)])]
        if kind == GU:
            r = h * 256 + (t // 4) * CH
            c0 = pl.multiple_of((s * 2 + c) * 1024, 1024)
            return [
                ((0, 1024), self.gate.at[pl.ds(r, CH), pl.ds(c0, 1024)]),
                ((1024, 1024), self.up.at[pl.ds(r, CH), pl.ds(c0, 1024)]),
            ]
        r = h * 256
        cq = pl.multiple_of((s * 2 + c) * 256, 256)
        return [((0, 256), self.wq.at[pl.ds(r, 256), pl.ds(cq, 256)])]

    def kv_piece(self, s, w):
        return w.at[pl.ds(self.h * 256, 256), pl.ds(pl.multiple_of(s * 256, 256), 256)]

    def turn(self, kind, t, pre):
        slot = self.slot(kind, t, pre)
        k = self.tick(kind, t)
        to = self.p.s if kind in (DOWN, OUT) else self.shard_of(t)

        def send(i, src, dst):
            if kind in (DOWN, OUT):
                pltpu.make_async_copy(src, dst, self.ag_recv.at[i, k]).start()
                return

            @pl.when(lax.rem(t, 4) == 0)
            def _():
                pltpu.make_async_copy(src, dst, self.ag_recv.at[i, k]).start()

            @pl.when(lax.rem(t, 4) != 0)
            def _():
                rcopy(src, dst, self.tsend.at[i, k], self.ag_recv.at[i, k], {"shard": to}).start()

        for i, (cols, dst) in enumerate(self.pieces(kind, t, self.p.s, to)):
            send(i, slot if cols is None else slot.at[:, pl.ds(*cols)], dst)
        if kind == QKV:
            src = slot.at[:, pl.ds(256, 256)]

            @pl.when(self.p.c == 0)
            def _():
                send(1, src, self.kv_piece(self.p.s, self.wk))

            @pl.when(self.p.c != 0)
            def _():
                send(1, src, self.kv_piece(self.p.s, self.wv))

    def spread_copy(self, i, k, ref):
        return rcopy(ref, ref, self.ag_send.at[i, k], self.ag_recv.at[i, k], self.dev(-self.step))

    def spread(self, kind, t, pre):
        k = self.tick(kind, t)
        s = self.p.s if kind in (DOWN, OUT) else self.shard_of(t)

        def go(i, ref, wait=True):
            if wait:
                self.spread_copy(i, k, ref).wait_recv()

            @pl.when(self.pos > 0)
            def _():
                self.spread_copy(i, k, ref).start()

            rcopy(ref, ref, self.cp_send.at[i, k], self.cp_recv.at[i, k], self.p.sibling()).start()

        for i, (_, ref) in enumerate(self.pieces(kind, t, s, None)):
            go(i, ref)
        if kind == QKV:
            self.spread_copy(1, k, self.kv_piece(s, self.wk)).wait_recv()

            @pl.when(self.p.c == 0)
            def _():
                go(1, self.kv_piece(s, self.wk), False)

            @pl.when(self.p.c != 0)
            def _():
                go(1, self.kv_piece(s, self.wv), False)

    def drain_reduce(self, kind, t, pre):
        @pl.when(self.pos < self.nz - 1)
        def _():
            self.rs_copy(kind, t, self.slot(kind, t, pre), pre).wait_send()

    def drain_turn(self, kind, t, pre):
        if kind not in (GU, QKV):
            return
        k = self.tick(kind, t)

        @pl.when(jnp.logical_and(self.pos == self.nz - 1, lax.rem(t, 4) != 0))
        def _():
            slot = self.slot(kind, t, pre)
            for i, (cols, dst) in enumerate(self.pieces(kind, t, self.p.s, None)):
                src = slot.at[:, pl.ds(*cols)]
                rcopy(src, dst, self.tsend.at[i, k], self.ag_recv.at[i, k], self.p.to(1)).wait_send()
            if kind == QKV:
                src = slot.at[:, pl.ds(256, 256)]
                dst = self.kv_piece(self.p.s, self.wk)
                rcopy(src, dst, self.tsend.at[1, k], self.ag_recv.at[1, k], self.p.to(1)).wait_send()

    def drain_spread(self, kind, t, pre):
        k = self.tick(kind, t)
        s = self.p.s if kind in (DOWN, OUT) else self.shard_of(t)
        refs = [ref for _, ref in self.pieces(kind, t, s, None)]
        if kind == QKV:
            refs.append(self.kv_piece(s, self.wk))
        for i, ref in enumerate(refs):

            @pl.when(self.pos > 0)
            def _():
                self.spread_copy(i, k, ref).wait_send()

            rcopy(ref, ref, self.cp_send.at[i, k], self.cp_recv.at[i, k], self.p.sibling()).wait()


N_TICKS, PRE = 30, 12
RS_SEMS = [DMA((N_TICKS,)), DMA((N_TICKS,))]
CHAIN_SEMS = RS_SEMS + [DMA((2, N_TICKS))] * 5


def loop(lo, hi, body):
    def step(t, _):
        body(t)
        return 0

    lax.fori_loop(lo, hi, step, 0)


COUNT = {DOWN: 8, GU: 16, OUT: 2, QKV: 4}


SKEW, TURN = 2, 3


def between(i, lo, hi):
    return jnp.logical_and(i >= lo, i < hi)


def each(i, lo, hi, act):
    for kind, n in COUNT.items():
        base = Chain.BASE[kind]
        for pre, first, last in ((True, 0, PRE), (False, PRE, N_TICKS)):
            a, b = max(lo, base, first), min(hi, base + n, last)
            if a < b:

                @pl.when(between(i, a, b))
                def _():
                    act(kind, i - base, pre)


def at_tick(t, when, act):
    @pl.when(t == when)
    def _():
        act()


def back_kernel(
    part_ref, h_ref, g_ref, gain_ref, gd_ref, ggu_ref, dhb_ref, dh_ref, gsum_ref, prea, preb, low, *scr
):
    p = Place()
    greet_line(p, plane_ids(p))
    sc = Scatter(p, part_ref, scr[:8])
    ga = Gather(p, low, dhb_ref, scr[8:13])
    ins = (gd_ref, ggu_ref, None, None)
    chains = [
        Chain(p, 0, ins, None, (prea, None, None), scr[13:15]),
        Chain(p, 1, ins, None, (preb, None, None), scr[15:17]),
    ]
    sc.start()
    sc.first()

    def norm():
        for h in (0, 1):
            r = pl.ds(h * sc.half, sc.half)
            dx = sc.total(h)
            res = h_ref[r]
            f = lax.rsqrt(jnp.mean(res * res, axis=1, keepdims=True) + norm_eps)
            hat = res * f
            term = jnp.sum(dx * hat, axis=0, keepdims=True)
            gsum_ref[...] = term if h == 0 else gsum_ref[...] + term
            dh = g_ref[r].astype(F32) + norm_backward_step(dx * gain_ref[...], hat, f)
            dh_ref[r] = dh
            low[r] = dh.astype(BF)
        ga.start()

    def tick(t):
        for ch in chains:
            each(t - SKEW * ch.pos, 0, PRE, ch.reduce)
        at_tick(t, 1, sc.relay)
        at_tick(t, 5, norm)
        at_tick(t, 7, ga.relay)

    loop(0, PRE + SKEW * (lax.axis_size("z") - 1), tick)
    ga.finish()
    sc.drain()

    def drain(i):
        for ch in chains:
            each(i, 0, PRE, ch.drain_reduce)

    loop(0, PRE, drain)


def back(part, h, g, gain2, g_down, g_gu):
    rows, width = h.shape
    return pl.pallas_call(
        back_kernel,
        out_shape=(
            jax.ShapeDtypeStruct((8 * rows, width), BF),
            jax.ShapeDtypeStruct((rows, width), F32),
            jax.ShapeDtypeStruct((1, width), F32),
            jax.ShapeDtypeStruct((PRE, CH, width), BF),
            jax.ShapeDtypeStruct((PRE, CH, width), BF),
        ),
        in_specs=[ANY, VM, VM, VM, VM, VM],
        out_specs=(ANY, VM, VM, VM, VM),
        scratch_shapes=[pltpu.VMEM((rows, width), BF)]
        + scatter_scratch(rows, width)
        + GATHER_SEMS
        + RS_SEMS * 2,
        compiler_params=params(2, 52),
        name="back",
    )(part, h, g, gain2, g_down, g_gu)


def last_kernel(
    part1_ref, part2_ref, x_ref, h_ref, dh_ref, gain_ref, gsum_ref, prea, preb, ggu_ref, go_ref, gqkv_ref,
    out_ref, grad_ref, gains_ref, gate, up, down, out, wq, wk, wv,
    bufa, bufb, qa, qb, tot, got, gz, gsend, grecv, *scr,
):
    p = Place()
    nz = lax.axis_size("z")
    z_all_enter(p)
    s1 = Scatter(p, part1_ref, scr[:8])
    s2 = Scatter(p, part2_ref, scr[8:16])
    ins = (None, ggu_ref, go_ref, gqkv_ref)
    outs = (gate, up, down, out, wq, wk, wv)
    n = len(CHAIN_SEMS)
    chains = [
        Chain(p, 0, ins, outs, (prea, bufa, qa), scr[16 : 16 + n]),
        Chain(p, 1, ins, outs, (preb, bufb, qb), scr[16 + n : 16 + 2 * n]),
    ]
    line = SKEW * (nz - 1)
    tot[0] = jnp.zeros_like(tot[0])
    s1.start()
    s2.start()
    s1.first()

    def gain_copy(k):
        dev = (p.sibling(), p.to(1), p.to(2))[k]
        return rcopy(tot.at[k], got.at[k], gsend.at[k], grecv.at[k], dev)

    def z_copy(k):
        return rcopy(
            tot.at[3], gz.at[p.z], gsend.at[2 + k], grecv.at[3 + p.z], {"z": lax.rem(p.z + k, nz)}
        )

    def z_landed(k):
        src = lax.rem(p.z + nz - k, nz)
        ref = gz.at[src]
        return rcopy(ref, ref, gsend.at[2 + k], grecv.at[3 + src], {"z": src})

    def finish1():
        for h in (0, 1):
            r = pl.ds(h * s1.half, s1.half)
            dx = s1.total(h)
            xf = x_ref[r].astype(F32)
            f = lax.rsqrt(jnp.mean(xf * xf, axis=1, keepdims=True) + norm_eps)
            hat = xf * f
            term = jnp.sum(dx * hat, axis=0, keepdims=True)
            tot[0, 0:1] = term if h == 0 else tot[0, 0:1] + term
            grad = dh_ref[r] + norm_backward_step(dx * gain_ref[...], hat, f)
            grad_ref[r] = grad.astype(BF)
        tot[0, 1:2] = gsum_ref[...]
        gain_copy(0).start()

    def add_gains(k):
        gain_copy(k).wait()
        tot[k + 1] = tot[k] + got[k]
        if k < 2:
            gain_copy(k + 1).start()
        else:
            for j in range(1, nz):
                z_copy(j).start()
            gz[p.z] = tot[3]

    def finish_gains():
        for j in range(1, nz):
            z_copy(j).wait_send()
            z_landed(j).wait_recv()
        total = gz[0]
        for j in range(1, nz):
            total = total + gz[j]
        gains_ref[...] = total

    def finish2():
        for h in (0, 1):
            r = pl.ds(h * s2.half, s2.half)
            out_ref[r] = (h_ref[r] + s2.total(h)).astype(BF)

    def tick(t):
        for ch in chains:
            each(t, 0, PRE, ch.turn_pre)
            each(t + PRE - SKEW * ch.pos, PRE, N_TICKS, ch.reduce)
        for ch in chains:
            each(t - TURN - line + SKEW * ch.pos, 0, N_TICKS, ch.spread)
        at_tick(t, 1, s1.relay)
        at_tick(t, 2, s2.first)
        at_tick(t, 5, finish1)
        at_tick(t, 6, s2.relay)
        for k in range(3):
            at_tick(t, 7 + 2 * k, functools.partial(add_gains, k))
        at_tick(t, 10, finish2)
        at_tick(t, 16, finish_gains)

    loop(0, N_TICKS + TURN + line, tick)
    s1.drain()
    s2.drain()

    def drain(i):
        for ch in chains:
            each(i, PRE, N_TICKS, ch.drain_reduce)
            each(i, 0, N_TICKS, ch.drain_turn)
            each(i, 0, N_TICKS, ch.drain_spread)

    loop(0, N_TICKS, drain)


def z_all_enter(p):
    barrier = pltpu.get_barrier_semaphore()
    nz = lax.axis_size("z")
    ids = plane_ids(p) + [{"z": lax.rem(p.z + k, nz)} for k in range(1, nz)]
    for d in ids:
        pl.semaphore_signal(barrier, inc=1, device_id=d, device_id_type=MESH)
    pl.semaphore_wait(barrier, len(ids))


def last(part1, part2, x, h, dh, gain1, gsum2, pre, g_gu, g_out, g_qkv, part, ff):
    rows, width = x.shape
    nz = lax.axis_size("z")
    shapes = [(part, ff), (part, ff), (ff // 4, width), (part, width), (part, width), (part, 1024), (part, 1024)]
    return pl.pallas_call(
        last_kernel,
        out_shape=(
            jax.ShapeDtypeStruct((rows, width), BF),
            jax.ShapeDtypeStruct((rows, width), BF),
            jax.ShapeDtypeStruct((8, width), F32),
        )
        + tuple(jax.ShapeDtypeStruct(s, BF) for s in shapes),
        in_specs=[ANY, ANY] + [VM] * 10,
        out_specs=(VM, VM, VM) + (ANY,) * 7,
        scratch_shapes=[
            pltpu.VMEM((26 - PRE, CH, width), BF),
            pltpu.VMEM((26 - PRE, CH, width), BF),
            pltpu.VMEM((4, 256, 512), BF),
            pltpu.VMEM((4, 256, 512), BF),
            pltpu.VMEM((4, 8, width), F32),
            pltpu.VMEM((3, 8, width), F32),
            pltpu.VMEM((nz, 8, width), F32),
            DMA((nz + 3,)),
            DMA((nz + 3,)),
        ]
        + scatter_scratch(rows, width) * 2
        + CHAIN_SEMS * 2,
        compiler_params=params(3, 62),
        name="last",
    )(part1, part2, x, h, dh, gain1, gsum2, *pre, g_gu, g_out, g_qkv)


def pieces(
    tokens,
    segment_ids,
    attn_gain,
    w_query,
    w_key,
    w_value,
    w_out,
    mlp_gain,
    w_gate,
    w_up,
    w_down,
    cotangent,
):
    rows, width = tokens.shape[1], tokens.shape[2]
    core = lax.axis_index("core")
    nc, ns = lax.axis_size("core"), lax.axis_size("shard")
    hd = HEAD_DIM
    ff = w_gate.shape[1]
    fb = ff // (nc * ns)
    part = width // ns

    x = tokens.reshape(rows, width)
    g = cotangent.reshape(rows, width)
    wo = lax.dynamic_slice_in_dim(w_out, core * hd, hd, 0)
    wd = lax.dynamic_slice_in_dim(w_down, core * fb, fb, 0)

    gains = jnp.concatenate([attn_gain[None], mlp_gain[None], jnp.zeros((6, part), BF)], 0).astype(F32)
    seg8 = jnp.broadcast_to(segment_ids, (8, rows))
    x_all, wqkv, seg, gains, wgate = enter(x, seg8, gains, w_query, w_key, w_value, w_gate)
    seg = seg[:, 0]
    gain1, gain2 = gains[:, 0].reshape(1, width), gains[:, 1].reshape(1, width)
    nseq = nc * ns

    iota = jnp.arange(rows, dtype=jnp.int32)
    same = seg[:, :, None] == seg[:, None, :]
    allowed = same & (iota[:, None] >= iota[None, :])[None]
    starts = jnp.sum((seg[:, None, :] < seg[:, :, None]).astype(jnp.int32), axis=2)
    positions = (iota[None, :] - starts).astype(F32)
    half = hd // 2
    inv_freq = rope_base ** (-(jnp.arange(half, dtype=F32) * 2.0 / hd))
    angles = positions[..., None] * inv_freq
    cosine, sine = jnp.cos(angles), jnp.sin(angles)

    xf_all = x_all.astype(F32)
    f1_all = lax.rsqrt(jnp.mean(xf_all * xf_all, axis=1, keepdims=True) + norm_eps)
    xn1 = (xf_all * f1_all * gain1).astype(BF)
    qkv = mm(xn1, wqkv).reshape(nseq, rows, 2 * hd)
    q = rotate(qkv[..., :hd], cosine, sine).astype(BF)
    kv_lin = qkv[..., hd:]
    kv_mine = jnp.where(core == 0, rotate(kv_lin, cosine, sine), kv_lin).astype(BF)
    swap = [(i, nc - 1 - i) for i in range(nc)]
    kv_other = lax.ppermute(kv_mine, "core", swap)
    k = jnp.where(core == 0, kv_mine, kv_other)
    v = jnp.where(core == 0, kv_other, kv_mine)
    scale = hd ** (-0.5)
    scores = jnp.einsum("bqd,bkd->bqk", q, k, preferred_element_type=F32) * scale
    scores = jnp.where(allowed, scores, mask_fill)
    top = jnp.max(scores, axis=-1, keepdims=True)
    ex = jnp.exp(scores - top)
    probs = ex / jnp.sum(ex, axis=-1, keepdims=True)
    pb = probs.astype(BF)
    attn = jnp.einsum("bqk,bkd->bqd", pb, v, preferred_element_type=F32).astype(BF)
    attn = attn.reshape(nseq * rows, hd)

    h, xn2, g_all, wup = middle(mm(attn, wo).astype(BF), x, gain2, g, w_up)

    gate, up = mm(xn2, wgate), mm(xn2, wup)
    sigma = jax.nn.sigmoid(gate)
    swish = gate * sigma
    hid = (swish * up).astype(BF)
    g_down = mm_tn(hid, g_all).astype(BF)
    dhid = mm_nt(g_all, wd)
    dgate = (dhid * up * sigma * (1.0 + gate * (1.0 - sigma))).astype(BF)
    dup = (dhid * swish).astype(BF)
    dgu = jnp.concatenate([dgate, dup], 1)
    g_gu = mm_tn(xn2, dgu).astype(BF)
    dhb, dh, gsum2, prea, preb = back((mm_nt(dgate, wgate) + mm_nt(dup, wup)).astype(BF), h, g, gain2, g_down, g_gu)
    g_out = mm_tn(attn, dhb).astype(BF)
    dattn = mm_nt(dhb, wo).astype(BF).reshape(nseq, rows, hd)
    dp = jnp.einsum("bqd,bkd->bqk", dattn, v, preferred_element_type=F32)
    dv = jnp.einsum("bqk,bqd->bkd", pb, dattn, preferred_element_type=F32)
    ds = (probs * (dp - jnp.sum(dp * probs, axis=-1, keepdims=True))).astype(BF)
    dq = jnp.einsum("bqk,bkd->bqd", ds, k, preferred_element_type=F32) * scale
    dk = jnp.einsum("bqk,bqd->bkd", ds, q, preferred_element_type=F32) * scale
    dq = rotate(dq, cosine, -sine).astype(BF)
    dk = rotate(dk, cosine, -sine)
    mine = jnp.where(core == 0, dk, dv)
    other = jnp.where(core == 0, dv, dk).astype(BF)
    dkv = (mine + lax.ppermute(other, "core", swap).astype(F32)).astype(BF)
    dqkv = jnp.concatenate([dq, dkv], -1).reshape(nseq * rows, 2 * hd)
    g_qkv = mm_tn(xn1, dqkv).astype(BF)
    output, input_grad, gain_g, gate_g, up_g, down_g, out_g, wq_g, wk_g, wv_g = last(
        mm_nt(dqkv, wqkv).astype(BF),
        mm(hid, wd).astype(BF),
        x,
        h,
        dh,
        gain1,
        gsum2,
        (prea, preb),
        g_gu,
        g_out,
        g_qkv,
        part,
        ff,
    )
    output = output.reshape(1, rows, width)
    input_grad = input_grad.reshape(1, rows, width)
    gain_g = lax.dynamic_slice_in_dim(gain_g, lax.axis_index("shard") * part, part, 1)
    return (
        output,
        input_grad,
        gain_g[0],
        wq_g.astype(F32),
        wk_g.astype(F32),
        wv_g.astype(F32),
        out_g.astype(F32),
        gain_g[1],
        gate_g.astype(F32),
        up_g.astype(F32),
        down_g.astype(F32),
    )


def contract_rows(left, right):
    return lax.dot_general(
        left, right, (((0,), (0,)), ((), ())), preferred_element_type=jnp.float32
    )


def contract_cols(left, right):
    return lax.dot_general(
        left, right, (((1,), (1,)), ((), ())), preferred_element_type=jnp.float32
    )


def scores_of(queries, keys, allowed):
    raw = jnp.einsum(
        "qgrd,kgd->grqk", queries, keys, preferred_element_type=jnp.float32
    ) * HEAD_DIM ** (-0.5)
    return jnp.where(allowed, raw, mask_fill)


def general(
    tokens,
    segment_ids,
    attn_gain,
    w_query,
    w_key,
    w_value,
    w_out,
    mlp_gain,
    w_gate,
    w_up,
    w_down,
    cotangent,
):
    rows = tokens.shape[1]
    width = tokens.shape[2]
    groups = HEADS // KV_HEADS
    q_cols = HEADS * HEAD_DIM
    kv_cols = KV_HEADS * HEAD_DIM
    layer_input_rows = tokens.reshape(rows, width).astype(jnp.float32)
    segments = segment_ids.reshape(rows)
    iota = jnp.arange(rows, dtype=jnp.int32)
    starts = jnp.sum((segments[None, :] < segments[:, None]).astype(jnp.int32), axis=1)
    positions = (iota - starts).astype(jnp.float32)
    allowed = (segments[:, None] == segments[None, :]) & (iota[:, None] >= iota[None, :])
    half = HEAD_DIM // 2
    inv_freq = rope_base ** (-(jnp.arange(half, dtype=jnp.float32) * 2.0 / HEAD_DIM))
    angles = positions[:, None] * inv_freq
    cosine = jnp.cos(angles)
    sine = jnp.sin(angles)
    first_norm_factor = lax.rsqrt(
        jnp.mean(layer_input_rows * layer_input_rows, axis=1, keepdims=True) + norm_eps
    )
    first_standardized = layer_input_rows * first_norm_factor
    gain_fragment = lax.all_gather(attn_gain, "shard", axis=0, tiled=True)
    query_piece = lax.all_gather(w_query, "shard", axis=0, tiled=True)
    key_piece = lax.all_gather(w_key, "shard", axis=0, tiled=True)
    value_piece = lax.all_gather(w_value, "shard", axis=0, tiled=True)
    normalized_rows = (first_standardized * gain_fragment.astype(jnp.float32)).astype(jnp.bfloat16)
    joined = jnp.concatenate([query_piece, key_piece, value_piece], 1)
    result = (
        jnp.dot(normalized_rows, joined, preferred_element_type=jnp.float32),
        normalized_rows,
        gain_fragment.astype(jnp.float32),
    )
    folded = result
    projected, normed_one, first_norm_gain = (folded[0], folded[1], folded[2])
    queries = rotate(
        projected[:, :q_cols].reshape(rows, KV_HEADS, groups, HEAD_DIM),
        cosine[:, None, None, :],
        sine[:, None, None, :],
    ).astype(jnp.bfloat16)
    keys = rotate(
        projected[:, q_cols : q_cols + kv_cols].reshape(rows, KV_HEADS, HEAD_DIM),
        cosine[:, None, :],
        sine[:, None, :],
    ).astype(jnp.bfloat16)
    values = projected[:, q_cols + kv_cols :].reshape(rows, KV_HEADS, HEAD_DIM).astype(jnp.bfloat16)
    scores = scores_of(queries, keys, allowed)
    top = jnp.max(scores, axis=-1, keepdims=True)
    log_total = top + jnp.log(jnp.sum(jnp.exp(scores - top), axis=-1, keepdims=True))
    probs = jnp.exp(scores - log_total)
    probs_low = probs.astype(jnp.bfloat16)
    attn = (
        jnp.einsum("grqk,kgd->qgrd", probs_low, values, preferred_element_type=jnp.float32)
        .reshape(rows, q_cols)
        .astype(jnp.bfloat16)
    )
    part = attn
    result = (
        jnp.dot(
            part,
            lax.all_gather(w_out, "shard", axis=0, tiled=True),
            preferred_element_type=jnp.float32,
        ),
    )
    folded_out = result
    residual_hidden_state = layer_input_rows + folded_out[0]
    second_norm_factor = lax.rsqrt(
        jnp.mean(residual_hidden_state * residual_hidden_state, axis=1, keepdims=True) + norm_eps
    )
    second_standardized = residual_hidden_state * second_norm_factor
    gain_fragment = lax.all_gather(mlp_gain, "shard", axis=0, tiled=True)
    gate_piece = lax.all_gather(w_gate, "shard", axis=0, tiled=True)
    up_piece = lax.all_gather(w_up, "shard", axis=0, tiled=True)
    normalized_rows = (second_standardized * gain_fragment.astype(jnp.float32)).astype(jnp.bfloat16)
    joined = jnp.concatenate([gate_piece, up_piece], 1)
    result = (
        jnp.dot(normalized_rows, joined, preferred_element_type=jnp.float32),
        normalized_rows,
        gain_fragment.astype(jnp.float32),
    )
    folded_mlp = result
    gate = folded_mlp[0][:, :FF]
    up_value = folded_mlp[0][:, FF:]
    normed_two = folded_mlp[1]
    second_norm_gain = folded_mlp[2]
    sigma = jax.nn.sigmoid(gate)
    swish = gate * sigma
    inner = (swish * up_value).astype(jnp.bfloat16)
    part = inner
    result = (
        jnp.dot(
            part,
            lax.all_gather(w_down, "shard", axis=0, tiled=True),
            preferred_element_type=jnp.float32,
        ),
    )
    output = (residual_hidden_state + result[0]).astype(jnp.bfloat16).reshape(1, rows, width)
    grad_out = cotangent.reshape(rows, width)
    grad_down = lax.psum_scatter(
        contract_rows(inner, grad_out).astype(jnp.bfloat16),
        "shard",
        scatter_dimension=0,
        tiled=True,
    )
    down_full, gate_full, up_full = (
        lax.all_gather(w_down, "shard", axis=0, tiled=True),
        lax.all_gather(w_gate, "shard", axis=0, tiled=True),
        lax.all_gather(w_up, "shard", axis=0, tiled=True),
    )
    grad_inner = contract_cols(grad_out, down_full)
    grad_gate = (grad_inner * up_value * sigma * (1.0 + gate * (1.0 - sigma))).astype(jnp.bfloat16)
    grad_up = (grad_inner * swish).astype(jnp.bfloat16)
    grad_mlp = jnp.concatenate([grad_gate, grad_up], 1)
    mlp_shards = lax.psum_scatter(
        contract_rows(normed_two, grad_mlp).astype(jnp.bfloat16),
        "shard",
        scatter_dimension=0,
        tiled=True,
    ).astype(jnp.float32)
    second_norm_gradient = contract_cols(grad_gate, gate_full) + contract_cols(grad_up, up_full)
    second_gain_products = jnp.sum(second_norm_gradient * second_standardized, axis=0)
    hidden_gradient = grad_out.astype(jnp.float32) + norm_backward_step(
        second_norm_gradient * second_norm_gain, second_standardized, second_norm_factor
    )
    grad_hidden_low = hidden_gradient.astype(jnp.bfloat16)
    grad_out_proj = lax.psum_scatter(
        contract_rows(attn, grad_hidden_low).astype(jnp.bfloat16),
        "shard",
        scatter_dimension=0,
        tiled=True,
    )
    grad_attn = contract_cols(grad_hidden_low, lax.all_gather(w_out, "shard", axis=0, tiled=True))
    grad_attn = grad_attn.astype(jnp.bfloat16).reshape(rows, KV_HEADS, groups, HEAD_DIM)
    scores_again = scores_of(queries, keys, allowed)
    probs_again = jnp.exp(scores_again - log_total)
    probs_again_low = probs_again.astype(jnp.bfloat16)
    grad_probs = jnp.einsum("qgrd,kgd->grqk", grad_attn, values, preferred_element_type=jnp.float32)
    grad_values = jnp.einsum(
        "grqk,qgrd->kgd", probs_again_low, grad_attn, preferred_element_type=jnp.float32
    )
    grad_scores = (
        probs_again * (grad_probs - jnp.sum(grad_probs * probs_again, axis=-1, keepdims=True))
    ).astype(jnp.bfloat16)
    grad_queries = jnp.einsum(
        "grqk,kgd->qgrd", grad_scores, keys, preferred_element_type=jnp.float32
    ) * HEAD_DIM ** (-0.5)
    grad_keys = jnp.einsum(
        "grqk,qgrd->kgd", grad_scores, queries, preferred_element_type=jnp.float32
    ) * HEAD_DIM ** (-0.5)
    grad_queries = rotate(grad_queries, cosine[:, None, None, :], -sine[:, None, None, :]).reshape(
        rows, q_cols
    )
    grad_keys = rotate(grad_keys, cosine[:, None, :], -sine[:, None, :]).reshape(rows, kv_cols)
    grad_joined = jnp.concatenate(
        [
            grad_queries.astype(jnp.bfloat16),
            grad_keys.astype(jnp.bfloat16),
            grad_values.reshape(rows, kv_cols).astype(jnp.bfloat16),
        ],
        1,
    )
    qkv_shards = lax.psum_scatter(
        contract_rows(normed_one, grad_joined).astype(jnp.bfloat16),
        "shard",
        scatter_dimension=0,
        tiled=True,
    ).astype(jnp.float32)
    local_qkv = jnp.concatenate([w_query, w_key, w_value], 1)
    first_norm_gradient = contract_cols(
        grad_joined, lax.all_gather(local_qkv, "shard", axis=0, tiled=True)
    )
    first_gain_products = jnp.sum(first_norm_gradient * first_standardized, axis=0)
    input_gradient_rows = hidden_gradient + norm_backward_step(
        first_norm_gradient * first_norm_gain, first_standardized, first_norm_factor
    )
    input_grad = input_gradient_rows.astype(jnp.bfloat16).reshape(1, rows, width)
    gain_one_grad, gain_two_grad = (
        lax.psum_scatter(first_gain_products, "shard", scatter_dimension=0, tiled=True),
        lax.psum_scatter(second_gain_products, "shard", scatter_dimension=0, tiled=True),
    )
    summed = (
        lax.psum(gain_one_grad.astype(jnp.bfloat16), "rep").astype(jnp.float32),
        lax.psum(qkv_shards[:, :q_cols].astype(jnp.bfloat16), "rep").astype(jnp.float32),
        lax.psum(qkv_shards[:, q_cols : q_cols + kv_cols].astype(jnp.bfloat16), "rep").astype(
            jnp.float32
        ),
        lax.psum(qkv_shards[:, q_cols + kv_cols :].astype(jnp.bfloat16), "rep").astype(jnp.float32),
        lax.psum(grad_out_proj, "rep").astype(jnp.float32),
        lax.psum(gain_two_grad.astype(jnp.bfloat16), "rep").astype(jnp.float32),
        lax.psum(mlp_shards[:, :FF].astype(jnp.bfloat16), "rep").astype(jnp.float32),
        lax.psum(mlp_shards[:, FF:].astype(jnp.bfloat16), "rep").astype(jnp.float32),
        lax.psum(grad_down, "rep").astype(jnp.float32),
    )
    return (
        output,
        input_grad,
        summed[0],
        summed[1],
        summed[2],
        summed[3],
        summed[4],
        summed[5],
        summed[6],
        summed[7],
        summed[8],
    )


def solution(mesh):
    rep, shard = mesh.devices.shape
    if shard == KV_HEADS and rep % 2 == 0:
        fine = Mesh(np.asarray(mesh.devices).reshape(rep // 2, 2, shard), ("z", "core", "shard"))
        body, every = pieces, ("z", "core", "shard")
    else:
        fine, body, every = mesh, general, ("rep", "shard")
    seqs, vec, mat = P(every, None, None), P("shard"), P("shard", None)
    in_specs = (seqs, P(every, None), vec, mat, mat, mat, mat, vec, mat, mat, mat, seqs)
    out_specs = (seqs, seqs, vec, mat, mat, mat, mat, vec, mat, mat, mat)
    return jax.shard_map(body, mesh=fine, in_specs=in_specs, out_specs=out_specs, check_vma=False)
```

```python
import functools

import jax
import jax.numpy as jnp
import numpy as np
from jax import lax
from jax.experimental import pallas as pl
from jax.experimental.pallas import tpu as pltpu
from jax.sharding import Mesh
from jax.sharding import PartitionSpec as P

HEADS = 8
KV_HEADS = 4
HEAD_DIM = 256
FF = 8192

rope_base = 1000042.0
norm_eps = 1e-06
mask_fill = -1e30

BF = jnp.bfloat16
F32 = jnp.float32
MESH = pl.DeviceIdType.MESH
ANY = pl.BlockSpec(memory_space=pl.ANY)
VM = pl.BlockSpec(memory_space=pltpu.VMEM)
DMA = pltpu.SemaphoreType.DMA


def mm(a, b):
    return jnp.dot(a, b, preferred_element_type=F32)


def mm_tn(a, b):
    return lax.dot_general(a, b, (((0,), (0,)), ((), ())), preferred_element_type=F32)


def mm_nt(a, b):
    return lax.dot_general(a, b, (((1,), (1,)), ((), ())), preferred_element_type=F32)


def rotate(values, cosine, sine):
    half = values.shape[-1] // 2
    first = values[..., :half]
    second = values[..., half:]
    return jnp.concatenate([first * cosine - second * sine, second * cosine + first * sine], -1)


def norm_backward_step(grad_hat, normalized_rows, factor):
    return factor * (
        grad_hat - normalized_rows * jnp.mean(grad_hat * normalized_rows, axis=1, keepdims=True)
    )


class Place:
    def __init__(self):
        self.z = lax.axis_index("z")
        self.c = lax.axis_index("core")
        self.s = lax.axis_index("shard")

    def shard(self, d):
        s = self.s
        if d == 0:
            return s
        if d == 1:
            return s + 1 - 2 * lax.rem(s, 2)
        if d == 2:
            return lax.rem(s + 2, 4)
        return 3 - s

    def to(self, d):
        return {"shard": self.shard(d)}

    def sibling(self):
        return {"core": 1 - self.c}


def greet(ids):
    barrier = pltpu.get_barrier_semaphore()
    for d in ids:
        pl.semaphore_signal(barrier, inc=1, device_id=d, device_id_type=MESH)
    pl.semaphore_wait(barrier, len(ids))


def rcopy(src, dst, send, recv, dev):
    return pltpu.make_async_remote_copy(
        src_ref=src, dst_ref=dst, send_sem=send, recv_sem=recv, device_id=dev, device_id_type=MESH
    )


GATHER_SEMS = [DMA((6,)), DMA((6,)), DMA((7,)), DMA((7,)), DMA((1,))]


class Gather:
    def __init__(self, p, src, out, sems):
        self.p, self.src, self.out = p, src, out
        self.send, self.recv, self.csend, self.crecv, self.lsem = sems
        self.rows = src.shape[0]
        self.half = self.rows // 2

    def at(self, d, h, core=None):
        core = self.p.c if core is None else core
        row = (core * 4 + self.p.shard(d)) * self.rows
        if h is None:
            return self.out.at[pl.ds(row, self.rows)]
        return self.out.at[pl.ds(row + h * self.half, self.half)]

    def move(self, k):
        d, h, to = [(0, 0, 1), (0, 1, 2), (0, 1, 1), (0, 0, 2), (1, 0, 2), (2, 1, 1)][k]
        dst = self.at(d, h)
        src = self.src.at[pl.ds(h * self.half, self.half)] if d == 0 else dst
        return rcopy(src, dst, self.send.at[k], self.recv.at[k], self.p.to(to))

    def landed(self, k):
        d, h = [(1, 0), (2, 1), (1, 1), (2, 0), (3, 0), (3, 1)][k]
        return self.at(d, h)

    def pass_on(self, k):
        here = self.src if k == 6 else self.landed(k)
        there = self.at(0, None) if k == 6 else self.landed(k)
        return rcopy(here, there, self.csend.at[k], self.crecv.at[k], self.p.sibling())

    def arrived(self, k):
        ref = self.landed(k)
        rcopy(ref, ref, self.send.at[k], self.recv.at[k], self.p.to(1)).wait_recv()
        self.pass_on(k).start()

    def start(self):
        for k in range(4):
            self.move(k).start()
        self.pass_on(6).start()
        pltpu.make_async_copy(self.src, self.at(0, None), self.lsem.at[0]).start()

    def relay(self):
        for k in (0, 1):
            self.arrived(k)
            self.move(4 + k).start()

    def early(self):
        for k in (2, 3):
            self.arrived(k)

    def finish(self, early=False):
        if not early:
            self.early()
        for k in (4, 5):
            self.arrived(k)
        for k in range(6):
            self.move(k).wait_send()
        for k in range(7):
            self.pass_on(k).wait()
        pltpu.make_async_copy(self.src, self.at(0, None), self.lsem.at[0]).wait()


SCATTER_SEMS = [DMA((4,)), DMA((4,)), DMA((4,)), DMA((6,)), DMA((6,))]
ORDER = (3, 1, 2, 0)


def scatter_scratch(rows, width):
    half = rows // 2
    return [
        pltpu.VMEM((4, rows, width), BF),
        pltpu.VMEM((4, rows, width), BF),
        pltpu.VMEM((6, half, width), BF),
    ] + SCATTER_SEMS


class Scatter:
    def __init__(self, p, part, scratch):
        self.p, self.part = p, part
        self.own, self.got, self.slot, self.lsem, self.csend, self.crecv, self.send, self.recv = scratch
        self.rows = self.own.shape[1]
        self.half = self.rows // 2

    def block(self, core, d):
        return self.part.at[pl.ds((core * 4 + self.p.shard(d)) * self.rows, self.rows)]

    def local(self, d):
        return pltpu.make_async_copy(self.block(self.p.c, d), self.own.at[d], self.lsem.at[d])

    def swap(self, d):
        src = self.block(1 - self.p.c, d)
        return rcopy(src, self.got.at[d], self.csend.at[d], self.crecv.at[d], self.p.sibling())

    def rowsof(self, h):
        return pl.ds(h * self.half, self.half)

    def move(self, k):
        d, h, to = [(3, 0, 1), (3, 1, 2), (1, 0, 1), (2, 1, 2), (2, 0, 2), (1, 1, 1)][k]
        return rcopy(
            self.own.at[d, self.rowsof(h)], self.slot.at[k], self.send.at[k], self.recv.at[k], self.p.to(to)
        )

    def start(self):
        for d in ORDER:
            self.swap(d).start()
            self.local(d).start()

    def pair(self, d):
        self.swap(d).wait_recv()
        self.local(d).wait()
        self.own[d] = (self.own[d].astype(F32) + self.got[d].astype(F32)).astype(BF)

    def first(self):
        self.pair(3)
        self.move(0).start()
        self.move(1).start()
        self.pair(1)
        self.move(2).start()
        self.pair(2)
        self.move(3).start()
        self.pair(0)

    def relay(self):
        for k, d, h in ((0, 2, 0), (1, 1, 1)):
            self.move(k).wait_recv()
            r = self.rowsof(h)
            self.own[d, r] = (self.own[d, r].astype(F32) + self.slot[k].astype(F32)).astype(BF)
            self.move(4 + k).start()

    def total(self, h):
        near, far = (2, 4) if h == 0 else (3, 5)
        self.move(near).wait_recv()
        self.move(far).wait_recv()
        return (
            self.own[0, self.rowsof(h)].astype(F32)
            + self.slot[near].astype(F32)
            + self.slot[far].astype(F32)
        )

    def drain(self):
        for k in range(6):
            self.move(k).wait_send()
        for d in range(4):
            self.swap(d).wait_send()


def params(cid, mb):
    return pltpu.CompilerParams(
        collective_id=cid, has_side_effects=True, vmem_limit_bytes=mb * 2**20
    )


def plane_ids(p):
    return [p.to(1), p.to(2), p.to(3), p.sibling()]


class Columns:
    def __init__(self, p, sems):
        self.p = p
        self.send, self.recv, self.lsem = sems

    def cols(self, j, d, src, width):
        return src.at[:, pl.ds(pl.multiple_of(j * width, width), width)]

    def copy(self, k, d, src, dst):
        if d == 0:
            return pltpu.make_async_copy(src, dst, self.lsem.at[k])
        return rcopy(src, dst, self.send.at[k, d - 1], self.recv.at[k, d - 1], self.p.to(d))


def rows_at(ref, r, n, c0, width):
    return ref.at[pl.ds(r, n), pl.ds(c0, width)]


def greet_line(p, ids):
    barrier = pltpu.get_barrier_semaphore()
    nz = lax.axis_size("z")
    for d in ids:
        pl.semaphore_signal(barrier, inc=1, device_id=d, device_id_type=MESH)

    @pl.when(p.z > 0)
    def _():
        pl.semaphore_signal(barrier, inc=1, device_id={"z": p.z - 1}, device_id_type=MESH)

    @pl.when(p.z < nz - 1)
    def _():
        pl.semaphore_signal(barrier, inc=1, device_id={"z": p.z + 1}, device_id_type=MESH)

    ends = jnp.where(p.z == 0, 1, 0) + jnp.where(p.z == nz - 1, 1, 0)
    pl.semaphore_wait(barrier, len(ids) + 2 - ends)


def relay_sems(nz):
    return [DMA((3,)), DMA((3,)), DMA((1,)), DMA((2, nz, 3)), DMA((nz, 3))]


class Relay:
    def __init__(self, p, w, dst, c0, sems):
        self.p, self.w, self.dst, self.c0 = p, w, dst, c0
        self.xs, self.xr, self.ls, self.zs, self.zr = sems
        self.nz = lax.axis_size("z")
        self.part = w.shape[0]
        self.n = self.part // self.nz
        self.fb = w.shape[1] // 8

    def cols(self, d):
        return pl.ds(pl.multiple_of((self.p.shard(d) * 2 + self.p.c) * self.fb, self.fb), self.fb)

    def rows(self, d, q):
        return self.dst.at[pl.ds(self.p.shard(d) * self.part + q * self.n, self.n), pl.ds(self.c0, self.fb)]

    def fetch(self, d):
        src = self.w.at[pl.ds(self.p.z * self.n, self.n), self.cols(d)]
        return rcopy(src, self.rows(0, self.p.z), self.xs.at[d - 1], self.xr.at[d - 1], self.p.to(d))

    def local(self):
        dst = self.dst.at[pl.ds(self.p.s * self.part, self.part), pl.ds(self.c0, self.fb)]
        return pltpu.make_async_copy(self.w.at[:, self.cols(0)], dst, self.ls.at[0])

    def along(self, way, q, d):
        ref = self.rows(d, q)
        to = {"z": self.p.z + (1 if way else -1)}
        return rcopy(ref, ref, self.zs.at[way, q, d - 1], self.zr.at[q, d - 1], to)

    def start(self):
        for d in (3, 1, 2):
            self.fetch(d).start()
        self.local().start()

    def can(self, way):
        return self.p.z < self.nz - 1 if way else self.p.z > 0

    def own(self):
        for d in (1, 2, 3):
            self.fetch(d).wait_recv()
        for way in (0, 1):

            @pl.when(self.can(way))
            def _():
                for d in (1, 2, 3):
                    self.along(way, self.p.z, d).start()

    def hop(self, k):
        for way in (0, 1):
            q = self.p.z - k if way else self.p.z + k
            there = q >= 0 if way else q < self.nz

            @pl.when(there)
            def _():
                for d in (1, 2, 3):
                    self.along(way, q, d).wait_recv()

            @pl.when(jnp.logical_and(there, self.can(way)))
            def _():
                for d in (1, 2, 3):
                    self.along(way, q, d).start()

    def finish(self):
        self.local().wait()
        for d in (1, 2, 3):
            self.fetch(d).wait_send()
        for k in range(self.nz):
            for way in (0, 1):
                q = self.p.z - k if way else self.p.z + k
                there = q >= 0 if way else q < self.nz

                @pl.when(jnp.logical_and(there, self.can(way)))
                def _():
                    for d in (1, 2, 3):
                        self.along(way, q, d).wait_send()


def enter_kernel(
    x_ref, seg_ref, gain_ref, wq_ref, wk_ref, wv_ref, wg_ref,
    xa_ref, wqkv_ref, sega_ref, gaina_ref, wgate_ref, *sems
):
    p = Place()
    others = [(0, 1)] + [(d, o) for d in (1, 2, 3) for o in (0, 1)]

    def dev(d, o):
        return {"core": 1 - p.c if o else p.c, "shard": p.shard(d)}

    greet_line(p, [dev(d, o) for d, o in others])
    ga = Gather(p, x_ref, xa_ref, sems[:5])
    co = Columns(p, sems[5:8])
    tsend, trecv, tlocal = sems[8:11]
    re = Relay(p, wg_ref, wgate_ref, 0, sems[11:16])
    re.start()
    ga.start()
    part = wq_ref.shape[0]
    hd = HEAD_DIM

    def small(k):
        d, o = others[k]
        block = sega_ref.at[p.c * 4 + p.s]
        yield rcopy(seg_ref, block, tsend.at[k], trecv.at[k], dev(d, o))
        if d and not o:
            yield rcopy(gain_ref, gaina_ref.at[p.s], tsend.at[7 + d - 1], trecv.at[7 + d - 1], dev(d, o))

    smalls = [cp for k in range(7) for cp in small(k)]
    smalls_here = [
        pltpu.make_async_copy(seg_ref, sega_ref.at[p.c * 4 + p.s], tlocal.at[0]),
        pltpu.make_async_copy(gain_ref, gaina_ref.at[p.s], tlocal.at[1]),
    ]
    for cp in smalls + smalls_here:
        cp.start()

    def q_copy(d):
        src = co.cols(p.shard(d) * 2 + p.c, d, wq_ref, hd)
        return co.copy(0, d, src, rows_at(wqkv_ref, p.s * part, part, 0, hd))

    def kv_copy(d, w):
        src = co.cols(p.shard(d), d, w, hd)
        return co.copy(1, d, src, rows_at(wqkv_ref, p.s * part, part, hd, hd))

    for d in (3, 1, 2, 0):
        q_copy(d).start()

        @pl.when(p.c == 0)
        def _():
            kv_copy(d, wk_ref).start()

        @pl.when(p.c != 0)
        def _():
            kv_copy(d, wv_ref).start()

    re.own()
    ga.relay()
    re.hop(1)
    ga.early()
    for k in range(2, lax.axis_size("z")):
        re.hop(k)
    ga.finish(early=True)
    for d in (3, 1, 2, 0):
        q_copy(d).wait()
        kv_copy(d, wk_ref).wait()
    for cp in smalls + smalls_here:
        cp.wait()
    re.finish()


def enter(x, seg, gains, wq, wk, wv, wg):
    rows, width = x.shape
    return pl.pallas_call(
        enter_kernel,
        out_shape=(
            jax.ShapeDtypeStruct((8 * rows, width), BF),
            jax.ShapeDtypeStruct((width, 2 * HEAD_DIM), BF),
            jax.ShapeDtypeStruct((8, *seg.shape), jnp.int32),
            jax.ShapeDtypeStruct((4, *gains.shape), F32),
            jax.ShapeDtypeStruct((width, wg.shape[1] // 8), BF),
        ),
        in_specs=[VM, VM, VM, ANY, ANY, ANY, ANY],
        out_specs=(ANY, ANY, VM, VM, ANY),
        scratch_shapes=GATHER_SEMS
        + [DMA((2, 3)), DMA((2, 3)), DMA((2,)), DMA((10,)), DMA((10,)), DMA((2,))]
        + relay_sems(lax.axis_size("z")),
        compiler_params=params(0, 16),
        name="enter",
    )(x, seg, gains, wq, wk, wv, wg)


def middle_kernel(part_ref, x_ref, gain_ref, g_ref, wu_ref, h_ref, xn_ref, ga_ref, wup_ref, xnb, *scr):
    p = Place()
    greet_line(p, plane_ids(p))
    sc = Scatter(p, part_ref, scr[:8])
    gx = Gather(p, xnb, xn_ref, scr[8:13])
    gg = Gather(p, g_ref, ga_ref, scr[13:18])
    re = Relay(p, wu_ref, wup_ref, 0, scr[18:23])
    sc.start()
    re.start()
    sc.first()
    re.own()
    gg.start()
    sc.relay()
    re.hop(1)
    half = sc.half
    for h in (0, 1):
        r = pl.ds(h * half, half)
        res = x_ref[r].astype(F32) + sc.total(h)
        h_ref[r] = res
        f = lax.rsqrt(jnp.mean(res * res, axis=1, keepdims=True) + norm_eps)
        xnb[r] = (res * f * gain_ref[...]).astype(BF)
    gx.start()
    gg.relay()
    for k in range(2, lax.axis_size("z")):
        re.hop(k)
    gg.early()
    gx.relay()
    gg.finish(early=True)
    gx.finish()
    sc.drain()
    re.finish()


def middle(part, x, gain2, g, wu):
    rows, width = x.shape
    return pl.pallas_call(
        middle_kernel,
        out_shape=(
            jax.ShapeDtypeStruct((rows, width), F32),
            jax.ShapeDtypeStruct((8 * rows, width), BF),
            jax.ShapeDtypeStruct((8 * rows, width), BF),
            jax.ShapeDtypeStruct((width, wu.shape[1] // 8), BF),
        ),
        in_specs=[ANY, VM, VM, VM, ANY],
        out_specs=(VM, ANY, ANY, ANY),
        scratch_shapes=[pltpu.VMEM((rows, width), BF)]
        + scatter_scratch(rows, width)
        + GATHER_SEMS * 2
        + relay_sems(lax.axis_size("z")),
        compiler_params=params(1, 48),
        name="middle",
    )(part, x, gain2, g, wu)


CH = 64
DOWN, GU, OUT, QKV = range(4)


class Chain:
    def __init__(self, p, h, ins, outs, bufs, sems):
        self.p, self.h = p, h
        self.ins = ins
        self.gate, self.up, self.down, self.out, self.wq, self.wk, self.wv = outs
        self.buf, self.bufq, self.ring, self.ring_sem = bufs
        self.rs_send, self.rs_recv, self.ag_send, self.ag_recv, self.cp_send, self.cp_recv, self.tsend = sems
        nz = lax.axis_size("z")
        self.nz = nz
        self.pos = nz - 1 - p.z if h == 0 else p.z
        self.step = -1 if h == 0 else 1

    def dev(self, by):
        return {"z": self.p.z + by}

    BASE = {DOWN: 0, GU: 8, OUT: 24, QKV: 26}

    def tick(self, kind, t):
        return self.BASE[kind] + t

    def shard_of(self, t):
        s, d = self.p.s, lax.rem(t, 4)
        one = s + 1 - 2 * lax.rem(s, 2)
        two = lax.rem(s + 2, 4)
        return jnp.where(d == 0, s, jnp.where(d == 1, one, jnp.where(d == 2, two, 3 - s)))

    def mine(self, kind, t):
        h = self.h
        if kind == DOWN:
            return self.ins[DOWN].at[pl.ds(h * 512 + t * CH, CH)]
        if kind == OUT:
            return self.ins[OUT].at[pl.ds(h * 128 + t * CH, CH)]
        row = self.shard_of(t) * 512 + h * 256
        if kind == QKV:
            return self.ins[QKV].at[pl.ds(row, 256)]
        return self.ins[GU].at[pl.ds(row + (t // 4) * CH, CH)]

    def fetch(self, kind, t):
        r = lax.rem(self.tick(kind, t), RING)
        return pltpu.make_async_copy(self.mine(kind, t), self.ring.at[r], self.ring_sem.at[r])

    def ahead(self, kind, t):
        @pl.when(self.pos > 0)
        def _():
            self.fetch(kind, t).start()

    def slot(self, kind, t):
        return self.bufq.at[t] if kind == QKV else self.buf.at[self.tick(kind, t)]

    def rs_copy(self, kind, t, src):
        k = self.tick(kind, t)
        return rcopy(
            src, self.slot(kind, t), self.rs_send.at[k], self.rs_recv.at[k], self.dev(self.step)
        )

    def reduce(self, kind, t):
        first, last = self.pos == 0, self.pos == self.nz - 1

        @pl.when(first)
        def _():
            self.rs_copy(kind, t, self.mine(kind, t)).start()

        @pl.when(jnp.logical_not(first))
        def _():
            slot = self.slot(kind, t)
            if kind in (DOWN, GU):
                self.fetch(kind, t).wait()
                own = self.ring.at[lax.rem(self.tick(kind, t), RING)]
            else:
                own = self.mine(kind, t)
            self.rs_copy(kind, t, slot).wait_recv()
            slot[...] = (slot[...].astype(F32) + own[...].astype(F32)).astype(BF)

        @pl.when(jnp.logical_and(jnp.logical_not(first), jnp.logical_not(last)))
        def _():
            self.rs_copy(kind, t, self.slot(kind, t)).start()

        @pl.when(last)
        def _():
            self.turn(kind, t)

    def pieces(self, kind, t, s, d_shard):
        h, c = self.h, self.p.c
        if kind == DOWN:
            return [(None, self.down.at[pl.ds(c * 1024 + h * 512 + t * CH, CH)])]
        if kind == OUT:
            return [(None, self.out.at[pl.ds(c * 256 + h * 128 + t * CH, CH)])]
        if kind == GU:
            r = h * 256 + (t // 4) * CH
            c0 = pl.multiple_of((s * 2 + c) * 1024, 1024)
            return [
                ((0, 1024), self.gate.at[pl.ds(r, CH), pl.ds(c0, 1024)]),
                ((1024, 1024), self.up.at[pl.ds(r, CH), pl.ds(c0, 1024)]),
            ]
        r = h * 256
        cq = pl.multiple_of((s * 2 + c) * 256, 256)
        return [((0, 256), self.wq.at[pl.ds(r, 256), pl.ds(cq, 256)])]

    def kv_piece(self, s, w):
        return w.at[pl.ds(self.h * 256, 256), pl.ds(pl.multiple_of(s * 256, 256), 256)]

    def turn(self, kind, t):
        slot = self.slot(kind, t)
        k = self.tick(kind, t)
        to = self.p.s if kind in (DOWN, OUT) else self.shard_of(t)

        def send(i, src, dst):
            if kind in (DOWN, OUT):
                pltpu.make_async_copy(src, dst, self.ag_recv.at[i, k]).start()
                return

            @pl.when(lax.rem(t, 4) == 0)
            def _():
                pltpu.make_async_copy(src, dst, self.ag_recv.at[i, k]).start()

            @pl.when(lax.rem(t, 4) != 0)
            def _():
                rcopy(src, dst, self.tsend.at[i, k], self.ag_recv.at[i, k], {"shard": to}).start()

        for i, (cols, dst) in enumerate(self.pieces(kind, t, self.p.s, to)):
            send(i, slot if cols is None else slot.at[:, pl.ds(*cols)], dst)
        if kind == QKV:
            src = slot.at[:, pl.ds(256, 256)]

            @pl.when(self.p.c == 0)
            def _():
                send(1, src, self.kv_piece(self.p.s, self.wk))

            @pl.when(self.p.c != 0)
            def _():
                send(1, src, self.kv_piece(self.p.s, self.wv))

    def spread_copy(self, i, k, ref):
        return rcopy(ref, ref, self.ag_send.at[i, k], self.ag_recv.at[i, k], self.dev(-self.step))

    def spread(self, kind, t):
        k = self.tick(kind, t)
        s = self.p.s if kind in (DOWN, OUT) else self.shard_of(t)

        def go(i, ref, wait=True):
            if wait:
                self.spread_copy(i, k, ref).wait_recv()

            @pl.when(self.pos > 0)
            def _():
                self.spread_copy(i, k, ref).start()

            rcopy(ref, ref, self.cp_send.at[i, k], self.cp_recv.at[i, k], self.p.sibling()).start()

        for i, (_, ref) in enumerate(self.pieces(kind, t, s, None)):
            go(i, ref)
        if kind == QKV:
            self.spread_copy(1, k, self.kv_piece(s, self.wk)).wait_recv()

            @pl.when(self.p.c == 0)
            def _():
                go(1, self.kv_piece(s, self.wk), False)

            @pl.when(self.p.c != 0)
            def _():
                go(1, self.kv_piece(s, self.wv), False)

    def drain_reduce(self, kind, t):
        @pl.when(self.pos < self.nz - 1)
        def _():
            self.rs_copy(kind, t, self.slot(kind, t)).wait_send()

        if kind not in (GU, QKV):
            return
        k = self.tick(kind, t)

        @pl.when(jnp.logical_and(self.pos == self.nz - 1, lax.rem(t, 4) != 0))
        def _():
            slot = self.slot(kind, t)
            for i, (cols, dst) in enumerate(self.pieces(kind, t, self.p.s, None)):
                src = slot.at[:, pl.ds(*cols)]
                rcopy(src, dst, self.tsend.at[i, k], self.ag_recv.at[i, k], self.p.to(1)).wait_send()
            if kind == QKV:
                src = slot.at[:, pl.ds(256, 256)]
                dst = self.kv_piece(self.p.s, self.wk)
                rcopy(src, dst, self.tsend.at[1, k], self.ag_recv.at[1, k], self.p.to(1)).wait_send()

    def drain_spread(self, kind, t):
        k = self.tick(kind, t)
        s = self.p.s if kind in (DOWN, OUT) else self.shard_of(t)
        refs = [ref for _, ref in self.pieces(kind, t, s, None)]
        if kind == QKV:
            refs.append(self.kv_piece(s, self.wk))
        for i, ref in enumerate(refs):

            @pl.when(self.pos > 0)
            def _():
                self.spread_copy(i, k, ref).wait_send()

            rcopy(ref, ref, self.cp_send.at[i, k], self.cp_recv.at[i, k], self.p.sibling()).wait()


N_TICKS, RING = 30, 4
CHAIN_SEMS = [DMA((N_TICKS,))] * 2 + [DMA((2, N_TICKS))] * 5


def loop(lo, hi, body):
    def step(t, _):
        body(t)
        return 0

    lax.fori_loop(lo, hi, step, 0)


COUNT = {DOWN: 8, GU: 16, OUT: 2, QKV: 4}


SKEW, TURN = 2, 3


def between(i, lo, hi):
    return jnp.logical_and(i >= lo, i < hi)


def each(i, lo, hi, act):
    for kind, n in COUNT.items():
        base = Chain.BASE[kind]
        a, b = max(lo, base), min(hi, base + n)
        if a < b:

            @pl.when(between(i, a, b))
            def _():
                act(kind, i - base)


def at_tick(t, when, act):
    @pl.when(t == when)
    def _():
        act()


def all_greet(p):
    nz = lax.axis_size("z")
    greet(plane_ids(p) + [{"z": lax.rem(p.z + k, nz)} for k in range(1, nz)])


class GainSums:
    def __init__(self, p, tot, got, gz, send, recv):
        self.p, self.tot, self.got, self.gz, self.send, self.recv = p, tot, got, gz, send, recv
        self.nz = lax.axis_size("z")

    def copy(self, k):
        dev = (self.p.sibling(), self.p.to(1), self.p.to(2))[k]
        return rcopy(self.tot.at[k], self.got.at[k], self.send.at[k], self.recv.at[k], dev)

    def along(self, k):
        to = {"z": lax.rem(self.p.z + k, self.nz)}
        return rcopy(
            self.tot.at[3], self.gz.at[self.p.z], self.send.at[2 + k], self.recv.at[3 + self.p.z], to
        )

    def landed(self, k):
        src = lax.rem(self.p.z + self.nz - k, self.nz)
        ref = self.gz.at[src]
        return rcopy(ref, ref, self.send.at[2 + k], self.recv.at[3 + src], {"z": src})

    def add(self, k):
        self.copy(k).wait()
        self.tot[k + 1] = self.tot[k] + self.got[k]
        if k < 2:
            self.copy(k + 1).start()
        else:
            for j in range(1, self.nz):
                self.along(j).start()
            self.gz[self.p.z] = self.tot[3]

    def finish(self):
        for j in range(1, self.nz):
            self.along(j).wait_send()
            self.landed(j).wait_recv()
        total = self.gz[0]
        for j in range(1, self.nz):
            total = total + self.gz[j]
        return total


class Attention:
    def __init__(self, p, hbm, wo, wqkv, part, gout, gqkv, bufs, sems):
        self.p, self.hbm, self.wo, self.wqkv, self.part = p, hbm, wo, wqkv, part
        self.gout, self.gqkv = gout, gqkv
        self.bufs, self.other, self.came, self.kept, self.dq, self.rows_out = bufs[:8], *bufs[8:]
        self.sem, self.send, self.recv, self.psem = sems
        self.n = self.rows_out.shape[1]

    def load(self, i, j):
        src = self.hbm[i]
        ref = src.at[pl.ds(j * self.n, self.n)] if len(src.shape) == 2 else src.at[j]
        b = lax.rem(j, 2)
        return pltpu.make_async_copy(ref, self.bufs[i].at[b], self.sem.at[i, b])

    def fetch(self, j):
        for i in range(7):
            self.load(i, j).start()

    def swap(self, j):
        return rcopy(self.other.at[j], self.came.at[j], self.send.at[j], self.recv.at[j], self.p.sibling())

    def first(self, j):
        for i in range(7):
            self.load(i, j).wait()

        @pl.when(j < 7)
        def _():
            self.fetch(j + 1)

        b = lax.rem(j, 2)
        dhb, q, k, v, attn, probs, turn = (self.bufs[i][b] for i in range(7))
        scale = HEAD_DIM ** (-0.5)
        half = HEAD_DIM // 2
        cosine, sine = turn[:, :half], turn[:, half:]
        dattn = mm_nt(dhb, self.wo[...]).astype(BF)
        g = mm_tn(attn, dhb)
        self.gout[...] = jnp.where(j == 0, g, self.gout[...] + g)
        dp = mm_nt(dattn, v)
        dv = mm_tn(probs.astype(BF), dattn)
        ds = (probs * (dp - jnp.sum(dp * probs, axis=-1, keepdims=True))).astype(BF)
        dq = rotate(mm(ds, k) * scale, cosine, -sine)
        dk = rotate(mm_tn(ds, q) * scale, cosine, -sine)
        zero = self.p.c == 0
        self.dq[b] = dq.astype(BF)
        self.kept[b] = jnp.where(zero, dk, dv)
        self.other[j] = jnp.where(zero, dv, dk).astype(BF)
        self.swap(j).start()
        self.load(7, j).start()

    def out_copy(self, j):
        b = lax.rem(j, 2)
        return pltpu.make_async_copy(self.rows_out.at[b], self.part.at[pl.ds(j * self.n, self.n)], self.psem.at[b])

    def second(self, j):
        b = lax.rem(j, 2)
        self.swap(j).wait()
        self.load(7, j).wait()
        dkv = (self.kept[b] + self.came[j].astype(F32)).astype(BF)
        dqkv = jnp.concatenate([self.dq[b], dkv], -1)
        g = mm_tn(self.bufs[7][b], dqkv)
        self.gqkv[...] = jnp.where(j == 0, g, self.gqkv[...] + g)

        @pl.when(j >= 2)
        def _():
            self.out_copy(j - 2).wait()

        self.rows_out[b] = mm_nt(dqkv, self.wqkv[...]).astype(BF)
        self.out_copy(j).start()

    def finish(self):
        self.out_copy(6).wait()
        self.out_copy(7).wait()


def tail_kernel(
    part_ref, dpart_ref, x_hbm, h_hbm, g_hbm, gain1_ref, gain2_ref, gd_ref, ggu_ref, wo_ref, wqkv_ref,
    q_ref, k_ref, v_ref, attn_ref, probs_ref, turn_ref, xn1_ref,
    out_hbm, grad_hbm, gains_ref, dhb_ref, p1_ref, gate, up, down, out, wq, wk, wv,
    bufa, bufb, qa, qb, ringa, ringb, ring_sem, tot, got, gz, gsend, grecv,
    low, xg, hb, dh, gout, gqkv, gout_low, gqkv_low, io_sem, free_sem, *scr
):
    p = Place()
    nz = lax.axis_size("z")
    s1 = Scatter(p, part_ref, scr[:8])
    s2 = Scatter(p, dpart_ref, scr[:8])
    s3 = Scatter(p, p1_ref, scr[:8])
    ga = Gather(p, low, dhb_ref, scr[8:13])
    sums = GainSums(p, tot, got, gz, gsend, grecv)
    hbm = (dhb_ref, q_ref, k_ref, v_ref, attn_ref, probs_ref, turn_ref, xn1_ref)
    at = Attention(p, hbm, wo_ref, wqkv_ref, p1_ref, gout, gqkv, scr[13:26], scr[26:30])
    ins = (gd_ref, ggu_ref, gout_low, gqkv_low)
    outs = (gate, up, down, out, wq, wk, wv)
    n = len(CHAIN_SEMS)
    chains = [
        Chain(p, 0, ins, outs, (bufa, qa, ringa, ring_sem.at[0]), scr[30 : 30 + n]),
        Chain(p, 1, ins, outs, (bufb, qb, ringb, ring_sem.at[1]), scr[30 + n : 30 + 2 * n]),
    ]
    line = SKEW * (nz - 1)
    half = s1.half

    def io(k):
        src, dst = [(h_hbm, hb), (g_hbm, xg), (x_hbm, xg), (low, out_hbm), (low, grad_hbm)][k]
        return pltpu.make_async_copy(src, dst, io_sem.at[k])

    io(0).start()
    io(1).start()
    tot[0] = jnp.zeros_like(tot[0])
    all_greet(p)
    s1.start()
    s1.first()

    def norm2():
        io(0).wait()
        io(1).wait()
        for h in (0, 1):
            r = pl.ds(h * half, half)
            dx = s1.total(h)
            res = hb[r]
            f = lax.rsqrt(jnp.mean(res * res, axis=1, keepdims=True) + norm_eps)
            hat = res * f
            term = jnp.sum(dx * hat, axis=0, keepdims=True)
            tot[0, 1:2] = term if h == 0 else tot[0, 1:2] + term
            d = xg[r].astype(F32) + norm_backward_step(dx * gain2_ref[...], hat, f)
            dh[r] = d
            low[r] = d.astype(BF)
        ga.start()
        io(2).start()

    def gathered():
        ga.finish()
        s1.drain()
        at.fetch(0)
        s2.start()

    def output():
        for h in (0, 1):
            r = pl.ds(h * half, half)
            low[r] = (hb[r] + s2.total(h)).astype(BF)
        io(3).start()
        s2.drain()
        for d in (p.to(1), p.to(2), p.sibling()):
            pl.semaphore_signal(free_sem, inc=1, device_id=d, device_id_type=MESH)

    def attended():
        at.finish()
        gout_low[...] = gout[...].astype(BF)
        gqkv_low[...] = gqkv[...].astype(BF)
        pl.semaphore_wait(free_sem, 3)
        s3.start()
        s3.first()

    def norm1():
        io(2).wait()
        io(3).wait()
        for h in (0, 1):
            r = pl.ds(h * half, half)
            dx = s3.total(h)
            xf = xg[r].astype(F32)
            f = lax.rsqrt(jnp.mean(xf * xf, axis=1, keepdims=True) + norm_eps)
            hat = xf * f
            term = jnp.sum(dx * hat, axis=0, keepdims=True)
            tot[0, 0:1] = term if h == 0 else tot[0, 0:1] + term
            low[r] = (dh[r] + norm_backward_step(dx * gain1_ref[...], hat, f)).astype(BF)
        io(4).start()
        sums.copy(0).start()

    def gains():
        gains_ref[...] = sums.finish()

    def tick(t):
        for ch in chains:
            each(t + 1 - SKEW * ch.pos, 0, 24, ch.ahead)
            each(t - SKEW * ch.pos, 0, N_TICKS, ch.reduce)
        for ch in chains:
            each(t - TURN - 2 * line + SKEW * ch.pos, 0, N_TICKS, ch.spread)
        at_tick(t, 1, s1.relay)
        at_tick(t, 5, norm2)
        at_tick(t, 7, ga.relay)
        at_tick(t, A0 - 1, gathered)
        pl.when(between(t, A0 + 1, A0 + 9))(lambda: at.second(t - A0 - 1))
        pl.when(between(t, A0, A0 + 8))(lambda: at.first(t - A0))
        at_tick(t, A0, s2.first)
        at_tick(t, A0 + 2, s2.relay)
        at_tick(t, A0 + 5, output)
        at_tick(t, A0 + 9, attended)
        at_tick(t, A0 + 11, s3.relay)
        at_tick(t, A0 + 14, norm1)
        for k in range(3):
            at_tick(t, A0 + 15 + k, functools.partial(sums.add, k))
        at_tick(t, A0 + 19, gains)

    loop(0, N_TICKS + TURN + 2 * line, tick)
    io(4).wait()
    s3.drain()

    def drain(i):
        for ch in chains:
            each(i, 0, N_TICKS, ch.drain_reduce)
            each(i, 0, N_TICKS, ch.drain_spread)

    loop(0, N_TICKS, drain)


A0 = 12


def tail(part, dpart, x, h, g, gain1, gain2, g_down, g_gu, wo, wqkv, heads, xn1, ff):
    rows, width = x.shape
    nz = lax.axis_size("z")
    hd, pr = HEAD_DIM, width // 4
    shapes = [(pr, ff), (pr, ff), (ff // 4, width), (pr, width), (pr, width), (pr, 1024), (pr, 1024)]
    sq = pltpu.VMEM((2, rows, hd), BF)
    wide = pltpu.VMEM((2, rows, width), BF)
    return pl.pallas_call(
        tail_kernel,
        out_shape=(
            jax.ShapeDtypeStruct((rows, width), BF),
            jax.ShapeDtypeStruct((rows, width), BF),
            jax.ShapeDtypeStruct((8, width), F32),
            jax.ShapeDtypeStruct((8 * rows, width), BF),
            jax.ShapeDtypeStruct((8 * rows, width), BF),
        )
        + tuple(jax.ShapeDtypeStruct(s, BF) for s in shapes),
        in_specs=[ANY] * 5 + [VM] * 2 + [ANY] * 2 + [VM] * 2 + [ANY] * 7,
        out_specs=(ANY, ANY, VM) + (ANY,) * 9,
        scratch_shapes=[
            pltpu.VMEM((26, CH, width), BF),
            pltpu.VMEM((26, CH, width), BF),
            pltpu.VMEM((4, 256, 512), BF),
            pltpu.VMEM((4, 256, 512), BF),
            pltpu.VMEM((RING, CH, width), BF),
            pltpu.VMEM((RING, CH, width), BF),
            DMA((2, RING)),
            pltpu.VMEM((4, 8, width), F32),
            pltpu.VMEM((3, 8, width), F32),
            pltpu.VMEM((nz, 8, width), F32),
            DMA((nz + 3,)),
            DMA((nz + 3,)),
            pltpu.VMEM((rows, width), BF),
            pltpu.VMEM((rows, width), BF),
            pltpu.VMEM((rows, width), F32),
            pltpu.VMEM((rows, width), F32),
            pltpu.VMEM((hd, width), F32),
            pltpu.VMEM((width, 2 * hd), F32),
            pltpu.VMEM((hd, width), BF),
            pltpu.VMEM((width, 2 * hd), BF),
            DMA((5,)),
            pltpu.SemaphoreType.REGULAR,
        ]
        + scatter_scratch(rows, width)
        + GATHER_SEMS
        + [wide, sq, sq, sq, sq]
        + [pltpu.VMEM((2, rows, rows), F32), pltpu.VMEM((2, rows, hd), F32), wide]
        + [pltpu.VMEM((8, rows, hd), BF)] * 2
        + [pltpu.VMEM((2, rows, hd), F32), sq, wide]
        + [DMA((8, 2)), DMA((8,)), DMA((8,)), DMA((2,))]
        + CHAIN_SEMS * 2,
        compiler_params=params(2, 63),
        name="tail",
    )(part, dpart, x, h, g, gain1, gain2, g_down, g_gu, wo, wqkv, *heads, xn1)


def pieces(
    tokens,
    segment_ids,
    attn_gain,
    w_query,
    w_key,
    w_value,
    w_out,
    mlp_gain,
    w_gate,
    w_up,
    w_down,
    cotangent,
):
    rows, width = tokens.shape[1], tokens.shape[2]
    core = lax.axis_index("core")
    nc, ns = lax.axis_size("core"), lax.axis_size("shard")
    hd = HEAD_DIM
    ff = w_gate.shape[1]
    fb = ff // (nc * ns)
    part = width // ns

    x = tokens.reshape(rows, width)
    g = cotangent.reshape(rows, width)
    wo = lax.dynamic_slice_in_dim(w_out, core * hd, hd, 0)
    wd = lax.dynamic_slice_in_dim(w_down, core * fb, fb, 0)

    gains = jnp.concatenate([attn_gain[None], mlp_gain[None], jnp.zeros((6, part), BF)], 0).astype(F32)
    seg8 = jnp.broadcast_to(segment_ids, (8, rows))
    x_all, wqkv, seg, gains, wgate = enter(x, seg8, gains, w_query, w_key, w_value, w_gate)
    seg = seg[:, 0]
    gain1, gain2 = gains[:, 0].reshape(1, width), gains[:, 1].reshape(1, width)
    nseq = nc * ns

    iota = jnp.arange(rows, dtype=jnp.int32)
    same = seg[:, :, None] == seg[:, None, :]
    allowed = same & (iota[:, None] >= iota[None, :])[None]
    starts = jnp.sum((seg[:, None, :] < seg[:, :, None]).astype(jnp.int32), axis=2)
    positions = (iota[None, :] - starts).astype(F32)
    half = hd // 2
    inv_freq = rope_base ** (-(jnp.arange(half, dtype=F32) * 2.0 / hd))
    angles = positions[..., None] * inv_freq
    cosine, sine = jnp.cos(angles), jnp.sin(angles)

    xf_all = x_all.astype(F32)
    f1_all = lax.rsqrt(jnp.mean(xf_all * xf_all, axis=1, keepdims=True) + norm_eps)
    xn1 = (xf_all * f1_all * gain1).astype(BF)
    qkv = mm(xn1, wqkv).reshape(nseq, rows, 2 * hd)
    q = rotate(qkv[..., :hd], cosine, sine).astype(BF)
    kv_lin = qkv[..., hd:]
    kv_mine = jnp.where(core == 0, rotate(kv_lin, cosine, sine), kv_lin).astype(BF)
    swap = [(i, nc - 1 - i) for i in range(nc)]
    kv_other = lax.ppermute(kv_mine, "core", swap)
    k = jnp.where(core == 0, kv_mine, kv_other)
    v = jnp.where(core == 0, kv_other, kv_mine)
    scale = hd ** (-0.5)
    scores = jnp.einsum("bqd,bkd->bqk", q, k, preferred_element_type=F32) * scale
    scores = jnp.where(allowed, scores, mask_fill)
    top = jnp.max(scores, axis=-1, keepdims=True)
    ex = jnp.exp(scores - top)
    probs = ex / jnp.sum(ex, axis=-1, keepdims=True)
    pb = probs.astype(BF)
    attn = jnp.einsum("bqk,bkd->bqd", pb, v, preferred_element_type=F32).astype(BF)
    attn = attn.reshape(nseq * rows, hd)

    h, xn2, g_all, wup = middle(mm(attn, wo).astype(BF), x, gain2, g, w_up)

    gate, up = mm(xn2, wgate), mm(xn2, wup)
    sigma = jax.nn.sigmoid(gate)
    swish = gate * sigma
    hid = (swish * up).astype(BF)
    g_down = mm_tn(hid, g_all).astype(BF)
    dhid = mm_nt(g_all, wd)
    dgate = (dhid * up * sigma * (1.0 + gate * (1.0 - sigma))).astype(BF)
    dup = (dhid * swish).astype(BF)
    dgu = jnp.concatenate([dgate, dup], 1)
    g_gu = mm_tn(xn2, dgu).astype(BF)
    heads = (q, k, v, attn, probs, jnp.concatenate([cosine, sine], -1))
    output, input_grad, gain_g, _, _, gate_g, up_g, down_g, out_g, wq_g, wk_g, wv_g = tail(
        (mm_nt(dgate, wgate) + mm_nt(dup, wup)).astype(BF),
        mm(hid, wd).astype(BF),
        x,
        h,
        g,
        gain1,
        gain2,
        g_down,
        g_gu,
        wo,
        wqkv,
        heads,
        xn1,
        ff,
    )
    output = output.reshape(1, rows, width)
    input_grad = input_grad.reshape(1, rows, width)
    gain_g = lax.dynamic_slice_in_dim(gain_g, lax.axis_index("shard") * part, part, 1)
    return (
        output,
        input_grad,
        gain_g[0],
        wq_g.astype(F32),
        wk_g.astype(F32),
        wv_g.astype(F32),
        out_g.astype(F32),
        gain_g[1],
        gate_g.astype(F32),
        up_g.astype(F32),
        down_g.astype(F32),
    )


def contract_rows(left, right):
    return lax.dot_general(
        left, right, (((0,), (0,)), ((), ())), preferred_element_type=jnp.float32
    )


def contract_cols(left, right):
    return lax.dot_general(
        left, right, (((1,), (1,)), ((), ())), preferred_element_type=jnp.float32
    )


def scores_of(queries, keys, allowed):
    raw = jnp.einsum(
        "qgrd,kgd->grqk", queries, keys, preferred_element_type=jnp.float32
    ) * HEAD_DIM ** (-0.5)
    return jnp.where(allowed, raw, mask_fill)


def general(
    tokens,
    segment_ids,
    attn_gain,
    w_query,
    w_key,
    w_value,
    w_out,
    mlp_gain,
    w_gate,
    w_up,
    w_down,
    cotangent,
):
    rows = tokens.shape[1]
    width = tokens.shape[2]
    groups = HEADS // KV_HEADS
    q_cols = HEADS * HEAD_DIM
    kv_cols = KV_HEADS * HEAD_DIM
    layer_input_rows = tokens.reshape(rows, width).astype(jnp.float32)
    segments = segment_ids.reshape(rows)
    iota = jnp.arange(rows, dtype=jnp.int32)
    starts = jnp.sum((segments[None, :] < segments[:, None]).astype(jnp.int32), axis=1)
    positions = (iota - starts).astype(jnp.float32)
    allowed = (segments[:, None] == segments[None, :]) & (iota[:, None] >= iota[None, :])
    half = HEAD_DIM // 2
    inv_freq = rope_base ** (-(jnp.arange(half, dtype=jnp.float32) * 2.0 / HEAD_DIM))
    angles = positions[:, None] * inv_freq
    cosine = jnp.cos(angles)
    sine = jnp.sin(angles)
    first_norm_factor = lax.rsqrt(
        jnp.mean(layer_input_rows * layer_input_rows, axis=1, keepdims=True) + norm_eps
    )
    first_standardized = layer_input_rows * first_norm_factor
    gain_fragment = lax.all_gather(attn_gain, "shard", axis=0, tiled=True)
    query_piece = lax.all_gather(w_query, "shard", axis=0, tiled=True)
    key_piece = lax.all_gather(w_key, "shard", axis=0, tiled=True)
    value_piece = lax.all_gather(w_value, "shard", axis=0, tiled=True)
    normalized_rows = (first_standardized * gain_fragment.astype(jnp.float32)).astype(jnp.bfloat16)
    joined = jnp.concatenate([query_piece, key_piece, value_piece], 1)
    result = (
        jnp.dot(normalized_rows, joined, preferred_element_type=jnp.float32),
        normalized_rows,
        gain_fragment.astype(jnp.float32),
    )
    folded = result
    projected, normed_one, first_norm_gain = (folded[0], folded[1], folded[2])
    queries = rotate(
        projected[:, :q_cols].reshape(rows, KV_HEADS, groups, HEAD_DIM),
        cosine[:, None, None, :],
        sine[:, None, None, :],
    ).astype(jnp.bfloat16)
    keys = rotate(
        projected[:, q_cols : q_cols + kv_cols].reshape(rows, KV_HEADS, HEAD_DIM),
        cosine[:, None, :],
        sine[:, None, :],
    ).astype(jnp.bfloat16)
    values = projected[:, q_cols + kv_cols :].reshape(rows, KV_HEADS, HEAD_DIM).astype(jnp.bfloat16)
    scores = scores_of(queries, keys, allowed)
    top = jnp.max(scores, axis=-1, keepdims=True)
    log_total = top + jnp.log(jnp.sum(jnp.exp(scores - top), axis=-1, keepdims=True))
    probs = jnp.exp(scores - log_total)
    probs_low = probs.astype(jnp.bfloat16)
    attn = (
        jnp.einsum("grqk,kgd->qgrd", probs_low, values, preferred_element_type=jnp.float32)
        .reshape(rows, q_cols)
        .astype(jnp.bfloat16)
    )
    part = attn
    result = (
        jnp.dot(
            part,
            lax.all_gather(w_out, "shard", axis=0, tiled=True),
            preferred_element_type=jnp.float32,
        ),
    )
    folded_out = result
    residual_hidden_state = layer_input_rows + folded_out[0]
    second_norm_factor = lax.rsqrt(
        jnp.mean(residual_hidden_state * residual_hidden_state, axis=1, keepdims=True) + norm_eps
    )
    second_standardized = residual_hidden_state * second_norm_factor
    gain_fragment = lax.all_gather(mlp_gain, "shard", axis=0, tiled=True)
    gate_piece = lax.all_gather(w_gate, "shard", axis=0, tiled=True)
    up_piece = lax.all_gather(w_up, "shard", axis=0, tiled=True)
    normalized_rows = (second_standardized * gain_fragment.astype(jnp.float32)).astype(jnp.bfloat16)
    joined = jnp.concatenate([gate_piece, up_piece], 1)
    result = (
        jnp.dot(normalized_rows, joined, preferred_element_type=jnp.float32),
        normalized_rows,
        gain_fragment.astype(jnp.float32),
    )
    folded_mlp = result
    gate = folded_mlp[0][:, :FF]
    up_value = folded_mlp[0][:, FF:]
    normed_two = folded_mlp[1]
    second_norm_gain = folded_mlp[2]
    sigma = jax.nn.sigmoid(gate)
    swish = gate * sigma
    inner = (swish * up_value).astype(jnp.bfloat16)
    part = inner
    result = (
        jnp.dot(
            part,
            lax.all_gather(w_down, "shard", axis=0, tiled=True),
            preferred_element_type=jnp.float32,
        ),
    )
    output = (residual_hidden_state + result[0]).astype(jnp.bfloat16).reshape(1, rows, width)
    grad_out = cotangent.reshape(rows, width)
    grad_down = lax.psum_scatter(
        contract_rows(inner, grad_out).astype(jnp.bfloat16),
        "shard",
        scatter_dimension=0,
        tiled=True,
    )
    down_full, gate_full, up_full = (
        lax.all_gather(w_down, "shard", axis=0, tiled=True),
        lax.all_gather(w_gate, "shard", axis=0, tiled=True),
        lax.all_gather(w_up, "shard", axis=0, tiled=True),
    )
    grad_inner = contract_cols(grad_out, down_full)
    grad_gate = (grad_inner * up_value * sigma * (1.0 + gate * (1.0 - sigma))).astype(jnp.bfloat16)
    grad_up = (grad_inner * swish).astype(jnp.bfloat16)
    grad_mlp = jnp.concatenate([grad_gate, grad_up], 1)
    mlp_shards = lax.psum_scatter(
        contract_rows(normed_two, grad_mlp).astype(jnp.bfloat16),
        "shard",
        scatter_dimension=0,
        tiled=True,
    ).astype(jnp.float32)
    second_norm_gradient = contract_cols(grad_gate, gate_full) + contract_cols(grad_up, up_full)
    second_gain_products = jnp.sum(second_norm_gradient * second_standardized, axis=0)
    hidden_gradient = grad_out.astype(jnp.float32) + norm_backward_step(
        second_norm_gradient * second_norm_gain, second_standardized, second_norm_factor
    )
    grad_hidden_low = hidden_gradient.astype(jnp.bfloat16)
    grad_out_proj = lax.psum_scatter(
        contract_rows(attn, grad_hidden_low).astype(jnp.bfloat16),
        "shard",
        scatter_dimension=0,
        tiled=True,
    )
    grad_attn = contract_cols(grad_hidden_low, lax.all_gather(w_out, "shard", axis=0, tiled=True))
    grad_attn = grad_attn.astype(jnp.bfloat16).reshape(rows, KV_HEADS, groups, HEAD_DIM)
    scores_again = scores_of(queries, keys, allowed)
    probs_again = jnp.exp(scores_again - log_total)
    probs_again_low = probs_again.astype(jnp.bfloat16)
    grad_probs = jnp.einsum("qgrd,kgd->grqk", grad_attn, values, preferred_element_type=jnp.float32)
    grad_values = jnp.einsum(
        "grqk,qgrd->kgd", probs_again_low, grad_attn, preferred_element_type=jnp.float32
    )
    grad_scores = (
        probs_again * (grad_probs - jnp.sum(grad_probs * probs_again, axis=-1, keepdims=True))
    ).astype(jnp.bfloat16)
    grad_queries = jnp.einsum(
        "grqk,kgd->qgrd", grad_scores, keys, preferred_element_type=jnp.float32
    ) * HEAD_DIM ** (-0.5)
    grad_keys = jnp.einsum(
        "grqk,qgrd->kgd", grad_scores, queries, preferred_element_type=jnp.float32
    ) * HEAD_DIM ** (-0.5)
    grad_queries = rotate(grad_queries, cosine[:, None, None, :], -sine[:, None, None, :]).reshape(
        rows, q_cols
    )
    grad_keys = rotate(grad_keys, cosine[:, None, :], -sine[:, None, :]).reshape(rows, kv_cols)
    grad_joined = jnp.concatenate(
        [
            grad_queries.astype(jnp.bfloat16),
            grad_keys.astype(jnp.bfloat16),
            grad_values.reshape(rows, kv_cols).astype(jnp.bfloat16),
        ],
        1,
    )
    qkv_shards = lax.psum_scatter(
        contract_rows(normed_one, grad_joined).astype(jnp.bfloat16),
        "shard",
        scatter_dimension=0,
        tiled=True,
    ).astype(jnp.float32)
    local_qkv = jnp.concatenate([w_query, w_key, w_value], 1)
    first_norm_gradient = contract_cols(
        grad_joined, lax.all_gather(local_qkv, "shard", axis=0, tiled=True)
    )
    first_gain_products = jnp.sum(first_norm_gradient * first_standardized, axis=0)
    input_gradient_rows = hidden_gradient + norm_backward_step(
        first_norm_gradient * first_norm_gain, first_standardized, first_norm_factor
    )
    input_grad = input_gradient_rows.astype(jnp.bfloat16).reshape(1, rows, width)
    gain_one_grad, gain_two_grad = (
        lax.psum_scatter(first_gain_products, "shard", scatter_dimension=0, tiled=True),
        lax.psum_scatter(second_gain_products, "shard", scatter_dimension=0, tiled=True),
    )
    summed = (
        lax.psum(gain_one_grad.astype(jnp.bfloat16), "rep").astype(jnp.float32),
        lax.psum(qkv_shards[:, :q_cols].astype(jnp.bfloat16), "rep").astype(jnp.float32),
        lax.psum(qkv_shards[:, q_cols : q_cols + kv_cols].astype(jnp.bfloat16), "rep").astype(
            jnp.float32
        ),
        lax.psum(qkv_shards[:, q_cols + kv_cols :].astype(jnp.bfloat16), "rep").astype(jnp.float32),
        lax.psum(grad_out_proj, "rep").astype(jnp.float32),
        lax.psum(gain_two_grad.astype(jnp.bfloat16), "rep").astype(jnp.float32),
        lax.psum(mlp_shards[:, :FF].astype(jnp.bfloat16), "rep").astype(jnp.float32),
        lax.psum(mlp_shards[:, FF:].astype(jnp.bfloat16), "rep").astype(jnp.float32),
        lax.psum(grad_down, "rep").astype(jnp.float32),
    )
    return (
        output,
        input_grad,
        summed[0],
        summed[1],
        summed[2],
        summed[3],
        summed[4],
        summed[5],
        summed[6],
        summed[7],
        summed[8],
    )


def solution(mesh):
    rep, shard = mesh.devices.shape
    if shard == KV_HEADS and rep % 2 == 0:
        fine = Mesh(np.asarray(mesh.devices).reshape(rep // 2, 2, shard), ("z", "core", "shard"))
        body, every = pieces, ("z", "core", "shard")
    else:
        fine, body, every = mesh, general, ("rep", "shard")
    seqs, vec, mat = P(every, None, None), P("shard"), P("shard", None)
    in_specs = (seqs, P(every, None), vec, mat, mat, mat, mat, vec, mat, mat, mat, seqs)
    out_specs = (seqs, seqs, vec, mat, mat, mat, mat, vec, mat, mat, mat)
    return jax.shard_map(body, mesh=fine, in_specs=in_specs, out_specs=out_specs, check_vma=False)
```

```python
import functools

import jax
import jax.numpy as jnp
import numpy as np
from jax import lax
from jax.experimental import pallas as pl
from jax.experimental.pallas import tpu as pltpu
from jax.sharding import Mesh
from jax.sharding import PartitionSpec as P

HEADS = 8
KV_HEADS = 4
HEAD_DIM = 256
FF = 8192

rope_base = 1000042.0
norm_eps = 1e-06
mask_fill = -1e30

BF = jnp.bfloat16
F32 = jnp.float32
MESH = pl.DeviceIdType.MESH
ANY = pl.BlockSpec(memory_space=pl.ANY)
VM = pl.BlockSpec(memory_space=pltpu.VMEM)
DMA = pltpu.SemaphoreType.DMA


def mm(a, b):
    return jnp.dot(a, b, preferred_element_type=F32)


def mm_tn(a, b):
    return lax.dot_general(a, b, (((0,), (0,)), ((), ())), preferred_element_type=F32)


def mm_nt(a, b):
    return lax.dot_general(a, b, (((1,), (1,)), ((), ())), preferred_element_type=F32)


def rotate(values, cosine, sine):
    half = values.shape[-1] // 2
    first = values[..., :half]
    second = values[..., half:]
    return jnp.concatenate([first * cosine - second * sine, second * cosine + first * sine], -1)


def norm_backward_step(grad_hat, normalized_rows, factor):
    return factor * (
        grad_hat - normalized_rows * jnp.mean(grad_hat * normalized_rows, axis=1, keepdims=True)
    )


class Place:
    def __init__(self):
        self.z = lax.axis_index("z")
        self.c = lax.axis_index("core")
        self.s = lax.axis_index("shard")

    def shard(self, d):
        s = self.s
        if d == 0:
            return s
        if d == 1:
            return s + 1 - 2 * lax.rem(s, 2)
        if d == 2:
            return lax.rem(s + 2, 4)
        return 3 - s

    def to(self, d):
        return {"shard": self.shard(d)}

    def sibling(self):
        return {"core": 1 - self.c}


def greet(ids):
    barrier = pltpu.get_barrier_semaphore()
    for d in ids:
        pl.semaphore_signal(barrier, inc=1, device_id=d, device_id_type=MESH)
    pl.semaphore_wait(barrier, len(ids))


def rcopy(src, dst, send, recv, dev):
    return pltpu.make_async_remote_copy(
        src_ref=src, dst_ref=dst, send_sem=send, recv_sem=recv, device_id=dev, device_id_type=MESH
    )


GATHER_SEMS = [DMA((6,)), DMA((6,)), DMA((7,)), DMA((7,)), DMA((1,))]


class Gather:
    def __init__(self, p, src, out, sems):
        self.p, self.src, self.out = p, src, out
        self.send, self.recv, self.csend, self.crecv, self.lsem = sems
        self.rows = src.shape[0]
        self.half = self.rows // 2

    def at(self, d, h, core=None):
        core = self.p.c if core is None else core
        row = (core * 4 + self.p.shard(d)) * self.rows
        if h is None:
            return self.out.at[pl.ds(row, self.rows)]
        return self.out.at[pl.ds(row + h * self.half, self.half)]

    def move(self, k):
        d, h, to = [(0, 0, 1), (0, 1, 2), (0, 1, 1), (0, 0, 2), (1, 0, 2), (2, 1, 1)][k]
        dst = self.at(d, h)
        src = self.src.at[pl.ds(h * self.half, self.half)] if d == 0 else dst
        return rcopy(src, dst, self.send.at[k], self.recv.at[k], self.p.to(to))

    def landed(self, k):
        d, h = [(1, 0), (2, 1), (1, 1), (2, 0), (3, 0), (3, 1)][k]
        return self.at(d, h)

    def pass_on(self, k):
        here = self.src if k == 6 else self.landed(k)
        there = self.at(0, None) if k == 6 else self.landed(k)
        return rcopy(here, there, self.csend.at[k], self.crecv.at[k], self.p.sibling())

    def arrived(self, k):
        ref = self.landed(k)
        rcopy(ref, ref, self.send.at[k], self.recv.at[k], self.p.to(1)).wait_recv()
        self.pass_on(k).start()

    def start(self):
        for k in range(4):
            self.move(k).start()
        self.pass_on(6).start()
        pltpu.make_async_copy(self.src, self.at(0, None), self.lsem.at[0]).start()

    def relay(self):
        for k in (0, 1):
            self.arrived(k)
            self.move(4 + k).start()

    def early(self):
        for k in (2, 3):
            self.arrived(k)

    def late(self):
        for k in (4, 5):
            self.arrived(k)

    def both(self, ks):
        for k in ks:
            self.pass_on(k).wait_recv()

    def home(self):
        self.both((6,))
        pltpu.make_async_copy(self.src, self.at(0, None), self.lsem.at[0]).wait()

    def close(self):
        for k in range(6):
            self.move(k).wait_send()
        for k in range(7):
            self.pass_on(k).wait_send()

    def finish(self, early=False):
        if not early:
            self.early()
        self.late()
        self.both(range(7))
        pltpu.make_async_copy(self.src, self.at(0, None), self.lsem.at[0]).wait()
        self.close()


SCATTER_SEMS = [DMA((4,)), DMA((4,)), DMA((4,)), DMA((6,)), DMA((6,))]
ORDER = (3, 1, 2, 0)


def scatter_scratch(rows, width):
    half = rows // 2
    return [
        pltpu.VMEM((4, rows, width), BF),
        pltpu.VMEM((4, rows, width), BF),
        pltpu.VMEM((6, half, width), BF),
    ] + SCATTER_SEMS


class Scatter:
    def __init__(self, p, part, scratch):
        self.p, self.part = p, part
        self.own, self.got, self.slot, self.lsem, self.csend, self.crecv, self.send, self.recv = scratch
        self.rows = self.own.shape[1]
        self.half = self.rows // 2

    def block(self, core, d):
        return self.part.at[pl.ds((core * 4 + self.p.shard(d)) * self.rows, self.rows)]

    def local(self, d):
        return pltpu.make_async_copy(self.block(self.p.c, d), self.own.at[d], self.lsem.at[d])

    def swap(self, d):
        src = self.block(1 - self.p.c, d)
        return rcopy(src, self.got.at[d], self.csend.at[d], self.crecv.at[d], self.p.sibling())

    def rowsof(self, h):
        return pl.ds(h * self.half, self.half)

    def move(self, k):
        d, h, to = [(3, 0, 1), (3, 1, 2), (1, 0, 1), (2, 1, 2), (2, 0, 2), (1, 1, 1)][k]
        return rcopy(
            self.own.at[d, self.rowsof(h)], self.slot.at[k], self.send.at[k], self.recv.at[k], self.p.to(to)
        )

    def start(self):
        for d in ORDER:
            self.swap(d).start()
            self.local(d).start()

    def pair(self, d):
        self.swap(d).wait_recv()
        self.local(d).wait()
        self.own[d] = (self.own[d].astype(F32) + self.got[d].astype(F32)).astype(BF)

    def first(self):
        self.pair(3)
        self.move(0).start()
        self.move(1).start()
        self.pair(1)
        self.move(2).start()
        self.pair(2)
        self.move(3).start()
        self.pair(0)

    def relay(self):
        for k, d, h in ((0, 2, 0), (1, 1, 1)):
            self.move(k).wait_recv()
            r = self.rowsof(h)
            self.own[d, r] = (self.own[d, r].astype(F32) + self.slot[k].astype(F32)).astype(BF)
            self.move(4 + k).start()

    def total(self, h):
        near, far = (2, 4) if h == 0 else (3, 5)
        self.move(near).wait_recv()
        self.move(far).wait_recv()
        return (
            self.own[0, self.rowsof(h)].astype(F32)
            + self.slot[near].astype(F32)
            + self.slot[far].astype(F32)
        )

    def drain(self):
        for k in range(6):
            self.move(k).wait_send()
        for d in range(4):
            self.swap(d).wait_send()


def params(cid, mb):
    return pltpu.CompilerParams(
        collective_id=cid, has_side_effects=True, vmem_limit_bytes=mb * 2**20
    )


def plane_ids(p):
    return [p.to(1), p.to(2), p.to(3), p.sibling()]


class Columns:
    def __init__(self, p, sems):
        self.p = p
        self.send, self.recv, self.lsem = sems

    def cols(self, j, d, src, width):
        return src.at[:, pl.ds(pl.multiple_of(j * width, width), width)]

    def copy(self, k, d, src, dst):
        if d == 0:
            return pltpu.make_async_copy(src, dst, self.lsem.at[k])
        return rcopy(src, dst, self.send.at[k, d - 1], self.recv.at[k, d - 1], self.p.to(d))


def rows_at(ref, r, n, c0, width):
    return ref.at[pl.ds(r, n), pl.ds(c0, width)]


def greet_line(p, ids):
    barrier = pltpu.get_barrier_semaphore()
    nz = lax.axis_size("z")
    for d in ids:
        pl.semaphore_signal(barrier, inc=1, device_id=d, device_id_type=MESH)

    @pl.when(p.z > 0)
    def _():
        pl.semaphore_signal(barrier, inc=1, device_id={"z": p.z - 1}, device_id_type=MESH)

    @pl.when(p.z < nz - 1)
    def _():
        pl.semaphore_signal(barrier, inc=1, device_id={"z": p.z + 1}, device_id_type=MESH)

    ends = jnp.where(p.z == 0, 1, 0) + jnp.where(p.z == nz - 1, 1, 0)
    pl.semaphore_wait(barrier, len(ids) + 2 - ends)


def relay_sems(nz):
    return [DMA((3,)), DMA((3,)), DMA((1,)), DMA((2, nz, 3)), DMA((nz, 3))]


class Relay:
    def __init__(self, p, w, dst, c0, sems):
        self.p, self.w, self.dst, self.c0 = p, w, dst, c0
        self.xs, self.xr, self.ls, self.zs, self.zr = sems
        self.nz = lax.axis_size("z")
        self.part = w.shape[0]
        self.n = self.part // self.nz
        self.fb = w.shape[1] // 8

    def cols(self, d):
        return pl.ds(pl.multiple_of((self.p.shard(d) * 2 + self.p.c) * self.fb, self.fb), self.fb)

    def rows(self, d, q):
        return self.dst.at[pl.ds(self.p.shard(d) * self.part + q * self.n, self.n), pl.ds(self.c0, self.fb)]

    def fetch(self, d):
        src = self.w.at[pl.ds(self.p.z * self.n, self.n), self.cols(d)]
        return rcopy(src, self.rows(0, self.p.z), self.xs.at[d - 1], self.xr.at[d - 1], self.p.to(d))

    def local(self):
        dst = self.dst.at[pl.ds(self.p.s * self.part, self.part), pl.ds(self.c0, self.fb)]
        return pltpu.make_async_copy(self.w.at[:, self.cols(0)], dst, self.ls.at[0])

    def along(self, way, q, d):
        ref = self.rows(d, q)
        to = {"z": self.p.z + (1 if way else -1)}
        return rcopy(ref, ref, self.zs.at[way, q, d - 1], self.zr.at[q, d - 1], to)

    def start(self):
        for d in (3, 1, 2):
            self.fetch(d).start()
        self.local().start()

    def can(self, way):
        return self.p.z < self.nz - 1 if way else self.p.z > 0

    def own(self):
        for d in (1, 2, 3):
            self.fetch(d).wait_recv()
        for way in (0, 1):

            @pl.when(self.can(way))
            def _():
                for d in (1, 2, 3):
                    self.along(way, self.p.z, d).start()

    def hop(self, k):
        for way in (0, 1):
            q = self.p.z - k if way else self.p.z + k
            there = q >= 0 if way else q < self.nz

            @pl.when(there)
            def _():
                for d in (1, 2, 3):
                    self.along(way, q, d).wait_recv()

            @pl.when(jnp.logical_and(there, self.can(way)))
            def _():
                for d in (1, 2, 3):
                    self.along(way, q, d).start()

    def finish(self):
        self.local().wait()
        for d in (1, 2, 3):
            self.fetch(d).wait_send()
        for k in range(self.nz):
            for way in (0, 1):
                q = self.p.z - k if way else self.p.z + k
                there = q >= 0 if way else q < self.nz

                @pl.when(jnp.logical_and(there, self.can(way)))
                def _():
                    for d in (1, 2, 3):
                        self.along(way, q, d).wait_send()


class Forward:
    def __init__(self, p, xa, xn1, wqkv, wo, seg, gain, freq, sc, ob, bufs, sems):
        self.p, self.xa, self.xn1 = p, xa, xn1
        self.wqkv, self.wo, self.seg, self.gain, self.freq = wqkv, wo, seg, gain, freq
        self.sc, self.ob = sc, ob
        self.xb, self.nb, self.q, self.k, self.v, self.attn, self.probs, self.turn, self.kept, self.came = bufs
        self.xsem, self.nsem, self.send, self.recv = sems
        self.n = self.xb.shape[1]

    def block(self, i):
        s, d = self.p.s, i // 2
        one = s + 1 - 2 * lax.rem(s, 2)
        two = lax.rem(s + 2, 4)
        shard = jnp.where(d == 0, s, jnp.where(d == 1, one, jnp.where(d == 2, two, 3 - s)))
        return lax.rem(i, 2) * 4 + shard

    def rows(self, ref, i):
        return ref.at[pl.ds(self.block(i) * self.n, self.n)]

    def load(self, i):
        b = lax.rem(i, 2)
        return pltpu.make_async_copy(self.rows(self.xa, i), self.xb.at[b], self.xsem.at[b])

    def store(self, i):
        b = lax.rem(i, 2)
        return pltpu.make_async_copy(self.nb.at[b], self.rows(self.xn1, i), self.nsem.at[b])

    def swap(self, i):
        return rcopy(self.kept.at[i], self.came.at[i], self.send.at[i], self.recv.at[i], self.p.sibling())

    def seg_of(self, i):
        row = self.seg[self.block(i)]
        return row[0:1], row.T[:, 0:1]

    def first(self, i):
        b, k = lax.rem(i, 2), self.block(i)
        self.load(i).wait()

        @pl.when(i >= 2)
        def _():
            self.store(i - 2).wait()

        x = self.xb[b].astype(F32)
        f = lax.rsqrt(jnp.mean(x * x, axis=1, keepdims=True) + norm_eps)
        xn = (x * f * self.gain).astype(BF)
        self.nb[b] = xn
        self.store(i).start()
        lin = mm(xn, self.wqkv[...])
        row, col = self.seg_of(i)
        start = jnp.sum((row < col).astype(F32), axis=1, keepdims=True)
        at = lax.broadcasted_iota(jnp.int32, (self.n, 1), 0).astype(F32)
        angle = (at - start) * self.freq
        cosine, sine = jnp.cos(angle), jnp.sin(angle)
        self.turn[k] = jnp.concatenate([cosine, sine], -1)
        hd = HEAD_DIM
        self.q[k] = rotate(lin[:, :hd], cosine, sine).astype(BF)
        kv = lin[:, hd:]
        self.kept[i] = jnp.where(self.p.c == 0, rotate(kv, cosine, sine), kv).astype(BF)
        self.swap(i).start()

    def second(self, i):
        n, k = self.n, self.block(i)
        self.swap(i).wait()
        mine, came = self.kept[i], self.came[i]
        key = jnp.where(self.p.c == 0, mine, came)
        value = jnp.where(self.p.c == 0, came, mine)
        self.k[k], self.v[k] = key, value
        row, col = self.seg_of(i)
        down = lax.broadcasted_iota(jnp.int32, (n, n), 0)
        over = lax.broadcasted_iota(jnp.int32, (n, n), 1)
        allowed = jnp.logical_and(row == col, down >= over)
        scores = jnp.where(allowed, mm_nt(self.q[k], key) * HEAD_DIM ** (-0.5), mask_fill)
        ex = jnp.exp(scores - jnp.max(scores, axis=-1, keepdims=True))
        probs = ex / jnp.sum(ex, axis=-1, keepdims=True)
        self.probs[k] = probs
        attn = mm(probs.astype(BF), value).astype(BF)
        self.attn[k] = attn
        term = mm(attn, self.wo[...]).astype(BF)
        d = i // 2
        mine_too = lax.rem(i, 2) == self.p.c

        @pl.when(mine_too)
        def _():
            self.sc.own[d] = term

        @pl.when(jnp.logical_not(mine_too))
        def _():
            self.ob[d] = term
            self.sc.swap(d).start()

    def finish(self):
        self.store(6).wait()
        self.store(7).wait()


class MadeScatter(Scatter):
    def __init__(self, p, made, scratch):
        super().__init__(p, None, scratch)
        self.made = made

    def swap(self, d):
        return rcopy(self.made.at[d], self.got.at[d], self.csend.at[d], self.crecv.at[d], self.p.sibling())

    def pair(self, d):
        self.swap(d).wait_recv()
        self.own[d] = (self.own[d].astype(F32) + self.got[d].astype(F32)).astype(BF)


def front_kernel(
    x_ref, seg_ref, gain_ref, freq_ref, wq_ref, wk_ref, wv_ref, wo_hbm, wg_ref, wu_ref, g_ref,
    h_ref, xn2_ref, ga_ref, wgu_ref, gaina_ref, xa_ref, wqkv_ref, xn1_ref, q_ref, k_ref, v_ref,
    attn_ref, probs_ref, turn_ref, *scr
):
    p = Place()
    nz = lax.axis_size("z")
    others = [(0, 1)] + [(d, o) for d in (1, 2, 3) for o in (0, 1)]

    def dev(d, o):
        return {"core": 1 - p.c if o else p.c, "shard": p.shard(d)}

    scr = list(scr)

    def take(n):
        out = scr[:n]
        del scr[:n]
        return out

    ga = Gather(p, x_ref, xa_ref, take(5))
    gg = Gather(p, g_ref, ga_ref, take(5))
    [xnb] = take(1)
    gx = Gather(p, xnb, xn2_ref, take(5))
    co = Columns(p, take(3))
    tsend, trecv, tlocal = take(3)
    fb = wgu_ref.shape[1] // 2
    re = [Relay(p, wg_ref, wgu_ref, 0, take(5)), Relay(p, wu_ref, wgu_ref, fb, take(5))]
    [made] = take(1)
    sc = MadeScatter(p, made, take(8))
    wqkv, wo, seg, lsem = take(4)
    bufs, sems = take(10), take(4)
    [osem] = take(1)
    part, hd = wq_ref.shape[0], HEAD_DIM

    load_wo = pltpu.make_async_copy(wo_hbm.at[pl.ds(p.c * hd, hd)], wo, lsem.at[0])
    load_wqkv = pltpu.make_async_copy(wqkv_ref, wqkv, lsem.at[1])
    load_wo.start()
    greet_line(p, [dev(d, o) for d, o in others])

    def q_copy(d):
        src = co.cols(p.shard(d) * 2 + p.c, d, wq_ref, hd)
        return co.copy(0, d, src, rows_at(wqkv_ref, p.s * part, part, 0, hd))

    def kv_copy(d, w):
        src = co.cols(p.shard(d), d, w, hd)
        return co.copy(1, d, src, rows_at(wqkv_ref, p.s * part, part, hd, hd))

    def small(k):
        d, o = others[k]
        yield rcopy(seg_ref, seg.at[p.c * 4 + p.s], tsend.at[k], trecv.at[k], dev(d, o))
        if d and not o:
            yield rcopy(gain_ref, gaina_ref.at[p.s], tsend.at[7 + d - 1], trecv.at[7 + d - 1], dev(d, o))

    smalls = [cp for k in range(7) for cp in small(k)] + [
        pltpu.make_async_copy(seg_ref, seg.at[p.c * 4 + p.s], tlocal.at[0]),
        pltpu.make_async_copy(gain_ref, gaina_ref.at[p.s], tlocal.at[1]),
    ]
    for cp in smalls:
        cp.start()
    for d in (3, 1, 2, 0):
        q_copy(d).start()

        @pl.when(p.c == 0)
        def _():
            kv_copy(d, wk_ref).start()

        @pl.when(p.c != 0)
        def _():
            kv_copy(d, wv_ref).start()

    ga.start()
    for cp in smalls:
        cp.wait()
    ga.relay()
    for d in (3, 1, 2, 0):
        q_copy(d).wait()
        kv_copy(d, wk_ref).wait()
    load_wqkv.start()
    ga.home()
    load_wo.wait()
    load_wqkv.wait()
    gain1 = jnp.concatenate([gaina_ref[j, 0:1] for j in range(4)], -1)
    gain2 = jnp.concatenate([gaina_ref[j, 1:2] for j in range(4)], -1)
    fw = Forward(p, xa_ref, xn1_ref, wqkv, wo, seg, gain1, freq_ref[...], sc, made, bufs, sems)

    def pair(d):
        sc.pair(d)
        if d == 3:
            sc.move(0).start()
            sc.move(1).start()
        elif d:
            sc.move(1 + d).start()

    def step(i):
        at_tick(i, 1, ga.early)
        at_tick(i, 2, lambda: ga.both((0, 2)))
        at_tick(i, 2, re[0].start)
        at_tick(i, 4, lambda: ga.both((1, 3)))
        at_tick(i, 4, re[1].start)
        at_tick(i, 5, ga.late)
        at_tick(i, 6, lambda: ga.both((4, 5)))
        at_tick(i, 7, re[0].own)

        @pl.when(jnp.logical_and(lax.rem(i, 2) == 0, i < 8))
        def _():
            fw.load(i).start()
            fw.load(i + 1).start()

        pl.when(i < 8)(lambda: fw.first(i))
        pl.when(i > 0)(lambda: fw.second(i - 1))
        for d in range(4):
            at_tick(i, 2 * d + 2, functools.partial(pair, d))

    loop(0, 9, step)
    saved = [
        pltpu.make_async_copy(a, b, osem.at[j])
        for j, (a, b) in enumerate(
            zip(bufs[2:8], (q_ref, k_ref, v_ref, attn_ref, probs_ref, turn_ref), strict=True)
        )
    ]
    for cp in saved:
        cp.start()
    re[1].own()
    re[0].hop(1)
    gg.start()
    sc.relay()
    half = sc.half
    for h in (0, 1):
        r = pl.ds(h * half, half)
        res = x_ref[r].astype(F32) + sc.total(h)
        h_ref[r] = res
        f = lax.rsqrt(jnp.mean(res * res, axis=1, keepdims=True) + norm_eps)
        xnb[r] = (res * f * gain2).astype(BF)
    gx.start()
    gg.relay()
    re[1].hop(1)
    for k in range(2, nz):
        re[0].hop(k)
    gg.early()
    gx.relay()
    for k in range(2, nz):
        re[1].hop(k)
    gg.finish(early=True)
    gx.finish()
    ga.close()
    sc.drain()
    fw.finish()
    for r in re:
        r.finish()
    for cp in saved:
        cp.wait()


def front(x, seg, gains, freq, wq, wk, wv, wo, wg, wu, g):
    rows, width = x.shape
    hd = HEAD_DIM
    nz = lax.axis_size("z")
    every = jax.ShapeDtypeStruct((8 * rows, width), BF)
    head = jax.ShapeDtypeStruct((8, rows, hd), BF)
    keep = pltpu.VMEM((8, rows, hd), BF)
    wide = pltpu.VMEM((2, rows, width), BF)
    return pl.pallas_call(
        front_kernel,
        out_shape=(
            jax.ShapeDtypeStruct((rows, width), F32),
            every,
            every,
            jax.ShapeDtypeStruct((width, wg.shape[1] // 4), BF),
            jax.ShapeDtypeStruct((4, *gains.shape), F32),
            every,
            jax.ShapeDtypeStruct((width, 2 * hd), BF),
            every,
            head,
            head,
            head,
            head,
            jax.ShapeDtypeStruct((8, rows, rows), F32),
            jax.ShapeDtypeStruct((8, rows, hd), F32),
        ),
        in_specs=[VM] * 4 + [ANY] * 6 + [VM],
        out_specs=(VM, ANY, ANY, ANY, VM) + (ANY,) * 9,
        scratch_shapes=GATHER_SEMS * 2
        + [pltpu.VMEM((rows, width), BF)]
        + GATHER_SEMS
        + [DMA((2, 3)), DMA((2, 3)), DMA((2,)), DMA((10,)), DMA((10,)), DMA((2,))]
        + relay_sems(nz) * 2
        + [pltpu.VMEM((4, rows, width), BF)]
        + scatter_scratch(rows, width)
        + [
            pltpu.VMEM((width, 2 * hd), BF),
            pltpu.VMEM((hd, width), BF),
            pltpu.VMEM((8, 8, rows), F32),
            DMA((2,)),
        ]
        + [wide, wide, keep, keep, keep, keep]
        + [pltpu.VMEM((8, rows, rows), F32), pltpu.VMEM((8, rows, hd), F32), keep, keep]
        + [DMA((2,)), DMA((2,)), DMA((8,)), DMA((8,)), DMA((6,))],
        compiler_params=params(0, 62),
        name="front",
    )(x, seg, gains, freq, wq, wk, wv, wo, wg, wu, g)


CH = 64
DOWN, GU, OUT, QKV = range(4)


class Chain:
    def __init__(self, p, h, ins, outs, bufs, sems):
        self.p, self.h = p, h
        self.ins = ins
        self.gate, self.up, self.down, self.out, self.wq, self.wk, self.wv = outs
        self.buf, self.bufq, self.ring, self.ring_sem = bufs
        self.rs_send, self.rs_recv, self.ag_send, self.ag_recv, self.cp_send, self.cp_recv, self.tsend = sems
        nz = lax.axis_size("z")
        self.nz = nz
        self.pos = nz - 1 - p.z if h == 0 else p.z
        self.step = -1 if h == 0 else 1

    def dev(self, by):
        return {"z": self.p.z + by}

    BASE = {DOWN: 0, GU: 8, OUT: 24, QKV: 26}

    def tick(self, kind, t):
        return self.BASE[kind] + t

    def shard_of(self, t):
        s, d = self.p.s, lax.rem(t, 4)
        one = s + 1 - 2 * lax.rem(s, 2)
        two = lax.rem(s + 2, 4)
        return jnp.where(d == 0, s, jnp.where(d == 1, one, jnp.where(d == 2, two, 3 - s)))

    def mine(self, kind, t):
        h = self.h
        if kind == DOWN:
            return self.ins[DOWN].at[pl.ds(h * 512 + t * CH, CH)]
        if kind == OUT:
            return self.ins[OUT].at[pl.ds(h * 128 + t * CH, CH)]
        row = self.shard_of(t) * 512 + h * 256
        if kind == QKV:
            return self.ins[QKV].at[pl.ds(row, 256)]
        return self.ins[GU].at[pl.ds(row + (t // 4) * CH, CH)]

    def fetch(self, kind, t):
        r = lax.rem(self.tick(kind, t), RING)
        return pltpu.make_async_copy(self.mine(kind, t), self.ring.at[r], self.ring_sem.at[r])

    def ahead(self, kind, t):
        @pl.when(self.pos > 0)
        def _():
            self.fetch(kind, t).start()

    def slot(self, kind, t):
        return self.bufq.at[t] if kind == QKV else self.buf.at[self.tick(kind, t)]

    def rs_copy(self, kind, t, src):
        k = self.tick(kind, t)
        return rcopy(
            src, self.slot(kind, t), self.rs_send.at[k], self.rs_recv.at[k], self.dev(self.step)
        )

    def reduce(self, kind, t):
        first, last = self.pos == 0, self.pos == self.nz - 1

        @pl.when(first)
        def _():
            self.rs_copy(kind, t, self.mine(kind, t)).start()

        @pl.when(jnp.logical_not(first))
        def _():
            slot = self.slot(kind, t)
            if kind in (DOWN, GU):
                self.fetch(kind, t).wait()
                own = self.ring.at[lax.rem(self.tick(kind, t), RING)]
            else:
                own = self.mine(kind, t)
            self.rs_copy(kind, t, slot).wait_recv()
            slot[...] = (slot[...].astype(F32) + own[...].astype(F32)).astype(BF)

        @pl.when(jnp.logical_and(jnp.logical_not(first), jnp.logical_not(last)))
        def _():
            self.rs_copy(kind, t, self.slot(kind, t)).start()

        @pl.when(last)
        def _():
            self.turn(kind, t)

    def pieces(self, kind, t, s, d_shard):
        h, c = self.h, self.p.c
        if kind == DOWN:
            return [(None, self.down.at[pl.ds(c * 1024 + h * 512 + t * CH, CH)])]
        if kind == OUT:
            return [(None, self.out.at[pl.ds(c * 256 + h * 128 + t * CH, CH)])]
        if kind == GU:
            r = h * 256 + (t // 4) * CH
            c0 = pl.multiple_of((s * 2 + c) * 1024, 1024)
            return [
                ((0, 1024), self.gate.at[pl.ds(r, CH), pl.ds(c0, 1024)]),
                ((1024, 1024), self.up.at[pl.ds(r, CH), pl.ds(c0, 1024)]),
            ]
        r = h * 256
        cq = pl.multiple_of((s * 2 + c) * 256, 256)
        return [((0, 256), self.wq.at[pl.ds(r, 256), pl.ds(cq, 256)])]

    def kv_piece(self, s, w):
        return w.at[pl.ds(self.h * 256, 256), pl.ds(pl.multiple_of(s * 256, 256), 256)]

    def turn(self, kind, t):
        slot = self.slot(kind, t)
        k = self.tick(kind, t)
        to = self.p.s if kind in (DOWN, OUT) else self.shard_of(t)

        def send(i, src, dst):
            if kind in (DOWN, OUT):
                pltpu.make_async_copy(src, dst, self.ag_recv.at[i, k]).start()
                return

            @pl.when(lax.rem(t, 4) == 0)
            def _():
                pltpu.make_async_copy(src, dst, self.ag_recv.at[i, k]).start()

            @pl.when(lax.rem(t, 4) != 0)
            def _():
                rcopy(src, dst, self.tsend.at[i, k], self.ag_recv.at[i, k], {"shard": to}).start()

        for i, (cols, dst) in enumerate(self.pieces(kind, t, self.p.s, to)):
            send(i, slot if cols is None else slot.at[:, pl.ds(*cols)], dst)
        if kind == QKV:
            src = slot.at[:, pl.ds(256, 256)]

            @pl.when(self.p.c == 0)
            def _():
                send(1, src, self.kv_piece(self.p.s, self.wk))

            @pl.when(self.p.c != 0)
            def _():
                send(1, src, self.kv_piece(self.p.s, self.wv))

    def spread_copy(self, i, k, ref):
        return rcopy(ref, ref, self.ag_send.at[i, k], self.ag_recv.at[i, k], self.dev(-self.step))

    def spread(self, kind, t):
        k = self.tick(kind, t)
        s = self.p.s if kind in (DOWN, OUT) else self.shard_of(t)

        def go(i, ref, wait=True):
            if wait:
                self.spread_copy(i, k, ref).wait_recv()

            @pl.when(self.pos > 0)
            def _():
                self.spread_copy(i, k, ref).start()

            rcopy(ref, ref, self.cp_send.at[i, k], self.cp_recv.at[i, k], self.p.sibling()).start()

        for i, (_, ref) in enumerate(self.pieces(kind, t, s, None)):
            go(i, ref)
        if kind == QKV:
            self.spread_copy(1, k, self.kv_piece(s, self.wk)).wait_recv()

            @pl.when(self.p.c == 0)
            def _():
                go(1, self.kv_piece(s, self.wk), False)

            @pl.when(self.p.c != 0)
            def _():
                go(1, self.kv_piece(s, self.wv), False)

    def drain_reduce(self, kind, t):
        @pl.when(self.pos < self.nz - 1)
        def _():
            self.rs_copy(kind, t, self.slot(kind, t)).wait_send()

        if kind not in (GU, QKV):
            return
        k = self.tick(kind, t)

        @pl.when(jnp.logical_and(self.pos == self.nz - 1, lax.rem(t, 4) != 0))
        def _():
            slot = self.slot(kind, t)
            for i, (cols, dst) in enumerate(self.pieces(kind, t, self.p.s, None)):
                src = slot.at[:, pl.ds(*cols)]
                rcopy(src, dst, self.tsend.at[i, k], self.ag_recv.at[i, k], self.p.to(1)).wait_send()
            if kind == QKV:
                src = slot.at[:, pl.ds(256, 256)]
                dst = self.kv_piece(self.p.s, self.wk)
                rcopy(src, dst, self.tsend.at[1, k], self.ag_recv.at[1, k], self.p.to(1)).wait_send()

    def drain_spread(self, kind, t):
        k = self.tick(kind, t)
        s = self.p.s if kind in (DOWN, OUT) else self.shard_of(t)
        refs = [ref for _, ref in self.pieces(kind, t, s, None)]
        if kind == QKV:
            refs.append(self.kv_piece(s, self.wk))
        for i, ref in enumerate(refs):

            @pl.when(self.pos > 0)
            def _():
                self.spread_copy(i, k, ref).wait_send()

            rcopy(ref, ref, self.cp_send.at[i, k], self.cp_recv.at[i, k], self.p.sibling()).wait()


N_TICKS, RING = 30, 4
CHAIN_SEMS = [DMA((N_TICKS,))] * 2 + [DMA((2, N_TICKS))] * 5


def loop(lo, hi, body):
    def step(t, _):
        body(t)
        return 0

    lax.fori_loop(lo, hi, step, 0)


COUNT = {DOWN: 8, GU: 16, OUT: 2, QKV: 4}


SKEW, TURN = 2, 3


def between(i, lo, hi):
    return jnp.logical_and(i >= lo, i < hi)


def each(i, lo, hi, act):
    for kind, n in COUNT.items():
        base = Chain.BASE[kind]
        a, b = max(lo, base), min(hi, base + n)
        if a < b:

            @pl.when(between(i, a, b))
            def _():
                act(kind, i - base)


def at_tick(t, when, act):
    @pl.when(t == when)
    def _():
        act()


def all_greet(p):
    nz = lax.axis_size("z")
    greet(plane_ids(p) + [{"z": lax.rem(p.z + k, nz)} for k in range(1, nz)])


class GainSums:
    def __init__(self, p, tot, got, gz, send, recv):
        self.p, self.tot, self.got, self.gz, self.send, self.recv = p, tot, got, gz, send, recv
        self.nz = lax.axis_size("z")

    def copy(self, k):
        dev = (self.p.sibling(), self.p.to(1), self.p.to(2))[k]
        return rcopy(self.tot.at[k], self.got.at[k], self.send.at[k], self.recv.at[k], dev)

    def along(self, k):
        to = {"z": lax.rem(self.p.z + k, self.nz)}
        return rcopy(
            self.tot.at[3], self.gz.at[self.p.z], self.send.at[2 + k], self.recv.at[3 + self.p.z], to
        )

    def landed(self, k):
        src = lax.rem(self.p.z + self.nz - k, self.nz)
        ref = self.gz.at[src]
        return rcopy(ref, ref, self.send.at[2 + k], self.recv.at[3 + src], {"z": src})

    def add(self, k):
        self.copy(k).wait()
        self.tot[k + 1] = self.tot[k] + self.got[k]
        if k < 2:
            self.copy(k + 1).start()
        else:
            for j in range(1, self.nz):
                self.along(j).start()
            self.gz[self.p.z] = self.tot[3]

    def finish(self):
        for j in range(1, self.nz):
            self.along(j).wait_send()
            self.landed(j).wait_recv()
        total = self.gz[0]
        for j in range(1, self.nz):
            total = total + self.gz[j]
        return total


class Attention:
    def __init__(self, p, hbm, wo, wqkv, part, gout, gqkv, bufs, sems):
        self.p, self.hbm, self.wo, self.wqkv, self.part = p, hbm, wo, wqkv, part
        self.gout, self.gqkv = gout, gqkv
        self.bufs, self.other, self.came, self.kept, self.dq, self.rows_out = bufs[:8], *bufs[8:]
        self.sem, self.send, self.recv, self.psem = sems
        self.n = self.rows_out.shape[1]

    def load(self, i, j):
        src = self.hbm[i]
        ref = src.at[pl.ds(j * self.n, self.n)] if len(src.shape) == 2 else src.at[j]
        b = lax.rem(j, 2)
        return pltpu.make_async_copy(ref, self.bufs[i].at[b], self.sem.at[i, b])

    def fetch(self, j):
        for i in range(7):
            self.load(i, j).start()

    def swap(self, j):
        return rcopy(self.other.at[j], self.came.at[j], self.send.at[j], self.recv.at[j], self.p.sibling())

    def first(self, j):
        for i in range(7):
            self.load(i, j).wait()

        @pl.when(j < 7)
        def _():
            self.fetch(j + 1)

        b = lax.rem(j, 2)
        dhb, q, k, v, attn, probs, turn = (self.bufs[i][b] for i in range(7))
        scale = HEAD_DIM ** (-0.5)
        half = HEAD_DIM // 2
        cosine, sine = turn[:, :half], turn[:, half:]
        dattn = mm_nt(dhb, self.wo[...]).astype(BF)
        g = mm_tn(attn, dhb)
        self.gout[...] = jnp.where(j == 0, g, self.gout[...] + g)
        dp = mm_nt(dattn, v)
        dv = mm_tn(probs.astype(BF), dattn)
        ds = (probs * (dp - jnp.sum(dp * probs, axis=-1, keepdims=True))).astype(BF)
        dq = rotate(mm(ds, k) * scale, cosine, -sine)
        dk = rotate(mm_tn(ds, q) * scale, cosine, -sine)
        zero = self.p.c == 0
        self.dq[b] = dq.astype(BF)
        self.kept[b] = jnp.where(zero, dk, dv)
        self.other[j] = jnp.where(zero, dv, dk).astype(BF)
        self.swap(j).start()
        self.load(7, j).start()

    def out_copy(self, j):
        b = lax.rem(j, 2)
        return pltpu.make_async_copy(self.rows_out.at[b], self.part.at[pl.ds(j * self.n, self.n)], self.psem.at[b])

    def second(self, j):
        b = lax.rem(j, 2)
        self.swap(j).wait()
        self.load(7, j).wait()
        dkv = (self.kept[b] + self.came[j].astype(F32)).astype(BF)
        dqkv = jnp.concatenate([self.dq[b], dkv], -1)
        g = mm_tn(self.bufs[7][b], dqkv)
        self.gqkv[...] = jnp.where(j == 0, g, self.gqkv[...] + g)

        @pl.when(j >= 2)
        def _():
            self.out_copy(j - 2).wait()

        self.rows_out[b] = mm_nt(dqkv, self.wqkv[...]).astype(BF)
        self.out_copy(j).start()

    def finish(self):
        self.out_copy(6).wait()
        self.out_copy(7).wait()


def tail_kernel(
    part_ref, dpart_ref, x_hbm, h_hbm, g_hbm, gain1_ref, gain2_ref, gd_ref, ggu_ref, wo_ref, wqkv_ref,
    q_ref, k_ref, v_ref, attn_ref, probs_ref, turn_ref, xn1_ref,
    out_hbm, grad_hbm, gains_ref, dhb_ref, p1_ref, gate, up, down, out, wq, wk, wv,
    bufa, bufb, qa, qb, ringa, ringb, ring_sem, tot, got, gz, gsend, grecv,
    low, xg, hb, dh, gout, gqkv, gout_low, gqkv_low, io_sem, free_sem, *scr
):
    p = Place()
    nz = lax.axis_size("z")
    s1 = Scatter(p, part_ref, scr[:8])
    s2 = Scatter(p, dpart_ref, scr[:8])
    s3 = Scatter(p, p1_ref, scr[:8])
    ga = Gather(p, low, dhb_ref, scr[8:13])
    sums = GainSums(p, tot, got, gz, gsend, grecv)
    hbm = (dhb_ref, q_ref, k_ref, v_ref, attn_ref, probs_ref, turn_ref, xn1_ref)
    at = Attention(p, hbm, wo_ref, wqkv_ref, p1_ref, gout, gqkv, scr[13:26], scr[26:30])
    ins = (gd_ref, ggu_ref, gout_low, gqkv_low)
    outs = (gate, up, down, out, wq, wk, wv)
    n = len(CHAIN_SEMS)
    chains = [
        Chain(p, 0, ins, outs, (bufa, qa, ringa, ring_sem.at[0]), scr[30 : 30 + n]),
        Chain(p, 1, ins, outs, (bufb, qb, ringb, ring_sem.at[1]), scr[30 + n : 30 + 2 * n]),
    ]
    line = SKEW * (nz - 1)
    half = s1.half

    def io(k):
        src, dst = [(h_hbm, hb), (g_hbm, xg), (x_hbm, xg), (low, out_hbm), (low, grad_hbm)][k]
        return pltpu.make_async_copy(src, dst, io_sem.at[k])

    io(0).start()
    io(1).start()
    tot[0] = jnp.zeros_like(tot[0])
    all_greet(p)
    s1.start()
    s1.first()

    def norm2():
        io(0).wait()
        io(1).wait()
        for h in (0, 1):
            r = pl.ds(h * half, half)
            dx = s1.total(h)
            res = hb[r]
            f = lax.rsqrt(jnp.mean(res * res, axis=1, keepdims=True) + norm_eps)
            hat = res * f
            term = jnp.sum(dx * hat, axis=0, keepdims=True)
            tot[0, 1:2] = term if h == 0 else tot[0, 1:2] + term
            d = xg[r].astype(F32) + norm_backward_step(dx * gain2_ref[...], hat, f)
            dh[r] = d
            low[r] = d.astype(BF)
        ga.start()
        io(2).start()

    def gathered():
        ga.finish()
        s1.drain()
        at.fetch(0)
        s2.start()

    def output():
        for h in (0, 1):
            r = pl.ds(h * half, half)
            low[r] = (hb[r] + s2.total(h)).astype(BF)
        io(3).start()
        s2.drain()
        for d in (p.to(1), p.to(2), p.sibling()):
            pl.semaphore_signal(free_sem, inc=1, device_id=d, device_id_type=MESH)

    def attended():
        at.finish()
        gout_low[...] = gout[...].astype(BF)
        gqkv_low[...] = gqkv[...].astype(BF)
        pl.semaphore_wait(free_sem, 3)
        s3.start()
        s3.first()

    def norm1():
        io(2).wait()
        io(3).wait()
        for h in (0, 1):
            r = pl.ds(h * half, half)
            dx = s3.total(h)
            xf = xg[r].astype(F32)
            f = lax.rsqrt(jnp.mean(xf * xf, axis=1, keepdims=True) + norm_eps)
            hat = xf * f
            term = jnp.sum(dx * hat, axis=0, keepdims=True)
            tot[0, 0:1] = term if h == 0 else tot[0, 0:1] + term
            low[r] = (dh[r] + norm_backward_step(dx * gain1_ref[...], hat, f)).astype(BF)
        io(4).start()
        sums.copy(0).start()

    def gains():
        gains_ref[...] = sums.finish()

    def tick(t):
        for ch in chains:
            each(t + 1 - SKEW * ch.pos, 0, 24, ch.ahead)
            each(t - SKEW * ch.pos, 0, N_TICKS, ch.reduce)
        for ch in chains:
            each(t - TURN - 2 * line + SKEW * ch.pos, 0, N_TICKS, ch.spread)
        at_tick(t, 1, s1.relay)
        at_tick(t, 5, norm2)
        at_tick(t, 7, ga.relay)
        at_tick(t, A0 - 1, gathered)
        pl.when(between(t, A0 + 1, A0 + 9))(lambda: at.second(t - A0 - 1))
        pl.when(between(t, A0, A0 + 8))(lambda: at.first(t - A0))
        at_tick(t, A0, s2.first)
        at_tick(t, A0 + 2, s2.relay)
        at_tick(t, A0 + 5, output)
        at_tick(t, A0 + 9, attended)
        at_tick(t, A0 + 11, s3.relay)
        at_tick(t, A0 + 14, norm1)
        for k in range(3):
            at_tick(t, A0 + 15 + k, functools.partial(sums.add, k))
        at_tick(t, A0 + 19, gains)

    loop(0, N_TICKS + TURN + 2 * line, tick)
    io(4).wait()
    s3.drain()

    def drain(i):
        for ch in chains:
            each(i, 0, N_TICKS, ch.drain_reduce)
            each(i, 0, N_TICKS, ch.drain_spread)

    loop(0, N_TICKS, drain)


A0 = 12


def tail(part, dpart, x, h, g, gain1, gain2, g_down, g_gu, wo, wqkv, heads, xn1, ff):
    rows, width = x.shape
    nz = lax.axis_size("z")
    hd, pr = HEAD_DIM, width // 4
    shapes = [(pr, ff), (pr, ff), (ff // 4, width), (pr, width), (pr, width), (pr, 1024), (pr, 1024)]
    sq = pltpu.VMEM((2, rows, hd), BF)
    wide = pltpu.VMEM((2, rows, width), BF)
    return pl.pallas_call(
        tail_kernel,
        out_shape=(
            jax.ShapeDtypeStruct((rows, width), BF),
            jax.ShapeDtypeStruct((rows, width), BF),
            jax.ShapeDtypeStruct((8, width), F32),
            jax.ShapeDtypeStruct((8 * rows, width), BF),
            jax.ShapeDtypeStruct((8 * rows, width), BF),
        )
        + tuple(jax.ShapeDtypeStruct(s, BF) for s in shapes),
        in_specs=[ANY] * 5 + [VM] * 2 + [ANY] * 2 + [VM] * 2 + [ANY] * 7,
        out_specs=(ANY, ANY, VM) + (ANY,) * 9,
        scratch_shapes=[
            pltpu.VMEM((26, CH, width), BF),
            pltpu.VMEM((26, CH, width), BF),
            pltpu.VMEM((4, 256, 512), BF),
            pltpu.VMEM((4, 256, 512), BF),
            pltpu.VMEM((RING, CH, width), BF),
            pltpu.VMEM((RING, CH, width), BF),
            DMA((2, RING)),
            pltpu.VMEM((4, 8, width), F32),
            pltpu.VMEM((3, 8, width), F32),
            pltpu.VMEM((nz, 8, width), F32),
            DMA((nz + 3,)),
            DMA((nz + 3,)),
            pltpu.VMEM((rows, width), BF),
            pltpu.VMEM((rows, width), BF),
            pltpu.VMEM((rows, width), F32),
            pltpu.VMEM((rows, width), F32),
            pltpu.VMEM((hd, width), F32),
            pltpu.VMEM((width, 2 * hd), F32),
            pltpu.VMEM((hd, width), BF),
            pltpu.VMEM((width, 2 * hd), BF),
            DMA((5,)),
            pltpu.SemaphoreType.REGULAR,
        ]
        + scatter_scratch(rows, width)
        + GATHER_SEMS
        + [wide, sq, sq, sq, sq]
        + [pltpu.VMEM((2, rows, rows), F32), pltpu.VMEM((2, rows, hd), F32), wide]
        + [pltpu.VMEM((8, rows, hd), BF)] * 2
        + [pltpu.VMEM((2, rows, hd), F32), sq, wide]
        + [DMA((8, 2)), DMA((8,)), DMA((8,)), DMA((2,))]
        + CHAIN_SEMS * 2,
        compiler_params=params(2, 63),
        name="tail",
    )(part, dpart, x, h, g, gain1, gain2, g_down, g_gu, wo, wqkv, *heads, xn1)


def pieces(
    tokens,
    segment_ids,
    attn_gain,
    w_query,
    w_key,
    w_value,
    w_out,
    mlp_gain,
    w_gate,
    w_up,
    w_down,
    cotangent,
):
    rows, width = tokens.shape[1], tokens.shape[2]
    core = lax.axis_index("core")
    nc, ns = lax.axis_size("core"), lax.axis_size("shard")
    hd = HEAD_DIM
    ff = w_gate.shape[1]
    fb = ff // (nc * ns)
    part = width // ns

    x = tokens.reshape(rows, width)
    g = cotangent.reshape(rows, width)
    wo = lax.dynamic_slice_in_dim(w_out, core * hd, hd, 0)
    wd = lax.dynamic_slice_in_dim(w_down, core * fb, fb, 0)

    gains = jnp.concatenate([attn_gain[None], mlp_gain[None], jnp.zeros((6, part), BF)], 0).astype(F32)
    seg = jnp.broadcast_to(segment_ids, (8, rows)).astype(F32)
    half = np.arange(hd // 2, dtype=np.float64) * 2.0 / hd
    freq = jnp.asarray((rope_base ** -half).astype(np.float32)[None])
    h, xn2, g_all, wgu, gains, _, wqkv, xn1, q, k, v, attn, probs, turn = front(
        x, seg, gains, freq, w_query, w_key, w_value, w_out, w_gate, w_up, g
    )
    gain1, gain2 = gains[:, 0].reshape(1, width), gains[:, 1].reshape(1, width)

    gu = mm(xn2, wgu)
    gate, up = gu[:, :fb], gu[:, fb:]
    sigma = jax.nn.sigmoid(gate)
    swish = gate * sigma
    hid = (swish * up).astype(BF)
    g_down = mm_tn(hid, g_all).astype(BF)
    dhid = mm_nt(g_all, wd)
    dgate = (dhid * up * sigma * (1.0 + gate * (1.0 - sigma))).astype(BF)
    dup = (dhid * swish).astype(BF)
    dgu = jnp.concatenate([dgate, dup], 1)
    g_gu = mm_tn(xn2, dgu).astype(BF)
    heads = (q, k, v, attn, probs, turn)
    output, input_grad, gain_g, _, _, gate_g, up_g, down_g, out_g, wq_g, wk_g, wv_g = tail(
        mm_nt(dgu, wgu).astype(BF),
        mm(hid, wd).astype(BF),
        x,
        h,
        g,
        gain1,
        gain2,
        g_down,
        g_gu,
        wo,
        wqkv,
        heads,
        xn1,
        ff,
    )
    output = output.reshape(1, rows, width)
    input_grad = input_grad.reshape(1, rows, width)
    gain_g = lax.dynamic_slice_in_dim(gain_g, lax.axis_index("shard") * part, part, 1)
    return (
        output,
        input_grad,
        gain_g[0],
        wq_g.astype(F32),
        wk_g.astype(F32),
        wv_g.astype(F32),
        out_g.astype(F32),
        gain_g[1],
        gate_g.astype(F32),
        up_g.astype(F32),
        down_g.astype(F32),
    )


def contract_rows(left, right):
    return lax.dot_general(
        left, right, (((0,), (0,)), ((), ())), preferred_element_type=jnp.float32
    )


def contract_cols(left, right):
    return lax.dot_general(
        left, right, (((1,), (1,)), ((), ())), preferred_element_type=jnp.float32
    )


def scores_of(queries, keys, allowed):
    raw = jnp.einsum(
        "qgrd,kgd->grqk", queries, keys, preferred_element_type=jnp.float32
    ) * HEAD_DIM ** (-0.5)
    return jnp.where(allowed, raw, mask_fill)


def general(
    tokens,
    segment_ids,
    attn_gain,
    w_query,
    w_key,
    w_value,
    w_out,
    mlp_gain,
    w_gate,
    w_up,
    w_down,
    cotangent,
):
    rows = tokens.shape[1]
    width = tokens.shape[2]
    groups = HEADS // KV_HEADS
    q_cols = HEADS * HEAD_DIM
    kv_cols = KV_HEADS * HEAD_DIM
    layer_input_rows = tokens.reshape(rows, width).astype(jnp.float32)
    segments = segment_ids.reshape(rows)
    iota = jnp.arange(rows, dtype=jnp.int32)
    starts = jnp.sum((segments[None, :] < segments[:, None]).astype(jnp.int32), axis=1)
    positions = (iota - starts).astype(jnp.float32)
    allowed = (segments[:, None] == segments[None, :]) & (iota[:, None] >= iota[None, :])
    half = HEAD_DIM // 2
    inv_freq = rope_base ** (-(jnp.arange(half, dtype=jnp.float32) * 2.0 / HEAD_DIM))
    angles = positions[:, None] * inv_freq
    cosine = jnp.cos(angles)
    sine = jnp.sin(angles)
    first_norm_factor = lax.rsqrt(
        jnp.mean(layer_input_rows * layer_input_rows, axis=1, keepdims=True) + norm_eps
    )
    first_standardized = layer_input_rows * first_norm_factor
    gain_fragment = lax.all_gather(attn_gain, "shard", axis=0, tiled=True)
    query_piece = lax.all_gather(w_query, "shard", axis=0, tiled=True)
    key_piece = lax.all_gather(w_key, "shard", axis=0, tiled=True)
    value_piece = lax.all_gather(w_value, "shard", axis=0, tiled=True)
    normalized_rows = (first_standardized * gain_fragment.astype(jnp.float32)).astype(jnp.bfloat16)
    joined = jnp.concatenate([query_piece, key_piece, value_piece], 1)
    result = (
        jnp.dot(normalized_rows, joined, preferred_element_type=jnp.float32),
        normalized_rows,
        gain_fragment.astype(jnp.float32),
    )
    folded = result
    projected, normed_one, first_norm_gain = (folded[0], folded[1], folded[2])
    queries = rotate(
        projected[:, :q_cols].reshape(rows, KV_HEADS, groups, HEAD_DIM),
        cosine[:, None, None, :],
        sine[:, None, None, :],
    ).astype(jnp.bfloat16)
    keys = rotate(
        projected[:, q_cols : q_cols + kv_cols].reshape(rows, KV_HEADS, HEAD_DIM),
        cosine[:, None, :],
        sine[:, None, :],
    ).astype(jnp.bfloat16)
    values = projected[:, q_cols + kv_cols :].reshape(rows, KV_HEADS, HEAD_DIM).astype(jnp.bfloat16)
    scores = scores_of(queries, keys, allowed)
    top = jnp.max(scores, axis=-1, keepdims=True)
    log_total = top + jnp.log(jnp.sum(jnp.exp(scores - top), axis=-1, keepdims=True))
    probs = jnp.exp(scores - log_total)
    probs_low = probs.astype(jnp.bfloat16)
    attn = (
        jnp.einsum("grqk,kgd->qgrd", probs_low, values, preferred_element_type=jnp.float32)
        .reshape(rows, q_cols)
        .astype(jnp.bfloat16)
    )
    part = attn
    result = (
        jnp.dot(
            part,
            lax.all_gather(w_out, "shard", axis=0, tiled=True),
            preferred_element_type=jnp.float32,
        ),
    )
    folded_out = result
    residual_hidden_state = layer_input_rows + folded_out[0]
    second_norm_factor = lax.rsqrt(
        jnp.mean(residual_hidden_state * residual_hidden_state, axis=1, keepdims=True) + norm_eps
    )
    second_standardized = residual_hidden_state * second_norm_factor
    gain_fragment = lax.all_gather(mlp_gain, "shard", axis=0, tiled=True)
    gate_piece = lax.all_gather(w_gate, "shard", axis=0, tiled=True)
    up_piece = lax.all_gather(w_up, "shard", axis=0, tiled=True)
    normalized_rows = (second_standardized * gain_fragment.astype(jnp.float32)).astype(jnp.bfloat16)
    joined = jnp.concatenate([gate_piece, up_piece], 1)
    result = (
        jnp.dot(normalized_rows, joined, preferred_element_type=jnp.float32),
        normalized_rows,
        gain_fragment.astype(jnp.float32),
    )
    folded_mlp = result
    gate = folded_mlp[0][:, :FF]
    up_value = folded_mlp[0][:, FF:]
    normed_two = folded_mlp[1]
    second_norm_gain = folded_mlp[2]
    sigma = jax.nn.sigmoid(gate)
    swish = gate * sigma
    inner = (swish * up_value).astype(jnp.bfloat16)
    part = inner
    result = (
        jnp.dot(
            part,
            lax.all_gather(w_down, "shard", axis=0, tiled=True),
            preferred_element_type=jnp.float32,
        ),
    )
    output = (residual_hidden_state + result[0]).astype(jnp.bfloat16).reshape(1, rows, width)
    grad_out = cotangent.reshape(rows, width)
    grad_down = lax.psum_scatter(
        contract_rows(inner, grad_out).astype(jnp.bfloat16),
        "shard",
        scatter_dimension=0,
        tiled=True,
    )
    down_full, gate_full, up_full = (
        lax.all_gather(w_down, "shard", axis=0, tiled=True),
        lax.all_gather(w_gate, "shard", axis=0, tiled=True),
        lax.all_gather(w_up, "shard", axis=0, tiled=True),
    )
    grad_inner = contract_cols(grad_out, down_full)
    grad_gate = (grad_inner * up_value * sigma * (1.0 + gate * (1.0 - sigma))).astype(jnp.bfloat16)
    grad_up = (grad_inner * swish).astype(jnp.bfloat16)
    grad_mlp = jnp.concatenate([grad_gate, grad_up], 1)
    mlp_shards = lax.psum_scatter(
        contract_rows(normed_two, grad_mlp).astype(jnp.bfloat16),
        "shard",
        scatter_dimension=0,
        tiled=True,
    ).astype(jnp.float32)
    second_norm_gradient = contract_cols(grad_gate, gate_full) + contract_cols(grad_up, up_full)
    second_gain_products = jnp.sum(second_norm_gradient * second_standardized, axis=0)
    hidden_gradient = grad_out.astype(jnp.float32) + norm_backward_step(
        second_norm_gradient * second_norm_gain, second_standardized, second_norm_factor
    )
    grad_hidden_low = hidden_gradient.astype(jnp.bfloat16)
    grad_out_proj = lax.psum_scatter(
        contract_rows(attn, grad_hidden_low).astype(jnp.bfloat16),
        "shard",
        scatter_dimension=0,
        tiled=True,
    )
    grad_attn = contract_cols(grad_hidden_low, lax.all_gather(w_out, "shard", axis=0, tiled=True))
    grad_attn = grad_attn.astype(jnp.bfloat16).reshape(rows, KV_HEADS, groups, HEAD_DIM)
    scores_again = scores_of(queries, keys, allowed)
    probs_again = jnp.exp(scores_again - log_total)
    probs_again_low = probs_again.astype(jnp.bfloat16)
    grad_probs = jnp.einsum("qgrd,kgd->grqk", grad_attn, values, preferred_element_type=jnp.float32)
    grad_values = jnp.einsum(
        "grqk,qgrd->kgd", probs_again_low, grad_attn, preferred_element_type=jnp.float32
    )
    grad_scores = (
        probs_again * (grad_probs - jnp.sum(grad_probs * probs_again, axis=-1, keepdims=True))
    ).astype(jnp.bfloat16)
    grad_queries = jnp.einsum(
        "grqk,kgd->qgrd", grad_scores, keys, preferred_element_type=jnp.float32
    ) * HEAD_DIM ** (-0.5)
    grad_keys = jnp.einsum(
        "grqk,qgrd->kgd", grad_scores, queries, preferred_element_type=jnp.float32
    ) * HEAD_DIM ** (-0.5)
    grad_queries = rotate(grad_queries, cosine[:, None, None, :], -sine[:, None, None, :]).reshape(
        rows, q_cols
    )
    grad_keys = rotate(grad_keys, cosine[:, None, :], -sine[:, None, :]).reshape(rows, kv_cols)
    grad_joined = jnp.concatenate(
        [
            grad_queries.astype(jnp.bfloat16),
            grad_keys.astype(jnp.bfloat16),
            grad_values.reshape(rows, kv_cols).astype(jnp.bfloat16),
        ],
        1,
    )
    qkv_shards = lax.psum_scatter(
        contract_rows(normed_one, grad_joined).astype(jnp.bfloat16),
        "shard",
        scatter_dimension=0,
        tiled=True,
    ).astype(jnp.float32)
    local_qkv = jnp.concatenate([w_query, w_key, w_value], 1)
    first_norm_gradient = contract_cols(
        grad_joined, lax.all_gather(local_qkv, "shard", axis=0, tiled=True)
    )
    first_gain_products = jnp.sum(first_norm_gradient * first_standardized, axis=0)
    input_gradient_rows = hidden_gradient + norm_backward_step(
        first_norm_gradient * first_norm_gain, first_standardized, first_norm_factor
    )
    input_grad = input_gradient_rows.astype(jnp.bfloat16).reshape(1, rows, width)
    gain_one_grad, gain_two_grad = (
        lax.psum_scatter(first_gain_products, "shard", scatter_dimension=0, tiled=True),
        lax.psum_scatter(second_gain_products, "shard", scatter_dimension=0, tiled=True),
    )
    summed = (
        lax.psum(gain_one_grad.astype(jnp.bfloat16), "rep").astype(jnp.float32),
        lax.psum(qkv_shards[:, :q_cols].astype(jnp.bfloat16), "rep").astype(jnp.float32),
        lax.psum(qkv_shards[:, q_cols : q_cols + kv_cols].astype(jnp.bfloat16), "rep").astype(
            jnp.float32
        ),
        lax.psum(qkv_shards[:, q_cols + kv_cols :].astype(jnp.bfloat16), "rep").astype(jnp.float32),
        lax.psum(grad_out_proj, "rep").astype(jnp.float32),
        lax.psum(gain_two_grad.astype(jnp.bfloat16), "rep").astype(jnp.float32),
        lax.psum(mlp_shards[:, :FF].astype(jnp.bfloat16), "rep").astype(jnp.float32),
        lax.psum(mlp_shards[:, FF:].astype(jnp.bfloat16), "rep").astype(jnp.float32),
        lax.psum(grad_down, "rep").astype(jnp.float32),
    )
    return (
        output,
        input_grad,
        summed[0],
        summed[1],
        summed[2],
        summed[3],
        summed[4],
        summed[5],
        summed[6],
        summed[7],
        summed[8],
    )


def solution(mesh):
    rep, shard = mesh.devices.shape
    if shard == KV_HEADS and rep % 2 == 0:
        fine = Mesh(np.asarray(mesh.devices).reshape(rep // 2, 2, shard), ("z", "core", "shard"))
        body, every = pieces, ("z", "core", "shard")
    else:
        fine, body, every = mesh, general, ("rep", "shard")
    seqs, vec, mat = P(every, None, None), P("shard"), P("shard", None)
    in_specs = (seqs, P(every, None), vec, mat, mat, mat, mat, vec, mat, mat, mat, seqs)
    out_specs = (seqs, seqs, vec, mat, mat, mat, mat, vec, mat, mat, mat)
    return jax.shard_map(body, mesh=fine, in_specs=in_specs, out_specs=out_specs, check_vma=False)
```

```python
import functools

import jax
import jax.numpy as jnp
import numpy as np
from jax import lax
from jax.experimental import pallas as pl
from jax.experimental.pallas import tpu as pltpu
from jax.sharding import Mesh
from jax.sharding import PartitionSpec as P

HEADS = 8
KV_HEADS = 4
HEAD_DIM = 256
FF = 8192

rope_base = 1000042.0
norm_eps = 1e-06
mask_fill = -1e30

BF = jnp.bfloat16
F32 = jnp.float32
MESH = pl.DeviceIdType.MESH
ANY = pl.BlockSpec(memory_space=pl.ANY)
VM = pl.BlockSpec(memory_space=pltpu.VMEM)
DMA = pltpu.SemaphoreType.DMA


def mm(a, b):
    return jnp.dot(a, b, preferred_element_type=F32)


def mm_tn(a, b):
    return lax.dot_general(a, b, (((0,), (0,)), ((), ())), preferred_element_type=F32)


def mm_nt(a, b):
    return lax.dot_general(a, b, (((1,), (1,)), ((), ())), preferred_element_type=F32)


def rotate(values, cosine, sine):
    half = values.shape[-1] // 2
    first = values[..., :half]
    second = values[..., half:]
    return jnp.concatenate([first * cosine - second * sine, second * cosine + first * sine], -1)


def norm_backward_step(grad_hat, normalized_rows, factor):
    return factor * (
        grad_hat - normalized_rows * jnp.mean(grad_hat * normalized_rows, axis=1, keepdims=True)
    )


class Place:
    def __init__(self):
        self.z = lax.axis_index("z")
        self.c = lax.axis_index("core")
        self.s = lax.axis_index("shard")

    def shard(self, d):
        s = self.s
        if d == 0:
            return s
        if d == 1:
            return s + 1 - 2 * lax.rem(s, 2)
        if d == 2:
            return lax.rem(s + 2, 4)
        return 3 - s

    def to(self, d):
        return {"shard": self.shard(d)}

    def sibling(self):
        return {"core": 1 - self.c}


def greet(ids):
    barrier = pltpu.get_barrier_semaphore()
    for d in ids:
        pl.semaphore_signal(barrier, inc=1, device_id=d, device_id_type=MESH)
    pl.semaphore_wait(barrier, len(ids))


def rcopy(src, dst, send, recv, dev):
    return pltpu.make_async_remote_copy(
        src_ref=src, dst_ref=dst, send_sem=send, recv_sem=recv, device_id=dev, device_id_type=MESH
    )


GATHER_SEMS = [DMA((6,)), DMA((6,)), DMA((7,)), DMA((7,)), DMA((1,))]


class Gather:
    def __init__(self, p, src, out, sems):
        self.p, self.src, self.out = p, src, out
        self.send, self.recv, self.csend, self.crecv, self.lsem = sems
        self.rows = src.shape[0]
        self.half = self.rows // 2

    def at(self, d, h, core=None):
        core = self.p.c if core is None else core
        row = (core * 4 + self.p.shard(d)) * self.rows
        if h is None:
            return self.out.at[pl.ds(row, self.rows)]
        return self.out.at[pl.ds(row + h * self.half, self.half)]

    def move(self, k):
        d, h, to = [(0, 0, 1), (0, 1, 2), (0, 1, 1), (0, 0, 2), (1, 0, 2), (2, 1, 1)][k]
        dst = self.at(d, h)
        src = self.src.at[pl.ds(h * self.half, self.half)] if d == 0 else dst
        return rcopy(src, dst, self.send.at[k], self.recv.at[k], self.p.to(to))

    def landed(self, k):
        d, h = [(1, 0), (2, 1), (1, 1), (2, 0), (3, 0), (3, 1)][k]
        return self.at(d, h)

    def pass_on(self, k):
        here = self.src if k == 6 else self.landed(k)
        there = self.at(0, None) if k == 6 else self.landed(k)
        return rcopy(here, there, self.csend.at[k], self.crecv.at[k], self.p.sibling())

    def arrived(self, k):
        ref = self.landed(k)
        rcopy(ref, ref, self.send.at[k], self.recv.at[k], self.p.to(1)).wait_recv()
        self.pass_on(k).start()

    def start(self):
        for k in range(4):
            self.move(k).start()
        self.pass_on(6).start()
        pltpu.make_async_copy(self.src, self.at(0, None), self.lsem.at[0]).start()

    def relay(self):
        for k in (0, 1):
            self.arrived(k)
            self.move(4 + k).start()

    def early(self):
        for k in (2, 3):
            self.arrived(k)

    def late(self):
        for k in (4, 5):
            self.arrived(k)

    def both(self, ks):
        for k in ks:
            self.pass_on(k).wait_recv()

    def home(self):
        self.both((6,))
        pltpu.make_async_copy(self.src, self.at(0, None), self.lsem.at[0]).wait()

    def close(self):
        for k in range(6):
            self.move(k).wait_send()
        for k in range(7):
            self.pass_on(k).wait_send()

    def finish(self, early=False):
        if not early:
            self.early()
        self.late()
        self.both(range(7))
        pltpu.make_async_copy(self.src, self.at(0, None), self.lsem.at[0]).wait()
        self.close()


SCATTER_SEMS = [DMA((4,)), DMA((4,)), DMA((4,)), DMA((6,)), DMA((6,))]
ORDER = (3, 1, 2, 0)


def scatter_scratch(rows, width):
    half = rows // 2
    return [
        pltpu.VMEM((4, rows, width), BF),
        pltpu.VMEM((4, rows, width), BF),
        pltpu.VMEM((6, half, width), BF),
    ] + SCATTER_SEMS


class Scatter:
    def __init__(self, p, part, scratch):
        self.p, self.part = p, part
        self.own, self.got, self.slot, self.lsem, self.csend, self.crecv, self.send, self.recv = scratch
        self.rows = self.own.shape[1]
        self.half = self.rows // 2

    def block(self, core, d):
        return self.part.at[pl.ds((core * 4 + self.p.shard(d)) * self.rows, self.rows)]

    def local(self, d):
        return pltpu.make_async_copy(self.block(self.p.c, d), self.own.at[d], self.lsem.at[d])

    def swap(self, d):
        src = self.block(1 - self.p.c, d)
        return rcopy(src, self.got.at[d], self.csend.at[d], self.crecv.at[d], self.p.sibling())

    def rowsof(self, h):
        return pl.ds(h * self.half, self.half)

    def move(self, k):
        d, h, to = [(3, 0, 1), (3, 1, 2), (1, 0, 1), (2, 1, 2), (2, 0, 2), (1, 1, 1)][k]
        return rcopy(
            self.own.at[d, self.rowsof(h)], self.slot.at[k], self.send.at[k], self.recv.at[k], self.p.to(to)
        )

    def start(self):
        for d in ORDER:
            self.swap(d).start()
            self.local(d).start()

    def pair(self, d):
        self.swap(d).wait_recv()
        self.local(d).wait()
        self.own[d] = (self.own[d].astype(F32) + self.got[d].astype(F32)).astype(BF)

    def first(self, k):
        self.pair(ORDER[k])
        for m in ((0, 1), (2,), (3,), ())[k]:
            self.move(m).start()

    def relay(self):
        for k, d, h in ((0, 2, 0), (1, 1, 1)):
            self.move(k).wait_recv()
            r = self.rowsof(h)
            self.own[d, r] = (self.own[d, r].astype(F32) + self.slot[k].astype(F32)).astype(BF)
            self.move(4 + k).start()

    def total(self, h):
        near, far = (2, 4) if h == 0 else (3, 5)
        self.move(near).wait_recv()
        self.move(far).wait_recv()
        return (
            self.own[0, self.rowsof(h)].astype(F32)
            + self.slot[near].astype(F32)
            + self.slot[far].astype(F32)
        )

    def drain(self):
        for k in range(6):
            self.move(k).wait_send()
        for d in range(4):
            self.swap(d).wait_send()


def params(cid, mb):
    return pltpu.CompilerParams(
        collective_id=cid, has_side_effects=True, vmem_limit_bytes=mb * 2**20
    )


def plane_ids(p):
    return [p.to(1), p.to(2), p.to(3), p.sibling()]


class Columns:
    def __init__(self, p, sems):
        self.p = p
        self.send, self.recv, self.lsem = sems

    def cols(self, j, d, src, width):
        return src.at[:, pl.ds(pl.multiple_of(j * width, width), width)]

    def copy(self, k, d, src, dst):
        if d == 0:
            return pltpu.make_async_copy(src, dst, self.lsem.at[k])
        return rcopy(src, dst, self.send.at[k, d - 1], self.recv.at[k, d - 1], self.p.to(d))


def rows_at(ref, r, n, c0, width):
    return ref.at[pl.ds(r, n), pl.ds(c0, width)]


def greet_line(p, ids):
    barrier = pltpu.get_barrier_semaphore()
    nz = lax.axis_size("z")
    for d in ids:
        pl.semaphore_signal(barrier, inc=1, device_id=d, device_id_type=MESH)

    @pl.when(p.z > 0)
    def _():
        pl.semaphore_signal(barrier, inc=1, device_id={"z": p.z - 1}, device_id_type=MESH)

    @pl.when(p.z < nz - 1)
    def _():
        pl.semaphore_signal(barrier, inc=1, device_id={"z": p.z + 1}, device_id_type=MESH)

    ends = jnp.where(p.z == 0, 1, 0) + jnp.where(p.z == nz - 1, 1, 0)
    pl.semaphore_wait(barrier, len(ids) + 2 - ends)


def relay_sems(nz):
    return [DMA((3,)), DMA((3,)), DMA((1,)), DMA((2, nz, 3)), DMA((nz, 3))]


class Relay:
    def __init__(self, p, w, dst, c0, sems):
        self.p, self.w, self.dst, self.c0 = p, w, dst, c0
        self.xs, self.xr, self.ls, self.zs, self.zr = sems
        self.nz = lax.axis_size("z")
        self.part = w.shape[0]
        self.n = self.part // self.nz
        self.fb = w.shape[1] // 8

    def cols(self, d):
        return pl.ds(pl.multiple_of((self.p.shard(d) * 2 + self.p.c) * self.fb, self.fb), self.fb)

    def rows(self, d, q):
        return self.dst.at[pl.ds(self.p.shard(d) * self.part + q * self.n, self.n), pl.ds(self.c0, self.fb)]

    def fetch(self, d):
        src = self.w.at[pl.ds(self.p.z * self.n, self.n), self.cols(d)]
        return rcopy(src, self.rows(0, self.p.z), self.xs.at[d - 1], self.xr.at[d - 1], self.p.to(d))

    def local(self):
        dst = self.dst.at[pl.ds(self.p.s * self.part, self.part), pl.ds(self.c0, self.fb)]
        return pltpu.make_async_copy(self.w.at[:, self.cols(0)], dst, self.ls.at[0])

    def along(self, way, q, d):
        ref = self.rows(d, q)
        to = {"z": self.p.z + (1 if way else -1)}
        return rcopy(ref, ref, self.zs.at[way, q, d - 1], self.zr.at[q, d - 1], to)

    def start(self):
        for d in (3, 1, 2):
            self.fetch(d).start()
        self.local().start()

    def can(self, way):
        return self.p.z < self.nz - 1 if way else self.p.z > 0

    def own(self):
        for d in (1, 2, 3):
            self.fetch(d).wait_recv()
        for way in (0, 1):

            @pl.when(self.can(way))
            def _():
                for d in (1, 2, 3):
                    self.along(way, self.p.z, d).start()

    def hop(self, k):
        for way in (0, 1):
            q = self.p.z - k if way else self.p.z + k
            there = q >= 0 if way else q < self.nz

            @pl.when(there)
            def _():
                for d in (1, 2, 3):
                    self.along(way, q, d).wait_recv()

            @pl.when(jnp.logical_and(there, self.can(way)))
            def _():
                for d in (1, 2, 3):
                    self.along(way, q, d).start()

    def finish(self):
        for d in (1, 2, 3):
            self.fetch(d).wait_send()
        for k in range(self.nz):
            for way in (0, 1):
                q = self.p.z - k if way else self.p.z + k
                there = q >= 0 if way else q < self.nz

                @pl.when(jnp.logical_and(there, self.can(way)))
                def _():
                    for d in (1, 2, 3):
                        self.along(way, q, d).wait_send()


class Forward:
    def __init__(self, p, xa, xn1, wqkv, wo, seg, gain, freq, sc, ob, bufs, sems):
        self.p, self.xa, self.xn1 = p, xa, xn1
        self.wqkv, self.wo, self.seg, self.gain, self.freq = wqkv, wo, seg, gain, freq
        self.sc, self.ob = sc, ob
        self.xb, self.nb, self.q, self.k, self.v, self.attn, self.probs, self.turn, self.kept, self.came = bufs
        self.xsem, self.nsem, self.send, self.recv = sems
        self.n = self.xb.shape[1]

    def block(self, i):
        s, d = self.p.s, i // 2
        one = s + 1 - 2 * lax.rem(s, 2)
        two = lax.rem(s + 2, 4)
        shard = jnp.where(d == 0, s, jnp.where(d == 1, one, jnp.where(d == 2, two, 3 - s)))
        return lax.rem(i, 2) * 4 + shard

    def rows(self, ref, i):
        return ref.at[pl.ds(self.block(i) * self.n, self.n)]

    def load(self, i):
        b = lax.rem(i, 2)
        return pltpu.make_async_copy(self.rows(self.xa, i), self.xb.at[b], self.xsem.at[b])

    def store(self, i):
        b = lax.rem(i, 2)
        return pltpu.make_async_copy(self.nb.at[b], self.rows(self.xn1, i), self.nsem.at[b])

    def swap(self, i):
        return rcopy(self.kept.at[i], self.came.at[i], self.send.at[i], self.recv.at[i], self.p.sibling())

    def seg_of(self, i):
        row = self.seg[self.block(i)]
        return row[0:1], row.T[:, 0:1]

    def first(self, i):
        b, k = lax.rem(i, 2), self.block(i)
        self.load(i).wait()

        @pl.when(i >= 2)
        def _():
            self.store(i - 2).wait()

        x = self.xb[b].astype(F32)
        f = lax.rsqrt(jnp.mean(x * x, axis=1, keepdims=True) + norm_eps)
        xn = (x * f * self.gain).astype(BF)
        self.nb[b] = xn
        self.store(i).start()
        lin = mm(xn, self.wqkv[...])
        row, col = self.seg_of(i)
        start = jnp.sum((row < col).astype(F32), axis=1, keepdims=True)
        at = lax.broadcasted_iota(jnp.int32, (self.n, 1), 0).astype(F32)
        angle = (at - start) * self.freq
        cosine, sine = jnp.cos(angle), jnp.sin(angle)
        self.turn[k] = jnp.concatenate([cosine, sine], -1)
        hd = HEAD_DIM
        self.q[k] = rotate(lin[:, :hd], cosine, sine).astype(BF)
        kv = lin[:, hd:]
        self.kept[i] = jnp.where(self.p.c == 0, rotate(kv, cosine, sine), kv).astype(BF)
        self.swap(i).start()

    def second(self, i):
        n, k = self.n, self.block(i)
        self.swap(i).wait()
        mine, came = self.kept[i], self.came[i]
        key = jnp.where(self.p.c == 0, mine, came)
        value = jnp.where(self.p.c == 0, came, mine)
        self.k[k], self.v[k] = key, value
        row, col = self.seg_of(i)
        down = lax.broadcasted_iota(jnp.int32, (n, n), 0)
        over = lax.broadcasted_iota(jnp.int32, (n, n), 1)
        allowed = jnp.logical_and(row == col, down >= over)
        scores = jnp.where(allowed, mm_nt(self.q[k], key) * HEAD_DIM ** (-0.5), mask_fill)
        ex = jnp.exp(scores - jnp.max(scores, axis=-1, keepdims=True))
        probs = ex / jnp.sum(ex, axis=-1, keepdims=True)
        self.probs[k] = probs
        attn = mm(probs.astype(BF), value).astype(BF)
        self.attn[k] = attn
        term = mm(attn, self.wo[...]).astype(BF)
        d = i // 2
        mine_too = lax.rem(i, 2) == self.p.c

        @pl.when(mine_too)
        def _():
            self.sc.own[d] = term

        @pl.when(jnp.logical_not(mine_too))
        def _():
            self.ob[d] = term
            self.sc.swap(d).start()

    def finish(self):
        self.store(6).wait()
        self.store(7).wait()


class MadeScatter(Scatter):
    def __init__(self, p, made, scratch):
        super().__init__(p, None, scratch)
        self.made = made

    def swap(self, d):
        return rcopy(self.made.at[d], self.got.at[d], self.csend.at[d], self.crecv.at[d], self.p.sibling())

    def pair(self, d):
        self.swap(d).wait_recv()
        self.own[d] = (self.own[d].astype(F32) + self.got[d].astype(F32)).astype(BF)


class Feed:
    def __init__(self, p, block, xn2, g, wgu, wd, outs, bufs, sems):
        self.p, self.block = p, block
        self.xn2, self.g, self.wgu, self.wd, self.outs = xn2, g, wgu, wd, outs
        self.xb, self.gb, self.made, self.got = bufs
        self.xsem, self.gsem, self.osem = sems
        self.n = self.xb.shape[1]
        self.fb = wd.shape[0]

    def rows(self, ref, i):
        return ref.at[pl.ds(self.block(i) * self.n, self.n)]

    def loads(self, i):
        b = lax.rem(i, 2)
        return [
            pltpu.make_async_copy(self.rows(self.xn2, i), self.xb.at[b], self.xsem.at[b]),
            pltpu.make_async_copy(self.rows(self.g, i), self.gb.at[b], self.gsem.at[b]),
        ]

    def stores(self, i):
        b = lax.rem(i, 2)
        srcs = (self.got.at[2 + b, :, pl.ds(0, self.fb)], self.made.at[b], self.made.at[2 + b], self.got.at[b])
        return [
            pltpu.make_async_copy(src, self.rows(out, i), self.osem.at[j, b])
            for j, (src, out) in enumerate(zip(srcs, self.outs, strict=True))
        ]

    def step(self, i):
        b, fb = lax.rem(i, 2), self.fb
        for cp in self.loads(i):
            cp.wait()

        @pl.when(i >= 2)
        def _():
            for cp in self.stores(i - 2):
                cp.wait()

        xn, g = self.xb[b], self.gb[b]
        gate, up = mm(xn, self.wgu[:, :fb]), mm(xn, self.wgu[:, fb:])
        sigma = jax.nn.sigmoid(gate)
        swish = gate * sigma
        hid = (swish * up).astype(BF)
        self.got[2 + b, :, :fb] = hid
        dhid = mm_nt(g, self.wd[...])
        dgate = (dhid * up * sigma * (1.0 + gate * (1.0 - sigma))).astype(BF)
        dup = (dhid * swish).astype(BF)
        self.made[b, :, :fb] = dgate
        self.made[b, :, fb:] = dup
        self.made[2 + b] = mm(hid, self.wd[...]).astype(BF)
        self.got[b] = mm_nt(self.made[b], self.wgu[...]).astype(BF)
        for cp in self.stores(i):
            cp.start()

    def finish(self):
        for i in (6, 7):
            for cp in self.stores(i):
                cp.wait()


def front_kernel(
    x_ref, seg_ref, gain_ref, freq_ref, wq_ref, wk_ref, wv_ref, wo_hbm, wg_ref, wu_ref, wd_hbm, g_ref,
    h_ref, xn2_ref, ga_ref, wgu_ref, gaina_ref, xa_ref, wqkv_ref, xn1_ref, q_ref, k_ref, v_ref,
    attn_ref, probs_ref, turn_ref, hid_ref, dgu_ref, dpart_ref, dx_ref, *scr
):
    p = Place()
    nz = lax.axis_size("z")
    others = [(0, 1)] + [(d, o) for d in (1, 2, 3) for o in (0, 1)]

    def dev(d, o):
        return {"core": 1 - p.c if o else p.c, "shard": p.shard(d)}

    scr = list(scr)

    def take(n):
        out = scr[:n]
        del scr[:n]
        return out

    ga = Gather(p, x_ref, xa_ref, take(5))
    gg = Gather(p, g_ref, ga_ref, take(5))
    [xnb] = take(1)
    gx = Gather(p, xnb, xn2_ref, take(5))
    co = Columns(p, take(3))
    tsend, trecv, tlocal = take(3)
    fb = wgu_ref.shape[1] // 2
    re = [Relay(p, wg_ref, wgu_ref, 0, take(5)), Relay(p, wu_ref, wgu_ref, fb, take(5))]
    [made] = take(1)
    sc = MadeScatter(p, made, take(8))
    wqkv, wo, seg, lsem = take(4)
    bufs, sems = take(10), take(4)
    [osem] = take(1)
    wgu, wd, gsem, fsem = take(4)
    part, hd = wq_ref.shape[0], HEAD_DIM

    load_wo = pltpu.make_async_copy(wo_hbm.at[pl.ds(p.c * hd, hd)], wo, lsem.at[0])
    load_wqkv = pltpu.make_async_copy(wqkv_ref, wqkv, lsem.at[1])
    load_wd = pltpu.make_async_copy(wd_hbm.at[pl.ds(p.c * fb, fb)], wd, lsem.at[2])
    load_wgu = pltpu.make_async_copy(wgu_ref, wgu, lsem.at[3])
    load_wo.start()
    load_wd.start()
    greet_line(p, [dev(d, o) for d, o in others])

    def q_copy(d):
        src = co.cols(p.shard(d) * 2 + p.c, d, wq_ref, hd)
        return co.copy(0, d, src, rows_at(wqkv_ref, p.s * part, part, 0, hd))

    def kv_copy(d, w):
        src = co.cols(p.shard(d), d, w, hd)
        return co.copy(1, d, src, rows_at(wqkv_ref, p.s * part, part, hd, hd))

    def small(k):
        d, o = others[k]
        yield rcopy(seg_ref, seg.at[p.c * 4 + p.s], tsend.at[k], trecv.at[k], dev(d, o))
        if d and not o:
            yield rcopy(gain_ref, gaina_ref.at[p.s], tsend.at[7 + d - 1], trecv.at[7 + d - 1], dev(d, o))

    smalls = [cp for k in range(7) for cp in small(k)] + [
        pltpu.make_async_copy(seg_ref, seg.at[p.c * 4 + p.s], tlocal.at[0]),
        pltpu.make_async_copy(gain_ref, gaina_ref.at[p.s], tlocal.at[1]),
    ]
    for cp in smalls:
        cp.start()
    for d in (3, 1, 2, 0):
        q_copy(d).start()

        @pl.when(p.c == 0)
        def _():
            kv_copy(d, wk_ref).start()

        @pl.when(p.c != 0)
        def _():
            kv_copy(d, wv_ref).start()

    ga.start()
    for cp in smalls:
        cp.wait()
    ga.relay()
    re[0].start()
    for d in (3, 1, 2, 0):
        q_copy(d).wait()
        kv_copy(d, wk_ref).wait()
    load_wqkv.start()
    ga.home()
    load_wo.wait()
    load_wqkv.wait()
    gain1 = jnp.concatenate([gaina_ref[j, 0:1] for j in range(4)], -1)
    gain2 = jnp.concatenate([gaina_ref[j, 1:2] for j in range(4)], -1)
    fw = Forward(p, xa_ref, xn1_ref, wqkv, wo, seg, gain1, freq_ref[...], sc, made, bufs, sems)

    def pair(d):
        sc.pair(d)
        if d == 3:
            sc.move(0).start()
            sc.move(1).start()
        elif d:
            sc.move(1 + d).start()

    def step(i):
        at_tick(i, 1, ga.early)
        at_tick(i, 1, re[1].start)
        at_tick(i, 2, lambda: ga.both((0, 2)))
        at_tick(i, 3, re[0].own)
        at_tick(i, 4, lambda: ga.both((1, 3)))
        at_tick(i, 4, re[1].own)
        at_tick(i, 5, ga.late)
        at_tick(i, 5, gg.start)
        at_tick(i, 6, lambda: ga.both((4, 5)))
        at_tick(i, 6, lambda: re[0].hop(1))
        at_tick(i, 8, lambda: re[1].hop(1))

        @pl.when(jnp.logical_and(lax.rem(i, 2) == 0, i < 8))
        def _():
            fw.load(i).start()
            fw.load(i + 1).start()

        pl.when(i < 8)(lambda: fw.first(i))
        pl.when(i > 0)(lambda: fw.second(i - 1))
        for d in range(4):
            at_tick(i, 2 * d + 2, functools.partial(pair, d))

    loop(0, 9, step)
    saved = [
        pltpu.make_async_copy(a, b, osem.at[j])
        for j, (a, b) in enumerate(
            zip(bufs[2:8], (q_ref, k_ref, v_ref, attn_ref, probs_ref, turn_ref), strict=True)
        )
    ]
    for cp in saved:
        cp.start()
    gg.relay()
    for k in range(2, nz - 1):
        re[0].hop(k)
    sc.relay()
    half = sc.half
    for h in (0, 1):
        r = pl.ds(h * half, half)
        res = x_ref[r].astype(F32) + sc.total(h)
        h_ref[r] = res
        f = lax.rsqrt(jnp.mean(res * res, axis=1, keepdims=True) + norm_eps)
        xnb[r] = (res * f * gain2).astype(BF)
    gx.start()
    for k in range(2, nz - 1):
        re[1].hop(k)
    re[0].hop(nz - 1)
    gg.early()
    gg.late()
    re[1].hop(nz - 1)
    for r in re:
        r.local().wait()
    load_wgu.start()
    fw.finish()
    sc.drain()
    load_wd.wait()
    gg.home()
    gx.home()
    gx.relay()
    load_wgu.wait()
    fd = Feed(
        p, fw.block, xn2_ref, ga_ref, wgu, wd, (hid_ref, dgu_ref, dpart_ref, dx_ref),
        (bufs[0], bufs[1], made, sc.got), (sems[0], gsem, fsem),
    )

    def feed(i):
        for ks, when in (((0, 2), 2), ((1, 3), 4), ((4, 5), 6)):
            at_tick(i, when, lambda ks=ks: (gx.both(ks), gg.both(ks)))

        @pl.when(lax.rem(i, 2) == 0)
        def _():
            for cp in fd.loads(i) + fd.loads(i + 1):
                cp.start()

        fd.step(i)
        at_tick(i, 1, gx.early)
        at_tick(i, 4, gx.late)

    loop(0, 8, feed)
    fd.finish()
    for gather in (ga, gg, gx):
        gather.close()
    for r in re:
        r.finish()
    for cp in saved:
        cp.wait()


def front(x, seg, gains, freq, wq, wk, wv, wo, wg, wu, wd, g):
    rows, width = x.shape
    hd = HEAD_DIM
    fb = wg.shape[1] // 8
    nz = lax.axis_size("z")
    every = jax.ShapeDtypeStruct((8 * rows, width), BF)
    head = jax.ShapeDtypeStruct((8, rows, hd), BF)
    keep = pltpu.VMEM((8, rows, hd), BF)
    wide = pltpu.VMEM((2, rows, width), BF)
    return pl.pallas_call(
        front_kernel,
        out_shape=(
            jax.ShapeDtypeStruct((rows, width), F32),
            every,
            every,
            jax.ShapeDtypeStruct((width, wg.shape[1] // 4), BF),
            jax.ShapeDtypeStruct((4, *gains.shape), F32),
            every,
            jax.ShapeDtypeStruct((width, 2 * hd), BF),
            every,
            head,
            head,
            head,
            head,
            jax.ShapeDtypeStruct((8, rows, rows), F32),
            jax.ShapeDtypeStruct((8, rows, hd), F32),
            jax.ShapeDtypeStruct((8 * rows, fb), BF),
            jax.ShapeDtypeStruct((8 * rows, 2 * fb), BF),
            every,
            every,
        ),
        in_specs=[VM] * 4 + [ANY] * 7 + [VM],
        out_specs=(VM, ANY, ANY, ANY, VM) + (ANY,) * 13,
        scratch_shapes=GATHER_SEMS * 2
        + [pltpu.VMEM((rows, width), BF)]
        + GATHER_SEMS
        + [DMA((2, 3)), DMA((2, 3)), DMA((2,)), DMA((10,)), DMA((10,)), DMA((2,))]
        + relay_sems(nz) * 2
        + [pltpu.VMEM((4, rows, width), BF)]
        + scatter_scratch(rows, width)
        + [
            pltpu.VMEM((width, 2 * hd), BF),
            pltpu.VMEM((hd, width), BF),
            pltpu.VMEM((8, 8, rows), F32),
            DMA((4,)),
        ]
        + [wide, wide, keep, keep, keep, keep]
        + [pltpu.VMEM((8, rows, rows), F32), pltpu.VMEM((8, rows, hd), F32), keep, keep]
        + [DMA((2,)), DMA((2,)), DMA((8,)), DMA((8,)), DMA((6,))]
        + [pltpu.VMEM((width, 2 * fb), BF), pltpu.VMEM((fb, width), BF), DMA((2,)), DMA((4, 2))],
        compiler_params=params(0, 63),
        name="front",
    )(x, seg, gains, freq, wq, wk, wv, wo, wg, wu, wd, g)


CH = 32
QR = 4 * CH
FINE = 64 // CH
DOWN, GU, OUT, QKV = range(4)
COUNT = {DOWN: 512 // CH, GU: 1024 // CH, OUT: 128 // CH, QKV: 1024 // QR}
N_TICKS = sum(COUNT.values())
EARLY = COUNT[DOWN] + COUNT[GU]


class Chain:
    def __init__(self, p, h, ins, outs, bufs, sems):
        self.p, self.h = p, h
        self.ins = ins
        self.gate, self.up, self.down, self.out, self.wq, self.wk, self.wv = outs
        self.buf, self.bufq, self.ring, self.ring_sem = bufs
        self.rs_send, self.rs_recv, self.ag_send, self.ag_recv, self.cp_send, self.cp_recv, self.tsend = sems
        nz = lax.axis_size("z")
        self.nz = nz
        self.pos = nz - 1 - p.z if h == 0 else p.z
        self.step = -1 if h == 0 else 1

    def dev(self, by):
        return {"z": self.p.z + by}

    BASE = {DOWN: 0, GU: COUNT[DOWN], OUT: EARLY, QKV: EARLY + COUNT[OUT]}

    def tick(self, kind, t):
        return self.BASE[kind] + t

    def shard_of(self, t):
        s, d = self.p.s, lax.rem(t, 4)
        one = s + 1 - 2 * lax.rem(s, 2)
        two = lax.rem(s + 2, 4)
        return jnp.where(d == 0, s, jnp.where(d == 1, one, jnp.where(d == 2, two, 3 - s)))

    def mine(self, kind, t):
        h = self.h
        if kind == DOWN:
            return self.ins[DOWN].at[pl.ds(h * 512 + t * CH, CH)]
        if kind == OUT:
            return self.ins[OUT].at[pl.ds(h * 128 + t * CH, CH)]
        row = self.shard_of(t) * 512 + h * 256
        if kind == QKV:
            return self.ins[QKV].at[pl.ds(row + (t // 4) * QR, QR)]
        return self.ins[GU].at[pl.ds(row + (t // 4) * CH, CH)]

    def fetch(self, kind, t):
        r = lax.rem(self.tick(kind, t), RING)
        return pltpu.make_async_copy(self.mine(kind, t), self.ring.at[r], self.ring_sem.at[r])

    def ahead(self, kind, t):
        @pl.when(self.pos > 0)
        def _():
            self.fetch(kind, t).start()

    def slot(self, kind, t):
        return self.bufq.at[t] if kind == QKV else self.buf.at[self.tick(kind, t)]

    def rs_copy(self, kind, t, src):
        k = self.tick(kind, t)
        return rcopy(
            src, self.slot(kind, t), self.rs_send.at[k], self.rs_recv.at[k], self.dev(self.step)
        )

    def begin(self, kind, t):
        @pl.when(self.pos == 0)
        def _():
            self.rs_copy(kind, t, self.mine(kind, t)).start()

    def reduce(self, kind, t):
        first, last = self.pos == 0, self.pos == self.nz - 1

        @pl.when(jnp.logical_not(first))
        def _():
            slot = self.slot(kind, t)
            if kind in (DOWN, GU):
                self.fetch(kind, t).wait()
                own = self.ring.at[lax.rem(self.tick(kind, t), RING)]
            else:
                own = self.mine(kind, t)
            self.rs_copy(kind, t, slot).wait_recv()
            slot[...] = (slot[...].astype(F32) + own[...].astype(F32)).astype(BF)

        @pl.when(jnp.logical_and(jnp.logical_not(first), jnp.logical_not(last)))
        def _():
            self.rs_copy(kind, t, self.slot(kind, t)).start()

        @pl.when(last)
        def _():
            self.turn(kind, t)

    def pieces(self, kind, t, s, d_shard):
        h, c = self.h, self.p.c
        if kind == DOWN:
            return [(None, self.down.at[pl.ds(c * 1024 + h * 512 + t * CH, CH)])]
        if kind == OUT:
            return [(None, self.out.at[pl.ds(c * 256 + h * 128 + t * CH, CH)])]
        if kind == GU:
            r = h * 256 + (t // 4) * CH
            c0 = pl.multiple_of((s * 2 + c) * 1024, 1024)
            return [
                ((0, 1024), self.gate.at[pl.ds(r, CH), pl.ds(c0, 1024)]),
                ((1024, 1024), self.up.at[pl.ds(r, CH), pl.ds(c0, 1024)]),
            ]
        r = h * 256 + (t // 4) * QR
        cq = pl.multiple_of((s * 2 + c) * 256, 256)
        return [((0, 256), self.wq.at[pl.ds(r, QR), pl.ds(cq, 256)])]

    def kv_piece(self, t, s, w):
        r = self.h * 256 + (t // 4) * QR
        return w.at[pl.ds(r, QR), pl.ds(pl.multiple_of(s * 256, 256), 256)]

    def turn(self, kind, t):
        slot = self.slot(kind, t)
        k = self.tick(kind, t)
        to = self.p.s if kind in (DOWN, OUT) else self.shard_of(t)

        def send(i, src, dst):
            if kind in (DOWN, OUT):
                pltpu.make_async_copy(src, dst, self.ag_recv.at[i, k]).start()
                return

            @pl.when(lax.rem(t, 4) == 0)
            def _():
                pltpu.make_async_copy(src, dst, self.ag_recv.at[i, k]).start()

            @pl.when(lax.rem(t, 4) != 0)
            def _():
                rcopy(src, dst, self.tsend.at[i, k], self.ag_recv.at[i, k], {"shard": to}).start()

        for i, (cols, dst) in enumerate(self.pieces(kind, t, self.p.s, to)):
            send(i, slot if cols is None else slot.at[:, pl.ds(*cols)], dst)
        if kind == QKV:
            src = slot.at[:, pl.ds(256, 256)]

            @pl.when(self.p.c == 0)
            def _():
                send(1, src, self.kv_piece(t, self.p.s, self.wk))

            @pl.when(self.p.c != 0)
            def _():
                send(1, src, self.kv_piece(t, self.p.s, self.wv))

    def spread_copy(self, i, k, ref):
        return rcopy(ref, ref, self.ag_send.at[i, k], self.ag_recv.at[i, k], self.dev(-self.step))

    def spread(self, kind, t):
        k = self.tick(kind, t)
        s = self.p.s if kind in (DOWN, OUT) else self.shard_of(t)

        def go(i, ref, wait=True):
            if wait:
                self.spread_copy(i, k, ref).wait_recv()

            @pl.when(self.pos > 0)
            def _():
                self.spread_copy(i, k, ref).start()

            rcopy(ref, ref, self.cp_send.at[i, k], self.cp_recv.at[i, k], self.p.sibling()).start()

        for i, (_, ref) in enumerate(self.pieces(kind, t, s, None)):
            go(i, ref)
        if kind == QKV:
            self.spread_copy(1, k, self.kv_piece(t, s, self.wk)).wait_recv()

            @pl.when(self.p.c == 0)
            def _():
                go(1, self.kv_piece(t, s, self.wk), False)

            @pl.when(self.p.c != 0)
            def _():
                go(1, self.kv_piece(t, s, self.wv), False)

    def drain_reduce(self, kind, t):
        k = self.tick(kind, t)

        @pl.when(self.pos < self.nz - 1)
        def _():
            self.rs_copy(kind, t, self.slot(kind, t)).wait_send()

        if kind not in (GU, QKV):
            return

        @pl.when(jnp.logical_and(self.pos == self.nz - 1, lax.rem(t, 4) != 0))
        def _():
            slot = self.slot(kind, t)
            for i, (cols, dst) in enumerate(self.pieces(kind, t, self.p.s, None)):
                src = slot.at[:, pl.ds(*cols)]
                rcopy(src, dst, self.tsend.at[i, k], self.ag_recv.at[i, k], self.p.to(1)).wait_send()
            if kind == QKV:
                src = slot.at[:, pl.ds(256, 256)]
                dst = self.kv_piece(t, self.p.s, self.wk)
                rcopy(src, dst, self.tsend.at[1, k], self.ag_recv.at[1, k], self.p.to(1)).wait_send()

    def drain_spread(self, kind, t):
        k = self.tick(kind, t)
        s = self.p.s if kind in (DOWN, OUT) else self.shard_of(t)
        refs = [ref for _, ref in self.pieces(kind, t, s, None)]
        if kind == QKV:
            refs.append(self.kv_piece(t, s, self.wk))
        for i, ref in enumerate(refs):

            @pl.when(self.pos > 0)
            def _():
                self.spread_copy(i, k, ref).wait_send()

            rcopy(ref, ref, self.cp_send.at[i, k], self.cp_recv.at[i, k], self.p.sibling()).wait()


RING = 4
CHAIN_SEMS = [DMA((N_TICKS,))] * 2 + [DMA((2, N_TICKS))] * 5


def loop(lo, hi, body):
    def step(t, _):
        body(t)
        return 0

    lax.fori_loop(lo, hi, step, 0)


SKEW, TURN = 2, 3


def between(i, lo, hi):
    return jnp.logical_and(i >= lo, i < hi)


def each(i, lo, hi, act):
    for kind, n in COUNT.items():
        base = Chain.BASE[kind]
        a, b = max(lo, base), min(hi, base + n)
        if isinstance(i, int):
            if a <= i < b:
                act(kind, i - base)
        elif a < b:

            @pl.when(between(i, a, b))
            def _():
                act(kind, i - base)


def at_tick(t, when, act):
    @pl.when(t == when)
    def _():
        act()


def all_greet(p):
    nz = lax.axis_size("z")
    greet(plane_ids(p) + [{"z": lax.rem(p.z + k, nz)} for k in range(1, nz)])


class GainSums:
    def __init__(self, p, tot, got, gz, send, recv):
        self.p, self.tot, self.got, self.gz, self.send, self.recv = p, tot, got, gz, send, recv
        self.nz = lax.axis_size("z")

    def copy(self, k):
        dev = (self.p.sibling(), self.p.to(1), self.p.to(2))[k]
        return rcopy(self.tot.at[k], self.got.at[k], self.send.at[k], self.recv.at[k], dev)

    def along(self, k):
        to = {"z": lax.rem(self.p.z + k, self.nz)}
        return rcopy(
            self.tot.at[3], self.gz.at[self.p.z], self.send.at[2 + k], self.recv.at[3 + self.p.z], to
        )

    def landed(self, k):
        src = lax.rem(self.p.z + self.nz - k, self.nz)
        ref = self.gz.at[src]
        return rcopy(ref, ref, self.send.at[2 + k], self.recv.at[3 + src], {"z": src})

    def add(self, k):
        self.copy(k).wait()
        self.tot[k + 1] = self.tot[k] + self.got[k]
        if k < 2:
            self.copy(k + 1).start()
        else:
            for j in range(1, self.nz):
                self.along(j).start()
            self.gz[self.p.z] = self.tot[3]

    def finish(self):
        for j in range(1, self.nz):
            self.along(j).wait_send()
            self.landed(j).wait_recv()
        total = self.gz[0]
        for j in range(1, self.nz):
            total = total + self.gz[j]
        return total


class Attention:
    def __init__(self, p, hbm, wo, wqkv, part, gout, gqkv, bufs, sems):
        self.p, self.hbm, self.wo, self.wqkv, self.part = p, hbm, wo, wqkv, part
        self.gout, self.gqkv = gout, gqkv
        self.bufs, self.other, self.came, self.kept, self.dq, self.rows_out = bufs[:8], *bufs[8:]
        self.sem, self.send, self.recv, self.psem = sems
        self.n = self.rows_out.shape[1]

    def load(self, i, j):
        src = self.hbm[i]
        ref = src.at[pl.ds(j * self.n, self.n)] if len(src.shape) == 2 else src.at[j]
        b = lax.rem(j, 2)
        return pltpu.make_async_copy(ref, self.bufs[i].at[b], self.sem.at[i, b])

    def fetch(self, j):
        for i in range(7):
            self.load(i, j).start()

    def swap(self, j):
        return rcopy(self.other.at[j], self.came.at[j], self.send.at[j], self.recv.at[j], self.p.sibling())

    def first(self, j):
        for i in range(7):
            self.load(i, j).wait()

        @pl.when(j < 7)
        def _():
            self.fetch(j + 1)

        b = lax.rem(j, 2)
        dhb, q, k, v, attn, probs, turn = (self.bufs[i][b] for i in range(7))
        scale = HEAD_DIM ** (-0.5)
        half = HEAD_DIM // 2
        cosine, sine = turn[:, :half], turn[:, half:]
        dattn = mm_nt(dhb, self.wo[...]).astype(BF)
        g = mm_tn(attn, dhb)
        self.gout[...] = jnp.where(j == 0, g, self.gout[...] + g)
        dp = mm_nt(dattn, v)
        dv = mm_tn(probs.astype(BF), dattn)
        ds = (probs * (dp - jnp.sum(dp * probs, axis=-1, keepdims=True))).astype(BF)
        dq = rotate(mm(ds, k) * scale, cosine, -sine)
        dk = rotate(mm_tn(ds, q) * scale, cosine, -sine)
        zero = self.p.c == 0
        self.dq[b] = dq.astype(BF)
        self.kept[b] = jnp.where(zero, dk, dv)
        self.other[j] = jnp.where(zero, dv, dk).astype(BF)
        self.swap(j).start()
        self.load(7, j).start()

    def out_copy(self, j):
        b = lax.rem(j, 2)
        return pltpu.make_async_copy(self.rows_out.at[b], self.part.at[pl.ds(j * self.n, self.n)], self.psem.at[b])

    def second(self, j):
        b = lax.rem(j, 2)
        self.swap(j).wait()
        self.load(7, j).wait()
        dkv = (self.kept[b] + self.came[j].astype(F32)).astype(BF)
        dqkv = jnp.concatenate([self.dq[b], dkv], -1)
        g = mm_tn(self.bufs[7][b], dqkv)
        self.gqkv[...] = jnp.where(j == 0, g, self.gqkv[...] + g)

        @pl.when(j >= 2)
        def _():
            self.out_copy(j - 2).wait()

        self.rows_out[b] = mm_nt(dqkv, self.wqkv[...]).astype(BF)
        self.out_copy(j).start()

    def finish(self):
        self.out_copy(6).wait()
        self.out_copy(7).wait()


def tail_kernel(
    part_ref, dpart_ref, x_hbm, h_hbm, g_hbm, gain1_ref, gain2_ref, gd_ref, ggu_ref, wo_ref, wqkv_ref,
    q_ref, k_ref, v_ref, attn_ref, probs_ref, turn_ref, xn1_ref,
    out_hbm, grad_hbm, gains_ref, dhb_ref, p1_ref, gate, up, down, out, wq, wk, wv,
    bufa, bufb, qa, qb, ringa, ringb, ring_sem, tot, got, gz, gsend, grecv,
    low, xg, hb, dh, gout, gqkv, gout_low, gqkv_low, io_sem, free_sem, *scr
):
    p = Place()
    nz = lax.axis_size("z")
    s1 = Scatter(p, part_ref, scr[:8])
    s2 = Scatter(p, dpart_ref, scr[:8])
    s3 = Scatter(p, p1_ref, scr[:8])
    ga = Gather(p, low, dhb_ref, scr[8:13])
    sums = GainSums(p, tot, got, gz, gsend, grecv)
    hbm = (dhb_ref, q_ref, k_ref, v_ref, attn_ref, probs_ref, turn_ref, xn1_ref)
    at = Attention(p, hbm, wo_ref, wqkv_ref, p1_ref, gout, gqkv, scr[13:26], scr[26:30])
    ins = (gd_ref, ggu_ref, gout_low, gqkv_low)
    outs = (gate, up, down, out, wq, wk, wv)
    n = len(CHAIN_SEMS)
    chains = [
        Chain(p, 0, ins, outs, (bufa, qa, ringa, ring_sem.at[0]), scr[30 : 30 + n]),
        Chain(p, 1, ins, outs, (bufb, qb, ringb, ring_sem.at[1]), scr[30 + n : 30 + 2 * n]),
    ]
    line = SKEW * (nz - 1)
    half = s1.half

    def io(k):
        src, dst = [(h_hbm, hb), (g_hbm, xg), (x_hbm, xg), (low, out_hbm), (low, grad_hbm)][k]
        return pltpu.make_async_copy(src, dst, io_sem.at[k])

    io(0).start()
    io(1).start()
    tot[0] = jnp.zeros_like(tot[0])
    all_greet(p)
    s1.start()

    def norm2():
        io(0).wait()
        io(1).wait()
        for h in (0, 1):
            r = pl.ds(h * half, half)
            dx = s1.total(h)
            res = hb[r]
            f = lax.rsqrt(jnp.mean(res * res, axis=1, keepdims=True) + norm_eps)
            hat = res * f
            term = jnp.sum(dx * hat, axis=0, keepdims=True)
            tot[0, 1:2] = term if h == 0 else tot[0, 1:2] + term
            d = xg[r].astype(F32) + norm_backward_step(dx * gain2_ref[...], hat, f)
            dh[r] = d
            low[r] = d.astype(BF)
        ga.start()
        io(2).start()

    def gathered():
        ga.finish()
        s1.drain()
        at.fetch(0)
        s2.start()

    def output():
        for h in (0, 1):
            r = pl.ds(h * half, half)
            low[r] = (hb[r] + s2.total(h)).astype(BF)
        io(3).start()
        s2.drain()
        for d in (p.to(1), p.to(2), p.sibling()):
            pl.semaphore_signal(free_sem, inc=1, device_id=d, device_id_type=MESH)

    def attended():
        at.finish()
        gout_low[...] = gout[...].astype(BF)
        gqkv_low[...] = gqkv[...].astype(BF)
        pl.semaphore_wait(free_sem, 3)
        s3.start()

    def norm1():
        io(2).wait()
        io(3).wait()
        for h in (0, 1):
            r = pl.ds(h * half, half)
            dx = s3.total(h)
            xf = xg[r].astype(F32)
            f = lax.rsqrt(jnp.mean(xf * xf, axis=1, keepdims=True) + norm_eps)
            hat = xf * f
            term = jnp.sum(dx * hat, axis=0, keepdims=True)
            tot[0, 0:1] = term if h == 0 else tot[0, 0:1] + term
            low[r] = (dh[r] + norm_backward_step(dx * gain1_ref[...], hat, f)).astype(BF)
        io(4).start()
        sums.copy(0).start()

    def gains():
        gains_ref[...] = sums.finish()

    def tick(t):
        for ch in chains:
            each(t + 1 - SKEW * ch.pos, 0, EARLY, ch.ahead)
            each(t, 0, N_TICKS, ch.begin)
            each(t - SKEW * ch.pos, 0, N_TICKS, ch.reduce)
        for ch in chains:
            each(t - TURN - 2 * line + SKEW * ch.pos, 0, N_TICKS, ch.spread)
        u = t // FINE
        for k in range(4):
            at_tick(t, k, functools.partial(s1.first, k))
            at_tick(t, FINE * A0 + k, functools.partial(s2.first, k))
            at_tick(t, FINE * (A0 + 9) + 1 + k, functools.partial(s3.first, k))

        @pl.when(lax.rem(t, FINE) == 0)
        def _():
            at_tick(u, 3, s1.relay)
            at_tick(u, 5, norm2)
            at_tick(u, 7, ga.relay)
            at_tick(u, A0 - 1, gathered)
            pl.when(between(u, A0 + 1, A0 + 9))(lambda: at.second(u - A0 - 1))
            pl.when(between(u, A0, A0 + 8))(lambda: at.first(u - A0))
            at_tick(u, A0 + 3, s2.relay)
            at_tick(u, A0 + 5, output)
            at_tick(u, A0 + 9, attended)
            at_tick(u, A0 + 12, s3.relay)
            at_tick(u, A0 + 14, norm1)
            for k in range(3):
                at_tick(u, A0 + 15 + k, functools.partial(sums.add, k))
            at_tick(u, A0 + 19, gains)

    loop(0, N_TICKS + TURN + 2 * line, tick)
    io(4).wait()
    s3.drain()

    def drain(i):
        for ch in chains:
            each(i, 0, N_TICKS, ch.drain_reduce)
            each(i, 0, N_TICKS, ch.drain_spread)

    loop(0, N_TICKS, drain)


A0 = 12


def tail(part, dpart, x, h, g, gain1, gain2, g_down, g_gu, wo, wqkv, heads, xn1, ff):
    rows, width = x.shape
    nz = lax.axis_size("z")
    hd, pr = HEAD_DIM, width // 4
    shapes = [(pr, ff), (pr, ff), (ff // 4, width), (pr, width), (pr, width), (pr, 1024), (pr, 1024)]
    sq = pltpu.VMEM((2, rows, hd), BF)
    wide = pltpu.VMEM((2, rows, width), BF)
    return pl.pallas_call(
        tail_kernel,
        out_shape=(
            jax.ShapeDtypeStruct((rows, width), BF),
            jax.ShapeDtypeStruct((rows, width), BF),
            jax.ShapeDtypeStruct((8, width), F32),
            jax.ShapeDtypeStruct((8 * rows, width), BF),
            jax.ShapeDtypeStruct((8 * rows, width), BF),
        )
        + tuple(jax.ShapeDtypeStruct(s, BF) for s in shapes),
        in_specs=[ANY] * 5 + [VM] * 2 + [ANY] * 2 + [VM] * 2 + [ANY] * 7,
        out_specs=(ANY, ANY, VM) + (ANY,) * 9,
        scratch_shapes=[
            pltpu.VMEM((N_TICKS - COUNT[QKV], CH, width), BF),
            pltpu.VMEM((N_TICKS - COUNT[QKV], CH, width), BF),
            pltpu.VMEM((COUNT[QKV], QR, 512), BF),
            pltpu.VMEM((COUNT[QKV], QR, 512), BF),
            pltpu.VMEM((RING, CH, width), BF),
            pltpu.VMEM((RING, CH, width), BF),
            DMA((2, RING)),
            pltpu.VMEM((4, 8, width), F32),
            pltpu.VMEM((3, 8, width), F32),
            pltpu.VMEM((nz, 8, width), F32),
            DMA((nz + 3,)),
            DMA((nz + 3,)),
            pltpu.VMEM((rows, width), BF),
            pltpu.VMEM((rows, width), BF),
            pltpu.VMEM((rows, width), F32),
            pltpu.VMEM((rows, width), F32),
            pltpu.VMEM((hd, width), F32),
            pltpu.VMEM((width, 2 * hd), F32),
            pltpu.VMEM((hd, width), BF),
            pltpu.VMEM((width, 2 * hd), BF),
            DMA((5,)),
            pltpu.SemaphoreType.REGULAR,
        ]
        + scatter_scratch(rows, width)
        + GATHER_SEMS
        + [wide, sq, sq, sq, sq]
        + [pltpu.VMEM((2, rows, rows), F32), pltpu.VMEM((2, rows, hd), F32), wide]
        + [pltpu.VMEM((8, rows, hd), BF)] * 2
        + [pltpu.VMEM((2, rows, hd), F32), sq, wide]
        + [DMA((8, 2)), DMA((8,)), DMA((8,)), DMA((2,))]
        + CHAIN_SEMS * 2,
        compiler_params=params(2, 63),
        name="tail",
    )(part, dpart, x, h, g, gain1, gain2, g_down, g_gu, wo, wqkv, *heads, xn1)


def widen_kernel(*refs):
    n = len(refs) // 2
    for a, b in zip(refs[:n], refs[n:], strict=True):
        b[...] = a[...].astype(F32)


def widen(arrays):
    steps = 8

    def spec(a):
        return pl.BlockSpec((a.shape[0] // steps, a.shape[1]), lambda i: (i, 0))

    return pl.pallas_call(
        widen_kernel,
        grid=(steps,),
        out_shape=tuple(jax.ShapeDtypeStruct(a.shape, F32) for a in arrays),
        in_specs=[spec(a) for a in arrays],
        out_specs=tuple(spec(a) for a in arrays),
        compiler_params=pltpu.CompilerParams(vmem_limit_bytes=48 * 2**20),
        name="widen",
    )(*arrays)


def pieces(
    tokens,
    segment_ids,
    attn_gain,
    w_query,
    w_key,
    w_value,
    w_out,
    mlp_gain,
    w_gate,
    w_up,
    w_down,
    cotangent,
):
    rows, width = tokens.shape[1], tokens.shape[2]
    core = lax.axis_index("core")
    nc, ns = lax.axis_size("core"), lax.axis_size("shard")
    hd = HEAD_DIM
    ff = w_gate.shape[1]
    fb = ff // (nc * ns)
    part = width // ns

    x = tokens.reshape(rows, width)
    g = cotangent.reshape(rows, width)
    wo = lax.dynamic_slice_in_dim(w_out, core * hd, hd, 0)
    gains = jnp.concatenate([attn_gain[None], mlp_gain[None], jnp.zeros((6, part), BF)], 0).astype(F32)
    seg = jnp.broadcast_to(segment_ids, (8, rows)).astype(F32)
    half = np.arange(hd // 2, dtype=np.float64) * 2.0 / hd
    freq = jnp.asarray((rope_base ** -half).astype(np.float32)[None])
    h, xn2, g_all, _, gains, _, wqkv, xn1, q, k, v, attn, probs, turn, hid, dgu, dpart, dxpart = front(
        x, seg, gains, freq, w_query, w_key, w_value, w_out, w_gate, w_up, w_down, g
    )
    gain1, gain2 = gains[:, 0].reshape(1, width), gains[:, 1].reshape(1, width)

    g_down = mm_tn(hid, g_all).astype(BF)
    g_gu = mm_tn(xn2, dgu).astype(BF)
    heads = (q, k, v, attn, probs, turn)
    output, input_grad, gain_g, _, _, gate_g, up_g, down_g, out_g, wq_g, wk_g, wv_g = tail(
        dxpart,
        dpart,
        x,
        h,
        g,
        gain1,
        gain2,
        g_down,
        g_gu,
        wo,
        wqkv,
        heads,
        xn1,
        ff,
    )
    output = output.reshape(1, rows, width)
    input_grad = input_grad.reshape(1, rows, width)
    gain_g = lax.dynamic_slice_in_dim(gain_g, lax.axis_index("shard") * part, part, 1)
    wide = widen((wq_g, wk_g, wv_g, out_g, gate_g, up_g, down_g))
    return (output, input_grad, gain_g[0], *wide[:4], gain_g[1], *wide[4:])


def contract_rows(left, right):
    return lax.dot_general(
        left, right, (((0,), (0,)), ((), ())), preferred_element_type=jnp.float32
    )


def contract_cols(left, right):
    return lax.dot_general(
        left, right, (((1,), (1,)), ((), ())), preferred_element_type=jnp.float32
    )


def scores_of(queries, keys, allowed):
    raw = jnp.einsum(
        "qgrd,kgd->grqk", queries, keys, preferred_element_type=jnp.float32
    ) * HEAD_DIM ** (-0.5)
    return jnp.where(allowed, raw, mask_fill)


def general(
    tokens,
    segment_ids,
    attn_gain,
    w_query,
    w_key,
    w_value,
    w_out,
    mlp_gain,
    w_gate,
    w_up,
    w_down,
    cotangent,
):
    rows = tokens.shape[1]
    width = tokens.shape[2]
    groups = HEADS // KV_HEADS
    q_cols = HEADS * HEAD_DIM
    kv_cols = KV_HEADS * HEAD_DIM
    layer_input_rows = tokens.reshape(rows, width).astype(jnp.float32)
    segments = segment_ids.reshape(rows)
    iota = jnp.arange(rows, dtype=jnp.int32)
    starts = jnp.sum((segments[None, :] < segments[:, None]).astype(jnp.int32), axis=1)
    positions = (iota - starts).astype(jnp.float32)
    allowed = (segments[:, None] == segments[None, :]) & (iota[:, None] >= iota[None, :])
    half = HEAD_DIM // 2
    inv_freq = rope_base ** (-(jnp.arange(half, dtype=jnp.float32) * 2.0 / HEAD_DIM))
    angles = positions[:, None] * inv_freq
    cosine = jnp.cos(angles)
    sine = jnp.sin(angles)
    first_norm_factor = lax.rsqrt(
        jnp.mean(layer_input_rows * layer_input_rows, axis=1, keepdims=True) + norm_eps
    )
    first_standardized = layer_input_rows * first_norm_factor
    gain_fragment = lax.all_gather(attn_gain, "shard", axis=0, tiled=True)
    query_piece = lax.all_gather(w_query, "shard", axis=0, tiled=True)
    key_piece = lax.all_gather(w_key, "shard", axis=0, tiled=True)
    value_piece = lax.all_gather(w_value, "shard", axis=0, tiled=True)
    normalized_rows = (first_standardized * gain_fragment.astype(jnp.float32)).astype(jnp.bfloat16)
    joined = jnp.concatenate([query_piece, key_piece, value_piece], 1)
    result = (
        jnp.dot(normalized_rows, joined, preferred_element_type=jnp.float32),
        normalized_rows,
        gain_fragment.astype(jnp.float32),
    )
    folded = result
    projected, normed_one, first_norm_gain = (folded[0], folded[1], folded[2])
    queries = rotate(
        projected[:, :q_cols].reshape(rows, KV_HEADS, groups, HEAD_DIM),
        cosine[:, None, None, :],
        sine[:, None, None, :],
    ).astype(jnp.bfloat16)
    keys = rotate(
        projected[:, q_cols : q_cols + kv_cols].reshape(rows, KV_HEADS, HEAD_DIM),
        cosine[:, None, :],
        sine[:, None, :],
    ).astype(jnp.bfloat16)
    values = projected[:, q_cols + kv_cols :].reshape(rows, KV_HEADS, HEAD_DIM).astype(jnp.bfloat16)
    scores = scores_of(queries, keys, allowed)
    top = jnp.max(scores, axis=-1, keepdims=True)
    log_total = top + jnp.log(jnp.sum(jnp.exp(scores - top), axis=-1, keepdims=True))
    probs = jnp.exp(scores - log_total)
    probs_low = probs.astype(jnp.bfloat16)
    attn = (
        jnp.einsum("grqk,kgd->qgrd", probs_low, values, preferred_element_type=jnp.float32)
        .reshape(rows, q_cols)
        .astype(jnp.bfloat16)
    )
    part = attn
    result = (
        jnp.dot(
            part,
            lax.all_gather(w_out, "shard", axis=0, tiled=True),
            preferred_element_type=jnp.float32,
        ),
    )
    folded_out = result
    residual_hidden_state = layer_input_rows + folded_out[0]
    second_norm_factor = lax.rsqrt(
        jnp.mean(residual_hidden_state * residual_hidden_state, axis=1, keepdims=True) + norm_eps
    )
    second_standardized = residual_hidden_state * second_norm_factor
    gain_fragment = lax.all_gather(mlp_gain, "shard", axis=0, tiled=True)
    gate_piece = lax.all_gather(w_gate, "shard", axis=0, tiled=True)
    up_piece = lax.all_gather(w_up, "shard", axis=0, tiled=True)
    normalized_rows = (second_standardized * gain_fragment.astype(jnp.float32)).astype(jnp.bfloat16)
    joined = jnp.concatenate([gate_piece, up_piece], 1)
    result = (
        jnp.dot(normalized_rows, joined, preferred_element_type=jnp.float32),
        normalized_rows,
        gain_fragment.astype(jnp.float32),
    )
    folded_mlp = result
    gate = folded_mlp[0][:, :FF]
    up_value = folded_mlp[0][:, FF:]
    normed_two = folded_mlp[1]
    second_norm_gain = folded_mlp[2]
    sigma = jax.nn.sigmoid(gate)
    swish = gate * sigma
    inner = (swish * up_value).astype(jnp.bfloat16)
    part = inner
    result = (
        jnp.dot(
            part,
            lax.all_gather(w_down, "shard", axis=0, tiled=True),
            preferred_element_type=jnp.float32,
        ),
    )
    output = (residual_hidden_state + result[0]).astype(jnp.bfloat16).reshape(1, rows, width)
    grad_out = cotangent.reshape(rows, width)
    grad_down = lax.psum_scatter(
        contract_rows(inner, grad_out).astype(jnp.bfloat16),
        "shard",
        scatter_dimension=0,
        tiled=True,
    )
    down_full, gate_full, up_full = (
        lax.all_gather(w_down, "shard", axis=0, tiled=True),
        lax.all_gather(w_gate, "shard", axis=0, tiled=True),
        lax.all_gather(w_up, "shard", axis=0, tiled=True),
    )
    grad_inner = contract_cols(grad_out, down_full)
    grad_gate = (grad_inner * up_value * sigma * (1.0 + gate * (1.0 - sigma))).astype(jnp.bfloat16)
    grad_up = (grad_inner * swish).astype(jnp.bfloat16)
    grad_mlp = jnp.concatenate([grad_gate, grad_up], 1)
    mlp_shards = lax.psum_scatter(
        contract_rows(normed_two, grad_mlp).astype(jnp.bfloat16),
        "shard",
        scatter_dimension=0,
        tiled=True,
    ).astype(jnp.float32)
    second_norm_gradient = contract_cols(grad_gate, gate_full) + contract_cols(grad_up, up_full)
    second_gain_products = jnp.sum(second_norm_gradient * second_standardized, axis=0)
    hidden_gradient = grad_out.astype(jnp.float32) + norm_backward_step(
        second_norm_gradient * second_norm_gain, second_standardized, second_norm_factor
    )
    grad_hidden_low = hidden_gradient.astype(jnp.bfloat16)
    grad_out_proj = lax.psum_scatter(
        contract_rows(attn, grad_hidden_low).astype(jnp.bfloat16),
        "shard",
        scatter_dimension=0,
        tiled=True,
    )
    grad_attn = contract_cols(grad_hidden_low, lax.all_gather(w_out, "shard", axis=0, tiled=True))
    grad_attn = grad_attn.astype(jnp.bfloat16).reshape(rows, KV_HEADS, groups, HEAD_DIM)
    scores_again = scores_of(queries, keys, allowed)
    probs_again = jnp.exp(scores_again - log_total)
    probs_again_low = probs_again.astype(jnp.bfloat16)
    grad_probs = jnp.einsum("qgrd,kgd->grqk", grad_attn, values, preferred_element_type=jnp.float32)
    grad_values = jnp.einsum(
        "grqk,qgrd->kgd", probs_again_low, grad_attn, preferred_element_type=jnp.float32
    )
    grad_scores = (
        probs_again * (grad_probs - jnp.sum(grad_probs * probs_again, axis=-1, keepdims=True))
    ).astype(jnp.bfloat16)
    grad_queries = jnp.einsum(
        "grqk,kgd->qgrd", grad_scores, keys, preferred_element_type=jnp.float32
    ) * HEAD_DIM ** (-0.5)
    grad_keys = jnp.einsum(
        "grqk,qgrd->kgd", grad_scores, queries, preferred_element_type=jnp.float32
    ) * HEAD_DIM ** (-0.5)
    grad_queries = rotate(grad_queries, cosine[:, None, None, :], -sine[:, None, None, :]).reshape(
        rows, q_cols
    )
    grad_keys = rotate(grad_keys, cosine[:, None, :], -sine[:, None, :]).reshape(rows, kv_cols)
    grad_joined = jnp.concatenate(
        [
            grad_queries.astype(jnp.bfloat16),
            grad_keys.astype(jnp.bfloat16),
            grad_values.reshape(rows, kv_cols).astype(jnp.bfloat16),
        ],
        1,
    )
    qkv_shards = lax.psum_scatter(
        contract_rows(normed_one, grad_joined).astype(jnp.bfloat16),
        "shard",
        scatter_dimension=0,
        tiled=True,
    ).astype(jnp.float32)
    local_qkv = jnp.concatenate([w_query, w_key, w_value], 1)
    first_norm_gradient = contract_cols(
        grad_joined, lax.all_gather(local_qkv, "shard", axis=0, tiled=True)
    )
    first_gain_products = jnp.sum(first_norm_gradient * first_standardized, axis=0)
    input_gradient_rows = hidden_gradient + norm_backward_step(
        first_norm_gradient * first_norm_gain, first_standardized, first_norm_factor
    )
    input_grad = input_gradient_rows.astype(jnp.bfloat16).reshape(1, rows, width)
    gain_one_grad, gain_two_grad = (
        lax.psum_scatter(first_gain_products, "shard", scatter_dimension=0, tiled=True),
        lax.psum_scatter(second_gain_products, "shard", scatter_dimension=0, tiled=True),
    )
    summed = (
        lax.psum(gain_one_grad.astype(jnp.bfloat16), "rep").astype(jnp.float32),
        lax.psum(qkv_shards[:, :q_cols].astype(jnp.bfloat16), "rep").astype(jnp.float32),
        lax.psum(qkv_shards[:, q_cols : q_cols + kv_cols].astype(jnp.bfloat16), "rep").astype(
            jnp.float32
        ),
        lax.psum(qkv_shards[:, q_cols + kv_cols :].astype(jnp.bfloat16), "rep").astype(jnp.float32),
        lax.psum(grad_out_proj, "rep").astype(jnp.float32),
        lax.psum(gain_two_grad.astype(jnp.bfloat16), "rep").astype(jnp.float32),
        lax.psum(mlp_shards[:, :FF].astype(jnp.bfloat16), "rep").astype(jnp.float32),
        lax.psum(mlp_shards[:, FF:].astype(jnp.bfloat16), "rep").astype(jnp.float32),
        lax.psum(grad_down, "rep").astype(jnp.float32),
    )
    return (
        output,
        input_grad,
        summed[0],
        summed[1],
        summed[2],
        summed[3],
        summed[4],
        summed[5],
        summed[6],
        summed[7],
        summed[8],
    )


def solution(mesh):
    rep, shard = mesh.devices.shape
    if shard == KV_HEADS and rep % 2 == 0:
        fine = Mesh(np.asarray(mesh.devices).reshape(rep // 2, 2, shard), ("z", "core", "shard"))
        body, every = pieces, ("z", "core", "shard")
    else:
        fine, body, every = mesh, general, ("rep", "shard")
    seqs, vec, mat = P(every, None, None), P("shard"), P("shard", None)
    in_specs = (seqs, P(every, None), vec, mat, mat, mat, mat, vec, mat, mat, mat, seqs)
    out_specs = (seqs, seqs, vec, mat, mat, mat, mat, vec, mat, mat, mat)
    return jax.shard_map(body, mesh=fine, in_specs=in_specs, out_specs=out_specs, check_vma=False)
```

```python
import functools

import jax
import jax.numpy as jnp
import numpy as np
from jax import lax
from jax.experimental import pallas as pl
from jax.experimental.pallas import tpu as pltpu
from jax.sharding import Mesh
from jax.sharding import PartitionSpec as P

HEADS = 8
KV_HEADS = 4
HEAD_DIM = 256
FF = 8192

rope_base = 1000042.0
norm_eps = 1e-06
mask_fill = -1e30

BF = jnp.bfloat16
F32 = jnp.float32
MESH = pl.DeviceIdType.MESH
ANY = pl.BlockSpec(memory_space=pl.ANY)
VM = pl.BlockSpec(memory_space=pltpu.VMEM)
DMA = pltpu.SemaphoreType.DMA


def mm(a, b):
    return jnp.dot(a, b, preferred_element_type=F32)


def mm_tn(a, b):
    return lax.dot_general(a, b, (((0,), (0,)), ((), ())), preferred_element_type=F32)


def mm_nt(a, b):
    return lax.dot_general(a, b, (((1,), (1,)), ((), ())), preferred_element_type=F32)


def rotate(values, cosine, sine):
    half = values.shape[-1] // 2
    first = values[..., :half]
    second = values[..., half:]
    return jnp.concatenate([first * cosine - second * sine, second * cosine + first * sine], -1)


def norm_backward_step(grad_hat, normalized_rows, factor):
    return factor * (
        grad_hat - normalized_rows * jnp.mean(grad_hat * normalized_rows, axis=1, keepdims=True)
    )


class Place:
    def __init__(self):
        self.z = lax.axis_index("z")
        self.c = lax.axis_index("core")
        self.s = lax.axis_index("shard")

    def shard(self, d):
        s = self.s
        if d == 0:
            return s
        if d == 1:
            return s + 1 - 2 * lax.rem(s, 2)
        if d == 2:
            return lax.rem(s + 2, 4)
        return 3 - s

    def shard_at(self, d):
        s = self.s
        one = s + 1 - 2 * lax.rem(s, 2)
        two = lax.rem(s + 2, 4)
        return jnp.where(d == 0, s, jnp.where(d == 1, one, jnp.where(d == 2, two, 3 - s)))

    def to(self, d):
        return {"shard": self.shard(d)}

    def sibling(self):
        return {"core": 1 - self.c}


def greet(ids):
    barrier = pltpu.get_barrier_semaphore()
    for d in ids:
        pl.semaphore_signal(barrier, inc=1, device_id=d, device_id_type=MESH)
    pl.semaphore_wait(barrier, len(ids))


def rcopy(src, dst, send, recv, dev):
    return pltpu.make_async_remote_copy(
        src_ref=src, dst_ref=dst, send_sem=send, recv_sem=recv, device_id=dev, device_id_type=MESH
    )


GATHER_SEMS = [DMA((6,)), DMA((6,)), DMA((7,)), DMA((7,)), DMA((1,))]


class Gather:
    def __init__(self, p, src, out, sems):
        self.p, self.src, self.out = p, src, out
        self.send, self.recv, self.csend, self.crecv, self.lsem = sems
        self.rows = src.shape[0]
        self.half = self.rows // 2

    def at(self, d, h, core=None):
        core = self.p.c if core is None else core
        row = (core * 4 + self.p.shard(d)) * self.rows
        if h is None:
            return self.out.at[pl.ds(row, self.rows)]
        return self.out.at[pl.ds(row + h * self.half, self.half)]

    def move(self, k):
        d, h, to = [(0, 0, 1), (0, 1, 2), (0, 1, 1), (0, 0, 2), (1, 0, 2), (2, 1, 1)][k]
        dst = self.at(d, h)
        src = self.src.at[pl.ds(h * self.half, self.half)] if d == 0 else dst
        return rcopy(src, dst, self.send.at[k], self.recv.at[k], self.p.to(to))

    def landed(self, k):
        d, h = [(1, 0), (2, 1), (1, 1), (2, 0), (3, 0), (3, 1)][k]
        return self.at(d, h)

    def pass_on(self, k):
        here = self.src if k == 6 else self.landed(k)
        there = self.at(0, None) if k == 6 else self.landed(k)
        return rcopy(here, there, self.csend.at[k], self.crecv.at[k], self.p.sibling())

    def arrived(self, k):
        ref = self.landed(k)
        rcopy(ref, ref, self.send.at[k], self.recv.at[k], self.p.to(1)).wait_recv()
        self.pass_on(k).start()

    def start(self):
        for k in range(4):
            self.move(k).start()
        self.pass_on(6).start()
        pltpu.make_async_copy(self.src, self.at(0, None), self.lsem.at[0]).start()

    def relay(self):
        for k in (0, 1):
            self.arrived(k)
            self.move(4 + k).start()

    def early(self):
        for k in (2, 3):
            self.arrived(k)

    def late(self):
        for k in (4, 5):
            self.arrived(k)

    def both(self, ks):
        for k in ks:
            self.pass_on(k).wait_recv()

    def home(self):
        self.both((6,))
        pltpu.make_async_copy(self.src, self.at(0, None), self.lsem.at[0]).wait()

    def close(self):
        for k in range(6):
            self.move(k).wait_send()
        for k in range(7):
            self.pass_on(k).wait_send()

    def finish(self, early=False):
        if not early:
            self.early()
        self.late()
        self.both(range(7))
        pltpu.make_async_copy(self.src, self.at(0, None), self.lsem.at[0]).wait()
        self.close()


SCATTER_SEMS = [DMA((4,)), DMA((4,)), DMA((4,)), DMA((6,)), DMA((6,))]
ORDER = (3, 1, 2, 0)


def scatter_scratch(rows, width):
    half = rows // 2
    return [
        pltpu.VMEM((4, rows, width), BF),
        pltpu.VMEM((4, rows, width), BF),
        pltpu.VMEM((6, half, width), BF),
    ] + SCATTER_SEMS


class Scatter:
    def __init__(self, p, part, scratch):
        self.p, self.part = p, part
        self.own, self.got, self.slot, self.lsem, self.csend, self.crecv, self.send, self.recv = scratch
        self.rows = self.own.shape[1]
        self.half = self.rows // 2

    def block(self, core, d):
        return self.part.at[pl.ds((core * 4 + self.p.shard(d)) * self.rows, self.rows)]

    def local(self, d):
        return pltpu.make_async_copy(self.block(self.p.c, d), self.own.at[d], self.lsem.at[d])

    def swap(self, d):
        src = self.block(1 - self.p.c, d)
        return rcopy(src, self.got.at[d], self.csend.at[d], self.crecv.at[d], self.p.sibling())

    def rowsof(self, h):
        return pl.ds(h * self.half, self.half)

    def move(self, k):
        d, h, to = [(3, 0, 1), (3, 1, 2), (1, 0, 1), (2, 1, 2), (2, 0, 2), (1, 1, 1)][k]
        return rcopy(
            self.own.at[d, self.rowsof(h)], self.slot.at[k], self.send.at[k], self.recv.at[k], self.p.to(to)
        )

    def start(self):
        for d in ORDER:
            self.swap(d).start()
            self.local(d).start()

    def pair(self, d):
        self.swap(d).wait_recv()
        self.local(d).wait()
        self.own[d] = (self.own[d].astype(F32) + self.got[d].astype(F32)).astype(BF)

    def first(self, k):
        self.pair(ORDER[k])
        for m in ((0, 1), (2,), (3,), ())[k]:
            self.move(m).start()

    def relay(self):
        for k, d, h in ((0, 2, 0), (1, 1, 1)):
            self.move(k).wait_recv()
            r = self.rowsof(h)
            self.own[d, r] = (self.own[d, r].astype(F32) + self.slot[k].astype(F32)).astype(BF)
            self.move(4 + k).start()

    def total(self, h):
        near, far = (2, 4) if h == 0 else (3, 5)
        self.move(near).wait_recv()
        self.move(far).wait_recv()
        return (
            self.own[0, self.rowsof(h)].astype(F32)
            + self.slot[near].astype(F32)
            + self.slot[far].astype(F32)
        )

    def drain(self):
        for k in range(6):
            self.move(k).wait_send()
        for d in range(4):
            self.swap(d).wait_send()


def params(cid, mb):
    return pltpu.CompilerParams(
        collective_id=cid, has_side_effects=True, vmem_limit_bytes=mb * 2**20
    )


def plane_ids(p):
    return [p.to(1), p.to(2), p.to(3), p.sibling()]


class Columns:
    def __init__(self, p, sems):
        self.p = p
        self.send, self.recv, self.lsem = sems

    def cols(self, j, d, src, width):
        return src.at[:, pl.ds(pl.multiple_of(j * width, width), width)]

    def copy(self, k, d, src, dst):
        if d == 0:
            return pltpu.make_async_copy(src, dst, self.lsem.at[k])
        return rcopy(src, dst, self.send.at[k, d - 1], self.recv.at[k, d - 1], self.p.to(d))


def rows_at(ref, r, n, c0, width):
    return ref.at[pl.ds(r, n), pl.ds(c0, width)]


def greet_line(p, ids):
    barrier = pltpu.get_barrier_semaphore()
    nz = lax.axis_size("z")
    for d in ids:
        pl.semaphore_signal(barrier, inc=1, device_id=d, device_id_type=MESH)

    @pl.when(p.z > 0)
    def _():
        pl.semaphore_signal(barrier, inc=1, device_id={"z": p.z - 1}, device_id_type=MESH)

    @pl.when(p.z < nz - 1)
    def _():
        pl.semaphore_signal(barrier, inc=1, device_id={"z": p.z + 1}, device_id_type=MESH)

    ends = jnp.where(p.z == 0, 1, 0) + jnp.where(p.z == nz - 1, 1, 0)
    pl.semaphore_wait(barrier, len(ids) + 2 - ends)


def relay_sems(nz):
    return [DMA((3,)), DMA((3,)), DMA((1,)), DMA((2, nz, 3)), DMA((nz, 3))]


class Relay:
    def __init__(self, p, w, dst, c0, sems):
        self.p, self.w, self.dst, self.c0 = p, w, dst, c0
        self.xs, self.xr, self.ls, self.zs, self.zr = sems
        self.nz = lax.axis_size("z")
        self.part = w.shape[0]
        self.n = self.part // self.nz
        self.fb = w.shape[1] // 8

    def cols(self, d):
        return pl.ds(pl.multiple_of((self.p.shard(d) * 2 + self.p.c) * self.fb, self.fb), self.fb)

    def rows(self, d, q):
        return self.dst.at[pl.ds(self.p.shard(d) * self.part + q * self.n, self.n), pl.ds(self.c0, self.fb)]

    def fetch(self, d):
        src = self.w.at[pl.ds(self.p.z * self.n, self.n), self.cols(d)]
        return rcopy(src, self.rows(0, self.p.z), self.xs.at[d - 1], self.xr.at[d - 1], self.p.to(d))

    def local(self):
        dst = self.dst.at[pl.ds(self.p.s * self.part, self.part), pl.ds(self.c0, self.fb)]
        return pltpu.make_async_copy(self.w.at[:, self.cols(0)], dst, self.ls.at[0])

    def along(self, way, q, d):
        ref = self.rows(d, q)
        to = {"z": self.p.z + (1 if way else -1)}
        return rcopy(ref, ref, self.zs.at[way, q, d - 1], self.zr.at[q, d - 1], to)

    def start(self):
        for d in (3, 1, 2):
            self.fetch(d).start()
        self.local().start()

    def can(self, way):
        return self.p.z < self.nz - 1 if way else self.p.z > 0

    def own(self):
        for d in (1, 2, 3):
            self.fetch(d).wait_recv()
        for way in (0, 1):

            @pl.when(self.can(way))
            def _():
                for d in (1, 2, 3):
                    self.along(way, self.p.z, d).start()

    def hop(self, k):
        for way in (0, 1):
            q = self.p.z - k if way else self.p.z + k
            there = q >= 0 if way else q < self.nz

            @pl.when(there)
            def _():
                for d in (1, 2, 3):
                    self.along(way, q, d).wait_recv()

            @pl.when(jnp.logical_and(there, self.can(way)))
            def _():
                for d in (1, 2, 3):
                    self.along(way, q, d).start()

    def finish(self):
        for d in (1, 2, 3):
            self.fetch(d).wait_send()
        for k in range(self.nz):
            for way in (0, 1):
                q = self.p.z - k if way else self.p.z + k
                there = q >= 0 if way else q < self.nz

                @pl.when(jnp.logical_and(there, self.can(way)))
                def _():
                    for d in (1, 2, 3):
                        self.along(way, q, d).wait_send()


class Forward:
    def __init__(self, p, xa, xn1, wqkv, wo, seg, gain, freq, sc, ob, bufs, sems):
        self.p, self.xa, self.xn1 = p, xa, xn1
        self.wqkv, self.wo, self.seg, self.gain, self.freq = wqkv, wo, seg, gain, freq
        self.sc, self.ob = sc, ob
        self.xb, self.nb, self.q, self.k, self.v, self.attn, self.probs, self.turn, self.kept, self.came = bufs
        self.xsem, self.nsem, self.send, self.recv = sems
        self.n = self.xb.shape[1]

    def block(self, i):
        return lax.rem(i, 2) * 4 + self.p.shard_at(i // 2)

    def rows(self, ref, i):
        return ref.at[pl.ds(self.block(i) * self.n, self.n)]

    def load(self, i):
        b = lax.rem(i, 2)
        return pltpu.make_async_copy(self.rows(self.xa, i), self.xb.at[b], self.xsem.at[b])

    def store(self, i):
        b = lax.rem(i, 2)
        return pltpu.make_async_copy(self.nb.at[b], self.rows(self.xn1, i), self.nsem.at[b])

    def swap(self, i):
        return rcopy(self.kept.at[i], self.came.at[i], self.send.at[i], self.recv.at[i], self.p.sibling())

    def seg_of(self, i):
        row = self.seg[self.block(i)]
        return row[0:1], row.T[:, 0:1]

    def first(self, i):
        b, k = lax.rem(i, 2), self.block(i)
        self.load(i).wait()

        @pl.when(i >= 2)
        def _():
            self.store(i - 2).wait()

        x = self.xb[b].astype(F32)
        f = lax.rsqrt(jnp.mean(x * x, axis=1, keepdims=True) + norm_eps)
        xn = (x * f * self.gain).astype(BF)
        self.nb[b] = xn
        self.store(i).start()
        lin = mm(xn, self.wqkv[...])
        row, col = self.seg_of(i)
        start = jnp.sum((row < col).astype(F32), axis=1, keepdims=True)
        at = lax.broadcasted_iota(jnp.int32, (self.n, 1), 0).astype(F32)
        angle = (at - start) * self.freq
        cosine, sine = jnp.cos(angle), jnp.sin(angle)
        self.turn[k] = jnp.concatenate([cosine, sine], -1)
        hd = HEAD_DIM
        self.q[k] = rotate(lin[:, :hd], cosine, sine).astype(BF)
        kv = lin[:, hd:]
        self.kept[i] = jnp.where(self.p.c == 0, rotate(kv, cosine, sine), kv).astype(BF)
        self.swap(i).start()

    def second(self, i):
        n, k = self.n, self.block(i)
        self.swap(i).wait()
        mine, came = self.kept[i], self.came[i]
        key = jnp.where(self.p.c == 0, mine, came)
        value = jnp.where(self.p.c == 0, came, mine)
        self.k[k], self.v[k] = key, value
        row, col = self.seg_of(i)
        down = lax.broadcasted_iota(jnp.int32, (n, n), 0)
        over = lax.broadcasted_iota(jnp.int32, (n, n), 1)
        allowed = jnp.logical_and(row == col, down >= over)
        scores = jnp.where(allowed, mm_nt(self.q[k], key) * HEAD_DIM ** (-0.5), mask_fill)
        ex = jnp.exp(scores - jnp.max(scores, axis=-1, keepdims=True))
        probs = ex / jnp.sum(ex, axis=-1, keepdims=True)
        self.probs[k] = probs
        attn = mm(probs.astype(BF), value).astype(BF)
        self.attn[k] = attn
        term = mm(attn, self.wo[...]).astype(BF)
        d = i // 2
        mine_too = lax.rem(i, 2) == self.p.c

        @pl.when(mine_too)
        def _():
            self.sc.own[d] = term

        @pl.when(jnp.logical_not(mine_too))
        def _():
            self.ob[d] = term
            self.sc.swap(d).start()

    def finish(self):
        self.store(6).wait()
        self.store(7).wait()


class MadeScatter(Scatter):
    def __init__(self, p, made, scratch):
        super().__init__(p, None, scratch)
        self.made = made

    def swap(self, d):
        return rcopy(self.made.at[d], self.got.at[d], self.csend.at[d], self.crecv.at[d], self.p.sibling())

    def pair(self, d):
        self.swap(d).wait_recv()
        self.own[d] = (self.own[d].astype(F32) + self.got[d].astype(F32)).astype(BF)


class Feed:
    def __init__(self, p, block, xn2, g, wgu, wd, outs, bufs, sems):
        self.p, self.block = p, block
        self.xn2, self.g, self.wgu, self.wd, self.outs = xn2, g, wgu, wd, outs
        self.xb, self.gb, self.made, self.got = bufs
        self.xsem, self.gsem, self.osem = sems
        self.n = self.xb.shape[1]
        self.fb = wd.shape[0]

    def rows(self, ref, i):
        return ref.at[pl.ds(self.block(i) * self.n, self.n)]

    def loads(self, i):
        b = lax.rem(i, 2)
        return [
            pltpu.make_async_copy(self.rows(self.xn2, i), self.xb.at[b], self.xsem.at[b]),
            pltpu.make_async_copy(self.rows(self.g, i), self.gb.at[b], self.gsem.at[b]),
        ]

    def stores(self, i):
        b = lax.rem(i, 2)
        srcs = (self.got.at[2 + b, :, pl.ds(0, self.fb)], self.made.at[b], self.made.at[2 + b], self.got.at[b])
        return [
            pltpu.make_async_copy(src, self.rows(out, i), self.osem.at[j, b])
            for j, (src, out) in enumerate(zip(srcs, self.outs, strict=True))
        ]

    def step(self, i):
        b, fb = lax.rem(i, 2), self.fb
        for cp in self.loads(i):
            cp.wait()

        @pl.when(i >= 2)
        def _():
            for cp in self.stores(i - 2):
                cp.wait()

        xn, g = self.xb[b], self.gb[b]
        gate, up = mm(xn, self.wgu[:, :fb]), mm(xn, self.wgu[:, fb:])
        sigma = jax.nn.sigmoid(gate)
        swish = gate * sigma
        hid = (swish * up).astype(BF)
        self.got[2 + b, :, :fb] = hid
        dhid = mm_nt(g, self.wd[...])
        dgate = (dhid * up * sigma * (1.0 + gate * (1.0 - sigma))).astype(BF)
        dup = (dhid * swish).astype(BF)
        self.made[b, :, :fb] = dgate
        self.made[b, :, fb:] = dup
        self.made[2 + b] = mm(hid, self.wd[...]).astype(BF)
        self.got[b] = mm_nt(self.made[b], self.wgu[...]).astype(BF)
        for cp in self.stores(i):
            cp.start()

    def finish(self):
        for i in (6, 7):
            for cp in self.stores(i):
                cp.wait()


def front_kernel(
    x_ref, seg_ref, gain_ref, freq_ref, wq_ref, wk_ref, wv_ref, wo_hbm, wg_ref, wu_ref, wd_hbm, g_ref,
    h_ref, xn2_ref, ga_ref, wgu_ref, gains_ref, xa_ref, wqkv_ref, xn1_ref, q_ref, k_ref, v_ref,
    attn_ref, probs_ref, turn_ref, hid_ref, dgu_ref, dpart_ref, dx_ref, *scr
):
    p = Place()
    nz = lax.axis_size("z")
    others = [(0, 1)] + [(d, o) for d in (1, 2, 3) for o in (0, 1)]

    def dev(d, o):
        return {"core": 1 - p.c if o else p.c, "shard": p.shard(d)}

    scr = list(scr)

    def take(n):
        out = scr[:n]
        del scr[:n]
        return out

    ga = Gather(p, x_ref, xa_ref, take(5))
    gg = Gather(p, g_ref, ga_ref, take(5))
    [xnb] = take(1)
    gx = Gather(p, xnb, xn2_ref, take(5))
    co = Columns(p, take(3))
    tsend, trecv, tlocal = take(3)
    fb = wgu_ref.shape[1] // 2
    re = [Relay(p, wg_ref, wgu_ref, 0, take(5)), Relay(p, wu_ref, wgu_ref, fb, take(5))]
    [made] = take(1)
    sc = MadeScatter(p, made, take(8))
    wqkv, wo, seg, gaina_ref, lsem = take(5)
    bufs, sems = take(10), take(4)
    [osem] = take(1)
    wgu, wd, gsem, fsem = take(4)
    part, hd = wq_ref.shape[0], HEAD_DIM

    load_wo = pltpu.make_async_copy(wo_hbm.at[pl.ds(p.c * hd, hd)], wo, lsem.at[0])
    load_wqkv = pltpu.make_async_copy(wqkv_ref, wqkv, lsem.at[1])
    load_wd = pltpu.make_async_copy(wd_hbm.at[pl.ds(p.c * fb, fb)], wd, lsem.at[2])
    load_wgu = pltpu.make_async_copy(wgu_ref, wgu, lsem.at[3])
    load_wo.start()
    load_wd.start()
    greet_line(p, [dev(d, o) for d, o in others])

    def q_copy(d):
        src = co.cols(p.shard(d) * 2 + p.c, d, wq_ref, hd)
        return co.copy(0, d, src, rows_at(wqkv_ref, p.s * part, part, 0, hd))

    def kv_copy(d, w):
        src = co.cols(p.shard(d), d, w, hd)
        return co.copy(1, d, src, rows_at(wqkv_ref, p.s * part, part, hd, hd))

    def small(k):
        d, o = others[k]
        yield rcopy(seg_ref, seg.at[p.c * 4 + p.s], tsend.at[k], trecv.at[k], dev(d, o))
        if d and not o:
            yield rcopy(gain_ref, gaina_ref.at[p.s], tsend.at[7 + d - 1], trecv.at[7 + d - 1], dev(d, o))

    smalls = [cp for k in range(7) for cp in small(k)] + [
        pltpu.make_async_copy(seg_ref, seg.at[p.c * 4 + p.s], tlocal.at[0]),
        pltpu.make_async_copy(gain_ref, gaina_ref.at[p.s], tlocal.at[1]),
    ]
    for cp in smalls:
        cp.start()
    for d in (3, 1, 2, 0):
        q_copy(d).start()

        @pl.when(p.c == 0)
        def _():
            kv_copy(d, wk_ref).start()

        @pl.when(p.c != 0)
        def _():
            kv_copy(d, wv_ref).start()

    ga.start()
    for cp in smalls:
        cp.wait()
    ga.relay()
    re[0].start()
    for d in (3, 1, 2, 0):
        q_copy(d).wait()
        kv_copy(d, wk_ref).wait()
    load_wqkv.start()
    ga.home()
    load_wo.wait()
    load_wqkv.wait()
    gain1 = jnp.concatenate([gaina_ref[j, 0:1] for j in range(4)], -1)
    gain2 = jnp.concatenate([gaina_ref[j, 1:2] for j in range(4)], -1)
    gains_ref[0:1], gains_ref[1:2] = gain1, gain2
    fw = Forward(p, xa_ref, xn1_ref, wqkv, wo, seg, gain1, freq_ref[...], sc, made, bufs, sems)

    def pair(d):
        sc.pair(d)
        if d == 3:
            sc.move(0).start()
            sc.move(1).start()
        elif d:
            sc.move(1 + d).start()

    def step(i):
        at_tick(i, 1, ga.early)
        at_tick(i, 1, re[1].start)
        at_tick(i, 2, lambda: ga.both((0, 2)))
        at_tick(i, 3, re[0].own)
        at_tick(i, 4, lambda: ga.both((1, 3)))
        at_tick(i, 4, re[1].own)
        at_tick(i, 5, ga.late)
        at_tick(i, 5, gg.start)
        at_tick(i, 6, lambda: ga.both((4, 5)))
        at_tick(i, 6, lambda: re[0].hop(1))
        at_tick(i, 8, lambda: re[1].hop(1))

        @pl.when(jnp.logical_and(lax.rem(i, 2) == 0, i < 8))
        def _():
            fw.load(i).start()
            fw.load(i + 1).start()

        pl.when(i < 8)(lambda: fw.first(i))
        pl.when(i > 0)(lambda: fw.second(i - 1))
        for d in range(4):
            at_tick(i, 2 * d + 2, functools.partial(pair, d))

    loop(0, 9, step)
    saved = [
        pltpu.make_async_copy(a, b, osem.at[j])
        for j, (a, b) in enumerate(
            zip(bufs[2:8], (q_ref, k_ref, v_ref, attn_ref, probs_ref, turn_ref), strict=True)
        )
    ]
    for cp in saved:
        cp.start()
    gg.relay()
    for k in range(2, nz - 1):
        re[0].hop(k)
    sc.relay()
    half = sc.half
    for h in (0, 1):
        r = pl.ds(h * half, half)
        res = x_ref[r].astype(F32) + sc.total(h)
        h_ref[r] = res
        f = lax.rsqrt(jnp.mean(res * res, axis=1, keepdims=True) + norm_eps)
        xnb[r] = (res * f * gain2).astype(BF)
    gx.start()
    for k in range(2, nz - 1):
        re[1].hop(k)
    re[0].hop(nz - 1)
    gg.early()
    gg.late()
    re[1].hop(nz - 1)
    for r in re:
        r.local().wait()
    load_wgu.start()
    fw.finish()
    sc.drain()
    load_wd.wait()
    gg.home()
    gx.home()
    gx.relay()
    load_wgu.wait()
    fd = Feed(
        p, fw.block, xn2_ref, ga_ref, wgu, wd, (hid_ref, dgu_ref, dpart_ref, dx_ref),
        (bufs[0], bufs[1], made, sc.got), (sems[0], gsem, fsem),
    )

    def feed(i):
        for ks, when in (((0, 2), 2), ((1, 3), 4), ((4, 5), 6)):
            at_tick(i, when, lambda ks=ks: (gx.both(ks), gg.both(ks)))

        @pl.when(lax.rem(i, 2) == 0)
        def _():
            for cp in fd.loads(i) + fd.loads(i + 1):
                cp.start()

        fd.step(i)
        at_tick(i, 1, gx.early)
        at_tick(i, 4, gx.late)

    loop(0, 8, feed)
    fd.finish()
    for gather in (ga, gg, gx):
        gather.close()
    for r in re:
        r.finish()
    for cp in saved:
        cp.wait()


def front(x, seg, gains, freq, wq, wk, wv, wo, wg, wu, wd, g):
    rows, width = x.shape
    hd = HEAD_DIM
    fb = wg.shape[1] // 8
    nz = lax.axis_size("z")
    every = jax.ShapeDtypeStruct((8 * rows, width), BF)
    head = jax.ShapeDtypeStruct((8, rows, hd), BF)
    keep = pltpu.VMEM((8, rows, hd), BF)
    wide = pltpu.VMEM((2, rows, width), BF)
    return pl.pallas_call(
        front_kernel,
        out_shape=(
            jax.ShapeDtypeStruct((rows, width), F32),
            every,
            every,
            jax.ShapeDtypeStruct((width, wg.shape[1] // 4), BF),
            jax.ShapeDtypeStruct((2, width), F32),
            every,
            jax.ShapeDtypeStruct((width, 2 * hd), BF),
            every,
            head,
            head,
            head,
            head,
            jax.ShapeDtypeStruct((8, rows, rows), F32),
            jax.ShapeDtypeStruct((8, rows, hd), F32),
            jax.ShapeDtypeStruct((8 * rows, fb), BF),
            jax.ShapeDtypeStruct((8 * rows, 2 * fb), BF),
            every,
            every,
        ),
        in_specs=[VM] * 4 + [ANY] * 7 + [VM],
        out_specs=(VM, ANY, ANY, ANY, VM) + (ANY,) * 13,
        scratch_shapes=GATHER_SEMS * 2
        + [pltpu.VMEM((rows, width), BF)]
        + GATHER_SEMS
        + [DMA((2, 3)), DMA((2, 3)), DMA((2,)), DMA((10,)), DMA((10,)), DMA((2,))]
        + relay_sems(nz) * 2
        + [pltpu.VMEM((4, rows, width), BF)]
        + scatter_scratch(rows, width)
        + [
            pltpu.VMEM((width, 2 * hd), BF),
            pltpu.VMEM((hd, width), BF),
            pltpu.VMEM((8, 8, rows), F32),
            pltpu.VMEM((4, *gains.shape), F32),
            DMA((4,)),
        ]
        + [wide, wide, keep, keep, keep, keep]
        + [pltpu.VMEM((8, rows, rows), F32), pltpu.VMEM((8, rows, hd), F32), keep, keep]
        + [DMA((2,)), DMA((2,)), DMA((8,)), DMA((8,)), DMA((6,))]
        + [pltpu.VMEM((width, 2 * fb), BF), pltpu.VMEM((fb, width), BF), DMA((2,)), DMA((4, 2))],
        compiler_params=params(0, 63),
        name="front",
    )(x, seg, gains, freq, wq, wk, wv, wo, wg, wu, wd, g)


CH = 32
QR = 4 * CH
FINE = 64 // CH
DOWN, GU, OUT, QKV = range(4)
COUNT = {DOWN: 512 // CH, GU: 1024 // CH, OUT: 128 // CH, QKV: 1024 // QR}
N_TICKS = sum(COUNT.values())
EARLY = COUNT[DOWN] + COUNT[GU]
GJ = COUNT[GU] // 4
SLOTS, N_SLOTTED = 12, EARLY + COUNT[OUT]


class Chain:
    def __init__(self, p, h, ins, outs, bufs, sems):
        self.p, self.h = p, h
        self.ins = ins
        self.gate, self.up, self.down, self.out, self.wq, self.wk, self.wv = outs
        self.buf, self.bufq, self.ring, self.ring_sem, self.credit = bufs
        self.rs_send, self.rs_recv, self.ag_send, self.ag_recv, self.cp_send, self.cp_recv, self.tsend = sems
        nz = lax.axis_size("z")
        self.nz = nz
        self.pos = nz - 1 - p.z if h == 0 else p.z
        self.step = -1 if h == 0 else 1

    def dev(self, by):
        return {"z": self.p.z + by}

    BASE = {DOWN: 0, GU: COUNT[DOWN], OUT: EARLY, QKV: EARLY + COUNT[OUT]}

    def tick(self, kind, t):
        return self.BASE[kind] + t

    def dist(self, kind, t):
        return t // GJ if kind == GU else lax.rem(t, 4)

    def row(self, kind, t):
        return lax.rem(t, GJ) * CH if kind == GU else (t // 4) * QR

    def shard_of(self, kind, t):
        return self.p.shard_at(self.dist(kind, t))

    def mine(self, kind, t):
        h = self.h
        if kind == DOWN:
            return self.ins[DOWN].at[pl.ds(h * 512 + t * CH, CH)]
        if kind == OUT:
            return self.ins[OUT].at[pl.ds(h * 128 + t * CH, CH)]
        row = self.shard_of(kind, t) * 512 + h * 256 + self.row(kind, t)
        return self.ins[kind].at[pl.ds(row, QR if kind == QKV else CH)]

    def fetch(self, kind, t):
        r = lax.rem(self.tick(kind, t), RING)
        return pltpu.make_async_copy(self.mine(kind, t), self.ring.at[r], self.ring_sem.at[r])

    def ahead(self, kind, t):
        @pl.when(self.pos > 0)
        def _():
            self.fetch(kind, t).start()

    def slot(self, kind, t):
        return self.bufq.at[t] if kind == QKV else self.buf.at[lax.rem(self.tick(kind, t), SLOTS)]

    def may_send(self, kind, t):
        if kind != QKV:

            @pl.when(self.tick(kind, t) >= SLOTS)
            def _():
                pl.semaphore_wait(self.credit, 1)

    def retire(self, kind, t):
        self.gone(kind, t)
        if kind != QKV:

            @pl.when(jnp.logical_and(self.pos > 0, self.tick(kind, t) < N_SLOTTED - SLOTS))
            def _():
                pl.semaphore_signal(self.credit, inc=1, device_id=self.dev(-self.step), device_id_type=MESH)

    def rs_copy(self, kind, t, src):
        k = self.tick(kind, t)
        return rcopy(
            src, self.slot(kind, t), self.rs_send.at[k], self.rs_recv.at[k], self.dev(self.step)
        )

    def begin(self, kind, t):
        @pl.when(self.pos == 0)
        def _():
            self.may_send(kind, t)
            self.rs_copy(kind, t, self.mine(kind, t)).start()

    def reduce(self, kind, t):
        first, last = self.pos == 0, self.pos == self.nz - 1

        @pl.when(jnp.logical_not(first))
        def _():
            slot = self.slot(kind, t)
            if kind in (DOWN, GU):
                self.fetch(kind, t).wait()
                own = self.ring.at[lax.rem(self.tick(kind, t), RING)]
            else:
                own = self.mine(kind, t)
            self.rs_copy(kind, t, slot).wait_recv()
            slot[...] = (slot[...].astype(F32) + own[...].astype(F32)).astype(BF)

        @pl.when(jnp.logical_and(jnp.logical_not(first), jnp.logical_not(last)))
        def _():
            self.may_send(kind, t)
            self.rs_copy(kind, t, self.slot(kind, t)).start()

        @pl.when(last)
        def _():
            self.turn(kind, t)

    def pieces(self, kind, t, s, d_shard):
        h, c = self.h, self.p.c
        if kind == DOWN:
            return [(None, self.down.at[pl.ds(c * 1024 + h * 512 + t * CH, CH)])]
        if kind == OUT:
            return [(None, self.out.at[pl.ds(c * 256 + h * 128 + t * CH, CH)])]
        if kind == GU:
            r = h * 256 + self.row(kind, t)
            c0 = pl.multiple_of((s * 2 + c) * 1024, 1024)
            return [
                ((0, 1024), self.gate.at[pl.ds(r, CH), pl.ds(c0, 1024)]),
                ((1024, 1024), self.up.at[pl.ds(r, CH), pl.ds(c0, 1024)]),
            ]
        r = h * 256 + (t // 4) * QR
        cq = pl.multiple_of((s * 2 + c) * 256, 256)
        return [((0, 256), self.wq.at[pl.ds(r, QR), pl.ds(cq, 256)])]

    def kv_piece(self, t, s, w):
        r = self.h * 256 + (t // 4) * QR
        return w.at[pl.ds(r, QR), pl.ds(pl.multiple_of(s * 256, 256), 256)]

    def turn(self, kind, t):
        slot = self.slot(kind, t)
        k = self.tick(kind, t)
        to = self.p.s if kind in (DOWN, OUT) else self.shard_of(kind, t)

        def send(i, src, dst):
            if kind in (DOWN, OUT):
                pltpu.make_async_copy(src, dst, self.ag_recv.at[i, k]).start()
                return

            @pl.when(self.dist(kind, t) == 0)
            def _():
                pltpu.make_async_copy(src, dst, self.ag_recv.at[i, k]).start()

            @pl.when(self.dist(kind, t) != 0)
            def _():
                rcopy(src, dst, self.tsend.at[i, k], self.ag_recv.at[i, k], {"shard": to}).start()

        for i, (cols, dst) in enumerate(self.pieces(kind, t, self.p.s, to)):
            send(i, slot if cols is None else slot.at[:, pl.ds(*cols)], dst)
        if kind == QKV:
            src = slot.at[:, pl.ds(256, 256)]

            @pl.when(self.p.c == 0)
            def _():
                send(1, src, self.kv_piece(t, self.p.s, self.wk))

            @pl.when(self.p.c != 0)
            def _():
                send(1, src, self.kv_piece(t, self.p.s, self.wv))

    def spread_copy(self, i, k, ref):
        return rcopy(ref, ref, self.ag_send.at[i, k], self.ag_recv.at[i, k], self.dev(-self.step))

    def spread(self, kind, t):
        k = self.tick(kind, t)
        s = self.p.s if kind in (DOWN, OUT) else self.shard_of(kind, t)

        def go(i, ref, wait=True):
            if wait:
                self.spread_copy(i, k, ref).wait_recv()

            @pl.when(self.pos > 0)
            def _():
                self.spread_copy(i, k, ref).start()

            rcopy(ref, ref, self.cp_send.at[i, k], self.cp_recv.at[i, k], self.p.sibling()).start()

        for i, (_, ref) in enumerate(self.pieces(kind, t, s, None)):
            go(i, ref)
        if kind == QKV:
            self.spread_copy(1, k, self.kv_piece(t, s, self.wk)).wait_recv()

            @pl.when(self.p.c == 0)
            def _():
                go(1, self.kv_piece(t, s, self.wk), False)

            @pl.when(self.p.c != 0)
            def _():
                go(1, self.kv_piece(t, s, self.wv), False)

    def gone(self, kind, t):
        k = self.tick(kind, t)

        @pl.when(self.pos < self.nz - 1)
        def _():
            self.rs_copy(kind, t, self.slot(kind, t)).wait_send()

        if kind not in (GU, QKV):
            return

        @pl.when(jnp.logical_and(self.pos == self.nz - 1, self.dist(kind, t) != 0))
        def _():
            slot = self.slot(kind, t)
            for i, (cols, dst) in enumerate(self.pieces(kind, t, self.p.s, None)):
                src = slot.at[:, pl.ds(*cols)]
                rcopy(src, dst, self.tsend.at[i, k], self.ag_recv.at[i, k], self.p.to(1)).wait_send()
            if kind == QKV:
                src = slot.at[:, pl.ds(256, 256)]
                dst = self.kv_piece(t, self.p.s, self.wk)
                rcopy(src, dst, self.tsend.at[1, k], self.ag_recv.at[1, k], self.p.to(1)).wait_send()

    def drain_spread(self, kind, t):
        k = self.tick(kind, t)
        s = self.p.s if kind in (DOWN, OUT) else self.shard_of(kind, t)
        refs = [ref for _, ref in self.pieces(kind, t, s, None)]
        if kind == QKV:
            refs.append(self.kv_piece(t, s, self.wk))
        for i, ref in enumerate(refs):

            @pl.when(self.pos > 0)
            def _():
                self.spread_copy(i, k, ref).wait_send()

            rcopy(ref, ref, self.cp_send.at[i, k], self.cp_recv.at[i, k], self.p.sibling()).wait()


RING = 4
CHAIN_SEMS = [DMA((N_TICKS,))] * 2 + [DMA((2, N_TICKS))] * 5


def loop(lo, hi, body):
    def step(t, _):
        body(t)
        return 0

    lax.fori_loop(lo, hi, step, 0)


SKEW, TURN, RETIRE = 2, 3, 4


def between(i, lo, hi):
    return jnp.logical_and(i >= lo, i < hi)


def each(i, lo, hi, act):
    for kind, n in COUNT.items():
        base = Chain.BASE[kind]
        a, b = max(lo, base), min(hi, base + n)
        if isinstance(i, int):
            if a <= i < b:
                act(kind, i - base)
        elif a < b:

            @pl.when(between(i, a, b))
            def _():
                act(kind, i - base)


def at_tick(t, when, act):
    @pl.when(t == when)
    def _():
        act()


def all_greet(p):
    nz = lax.axis_size("z")
    greet(plane_ids(p) + [{"z": lax.rem(p.z + k, nz)} for k in range(1, nz)])


class GainSums:
    def __init__(self, p, tot, got, gz, send, recv):
        self.p, self.tot, self.got, self.gz, self.send, self.recv = p, tot, got, gz, send, recv
        self.nz = lax.axis_size("z")

    def copy(self, k):
        dev = (self.p.sibling(), self.p.to(1), self.p.to(2))[k]
        return rcopy(self.tot.at[k], self.got.at[k], self.send.at[k], self.recv.at[k], dev)

    def along(self, k):
        to = {"z": lax.rem(self.p.z + k, self.nz)}
        return rcopy(
            self.tot.at[3], self.gz.at[self.p.z], self.send.at[2 + k], self.recv.at[3 + self.p.z], to
        )

    def landed(self, k):
        src = lax.rem(self.p.z + self.nz - k, self.nz)
        ref = self.gz.at[src]
        return rcopy(ref, ref, self.send.at[2 + k], self.recv.at[3 + src], {"z": src})

    def add(self, k):
        self.copy(k).wait()
        self.tot[k + 1] = self.tot[k] + self.got[k]
        if k < 2:
            self.copy(k + 1).start()
        else:
            for j in range(1, self.nz):
                self.along(j).start()
            self.gz[self.p.z] = self.tot[3]

    def finish(self):
        for j in range(1, self.nz):
            self.along(j).wait_send()
            self.landed(j).wait_recv()
        total = self.gz[0]
        for j in range(1, self.nz):
            total = total + self.gz[j]
        return total


class Attention:
    def __init__(self, p, hbm, wo, wqkv, part, gout, gqkv, bufs, sems):
        self.p, self.hbm, self.wo, self.wqkv, self.part = p, hbm, wo, wqkv, part
        self.gout, self.gqkv = gout, gqkv
        self.bufs, self.other, self.came, self.kept, self.dq, self.rows_out = bufs[:8], *bufs[8:]
        self.sem, self.send, self.recv, self.psem = sems
        self.n = self.rows_out.shape[1]

    def load(self, i, j):
        src = self.hbm[i]
        ref = src.at[pl.ds(j * self.n, self.n)] if len(src.shape) == 2 else src.at[j]
        b = lax.rem(j, 2)
        return pltpu.make_async_copy(ref, self.bufs[i].at[b], self.sem.at[i, b])

    def fetch(self, j):
        for i in range(7):
            self.load(i, j).start()

    def swap(self, j):
        return rcopy(self.other.at[j], self.came.at[j], self.send.at[j], self.recv.at[j], self.p.sibling())

    def first(self, j):
        for i in range(7):
            self.load(i, j).wait()

        @pl.when(j < 7)
        def _():
            self.fetch(j + 1)

        b = lax.rem(j, 2)
        dhb, q, k, v, attn, probs, turn = (self.bufs[i][b] for i in range(7))
        scale = HEAD_DIM ** (-0.5)
        half = HEAD_DIM // 2
        cosine, sine = turn[:, :half], turn[:, half:]
        dattn = mm_nt(dhb, self.wo[...]).astype(BF)
        g = mm_tn(attn, dhb)
        self.gout[...] = jnp.where(j == 0, g, self.gout[...] + g)
        dp = mm_nt(dattn, v)
        dv = mm_tn(probs.astype(BF), dattn)
        ds = (probs * (dp - jnp.sum(dp * probs, axis=-1, keepdims=True))).astype(BF)
        dq = rotate(mm(ds, k) * scale, cosine, -sine)
        dk = rotate(mm_tn(ds, q) * scale, cosine, -sine)
        zero = self.p.c == 0
        self.dq[b] = dq.astype(BF)
        self.kept[b] = jnp.where(zero, dk, dv)
        self.other[j] = jnp.where(zero, dv, dk).astype(BF)
        self.swap(j).start()
        self.load(7, j).start()

    def out_copy(self, j):
        b = lax.rem(j, 2)
        return pltpu.make_async_copy(self.rows_out.at[b], self.part.at[pl.ds(j * self.n, self.n)], self.psem.at[b])

    def second(self, j):
        b = lax.rem(j, 2)
        self.swap(j).wait()
        self.load(7, j).wait()
        dkv = (self.kept[b] + self.came[j].astype(F32)).astype(BF)
        dqkv = jnp.concatenate([self.dq[b], dkv], -1)
        g = mm_tn(self.bufs[7][b], dqkv)
        self.gqkv[...] = jnp.where(j == 0, g, self.gqkv[...] + g)

        @pl.when(j >= 2)
        def _():
            self.out_copy(j - 2).wait()

        self.rows_out[b] = mm_nt(dqkv, self.wqkv[...]).astype(BF)
        self.out_copy(j).start()

    def finish(self):
        self.out_copy(6).wait()
        self.out_copy(7).wait()


class Outer:
    def __init__(self, p, xn2, dgu_hbm, dgu, xc, made, out, sems):
        self.p, self.xn2, self.dgu_hbm, self.dgu, self.xc, self.made, self.out = p, xn2, dgu_hbm, dgu, xc, made, out
        self.dsem, self.xsem, self.osem = sems

    def row(self, n):
        return pl.multiple_of(self.p.shard_at(n // 2) * 512 + lax.rem(n, 2) * 256, 256)

    def whole(self):
        return pltpu.make_async_copy(self.dgu_hbm, self.dgu, self.dsem.at[0])

    def load(self, n):
        b = lax.rem(n, 2)
        return pltpu.make_async_copy(self.xn2.at[:, pl.ds(self.row(n), 256)], self.xc.at[b], self.xsem.at[b])

    def store(self, n):
        b = lax.rem(n, 2)
        return pltpu.make_async_copy(self.made.at[b], self.out.at[pl.ds(self.row(n), 256)], self.osem.at[b])

    def step(self, n):
        @pl.when(n == 0)
        def _():
            self.whole().wait()

        @pl.when(n > 0)
        def _():
            self.store(n - 1).wait()

        self.load(n).wait()

        @pl.when(n < 7)
        def _():
            self.load(n + 1).start()

        b = lax.rem(n, 2)
        self.made[b] = mm_tn(self.xc[b], self.dgu[...]).astype(BF)
        self.store(n).start()


def tail_kernel(
    part_ref, dpart_ref, x_hbm, h_hbm, g_hbm, gain_ref, gd_ref, xn2_ref, dgu_hbm, wo_hbm, wqkv_ref,
    q_ref, k_ref, v_ref, attn_ref, probs_ref, turn_ref, xn1_ref,
    out_hbm, grad_hbm, gains_ref, dhb_ref, p1_ref, ggu_ref, gate, up, down, out, wq, wk, wv,
    bufa, bufb, qa, qb, ringa, ringb, ring_sem, credita, creditb, dgu, xc, dsem, xsem, osem, tot, got, gz, gsend, grecv,
    low, xg, hb, dh, gout, gqkv, gout_low, gqkv_low, wo_ref, io_sem, free_sem, *scr
):
    p = Place()
    nz = lax.axis_size("z")
    s1 = Scatter(p, part_ref, scr[:8])
    s2 = Scatter(p, dpart_ref, scr[:8])
    s3 = Scatter(p, p1_ref, scr[:8])
    ga = Gather(p, low, dhb_ref, scr[8:13])
    sums = GainSums(p, tot, got, gz, gsend, grecv)
    hbm = (dhb_ref, q_ref, k_ref, v_ref, attn_ref, probs_ref, turn_ref, xn1_ref)
    at = Attention(p, hbm, wo_ref, wqkv_ref, p1_ref, gout, gqkv, scr[13:26], scr[26:30])
    gu = Outer(p, xn2_ref, dgu_hbm, dgu, xc, at.rows_out, ggu_ref, (dsem, xsem, osem))
    ins = (gd_ref, ggu_ref, gout_low, gqkv_low)
    outs = (gate, up, down, out, wq, wk, wv)
    n = len(CHAIN_SEMS)
    chains = [
        Chain(p, 0, ins, outs, (bufa, qa, ringa, ring_sem.at[0], credita), scr[30 : 30 + n]),
        Chain(p, 1, ins, outs, (bufb, qb, ringb, ring_sem.at[1], creditb), scr[30 + n : 30 + 2 * n]),
    ]
    line = SKEW * (nz - 1)
    half = s1.half

    def io(k):
        wo = wo_hbm.at[pl.ds(p.c * HEAD_DIM, HEAD_DIM)]
        src, dst = [(h_hbm, hb), (g_hbm, xg), (x_hbm, xg), (low, out_hbm), (low, grad_hbm), (wo, wo_ref)][k]
        return pltpu.make_async_copy(src, dst, io_sem.at[k])

    io(0).start()
    io(1).start()
    io(5).start()
    gu.whole().start()
    gu.load(0).start()
    tot[0] = jnp.zeros_like(tot[0])
    all_greet(p)
    s1.start()

    def norm2():
        for k in (0, 1, 5):
            io(k).wait()
        for h in (0, 1):
            r = pl.ds(h * half, half)
            dx = s1.total(h)
            res = hb[r]
            f = lax.rsqrt(jnp.mean(res * res, axis=1, keepdims=True) + norm_eps)
            hat = res * f
            term = jnp.sum(dx * hat, axis=0, keepdims=True)
            tot[0, 1:2] = term if h == 0 else tot[0, 1:2] + term
            d = xg[r].astype(F32) + norm_backward_step(dx * gain_ref[1:2], hat, f)
            dh[r] = d
            low[r] = d.astype(BF)
        ga.start()
        io(2).start()

    def gathered():
        ga.finish()
        s1.drain()
        at.fetch(0)
        s2.start()

    def output():
        for h in (0, 1):
            r = pl.ds(h * half, half)
            low[r] = (hb[r] + s2.total(h)).astype(BF)
        io(3).start()
        s2.drain()
        for d in (p.to(1), p.to(2), p.sibling()):
            pl.semaphore_signal(free_sem, inc=1, device_id=d, device_id_type=MESH)

    def attended():
        at.finish()
        gout_low[...] = gout[...].astype(BF)
        gqkv_low[...] = gqkv[...].astype(BF)
        pl.semaphore_wait(free_sem, 3)
        s3.start()

    def norm1():
        io(2).wait()
        io(3).wait()
        for h in (0, 1):
            r = pl.ds(h * half, half)
            dx = s3.total(h)
            xf = xg[r].astype(F32)
            f = lax.rsqrt(jnp.mean(xf * xf, axis=1, keepdims=True) + norm_eps)
            hat = xf * f
            term = jnp.sum(dx * hat, axis=0, keepdims=True)
            tot[0, 0:1] = term if h == 0 else tot[0, 0:1] + term
            low[r] = (dh[r] + norm_backward_step(dx * gain_ref[0:1], hat, f)).astype(BF)
        io(4).start()
        sums.copy(0).start()

    def gains():
        gains_ref[...] = sums.finish()

    def tick(t):
        for ch in chains:
            each(t + 1 - SKEW * ch.pos, 0, EARLY, ch.ahead)
            each(t, 0, N_TICKS, ch.begin)
            each(t - SKEW * ch.pos, 0, N_TICKS, ch.reduce)
        for ch in chains:
            each(t - TURN - 2 * line + SKEW * ch.pos, 0, N_TICKS, ch.spread)
            each(t - RETIRE - SKEW * ch.pos, 0, N_SLOTTED, ch.retire)
        u = t // FINE
        pl.when(jnp.logical_and(between(t, 2, 18), lax.rem(t, 2) == 0))(lambda: gu.step((t - 2) // 2))
        at_tick(t, 18, lambda: gu.store(7).wait())
        for k in range(4):
            at_tick(t, k, functools.partial(s1.first, k))
            at_tick(t, FINE * A0 + k, functools.partial(s2.first, k))
            at_tick(t, FINE * (A0 + 9) + 1 + k, functools.partial(s3.first, k))

        @pl.when(lax.rem(t, FINE) == 0)
        def _():
            at_tick(u, 3, s1.relay)
            at_tick(u, 5, norm2)
            at_tick(u, 7, ga.relay)
            at_tick(u, A0 - 1, gathered)
            pl.when(between(u, A0 + 1, A0 + 9))(lambda: at.second(u - A0 - 1))
            pl.when(between(u, A0, A0 + 8))(lambda: at.first(u - A0))
            at_tick(u, A0 + 3, s2.relay)
            at_tick(u, A0 + 5, output)
            at_tick(u, A0 + 9, attended)
            at_tick(u, A0 + 12, s3.relay)
            at_tick(u, A0 + 14, norm1)
            for k in range(3):
                at_tick(u, A0 + 15 + k, functools.partial(sums.add, k))
            at_tick(u, A0 + 19, gains)

    loop(0, N_TICKS + TURN + 2 * line, tick)
    io(4).wait()
    s3.drain()

    def drain(i):
        for ch in chains:
            each(i, N_SLOTTED, N_TICKS, ch.gone)
            each(i, 0, N_TICKS, ch.drain_spread)

    loop(0, N_TICKS, drain)


A0 = 12


def tail(part, dpart, x, h, g, gains, g_down, xn2, dgu, wo, wqkv, heads, xn1, ff):
    rows, width = x.shape
    nz = lax.axis_size("z")
    hd, pr = HEAD_DIM, width // 4
    shapes = [(pr, ff), (pr, ff), (ff // 4, width), (pr, width), (pr, width), (pr, 1024), (pr, 1024)]
    sq = pltpu.VMEM((2, rows, hd), BF)
    wide = pltpu.VMEM((2, rows, width), BF)
    return pl.pallas_call(
        tail_kernel,
        out_shape=(
            jax.ShapeDtypeStruct((rows, width), BF),
            jax.ShapeDtypeStruct((rows, width), BF),
            jax.ShapeDtypeStruct((8, width), F32),
            jax.ShapeDtypeStruct((8 * rows, width), BF),
            jax.ShapeDtypeStruct((8 * rows, width), BF),
            jax.ShapeDtypeStruct((width, width), BF),
        )
        + tuple(jax.ShapeDtypeStruct(s, BF) for s in shapes),
        in_specs=[ANY] * 5 + [VM] + [ANY] * 4 + [VM] + [ANY] * 7,
        out_specs=(ANY, ANY, VM) + (ANY,) * 10,
        scratch_shapes=[
            pltpu.VMEM((SLOTS, CH, width), BF),
            pltpu.VMEM((SLOTS, CH, width), BF),
            pltpu.VMEM((COUNT[QKV], QR, 512), BF),
            pltpu.VMEM((COUNT[QKV], QR, 512), BF),
            pltpu.VMEM((RING, CH, width), BF),
            pltpu.VMEM((RING, CH, width), BF),
            DMA((2, RING)),
            pltpu.SemaphoreType.REGULAR,
            pltpu.SemaphoreType.REGULAR,
            pltpu.VMEM((8 * rows, width), BF),
            pltpu.VMEM((2, width, 256), BF),
            DMA((1,)),
            DMA((2,)),
            DMA((2,)),
            pltpu.VMEM((4, 8, width), F32),
            pltpu.VMEM((3, 8, width), F32),
            pltpu.VMEM((nz, 8, width), F32),
            DMA((nz + 3,)),
            DMA((nz + 3,)),
            pltpu.VMEM((rows, width), BF),
            pltpu.VMEM((rows, width), BF),
            pltpu.VMEM((rows, width), F32),
            pltpu.VMEM((rows, width), F32),
            pltpu.VMEM((hd, width), F32),
            pltpu.VMEM((width, 2 * hd), F32),
            pltpu.VMEM((hd, width), BF),
            pltpu.VMEM((width, 2 * hd), BF),
            pltpu.VMEM((hd, width), BF),
            DMA((6,)),
            pltpu.SemaphoreType.REGULAR,
        ]
        + scatter_scratch(rows, width)
        + GATHER_SEMS
        + [wide, sq, sq, sq, sq]
        + [pltpu.VMEM((2, rows, rows), F32), pltpu.VMEM((2, rows, hd), F32), wide]
        + [pltpu.VMEM((8, rows, hd), BF)] * 2
        + [pltpu.VMEM((2, rows, hd), F32), sq, wide]
        + [DMA((8, 2)), DMA((8,)), DMA((8,)), DMA((2,))]
        + CHAIN_SEMS * 2,
        compiler_params=params(2, 63),
        name="tail",
    )(part, dpart, x, h, g, gains, g_down, xn2, dgu, wo, wqkv, *heads, xn1)


def widen_kernel(*refs):
    n = len(refs) // 2
    for a, b in zip(refs[:n], refs[n:], strict=True):
        b[...] = a[...].astype(F32)


def widen(arrays):
    steps = 8

    def spec(a):
        return pl.BlockSpec((a.shape[0] // steps, a.shape[1]), lambda i: (i, 0))

    return pl.pallas_call(
        widen_kernel,
        grid=(steps,),
        out_shape=tuple(jax.ShapeDtypeStruct(a.shape, F32) for a in arrays),
        in_specs=[spec(a) for a in arrays],
        out_specs=tuple(spec(a) for a in arrays),
        compiler_params=pltpu.CompilerParams(vmem_limit_bytes=62 * 2**20),
        name="widen",
    )(*arrays)


def pieces(
    tokens,
    segment_ids,
    attn_gain,
    w_query,
    w_key,
    w_value,
    w_out,
    mlp_gain,
    w_gate,
    w_up,
    w_down,
    cotangent,
):
    rows, width = tokens.shape[1], tokens.shape[2]
    ns = lax.axis_size("shard")
    hd = HEAD_DIM
    ff = w_gate.shape[1]
    part = width // ns

    x = tokens.reshape(rows, width)
    g = cotangent.reshape(rows, width)
    gains = jnp.concatenate([attn_gain[None], mlp_gain[None], jnp.zeros((6, part), BF)], 0).astype(F32)
    seg = jnp.broadcast_to(segment_ids, (8, rows)).astype(F32)
    half = np.arange(hd // 2, dtype=np.float64) * 2.0 / hd
    freq = jnp.asarray((rope_base ** -half).astype(np.float32)[None])
    h, xn2, g_all, _, gains, _, wqkv, xn1, q, k, v, attn, probs, turn, hid, dgu, dpart, dxpart = front(
        x, seg, gains, freq, w_query, w_key, w_value, w_out, w_gate, w_up, w_down, g
    )
    g_down = mm_tn(hid, g_all).astype(BF)
    heads = (q, k, v, attn, probs, turn)
    output, input_grad, gain_g, _, _, _, gate_g, up_g, down_g, out_g, wq_g, wk_g, wv_g = tail(
        dxpart,
        dpart,
        x,
        h,
        g,
        gains,
        g_down,
        xn2,
        dgu,
        w_out,
        wqkv,
        heads,
        xn1,
        ff,
    )
    output = output.reshape(1, rows, width)
    input_grad = input_grad.reshape(1, rows, width)
    gain_g = lax.dynamic_slice_in_dim(gain_g, lax.axis_index("shard") * part, part, 1)
    wide = widen((wq_g, wk_g, wv_g, out_g, gate_g, up_g, down_g))
    return (output, input_grad, gain_g[0], *wide[:4], gain_g[1], *wide[4:])


def contract_rows(left, right):
    return lax.dot_general(
        left, right, (((0,), (0,)), ((), ())), preferred_element_type=jnp.float32
    )


def contract_cols(left, right):
    return lax.dot_general(
        left, right, (((1,), (1,)), ((), ())), preferred_element_type=jnp.float32
    )


def scores_of(queries, keys, allowed):
    raw = jnp.einsum(
        "qgrd,kgd->grqk", queries, keys, preferred_element_type=jnp.float32
    ) * HEAD_DIM ** (-0.5)
    return jnp.where(allowed, raw, mask_fill)


def general(
    tokens,
    segment_ids,
    attn_gain,
    w_query,
    w_key,
    w_value,
    w_out,
    mlp_gain,
    w_gate,
    w_up,
    w_down,
    cotangent,
):
    rows = tokens.shape[1]
    width = tokens.shape[2]
    groups = HEADS // KV_HEADS
    q_cols = HEADS * HEAD_DIM
    kv_cols = KV_HEADS * HEAD_DIM
    layer_input_rows = tokens.reshape(rows, width).astype(jnp.float32)
    segments = segment_ids.reshape(rows)
    iota = jnp.arange(rows, dtype=jnp.int32)
    starts = jnp.sum((segments[None, :] < segments[:, None]).astype(jnp.int32), axis=1)
    positions = (iota - starts).astype(jnp.float32)
    allowed = (segments[:, None] == segments[None, :]) & (iota[:, None] >= iota[None, :])
    half = HEAD_DIM // 2
    inv_freq = rope_base ** (-(jnp.arange(half, dtype=jnp.float32) * 2.0 / HEAD_DIM))
    angles = positions[:, None] * inv_freq
    cosine = jnp.cos(angles)
    sine = jnp.sin(angles)
    first_norm_factor = lax.rsqrt(
        jnp.mean(layer_input_rows * layer_input_rows, axis=1, keepdims=True) + norm_eps
    )
    first_standardized = layer_input_rows * first_norm_factor
    gain_fragment = lax.all_gather(attn_gain, "shard", axis=0, tiled=True)
    query_piece = lax.all_gather(w_query, "shard", axis=0, tiled=True)
    key_piece = lax.all_gather(w_key, "shard", axis=0, tiled=True)
    value_piece = lax.all_gather(w_value, "shard", axis=0, tiled=True)
    normalized_rows = (first_standardized * gain_fragment.astype(jnp.float32)).astype(jnp.bfloat16)
    joined = jnp.concatenate([query_piece, key_piece, value_piece], 1)
    result = (
        jnp.dot(normalized_rows, joined, preferred_element_type=jnp.float32),
        normalized_rows,
        gain_fragment.astype(jnp.float32),
    )
    folded = result
    projected, normed_one, first_norm_gain = (folded[0], folded[1], folded[2])
    queries = rotate(
        projected[:, :q_cols].reshape(rows, KV_HEADS, groups, HEAD_DIM),
        cosine[:, None, None, :],
        sine[:, None, None, :],
    ).astype(jnp.bfloat16)
    keys = rotate(
        projected[:, q_cols : q_cols + kv_cols].reshape(rows, KV_HEADS, HEAD_DIM),
        cosine[:, None, :],
        sine[:, None, :],
    ).astype(jnp.bfloat16)
    values = projected[:, q_cols + kv_cols :].reshape(rows, KV_HEADS, HEAD_DIM).astype(jnp.bfloat16)
    scores = scores_of(queries, keys, allowed)
    top = jnp.max(scores, axis=-1, keepdims=True)
    log_total = top + jnp.log(jnp.sum(jnp.exp(scores - top), axis=-1, keepdims=True))
    probs = jnp.exp(scores - log_total)
    probs_low = probs.astype(jnp.bfloat16)
    attn = (
        jnp.einsum("grqk,kgd->qgrd", probs_low, values, preferred_element_type=jnp.float32)
        .reshape(rows, q_cols)
        .astype(jnp.bfloat16)
    )
    part = attn
    result = (
        jnp.dot(
            part,
            lax.all_gather(w_out, "shard", axis=0, tiled=True),
            preferred_element_type=jnp.float32,
        ),
    )
    folded_out = result
    residual_hidden_state = layer_input_rows + folded_out[0]
    second_norm_factor = lax.rsqrt(
        jnp.mean(residual_hidden_state * residual_hidden_state, axis=1, keepdims=True) + norm_eps
    )
    second_standardized = residual_hidden_state * second_norm_factor
    gain_fragment = lax.all_gather(mlp_gain, "shard", axis=0, tiled=True)
    gate_piece = lax.all_gather(w_gate, "shard", axis=0, tiled=True)
    up_piece = lax.all_gather(w_up, "shard", axis=0, tiled=True)
    normalized_rows = (second_standardized * gain_fragment.astype(jnp.float32)).astype(jnp.bfloat16)
    joined = jnp.concatenate([gate_piece, up_piece], 1)
    result = (
        jnp.dot(normalized_rows, joined, preferred_element_type=jnp.float32),
        normalized_rows,
        gain_fragment.astype(jnp.float32),
    )
    folded_mlp = result
    gate = folded_mlp[0][:, :FF]
    up_value = folded_mlp[0][:, FF:]
    normed_two = folded_mlp[1]
    second_norm_gain = folded_mlp[2]
    sigma = jax.nn.sigmoid(gate)
    swish = gate * sigma
    inner = (swish * up_value).astype(jnp.bfloat16)
    part = inner
    result = (
        jnp.dot(
            part,
            lax.all_gather(w_down, "shard", axis=0, tiled=True),
            preferred_element_type=jnp.float32,
        ),
    )
    output = (residual_hidden_state + result[0]).astype(jnp.bfloat16).reshape(1, rows, width)
    grad_out = cotangent.reshape(rows, width)
    grad_down = lax.psum_scatter(
        contract_rows(inner, grad_out).astype(jnp.bfloat16),
        "shard",
        scatter_dimension=0,
        tiled=True,
    )
    down_full, gate_full, up_full = (
        lax.all_gather(w_down, "shard", axis=0, tiled=True),
        lax.all_gather(w_gate, "shard", axis=0, tiled=True),
        lax.all_gather(w_up, "shard", axis=0, tiled=True),
    )
    grad_inner = contract_cols(grad_out, down_full)
    grad_gate = (grad_inner * up_value * sigma * (1.0 + gate * (1.0 - sigma))).astype(jnp.bfloat16)
    grad_up = (grad_inner * swish).astype(jnp.bfloat16)
    grad_mlp = jnp.concatenate([grad_gate, grad_up], 1)
    mlp_shards = lax.psum_scatter(
        contract_rows(normed_two, grad_mlp).astype(jnp.bfloat16),
        "shard",
        scatter_dimension=0,
        tiled=True,
    ).astype(jnp.float32)
    second_norm_gradient = contract_cols(grad_gate, gate_full) + contract_cols(grad_up, up_full)
    second_gain_products = jnp.sum(second_norm_gradient * second_standardized, axis=0)
    hidden_gradient = grad_out.astype(jnp.float32) + norm_backward_step(
        second_norm_gradient * second_norm_gain, second_standardized, second_norm_factor
    )
    grad_hidden_low = hidden_gradient.astype(jnp.bfloat16)
    grad_out_proj = lax.psum_scatter(
        contract_rows(attn, grad_hidden_low).astype(jnp.bfloat16),
        "shard",
        scatter_dimension=0,
        tiled=True,
    )
    grad_attn = contract_cols(grad_hidden_low, lax.all_gather(w_out, "shard", axis=0, tiled=True))
    grad_attn = grad_attn.astype(jnp.bfloat16).reshape(rows, KV_HEADS, groups, HEAD_DIM)
    scores_again = scores_of(queries, keys, allowed)
    probs_again = jnp.exp(scores_again - log_total)
    probs_again_low = probs_again.astype(jnp.bfloat16)
    grad_probs = jnp.einsum("qgrd,kgd->grqk", grad_attn, values, preferred_element_type=jnp.float32)
    grad_values = jnp.einsum(
        "grqk,qgrd->kgd", probs_again_low, grad_attn, preferred_element_type=jnp.float32
    )
    grad_scores = (
        probs_again * (grad_probs - jnp.sum(grad_probs * probs_again, axis=-1, keepdims=True))
    ).astype(jnp.bfloat16)
    grad_queries = jnp.einsum(
        "grqk,kgd->qgrd", grad_scores, keys, preferred_element_type=jnp.float32
    ) * HEAD_DIM ** (-0.5)
    grad_keys = jnp.einsum(
        "grqk,qgrd->kgd", grad_scores, queries, preferred_element_type=jnp.float32
    ) * HEAD_DIM ** (-0.5)
    grad_queries = rotate(grad_queries, cosine[:, None, None, :], -sine[:, None, None, :]).reshape(
        rows, q_cols
    )
    grad_keys = rotate(grad_keys, cosine[:, None, :], -sine[:, None, :]).reshape(rows, kv_cols)
    grad_joined = jnp.concatenate(
        [
            grad_queries.astype(jnp.bfloat16),
            grad_keys.astype(jnp.bfloat16),
            grad_values.reshape(rows, kv_cols).astype(jnp.bfloat16),
        ],
        1,
    )
    qkv_shards = lax.psum_scatter(
        contract_rows(normed_one, grad_joined).astype(jnp.bfloat16),
        "shard",
        scatter_dimension=0,
        tiled=True,
    ).astype(jnp.float32)
    local_qkv = jnp.concatenate([w_query, w_key, w_value], 1)
    first_norm_gradient = contract_cols(
        grad_joined, lax.all_gather(local_qkv, "shard", axis=0, tiled=True)
    )
    first_gain_products = jnp.sum(first_norm_gradient * first_standardized, axis=0)
    input_gradient_rows = hidden_gradient + norm_backward_step(
        first_norm_gradient * first_norm_gain, first_standardized, first_norm_factor
    )
    input_grad = input_gradient_rows.astype(jnp.bfloat16).reshape(1, rows, width)
    gain_one_grad, gain_two_grad = (
        lax.psum_scatter(first_gain_products, "shard", scatter_dimension=0, tiled=True),
        lax.psum_scatter(second_gain_products, "shard", scatter_dimension=0, tiled=True),
    )
    summed = (
        lax.psum(gain_one_grad.astype(jnp.bfloat16), "rep").astype(jnp.float32),
        lax.psum(qkv_shards[:, :q_cols].astype(jnp.bfloat16), "rep").astype(jnp.float32),
        lax.psum(qkv_shards[:, q_cols : q_cols + kv_cols].astype(jnp.bfloat16), "rep").astype(
            jnp.float32
        ),
        lax.psum(qkv_shards[:, q_cols + kv_cols :].astype(jnp.bfloat16), "rep").astype(jnp.float32),
        lax.psum(grad_out_proj, "rep").astype(jnp.float32),
        lax.psum(gain_two_grad.astype(jnp.bfloat16), "rep").astype(jnp.float32),
        lax.psum(mlp_shards[:, :FF].astype(jnp.bfloat16), "rep").astype(jnp.float32),
        lax.psum(mlp_shards[:, FF:].astype(jnp.bfloat16), "rep").astype(jnp.float32),
        lax.psum(grad_down, "rep").astype(jnp.float32),
    )
    return (
        output,
        input_grad,
        summed[0],
        summed[1],
        summed[2],
        summed[3],
        summed[4],
        summed[5],
        summed[6],
        summed[7],
        summed[8],
    )


def solution(mesh):
    rep, shard = mesh.devices.shape
    if shard == KV_HEADS and rep % 2 == 0:
        fine = Mesh(np.asarray(mesh.devices).reshape(rep // 2, 2, shard), ("z", "core", "shard"))
        body, every = pieces, ("z", "core", "shard")
    else:
        fine, body, every = mesh, general, ("rep", "shard")
    seqs, vec, mat = P(every, None, None), P("shard"), P("shard", None)
    in_specs = (seqs, P(every, None), vec, mat, mat, mat, mat, vec, mat, mat, mat, seqs)
    out_specs = (seqs, seqs, vec, mat, mat, mat, mat, vec, mat, mat, mat)
    return jax.shard_map(body, mesh=fine, in_specs=in_specs, out_specs=out_specs, check_vma=False)
```

```python
import functools

import jax
import jax.numpy as jnp
import numpy as np
from jax import lax
from jax.experimental import pallas as pl
from jax.experimental.pallas import tpu as pltpu
from jax.sharding import Mesh
from jax.sharding import PartitionSpec as P

HEADS = 8
KV_HEADS = 4
HEAD_DIM = 256
FF = 8192

rope_base = 1000042.0
norm_eps = 1e-06
mask_fill = -1e30

BF = jnp.bfloat16
F32 = jnp.float32
MESH = pl.DeviceIdType.MESH
ANY = pl.BlockSpec(memory_space=pl.ANY)
VM = pl.BlockSpec(memory_space=pltpu.VMEM)
DMA = pltpu.SemaphoreType.DMA


def mm(a, b):
    return jnp.dot(a, b, preferred_element_type=F32)


def mm_tn(a, b):
    return lax.dot_general(a, b, (((0,), (0,)), ((), ())), preferred_element_type=F32)


def mm_nt(a, b):
    return lax.dot_general(a, b, (((1,), (1,)), ((), ())), preferred_element_type=F32)


def rotate(values, cosine, sine):
    half = values.shape[-1] // 2
    first = values[..., :half]
    second = values[..., half:]
    return jnp.concatenate([first * cosine - second * sine, second * cosine + first * sine], -1)


def norm_backward_step(grad_hat, normalized_rows, factor):
    return factor * (
        grad_hat - normalized_rows * jnp.mean(grad_hat * normalized_rows, axis=1, keepdims=True)
    )


class Place:
    def __init__(self):
        self.z = lax.axis_index("z")
        self.c = lax.axis_index("core")
        self.s = lax.axis_index("shard")

    def shard(self, d):
        s = self.s
        if d == 0:
            return s
        if d == 1:
            return s + 1 - 2 * lax.rem(s, 2)
        if d == 2:
            return lax.rem(s + 2, 4)
        return 3 - s

    def shard_at(self, d):
        s = self.s
        one = s + 1 - 2 * lax.rem(s, 2)
        two = lax.rem(s + 2, 4)
        return jnp.where(d == 0, s, jnp.where(d == 1, one, jnp.where(d == 2, two, 3 - s)))

    def to(self, d):
        return {"shard": self.shard(d)}

    def sibling(self):
        return {"core": 1 - self.c}


def greet(ids):
    barrier = pltpu.get_barrier_semaphore()
    for d in ids:
        pl.semaphore_signal(barrier, inc=1, device_id=d, device_id_type=MESH)
    pl.semaphore_wait(barrier, len(ids))


def rcopy(src, dst, send, recv, dev):
    return pltpu.make_async_remote_copy(
        src_ref=src, dst_ref=dst, send_sem=send, recv_sem=recv, device_id=dev, device_id_type=MESH
    )


GATHER_SEMS = [DMA((6,)), DMA((6,)), DMA((7,)), DMA((7,)), DMA((1,))]


class Gather:
    def __init__(self, p, src, out, sems):
        self.p, self.src, self.out = p, src, out
        self.send, self.recv, self.csend, self.crecv, self.lsem = sems
        self.rows = src.shape[0]
        self.half = self.rows // 2

    def at(self, d, h, core=None):
        core = self.p.c if core is None else core
        row = (core * 4 + self.p.shard(d)) * self.rows
        if h is None:
            return self.out.at[pl.ds(row, self.rows)]
        return self.out.at[pl.ds(row + h * self.half, self.half)]

    def move(self, k):
        d, h, to = [(0, 0, 1), (0, 1, 2), (0, 1, 1), (0, 0, 2), (1, 0, 2), (2, 1, 1)][k]
        dst = self.at(d, h)
        src = self.src.at[pl.ds(h * self.half, self.half)] if d == 0 else dst
        return rcopy(src, dst, self.send.at[k], self.recv.at[k], self.p.to(to))

    def landed(self, k):
        d, h = [(1, 0), (2, 1), (1, 1), (2, 0), (3, 0), (3, 1)][k]
        return self.at(d, h)

    def pass_on(self, k):
        here = self.src if k == 6 else self.landed(k)
        there = self.at(0, None) if k == 6 else self.landed(k)
        return rcopy(here, there, self.csend.at[k], self.crecv.at[k], self.p.sibling())

    def arrived(self, k):
        ref = self.landed(k)
        rcopy(ref, ref, self.send.at[k], self.recv.at[k], self.p.to(1)).wait_recv()
        self.pass_on(k).start()

    def start(self):
        for k in range(4):
            self.move(k).start()
        self.pass_on(6).start()
        pltpu.make_async_copy(self.src, self.at(0, None), self.lsem.at[0]).start()

    def relay(self):
        for k in (0, 1):
            self.arrived(k)
            self.move(4 + k).start()

    def early(self):
        for k in (2, 3):
            self.arrived(k)

    def late(self):
        for k in (4, 5):
            self.arrived(k)

    def both(self, ks):
        for k in ks:
            self.pass_on(k).wait_recv()

    def home(self):
        self.both((6,))
        pltpu.make_async_copy(self.src, self.at(0, None), self.lsem.at[0]).wait()

    def close(self):
        for k in range(6):
            self.move(k).wait_send()
        for k in range(7):
            self.pass_on(k).wait_send()

    def finish(self, early=False):
        if not early:
            self.early()
        self.late()
        self.both(range(7))
        pltpu.make_async_copy(self.src, self.at(0, None), self.lsem.at[0]).wait()
        self.close()


SCATTER_SEMS = [DMA((4,)), DMA((4,)), DMA((4,)), DMA((6,)), DMA((6,))]
ORDER = (3, 1, 2, 0)


def scatter_scratch(rows, width):
    half = rows // 2
    return [
        pltpu.VMEM((4, rows, width), BF),
        pltpu.VMEM((4, rows, width), BF),
        pltpu.VMEM((6, half, width), BF),
    ] + SCATTER_SEMS


class Scatter:
    def __init__(self, p, part, scratch):
        self.p, self.part = p, part
        self.own, self.got, self.slot, self.lsem, self.csend, self.crecv, self.send, self.recv = scratch
        self.rows = self.own.shape[1]
        self.half = self.rows // 2

    def block(self, core, d):
        return self.part.at[pl.ds((core * 4 + self.p.shard(d)) * self.rows, self.rows)]

    def local(self, d):
        return pltpu.make_async_copy(self.block(self.p.c, d), self.own.at[d], self.lsem.at[d])

    def swap(self, d):
        src = self.block(1 - self.p.c, d)
        return rcopy(src, self.got.at[d], self.csend.at[d], self.crecv.at[d], self.p.sibling())

    def rowsof(self, h):
        return pl.ds(h * self.half, self.half)

    def move(self, k):
        d, h, to = [(3, 0, 1), (3, 1, 2), (1, 0, 1), (2, 1, 2), (2, 0, 2), (1, 1, 1)][k]
        return rcopy(
            self.own.at[d, self.rowsof(h)], self.slot.at[k], self.send.at[k], self.recv.at[k], self.p.to(to)
        )

    def start(self):
        for d in ORDER:
            self.swap(d).start()
            self.local(d).start()

    def pair(self, d):
        self.swap(d).wait_recv()
        self.local(d).wait()
        self.own[d] = (self.own[d].astype(F32) + self.got[d].astype(F32)).astype(BF)

    def first(self, k):
        self.pair(ORDER[k])
        for m in ((0, 1), (2,), (3,), ())[k]:
            self.move(m).start()

    def relay(self):
        for k, d, h in ((0, 2, 0), (1, 1, 1)):
            self.move(k).wait_recv()
            r = self.rowsof(h)
            self.own[d, r] = (self.own[d, r].astype(F32) + self.slot[k].astype(F32)).astype(BF)
            self.move(4 + k).start()

    def total(self, h):
        near, far = (2, 4) if h == 0 else (3, 5)
        self.move(near).wait_recv()
        self.move(far).wait_recv()
        return (
            self.own[0, self.rowsof(h)].astype(F32)
            + self.slot[near].astype(F32)
            + self.slot[far].astype(F32)
        )

    def drain(self):
        for k in range(6):
            self.move(k).wait_send()
        for d in range(4):
            self.swap(d).wait_send()


def params(cid, mb):
    return pltpu.CompilerParams(
        collective_id=cid, has_side_effects=True, vmem_limit_bytes=mb * 2**20
    )


def plane_ids(p):
    return [p.to(1), p.to(2), p.to(3), p.sibling()]


class Columns:
    def __init__(self, p, sems):
        self.p = p
        self.send, self.recv, self.lsem = sems

    def cols(self, j, d, src, width):
        return src.at[:, pl.ds(pl.multiple_of(j * width, width), width)]

    def copy(self, k, d, src, dst):
        if d == 0:
            return pltpu.make_async_copy(src, dst, self.lsem.at[k])
        return rcopy(src, dst, self.send.at[k, d - 1], self.recv.at[k, d - 1], self.p.to(d))


def rows_at(ref, r, n, c0, width):
    return ref.at[pl.ds(r, n), pl.ds(c0, width)]


def greet_line(p, ids):
    barrier = pltpu.get_barrier_semaphore()
    nz = lax.axis_size("z")
    for d in ids:
        pl.semaphore_signal(barrier, inc=1, device_id=d, device_id_type=MESH)

    @pl.when(p.z > 0)
    def _():
        pl.semaphore_signal(barrier, inc=1, device_id={"z": p.z - 1}, device_id_type=MESH)

    @pl.when(p.z < nz - 1)
    def _():
        pl.semaphore_signal(barrier, inc=1, device_id={"z": p.z + 1}, device_id_type=MESH)

    ends = jnp.where(p.z == 0, 1, 0) + jnp.where(p.z == nz - 1, 1, 0)
    pl.semaphore_wait(barrier, len(ids) + 2 - ends)


def relay_sems(nz):
    return [DMA((3,)), DMA((3,)), DMA((1,)), DMA((2, nz, 3)), DMA((nz, 3))]


class Relay:
    def __init__(self, p, w, dst, c0, sems):
        self.p, self.w, self.dst, self.c0 = p, w, dst, c0
        self.xs, self.xr, self.ls, self.zs, self.zr = sems
        self.nz = lax.axis_size("z")
        self.part = w.shape[0]
        self.n = self.part // self.nz
        self.fb = w.shape[1] // 8

    def cols(self, d):
        return pl.ds(pl.multiple_of((self.p.shard(d) * 2 + self.p.c) * self.fb, self.fb), self.fb)

    def rows(self, d, q):
        return self.dst.at[pl.ds(self.p.shard(d) * self.part + q * self.n, self.n), pl.ds(self.c0, self.fb)]

    def fetch(self, d):
        src = self.w.at[pl.ds(self.p.z * self.n, self.n), self.cols(d)]
        return rcopy(src, self.rows(0, self.p.z), self.xs.at[d - 1], self.xr.at[d - 1], self.p.to(d))

    def local(self):
        dst = self.dst.at[pl.ds(self.p.s * self.part, self.part), pl.ds(self.c0, self.fb)]
        return pltpu.make_async_copy(self.w.at[:, self.cols(0)], dst, self.ls.at[0])

    def along(self, way, q, d):
        ref = self.rows(d, q)
        to = {"z": self.p.z + (1 if way else -1)}
        return rcopy(ref, ref, self.zs.at[way, q, d - 1], self.zr.at[q, d - 1], to)

    def start(self):
        for d in (3, 1, 2):
            self.fetch(d).start()
        self.local().start()

    def can(self, way):
        return self.p.z < self.nz - 1 if way else self.p.z > 0

    def own(self):
        for d in (1, 2, 3):
            self.fetch(d).wait_recv()
        for way in (0, 1):

            @pl.when(self.can(way))
            def _():
                for d in (1, 2, 3):
                    self.along(way, self.p.z, d).start()

    def hop(self, k):
        for way in (0, 1):
            q = self.p.z - k if way else self.p.z + k
            there = q >= 0 if way else q < self.nz

            @pl.when(there)
            def _():
                for d in (1, 2, 3):
                    self.along(way, q, d).wait_recv()

            @pl.when(jnp.logical_and(there, self.can(way)))
            def _():
                for d in (1, 2, 3):
                    self.along(way, q, d).start()

    def finish(self):
        for d in (1, 2, 3):
            self.fetch(d).wait_send()
        for k in range(self.nz):
            for way in (0, 1):
                q = self.p.z - k if way else self.p.z + k
                there = q >= 0 if way else q < self.nz

                @pl.when(jnp.logical_and(there, self.can(way)))
                def _():
                    for d in (1, 2, 3):
                        self.along(way, q, d).wait_send()


class Forward:
    def __init__(self, p, xa, xn1, wqkv, wo, seg, gain, freq, sc, ob, bufs, sems):
        self.p, self.xa, self.xn1 = p, xa, xn1
        self.wqkv, self.wo, self.seg, self.gain, self.freq = wqkv, wo, seg, gain, freq
        self.sc, self.ob = sc, ob
        self.xb, self.nb, self.q, self.k, self.v, self.attn, self.probs, self.turn, self.kept, self.came = bufs
        self.xsem, self.nsem, self.send, self.recv = sems
        self.n = self.xb.shape[1]

    def block(self, i):
        return lax.rem(i, 2) * 4 + self.p.shard_at(i // 2)

    def rows(self, ref, i):
        return ref.at[pl.ds(self.block(i) * self.n, self.n)]

    def load(self, i):
        b = lax.rem(i, 2)
        return pltpu.make_async_copy(self.rows(self.xa, i), self.xb.at[b], self.xsem.at[b])

    def store(self, i):
        b = lax.rem(i, 2)
        return pltpu.make_async_copy(self.nb.at[b], self.rows(self.xn1, i), self.nsem.at[b])

    def swap(self, i):
        return rcopy(self.kept.at[i], self.came.at[i], self.send.at[i], self.recv.at[i], self.p.sibling())

    def seg_of(self, i):
        row = self.seg[self.block(i)]
        return row[0:1], row.T[:, 0:1]

    def first(self, i):
        b, k = lax.rem(i, 2), self.block(i)
        self.load(i).wait()

        @pl.when(i >= 2)
        def _():
            self.store(i - 2).wait()

        x = self.xb[b].astype(F32)
        f = lax.rsqrt(jnp.mean(x * x, axis=1, keepdims=True) + norm_eps)
        xn = (x * f * self.gain).astype(BF)
        self.nb[b] = xn
        self.store(i).start()
        lin = mm(xn, self.wqkv[...])
        row, col = self.seg_of(i)
        start = jnp.sum((row < col).astype(F32), axis=1, keepdims=True)
        at = lax.broadcasted_iota(jnp.int32, (self.n, 1), 0).astype(F32)
        angle = (at - start) * self.freq
        cosine, sine = jnp.cos(angle), jnp.sin(angle)
        self.turn[k] = jnp.concatenate([cosine, sine], -1)
        hd = HEAD_DIM
        self.q[k] = rotate(lin[:, :hd], cosine, sine).astype(BF)
        kv = lin[:, hd:]
        self.kept[i] = jnp.where(self.p.c == 0, rotate(kv, cosine, sine), kv).astype(BF)
        self.swap(i).start()

    def second(self, i):
        n, k = self.n, self.block(i)
        self.swap(i).wait()
        mine, came = self.kept[i], self.came[i]
        key = jnp.where(self.p.c == 0, mine, came)
        value = jnp.where(self.p.c == 0, came, mine)
        self.k[k], self.v[k] = key, value
        row, col = self.seg_of(i)
        down = lax.broadcasted_iota(jnp.int32, (n, n), 0)
        over = lax.broadcasted_iota(jnp.int32, (n, n), 1)
        allowed = jnp.logical_and(row == col, down >= over)
        scores = jnp.where(allowed, mm_nt(self.q[k], key) * HEAD_DIM ** (-0.5), mask_fill)
        ex = jnp.exp(scores - jnp.max(scores, axis=-1, keepdims=True))
        probs = ex / jnp.sum(ex, axis=-1, keepdims=True)
        self.probs[k] = probs
        attn = mm(probs.astype(BF), value).astype(BF)
        self.attn[k] = attn
        term = mm(attn, self.wo[...]).astype(BF)
        d = i // 2
        mine_too = lax.rem(i, 2) == self.p.c

        @pl.when(mine_too)
        def _():
            self.sc.own[d] = term

        @pl.when(jnp.logical_not(mine_too))
        def _():
            self.ob[d] = term
            self.sc.swap(d).start()

    def finish(self):
        self.store(6).wait()
        self.store(7).wait()


class MadeScatter(Scatter):
    def __init__(self, p, made, scratch):
        super().__init__(p, None, scratch)
        self.made = made

    def swap(self, d):
        return rcopy(self.made.at[d], self.got.at[d], self.csend.at[d], self.crecv.at[d], self.p.sibling())

    def pair(self, d):
        self.swap(d).wait_recv()
        self.own[d] = (self.own[d].astype(F32) + self.got[d].astype(F32)).astype(BF)


class Feed:
    def __init__(self, p, block, xn2, g, wgu, wd, outs, bufs, sems):
        self.p, self.block = p, block
        self.xn2, self.g, self.wgu, self.wd, self.outs = xn2, g, wgu, wd, outs
        self.xb, self.gb, self.made, self.got = bufs
        self.xsem, self.gsem, self.osem = sems
        self.n = self.xb.shape[1]
        self.fb = wd.shape[0]

    def rows(self, ref, i):
        return ref.at[pl.ds(self.block(i) * self.n, self.n)]

    def loads(self, i):
        b = lax.rem(i, 2)
        return [
            pltpu.make_async_copy(self.rows(self.xn2, i), self.xb.at[b], self.xsem.at[b]),
            pltpu.make_async_copy(self.rows(self.g, i), self.gb.at[b], self.gsem.at[b]),
        ]

    def stores(self, i):
        b = lax.rem(i, 2)
        srcs = (self.got.at[2 + b, :, pl.ds(0, self.fb)], self.made.at[b], self.got.at[b])
        return [
            pltpu.make_async_copy(src, self.rows(out, i), self.osem.at[j, b])
            for j, (src, out) in enumerate(zip(srcs, self.outs, strict=True))
        ]

    def step(self, i):
        b, fb = lax.rem(i, 2), self.fb
        for cp in self.loads(i):
            cp.wait()

        @pl.when(i >= 2)
        def _():
            for cp in self.stores(i - 2):
                cp.wait()

        xn, g = self.xb[b], self.gb[b]
        gate, up = mm(xn, self.wgu[:, :fb]), mm(xn, self.wgu[:, fb:])
        sigma = jax.nn.sigmoid(gate)
        swish = gate * sigma
        hid = (swish * up).astype(BF)
        self.got[2 + b, :, :fb] = hid
        dhid = mm_nt(g, self.wd[...])
        dgate = (dhid * up * sigma * (1.0 + gate * (1.0 - sigma))).astype(BF)
        dup = (dhid * swish).astype(BF)
        self.made[b, :, :fb] = dgate
        self.made[b, :, fb:] = dup
        self.got[b] = mm_nt(self.made[b], self.wgu[...]).astype(BF)
        for cp in self.stores(i):
            cp.start()

    def finish(self):
        for i in (6, 7):
            for cp in self.stores(i):
                cp.wait()


def front_kernel(
    x_ref, seg_ref, gain_ref, freq_ref, wq_ref, wk_ref, wv_ref, wo_hbm, wg_ref, wu_ref, wd_hbm, g_ref,
    h_ref, xn2_ref, ga_ref, wgu_ref, gains_ref, xa_ref, wqkv_ref, xn1_ref, q_ref, k_ref, v_ref,
    attn_ref, probs_ref, turn_ref, hid_ref, dgu_ref, dx_ref, *scr
):
    p = Place()
    nz = lax.axis_size("z")
    others = [(0, 1)] + [(d, o) for d in (1, 2, 3) for o in (0, 1)]

    def dev(d, o):
        return {"core": 1 - p.c if o else p.c, "shard": p.shard(d)}

    scr = list(scr)

    def take(n):
        out = scr[:n]
        del scr[:n]
        return out

    ga = Gather(p, x_ref, xa_ref, take(5))
    gg = Gather(p, g_ref, ga_ref, take(5))
    [xnb] = take(1)
    gx = Gather(p, xnb, xn2_ref, take(5))
    co = Columns(p, take(3))
    tsend, trecv, tlocal = take(3)
    fb = wgu_ref.shape[1] // 2
    re = [Relay(p, wg_ref, wgu_ref, 0, take(5)), Relay(p, wu_ref, wgu_ref, fb, take(5))]
    [made] = take(1)
    sc = MadeScatter(p, made, take(8))
    wqkv, wo, seg, seg8, gaina_ref, lsem = take(6)
    bufs, sems = take(10), take(4)
    [osem] = take(1)
    wgu, wd, gsem, fsem = take(4)
    part, hd = wq_ref.shape[0], HEAD_DIM

    load_wo = pltpu.make_async_copy(wo_hbm.at[pl.ds(p.c * hd, hd)], wo, lsem.at[0])
    load_wqkv = pltpu.make_async_copy(wqkv_ref, wqkv, lsem.at[1])
    load_wd = pltpu.make_async_copy(wd_hbm.at[pl.ds(p.c * fb, fb)], wd, lsem.at[2])
    load_wgu = pltpu.make_async_copy(wgu_ref, wgu, lsem.at[3])
    load_wo.start()
    load_wd.start()
    seg8[...] = jnp.broadcast_to(seg_ref[...].astype(F32), seg8.shape)
    greet_line(p, [dev(d, o) for d, o in others])

    def q_copy(d):
        src = co.cols(p.shard(d) * 2 + p.c, d, wq_ref, hd)
        return co.copy(0, d, src, rows_at(wqkv_ref, p.s * part, part, 0, hd))

    def kv_copy(d, w):
        src = co.cols(p.shard(d), d, w, hd)
        return co.copy(1, d, src, rows_at(wqkv_ref, p.s * part, part, hd, hd))

    def small(k):
        d, o = others[k]
        yield rcopy(seg8, seg.at[p.c * 4 + p.s], tsend.at[k], trecv.at[k], dev(d, o))
        if d and not o:
            yield rcopy(gain_ref, gaina_ref.at[p.s], tsend.at[7 + d - 1], trecv.at[7 + d - 1], dev(d, o))

    smalls = [cp for k in range(7) for cp in small(k)] + [
        pltpu.make_async_copy(seg8, seg.at[p.c * 4 + p.s], tlocal.at[0]),
        pltpu.make_async_copy(gain_ref, gaina_ref.at[p.s], tlocal.at[1]),
    ]
    for cp in smalls:
        cp.start()
    for d in (3, 1, 2, 0):
        q_copy(d).start()

        @pl.when(p.c == 0)
        def _():
            kv_copy(d, wk_ref).start()

        @pl.when(p.c != 0)
        def _():
            kv_copy(d, wv_ref).start()

    ga.start()
    for cp in smalls:
        cp.wait()
    ga.relay()
    re[0].start()
    for d in (3, 1, 2, 0):
        q_copy(d).wait()
        kv_copy(d, wk_ref).wait()
    load_wqkv.start()
    ga.home()
    load_wo.wait()
    load_wqkv.wait()
    gain1 = jnp.concatenate([gaina_ref[j, 0:1] for j in range(4)], -1)
    gain2 = jnp.concatenate([gaina_ref[j, 1:2] for j in range(4)], -1)
    gains_ref[0:1], gains_ref[1:2] = gain1, gain2
    fw = Forward(p, xa_ref, xn1_ref, wqkv, wo, seg, gain1, freq_ref[...], sc, made, bufs, sems)

    def pair(d):
        sc.pair(d)
        if d == 3:
            sc.move(0).start()
            sc.move(1).start()
        elif d:
            sc.move(1 + d).start()

    def step(i):
        at_tick(i, 1, ga.early)
        at_tick(i, 1, re[1].start)
        at_tick(i, 2, lambda: ga.both((0, 2)))
        at_tick(i, 3, re[0].own)
        at_tick(i, 4, lambda: ga.both((1, 3)))
        at_tick(i, 4, re[1].own)
        at_tick(i, 5, ga.late)
        at_tick(i, 5, gg.start)
        at_tick(i, 6, lambda: ga.both((4, 5)))
        at_tick(i, 6, lambda: re[0].hop(1))
        at_tick(i, 8, lambda: re[1].hop(1))

        @pl.when(jnp.logical_and(lax.rem(i, 2) == 0, i < 8))
        def _():
            fw.load(i).start()
            fw.load(i + 1).start()

        pl.when(i < 8)(lambda: fw.first(i))
        pl.when(i > 0)(lambda: fw.second(i - 1))
        for d in range(4):
            at_tick(i, 2 * d + 2, functools.partial(pair, d))

    loop(0, 9, step)
    saved = [
        pltpu.make_async_copy(a, b, osem.at[j])
        for j, (a, b) in enumerate(
            zip(bufs[2:8], (q_ref, k_ref, v_ref, attn_ref, probs_ref, turn_ref), strict=True)
        )
    ]
    for cp in saved:
        cp.start()
    gg.relay()
    for k in range(2, nz - 1):
        re[0].hop(k)
    sc.relay()
    half = sc.half
    for h in (0, 1):
        r = pl.ds(h * half, half)
        res = x_ref[r].astype(F32) + sc.total(h)
        h_ref[r] = res
        f = lax.rsqrt(jnp.mean(res * res, axis=1, keepdims=True) + norm_eps)
        xnb[r] = (res * f * gain2).astype(BF)
    gx.start()
    for k in range(2, nz - 1):
        re[1].hop(k)
    re[0].hop(nz - 1)
    gg.early()
    gg.late()
    re[1].hop(nz - 1)
    for r in re:
        r.local().wait()
    load_wgu.start()
    fw.finish()
    sc.drain()
    load_wd.wait()
    gg.home()
    gx.home()
    gx.relay()
    load_wgu.wait()
    fd = Feed(
        p, fw.block, xn2_ref, ga_ref, wgu, wd, (hid_ref, dgu_ref, dx_ref),
        (bufs[0], bufs[1], made, sc.got), (sems[0], gsem, fsem),
    )

    def feed(i):
        for ks, when in (((0, 2), 2), ((1, 3), 4), ((4, 5), 6)):
            at_tick(i, when, lambda ks=ks: (gx.both(ks), gg.both(ks)))

        @pl.when(lax.rem(i, 2) == 0)
        def _():
            for cp in fd.loads(i) + fd.loads(i + 1):
                cp.start()

        fd.step(i)
        at_tick(i, 1, gx.early)
        at_tick(i, 4, gx.late)

    loop(0, 8, feed)
    fd.finish()
    for gather in (ga, gg, gx):
        gather.close()
    for r in re:
        r.finish()
    for cp in saved:
        cp.wait()


def front(x, seg, gains, freq, wq, wk, wv, wo, wg, wu, wd, g):
    rows, width = x.shape
    hd = HEAD_DIM
    fb = wg.shape[1] // 8
    nz = lax.axis_size("z")
    every = jax.ShapeDtypeStruct((8 * rows, width), BF)
    head = jax.ShapeDtypeStruct((8, rows, hd), BF)
    keep = pltpu.VMEM((8, rows, hd), BF)
    wide = pltpu.VMEM((2, rows, width), BF)
    return pl.pallas_call(
        front_kernel,
        out_shape=(
            jax.ShapeDtypeStruct((rows, width), F32),
            every,
            every,
            jax.ShapeDtypeStruct((width, wg.shape[1] // 4), BF),
            jax.ShapeDtypeStruct((2, width), F32),
            every,
            jax.ShapeDtypeStruct((width, 2 * hd), BF),
            every,
            head,
            head,
            head,
            head,
            jax.ShapeDtypeStruct((8, rows, rows), F32),
            jax.ShapeDtypeStruct((8, rows, hd), F32),
            jax.ShapeDtypeStruct((8 * rows, fb), BF),
            jax.ShapeDtypeStruct((8 * rows, 2 * fb), BF),
            every,
        ),
        in_specs=[VM] * 4 + [ANY] * 7 + [VM],
        out_specs=(VM, ANY, ANY, ANY, VM) + (ANY,) * 12,
        scratch_shapes=GATHER_SEMS * 2
        + [pltpu.VMEM((rows, width), BF)]
        + GATHER_SEMS
        + [DMA((2, 3)), DMA((2, 3)), DMA((2,)), DMA((10,)), DMA((10,)), DMA((2,))]
        + relay_sems(nz) * 2
        + [pltpu.VMEM((4, rows, width), BF)]
        + scatter_scratch(rows, width)
        + [
            pltpu.VMEM((width, 2 * hd), BF),
            pltpu.VMEM((hd, width), BF),
            pltpu.VMEM((8, 8, rows), F32),
            pltpu.VMEM((8, rows), F32),
            pltpu.VMEM((4, *gains.shape), F32),
            DMA((4,)),
        ]
        + [wide, wide, keep, keep, keep, keep]
        + [pltpu.VMEM((8, rows, rows), F32), pltpu.VMEM((8, rows, hd), F32), keep, keep]
        + [DMA((2,)), DMA((2,)), DMA((8,)), DMA((8,)), DMA((6,))]
        + [pltpu.VMEM((width, 2 * fb), BF), pltpu.VMEM((fb, width), BF), DMA((2,)), DMA((3, 2))],
        compiler_params=params(0, 63),
        name="front",
    )(x, seg, gains, freq, wq, wk, wv, wo, wg, wu, wd, g)


CH = 32
QR = 4 * CH
FINE = 64 // CH
DOWN, GU, OUT, QKV = range(4)
COUNT = {DOWN: 512 // CH, GU: 1024 // CH, OUT: 128 // CH, QKV: 1024 // QR}
N_TICKS = sum(COUNT.values())
EARLY = COUNT[DOWN] + COUNT[GU]
GJ = COUNT[GU] // 4
SLOTS, N_SLOTTED = 12, EARLY + COUNT[OUT]


class Chain:
    def __init__(self, p, h, ins, outs, bufs, sems):
        self.p, self.h = p, h
        self.ins = ins
        self.gate, self.up, self.down, self.out, self.wq, self.wk, self.wv = outs
        self.buf, self.bufq, self.ring, self.ring_sem, self.credit = bufs
        self.rs_send, self.rs_recv, self.ag_send, self.ag_recv, self.cp_send, self.cp_recv, self.tsend = sems
        nz = lax.axis_size("z")
        self.nz = nz
        self.pos = nz - 1 - p.z if h == 0 else p.z
        self.step = -1 if h == 0 else 1

    def dev(self, by):
        return {"z": self.p.z + by}

    BASE = {GU: 0, DOWN: COUNT[GU], OUT: EARLY, QKV: EARLY + COUNT[OUT]}

    def tick(self, kind, t):
        return self.BASE[kind] + t

    def dist(self, kind, t):
        return t // GJ if kind == GU else lax.rem(t, 4)

    def row(self, kind, t):
        return lax.rem(t, GJ) * CH if kind == GU else (t // 4) * QR

    def shard_of(self, kind, t):
        return self.p.shard_at(self.dist(kind, t))

    def mine(self, kind, t):
        h = self.h
        if kind == DOWN:
            return self.ins[DOWN].at[pl.ds(h * 512 + t * CH, CH)]
        if kind == OUT:
            return self.ins[OUT].at[pl.ds(h * 128 + t * CH, CH)]
        row = self.shard_of(kind, t) * 512 + h * 256 + self.row(kind, t)
        return self.ins[kind].at[pl.ds(row, QR if kind == QKV else CH)]

    def fetch(self, kind, t):
        r = lax.rem(self.tick(kind, t), RING)
        return pltpu.make_async_copy(self.mine(kind, t), self.ring.at[r], self.ring_sem.at[r])

    def ahead(self, kind, t):
        @pl.when(self.pos > 0)
        def _():
            self.fetch(kind, t).start()

    def slot(self, kind, t):
        return self.bufq.at[t] if kind == QKV else self.buf.at[lax.rem(self.tick(kind, t), SLOTS)]

    def may_send(self, kind, t):
        if kind != QKV:

            @pl.when(self.tick(kind, t) >= SLOTS)
            def _():
                pl.semaphore_wait(self.credit, 1)

    def retire(self, kind, t):
        self.gone(kind, t)
        if kind != QKV:

            @pl.when(jnp.logical_and(self.pos > 0, self.tick(kind, t) < N_SLOTTED - SLOTS))
            def _():
                pl.semaphore_signal(self.credit, inc=1, device_id=self.dev(-self.step), device_id_type=MESH)

    def rs_copy(self, kind, t, src):
        k = self.tick(kind, t)
        return rcopy(
            src, self.slot(kind, t), self.rs_send.at[k], self.rs_recv.at[k], self.dev(self.step)
        )

    def begin(self, kind, t):
        @pl.when(self.pos == 0)
        def _():
            self.may_send(kind, t)
            self.rs_copy(kind, t, self.mine(kind, t)).start()

    def reduce(self, kind, t):
        first, last = self.pos == 0, self.pos == self.nz - 1

        @pl.when(jnp.logical_not(first))
        def _():
            slot = self.slot(kind, t)
            if kind in (DOWN, GU):
                self.fetch(kind, t).wait()
                own = self.ring.at[lax.rem(self.tick(kind, t), RING)]
            else:
                own = self.mine(kind, t)
            self.rs_copy(kind, t, slot).wait_recv()
            slot[...] = (slot[...].astype(F32) + own[...].astype(F32)).astype(BF)

        @pl.when(jnp.logical_and(jnp.logical_not(first), jnp.logical_not(last)))
        def _():
            self.may_send(kind, t)
            self.rs_copy(kind, t, self.slot(kind, t)).start()

        @pl.when(last)
        def _():
            self.turn(kind, t)

    def pieces(self, kind, t, s, d_shard):
        h, c = self.h, self.p.c
        if kind == DOWN:
            return [(None, self.down.at[pl.ds(c * 1024 + h * 512 + t * CH, CH)])]
        if kind == OUT:
            return [(None, self.out.at[pl.ds(c * 256 + h * 128 + t * CH, CH)])]
        if kind == GU:
            r = h * 256 + self.row(kind, t)
            c0 = pl.multiple_of((s * 2 + c) * 1024, 1024)
            return [
                ((0, 1024), self.gate.at[pl.ds(r, CH), pl.ds(c0, 1024)]),
                ((1024, 1024), self.up.at[pl.ds(r, CH), pl.ds(c0, 1024)]),
            ]
        r = h * 256 + (t // 4) * QR
        cq = pl.multiple_of((s * 2 + c) * 256, 256)
        return [((0, 256), self.wq.at[pl.ds(r, QR), pl.ds(cq, 256)])]

    def kv_piece(self, t, s, w):
        r = self.h * 256 + (t // 4) * QR
        return w.at[pl.ds(r, QR), pl.ds(pl.multiple_of(s * 256, 256), 256)]

    def turn(self, kind, t):
        slot = self.slot(kind, t)
        k = self.tick(kind, t)
        to = self.p.s if kind in (DOWN, OUT) else self.shard_of(kind, t)

        def send(i, src, dst):
            if kind in (DOWN, OUT):
                pltpu.make_async_copy(src, dst, self.ag_recv.at[i, k]).start()
                return

            @pl.when(self.dist(kind, t) == 0)
            def _():
                pltpu.make_async_copy(src, dst, self.ag_recv.at[i, k]).start()

            @pl.when(self.dist(kind, t) != 0)
            def _():
                rcopy(src, dst, self.tsend.at[i, k], self.ag_recv.at[i, k], {"shard": to}).start()

        for i, (cols, dst) in enumerate(self.pieces(kind, t, self.p.s, to)):
            send(i, slot if cols is None else slot.at[:, pl.ds(*cols)], dst)
        if kind == QKV:
            src = slot.at[:, pl.ds(256, 256)]

            @pl.when(self.p.c == 0)
            def _():
                send(1, src, self.kv_piece(t, self.p.s, self.wk))

            @pl.when(self.p.c != 0)
            def _():
                send(1, src, self.kv_piece(t, self.p.s, self.wv))

    def spread_copy(self, i, k, ref):
        return rcopy(ref, ref, self.ag_send.at[i, k], self.ag_recv.at[i, k], self.dev(-self.step))

    def spread(self, kind, t):
        k = self.tick(kind, t)
        s = self.p.s if kind in (DOWN, OUT) else self.shard_of(kind, t)

        def go(i, ref, wait=True):
            if wait:
                self.spread_copy(i, k, ref).wait_recv()

            @pl.when(self.pos > 0)
            def _():
                self.spread_copy(i, k, ref).start()

            rcopy(ref, ref, self.cp_send.at[i, k], self.cp_recv.at[i, k], self.p.sibling()).start()

        for i, (_, ref) in enumerate(self.pieces(kind, t, s, None)):
            go(i, ref)
        if kind == QKV:
            self.spread_copy(1, k, self.kv_piece(t, s, self.wk)).wait_recv()

            @pl.when(self.p.c == 0)
            def _():
                go(1, self.kv_piece(t, s, self.wk), False)

            @pl.when(self.p.c != 0)
            def _():
                go(1, self.kv_piece(t, s, self.wv), False)

    def gone(self, kind, t):
        k = self.tick(kind, t)

        @pl.when(self.pos < self.nz - 1)
        def _():
            self.rs_copy(kind, t, self.slot(kind, t)).wait_send()

        if kind not in (GU, QKV):
            return

        @pl.when(jnp.logical_and(self.pos == self.nz - 1, self.dist(kind, t) != 0))
        def _():
            slot = self.slot(kind, t)
            for i, (cols, dst) in enumerate(self.pieces(kind, t, self.p.s, None)):
                src = slot.at[:, pl.ds(*cols)]
                rcopy(src, dst, self.tsend.at[i, k], self.ag_recv.at[i, k], self.p.to(1)).wait_send()
            if kind == QKV:
                src = slot.at[:, pl.ds(256, 256)]
                dst = self.kv_piece(t, self.p.s, self.wk)
                rcopy(src, dst, self.tsend.at[1, k], self.ag_recv.at[1, k], self.p.to(1)).wait_send()

    def drain_spread(self, kind, t):
        k = self.tick(kind, t)
        s = self.p.s if kind in (DOWN, OUT) else self.shard_of(kind, t)
        refs = [ref for _, ref in self.pieces(kind, t, s, None)]
        if kind == QKV:
            refs.append(self.kv_piece(t, s, self.wk))
        for i, ref in enumerate(refs):

            @pl.when(self.pos > 0)
            def _():
                self.spread_copy(i, k, ref).wait_send()

            rcopy(ref, ref, self.cp_send.at[i, k], self.cp_recv.at[i, k], self.p.sibling()).wait()


RING = 4
CHAIN_SEMS = [DMA((N_TICKS,))] * 2 + [DMA((2, N_TICKS))] * 5


def loop(lo, hi, body):
    def step(t, _):
        body(t)
        return 0

    lax.fori_loop(lo, hi, step, 0)


SKEW, TURN, RETIRE = 2, 3, 4


def between(i, lo, hi):
    return jnp.logical_and(i >= lo, i < hi)


def each(i, lo, hi, act):
    for kind, n in COUNT.items():
        base = Chain.BASE[kind]
        a, b = max(lo, base), min(hi, base + n)
        if isinstance(i, int):
            if a <= i < b:
                act(kind, i - base)
        elif a < b:

            @pl.when(between(i, a, b))
            def _():
                act(kind, i - base)


def at_tick(t, when, act):
    @pl.when(t == when)
    def _():
        act()


def all_greet(p):
    nz = lax.axis_size("z")
    greet(plane_ids(p) + [{"z": lax.rem(p.z + k, nz)} for k in range(1, nz)])


class GainSums:
    def __init__(self, p, tot, got, gz, send, recv):
        self.p, self.tot, self.got, self.gz, self.send, self.recv = p, tot, got, gz, send, recv
        self.nz = lax.axis_size("z")

    def copy(self, k):
        dev = (self.p.sibling(), self.p.to(1), self.p.to(2))[k]
        return rcopy(self.tot.at[k], self.got.at[k], self.send.at[k], self.recv.at[k], dev)

    def along(self, k):
        to = {"z": lax.rem(self.p.z + k, self.nz)}
        return rcopy(
            self.tot.at[3], self.gz.at[self.p.z], self.send.at[2 + k], self.recv.at[3 + self.p.z], to
        )

    def landed(self, k):
        src = lax.rem(self.p.z + self.nz - k, self.nz)
        ref = self.gz.at[src]
        return rcopy(ref, ref, self.send.at[2 + k], self.recv.at[3 + src], {"z": src})

    def add(self, k):
        self.copy(k).wait()
        self.tot[k + 1] = self.tot[k] + self.got[k]
        if k < 2:
            self.copy(k + 1).start()
        else:
            for j in range(1, self.nz):
                self.along(j).start()
            self.gz[self.p.z] = self.tot[3]

    def finish(self):
        for j in range(1, self.nz):
            self.along(j).wait_send()
            self.landed(j).wait_recv()
        total = self.gz[0]
        for j in range(1, self.nz):
            total = total + self.gz[j]
        return total


class Attention:
    def __init__(self, p, hbm, wo, wqkv, part, gout, gqkv, bufs, sems):
        self.p, self.hbm, self.wo, self.wqkv, self.part = p, hbm, wo, wqkv, part
        self.gout, self.gqkv = gout, gqkv
        self.bufs, self.other, self.came, self.kept, self.dq, self.rows_out = bufs[:8], *bufs[8:]
        self.sem, self.send, self.recv, self.psem = sems
        self.n = self.rows_out.shape[1]

    def load(self, i, j):
        src = self.hbm[i]
        ref = src.at[pl.ds(j * self.n, self.n)] if len(src.shape) == 2 else src.at[j]
        b = lax.rem(j, 2)
        return pltpu.make_async_copy(ref, self.bufs[i].at[b], self.sem.at[i, b])

    def fetch(self, j):
        for i in range(7):
            self.load(i, j).start()

    def swap(self, j):
        return rcopy(self.other.at[j], self.came.at[j], self.send.at[j], self.recv.at[j], self.p.sibling())

    def first(self, j):
        for i in range(7):
            self.load(i, j).wait()

        @pl.when(j < 7)
        def _():
            self.fetch(j + 1)

        b = lax.rem(j, 2)
        dhb, q, k, v, attn, probs, turn = (self.bufs[i][b] for i in range(7))
        scale = HEAD_DIM ** (-0.5)
        half = HEAD_DIM // 2
        cosine, sine = turn[:, :half], turn[:, half:]
        dattn = mm_nt(dhb, self.wo[...]).astype(BF)
        g = mm_tn(attn, dhb)
        self.gout[...] = jnp.where(j == 0, g, self.gout[...] + g)
        dp = mm_nt(dattn, v)
        dv = mm_tn(probs.astype(BF), dattn)
        ds = (probs * (dp - jnp.sum(dp * probs, axis=-1, keepdims=True))).astype(BF)
        dq = rotate(mm(ds, k) * scale, cosine, -sine)
        dk = rotate(mm_tn(ds, q) * scale, cosine, -sine)
        zero = self.p.c == 0
        self.dq[b] = dq.astype(BF)
        self.kept[b] = jnp.where(zero, dk, dv)
        self.other[j] = jnp.where(zero, dv, dk).astype(BF)
        self.swap(j).start()
        self.load(7, j).start()

    def out_copy(self, j):
        b = lax.rem(j, 2)
        return pltpu.make_async_copy(self.rows_out.at[b], self.part.at[pl.ds(j * self.n, self.n)], self.psem.at[b])

    def second(self, j):
        b = lax.rem(j, 2)
        self.swap(j).wait()
        self.load(7, j).wait()
        dkv = (self.kept[b] + self.came[j].astype(F32)).astype(BF)
        dqkv = jnp.concatenate([self.dq[b], dkv], -1)
        g = mm_tn(self.bufs[7][b], dqkv)
        self.gqkv[...] = jnp.where(j == 0, g, self.gqkv[...] + g)

        @pl.when(j >= 2)
        def _():
            self.out_copy(j - 2).wait()

        self.rows_out[b] = mm_nt(dqkv, self.wqkv[...]).astype(BF)
        self.out_copy(j).start()

    def finish(self):
        self.out_copy(6).wait()
        self.out_copy(7).wait()


class Outer:
    def __init__(self, p, left, right_hbm, right, xc, out, row, sems):
        self.p, self.left, self.right_hbm, self.right, self.xc, self.out = p, left, right_hbm, right, xc, out
        self.row = row
        self.dsem, self.xsem, self.osem = sems

    def whole(self):
        return pltpu.make_async_copy(self.right_hbm, self.right, self.dsem.at[0])

    def load(self, n):
        b = lax.rem(n, 2)
        cols = pl.ds(pl.multiple_of(self.row(n), 256), 256)
        return pltpu.make_async_copy(self.left.at[:, cols], self.xc.at[b], self.xsem.at[b])

    def store(self, n, made):
        rows = pl.ds(pl.multiple_of(self.row(n), 256), 256)
        return pltpu.make_async_copy(made, self.out.at[rows], self.osem.at[0])

    def step(self, n, last, made):
        @pl.when(n == 0)
        def _():
            self.whole().wait()

        @pl.when(n > 0)
        def _():
            self.store(n - 1, made).wait()

        self.block(n, last, made)

    def block(self, n, last, made):
        self.load(n).wait()

        @pl.when(n < last)
        def _():
            self.load(n + 1).start()

        made[...] = mm_tn(self.xc[lax.rem(n, 2)], self.right[...]).astype(BF)
        self.store(n, made).start()


class Product:
    def __init__(self, hid, wd_hbm, right, made, out, sems):
        self.hid, self.wd_hbm, self.right, self.made, self.out = hid, wd_hbm, right, made, out
        self.wsem, self.hsem, self.osem = sems
        self.n, self.fb = made.shape[1], hid.shape[1]

    def weights(self):
        return pltpu.make_async_copy(self.wd_hbm, self.right.at[pl.ds(0, self.fb)], self.wsem.at[0])

    def space(self, i):
        return pl.ds(self.fb + lax.rem(i, 2) * self.n, self.n)

    def load(self, i):
        dst = self.right.at[self.space(i), pl.ds(0, self.fb)]
        return pltpu.make_async_copy(self.hid.at[pl.ds(i * self.n, self.n)], dst, self.hsem.at[lax.rem(i, 2)])

    def store(self, i):
        b = lax.rem(i, 2)
        return pltpu.make_async_copy(self.made.at[b], self.out.at[pl.ds(i * self.n, self.n)], self.osem.at[b])

    def start(self):
        self.weights().start()
        self.load(0).start()

    def step(self, i):
        @pl.when(i == 0)
        def _():
            self.weights().wait()

        self.load(i).wait()

        @pl.when(i < 7)
        def _():
            self.load(i + 1).start()

        @pl.when(i >= 2)
        def _():
            self.store(i - 2).wait()

        h = self.right[self.space(i), : self.fb]
        self.made[lax.rem(i, 2)] = mm(h, self.right[: self.fb]).astype(BF)
        self.store(i).start()

    def finish(self):
        self.store(6).wait()
        self.store(7).wait()


def tail_kernel(
    part_ref, x_hbm, h_hbm, g_hbm, gain_ref, hid_ref, ga_ref, xn2_ref, dgu_hbm, wd_hbm, wo_hbm, wqkv_ref,
    q_ref, k_ref, v_ref, attn_ref, probs_ref, turn_ref, xn1_ref,
    out_hbm, grad_hbm, gains_ref, dhb_ref, p1_ref, ggu_ref, gd_ref, dpart_ref, gate, up, down, out, wq, wk, wv,
    bufa, bufb, qa, qb, ringa, ringb, ring_sem, credita, creditb, big, xc, dsem, xsem, osem, psem, hsem, psem2, tot, got, gz, gsend, grecv,
    low, xg, hb, dh, gout, gqkv, gout_low, gqkv_low, wo_ref, io_sem, free_sem, *scr
):
    p = Place()
    nz = lax.axis_size("z")
    s1 = Scatter(p, part_ref, scr[:8])
    s2 = Scatter(p, dpart_ref, scr[:8])
    s3 = Scatter(p, p1_ref, scr[:8])
    ga = Gather(p, low, dhb_ref, scr[8:13])
    sums = GainSums(p, tot, got, gz, gsend, grecv)
    hbm = (dhb_ref, q_ref, k_ref, v_ref, attn_ref, probs_ref, turn_ref, xn1_ref)
    at = Attention(p, hbm, wo_ref, wqkv_ref, p1_ref, gout, gqkv, scr[13:26], scr[26:30])
    gu = Outer(
        p, xn2_ref, dgu_hbm, big, xc, ggu_ref,
        lambda n: p.shard_at(n // 2) * 512 + lax.rem(n, 2) * 256,
        (dsem, xsem.at[0], osem.at[0]),
    )
    gd = Outer(
        p, hid_ref, ga_ref, big, xc, gd_ref,
        lambda n: lax.rem(n, 2) * 512 + (n // 2) * 256,
        (dsem.at[pl.ds(1, 1)], xsem.at[1], osem.at[1]),
    )
    made = at.rows_out.at[0]
    fb = hid_ref.shape[1]
    wd = wd_hbm.at[pl.ds(p.c * fb, fb)]
    pr = Product(hid_ref, wd, big, at.rows_out, dpart_ref, (psem.at[pl.ds(0, 1)], hsem, psem2))
    ins = (gd_ref, ggu_ref, gout_low, gqkv_low)
    outs = (gate, up, down, out, wq, wk, wv)
    n = len(CHAIN_SEMS)
    chains = [
        Chain(p, 0, ins, outs, (bufa, qa, ringa, ring_sem.at[0], credita), scr[30 : 30 + n]),
        Chain(p, 1, ins, outs, (bufb, qb, ringb, ring_sem.at[1], creditb), scr[30 + n : 30 + 2 * n]),
    ]
    line = SKEW * (nz - 1)
    half = s1.half

    def io(k):
        wo = wo_hbm.at[pl.ds(p.c * HEAD_DIM, HEAD_DIM)]
        src, dst = [(h_hbm, hb), (g_hbm, xg), (x_hbm, xg), (low, out_hbm), (low, grad_hbm), (wo, wo_ref)][k]
        return pltpu.make_async_copy(src, dst, io_sem.at[k])

    io(0).start()
    io(1).start()
    io(5).start()
    gu.whole().start()
    gu.load(0).start()
    tot[0] = jnp.zeros_like(tot[0])
    all_greet(p)
    s1.start()
    s1.first(0)
    gu.step(0, 7, made)
    s1.first(1)
    gu.step(1, 7, made)
    gu.store(1, made).wait()

    def norm2():
        for k in (0, 1, 5):
            io(k).wait()
        for h in (0, 1):
            r = pl.ds(h * half, half)
            dx = s1.total(h)
            res = hb[r]
            f = lax.rsqrt(jnp.mean(res * res, axis=1, keepdims=True) + norm_eps)
            hat = res * f
            term = jnp.sum(dx * hat, axis=0, keepdims=True)
            tot[0, 1:2] = term if h == 0 else tot[0, 1:2] + term
            d = xg[r].astype(F32) + norm_backward_step(dx * gain_ref[1:2], hat, f)
            dh[r] = d
            low[r] = d.astype(BF)
        ga.start()
        io(2).start()

    def gathered():
        ga.finish()
        s1.drain()
        at.fetch(0)
        s2.start()

    def output():
        for h in (0, 1):
            r = pl.ds(h * half, half)
            low[r] = (hb[r] + s2.total(h)).astype(BF)
        io(3).start()
        s2.drain()
        for d in (p.to(1), p.to(2), p.sibling()):
            pl.semaphore_signal(free_sem, inc=1, device_id=d, device_id_type=MESH)

    def attended():
        at.finish()
        gout_low[...] = gout[...].astype(BF)
        gqkv_low[...] = gqkv[...].astype(BF)
        pl.semaphore_wait(free_sem, 3)
        s3.start()

    def norm1():
        io(2).wait()
        io(3).wait()
        for h in (0, 1):
            r = pl.ds(h * half, half)
            dx = s3.total(h)
            xf = xg[r].astype(F32)
            f = lax.rsqrt(jnp.mean(xf * xf, axis=1, keepdims=True) + norm_eps)
            hat = xf * f
            term = jnp.sum(dx * hat, axis=0, keepdims=True)
            tot[0, 0:1] = term if h == 0 else tot[0, 0:1] + term
            low[r] = (dh[r] + norm_backward_step(dx * gain_ref[0:1], hat, f)).astype(BF)
        io(4).start()
        sums.copy(0).start()

    def gains():
        gains_ref[...] = sums.finish()

    def gate_up(n):
        @pl.when(n > 2)
        def _():
            gu.store(n - 1, made).wait()

        gu.block(n, 7, made)

    def products():
        gu.store(7, made).wait()
        pr.start()

    def two_products(i):
        pr.step(i)
        pr.step(i + 1)

    def downs():
        pr.finish()
        gd.whole().start()
        gd.load(0).start()

    def tick(t):
        for ch in chains:
            each(t + 1 - SKEW * ch.pos, 0, EARLY, ch.ahead)
            each(t, 0, N_TICKS, ch.begin)
            each(t - SKEW * ch.pos, 0, N_TICKS, ch.reduce)
        for ch in chains:
            each(t - TURN - 2 * line + SKEW * ch.pos, 0, N_TICKS, ch.spread)
            each(t - RETIRE - SKEW * ch.pos, 0, N_SLOTTED, ch.retire)
        u = t // FINE
        pl.when(jnp.logical_and(between(t, 2, 14), lax.rem(t, 2) == 0))(lambda: gate_up(t // 2 + 1))
        at_tick(t, 14, products)
        pl.when(between(t, 16, 20))(lambda: two_products(2 * (t - 16)))
        at_tick(t, 20, downs)
        pl.when(jnp.logical_and(between(t, 25, 33), lax.rem(t, 2) == 1))(
            lambda: gd.step((t - 25) // 2, 3, gout_low)
        )
        at_tick(t, 33, lambda: gd.store(3, gout_low).wait())
        for k in range(4):
            if k >= 2:
                at_tick(t, k - 2, functools.partial(s1.first, k))
            at_tick(t, FINE * A0 + k, functools.partial(s2.first, k))
            at_tick(t, FINE * (A0 + 9) + 1 + k, functools.partial(s3.first, k))

        @pl.when(lax.rem(t, FINE) == 0)
        def _():
            at_tick(u, 3, s1.relay)
            at_tick(u, 5, norm2)
            at_tick(u, 7, ga.relay)
            at_tick(u, A0 - 1, gathered)
            pl.when(between(u, A0 + 1, A0 + 9))(lambda: at.second(u - A0 - 1))
            pl.when(between(u, A0, A0 + 8))(lambda: at.first(u - A0))
            at_tick(u, A0 + 3, s2.relay)
            at_tick(u, A0 + 5, output)
            at_tick(u, A0 + 9, attended)
            at_tick(u, A0 + 12, s3.relay)
            at_tick(u, A0 + 14, norm1)
            for k in range(3):
                at_tick(u, A0 + 15 + k, functools.partial(sums.add, k))
            at_tick(u, A0 + 19, gains)

    loop(0, N_TICKS + TURN + 2 * line, tick)
    io(4).wait()
    s3.drain()

    def drain(i):
        for ch in chains:
            each(i, N_SLOTTED, N_TICKS, ch.gone)
            each(i, 0, N_TICKS, ch.drain_spread)

    loop(0, N_TICKS, drain)


A0 = 12


def tail(part, x, h, g, gains, hid, g_all, xn2, dgu, wd, wo, wqkv, heads, xn1, ff):
    rows, width = x.shape
    nz = lax.axis_size("z")
    hd, pr = HEAD_DIM, width // 4
    shapes = [(pr, ff), (pr, ff), (ff // 4, width), (pr, width), (pr, width), (pr, 1024), (pr, 1024)]
    sq = pltpu.VMEM((2, rows, hd), BF)
    wide = pltpu.VMEM((2, rows, width), BF)
    return pl.pallas_call(
        tail_kernel,
        out_shape=(
            jax.ShapeDtypeStruct((rows, width), BF),
            jax.ShapeDtypeStruct((rows, width), BF),
            jax.ShapeDtypeStruct((8, width), F32),
            jax.ShapeDtypeStruct((8 * rows, width), BF),
            jax.ShapeDtypeStruct((8 * rows, width), BF),
            jax.ShapeDtypeStruct((width, width), BF),
            jax.ShapeDtypeStruct((hid.shape[1], width), BF),
            jax.ShapeDtypeStruct((8 * rows, width), BF),
        )
        + tuple(jax.ShapeDtypeStruct(s, BF) for s in shapes),
        in_specs=[ANY] * 4 + [VM] + [ANY] * 6 + [VM] + [ANY] * 7,
        out_specs=(ANY, ANY, VM) + (ANY,) * 12,
        scratch_shapes=[
            pltpu.VMEM((SLOTS, CH, width), BF),
            pltpu.VMEM((SLOTS, CH, width), BF),
            pltpu.VMEM((COUNT[QKV], QR, 512), BF),
            pltpu.VMEM((COUNT[QKV], QR, 512), BF),
            pltpu.VMEM((RING, CH, width), BF),
            pltpu.VMEM((RING, CH, width), BF),
            DMA((2, RING)),
            pltpu.SemaphoreType.REGULAR,
            pltpu.SemaphoreType.REGULAR,
            pltpu.VMEM((8 * rows, width), BF),
            pltpu.VMEM((2, width, 256), BF),
            DMA((2,)),
            DMA((2, 2)),
            DMA((2, 1)),
            DMA((2,)),
            DMA((2,)),
            DMA((2,)),
            pltpu.VMEM((4, 8, width), F32),
            pltpu.VMEM((3, 8, width), F32),
            pltpu.VMEM((nz, 8, width), F32),
            DMA((nz + 3,)),
            DMA((nz + 3,)),
            pltpu.VMEM((rows, width), BF),
            pltpu.VMEM((rows, width), BF),
            pltpu.VMEM((rows, width), F32),
            pltpu.VMEM((rows, width), F32),
            pltpu.VMEM((hd, width), F32),
            pltpu.VMEM((width, 2 * hd), F32),
            pltpu.VMEM((hd, width), BF),
            pltpu.VMEM((width, 2 * hd), BF),
            pltpu.VMEM((hd, width), BF),
            DMA((6,)),
            pltpu.SemaphoreType.REGULAR,
        ]
        + scatter_scratch(rows, width)
        + GATHER_SEMS
        + [wide, sq, sq, sq, sq]
        + [pltpu.VMEM((2, rows, rows), F32), pltpu.VMEM((2, rows, hd), F32), wide]
        + [pltpu.VMEM((8, rows, hd), BF)] * 2
        + [pltpu.VMEM((2, rows, hd), F32), sq, wide]
        + [DMA((8, 2)), DMA((8,)), DMA((8,)), DMA((2,))]
        + CHAIN_SEMS * 2,
        compiler_params=params(2, 63),
        name="tail",
    )(part, x, h, g, gains, hid, g_all, xn2, dgu, wd, wo, wqkv, *heads, xn1)


def widen_kernel(*refs):
    n = len(refs) // 2
    for a, b in zip(refs[:n], refs[n:], strict=True):
        b[...] = a[...].astype(b.dtype)


def widen(arrays, kept):
    shapes = [jax.ShapeDtypeStruct(a.shape, F32) for a in arrays]
    shapes += [jax.ShapeDtypeStruct(a.shape, a.dtype) for a in kept]
    arrays = (*arrays, *kept)
    steps = 8

    def spec(a):
        return pl.BlockSpec((a.shape[0] // steps, a.shape[1]), lambda i: (i, 0))

    return pl.pallas_call(
        widen_kernel,
        grid=(steps,),
        out_shape=tuple(shapes),
        in_specs=[spec(a) for a in arrays],
        out_specs=tuple(spec(a) for a in arrays),
        compiler_params=pltpu.CompilerParams(vmem_limit_bytes=62 * 2**20),
        name="widen",
    )(*arrays)


def pieces(
    tokens,
    segment_ids,
    attn_gain,
    w_query,
    w_key,
    w_value,
    w_out,
    mlp_gain,
    w_gate,
    w_up,
    w_down,
    cotangent,
):
    rows, width = tokens.shape[1], tokens.shape[2]
    ns = lax.axis_size("shard")
    hd = HEAD_DIM
    ff = w_gate.shape[1]
    part = width // ns

    x = tokens.reshape(rows, width)
    g = cotangent.reshape(rows, width)
    gains = jnp.concatenate([attn_gain[None], mlp_gain[None], jnp.zeros((6, part), BF)], 0).astype(F32)
    half = np.arange(hd // 2, dtype=np.float64) * 2.0 / hd
    freq = jnp.asarray((rope_base ** -half).astype(np.float32)[None])
    h, xn2, g_all, _, gains, _, wqkv, xn1, q, k, v, attn, probs, turn, hid, dgu, dxpart = front(
        x, segment_ids, gains, freq, w_query, w_key, w_value, w_out, w_gate, w_up, w_down, g
    )
    heads = (q, k, v, attn, probs, turn)
    output, input_grad, gain_g, _, _, _, _, _, gate_g, up_g, down_g, out_g, wq_g, wk_g, wv_g = tail(
        dxpart,
        x,
        h,
        g,
        gains,
        hid,
        g_all,
        xn2,
        dgu,
        w_down,
        w_out,
        wqkv,
        heads,
        xn1,
        ff,
    )
    gain_g = lax.dynamic_slice_in_dim(gain_g, lax.axis_index("shard") * part, part, 1)
    wide = widen((wq_g, wk_g, wv_g, out_g, gate_g, up_g, down_g), (output, input_grad))
    output, input_grad = (a.reshape(1, rows, width) for a in wide[7:])
    return (output, input_grad, gain_g[0], *wide[:4], gain_g[1], *wide[4:7])


def contract_rows(left, right):
    return lax.dot_general(
        left, right, (((0,), (0,)), ((), ())), preferred_element_type=jnp.float32
    )


def contract_cols(left, right):
    return lax.dot_general(
        left, right, (((1,), (1,)), ((), ())), preferred_element_type=jnp.float32
    )


def scores_of(queries, keys, allowed):
    raw = jnp.einsum(
        "qgrd,kgd->grqk", queries, keys, preferred_element_type=jnp.float32
    ) * HEAD_DIM ** (-0.5)
    return jnp.where(allowed, raw, mask_fill)


def general(
    tokens,
    segment_ids,
    attn_gain,
    w_query,
    w_key,
    w_value,
    w_out,
    mlp_gain,
    w_gate,
    w_up,
    w_down,
    cotangent,
):
    rows = tokens.shape[1]
    width = tokens.shape[2]
    groups = HEADS // KV_HEADS
    q_cols = HEADS * HEAD_DIM
    kv_cols = KV_HEADS * HEAD_DIM
    layer_input_rows = tokens.reshape(rows, width).astype(jnp.float32)
    segments = segment_ids.reshape(rows)
    iota = jnp.arange(rows, dtype=jnp.int32)
    starts = jnp.sum((segments[None, :] < segments[:, None]).astype(jnp.int32), axis=1)
    positions = (iota - starts).astype(jnp.float32)
    allowed = (segments[:, None] == segments[None, :]) & (iota[:, None] >= iota[None, :])
    half = HEAD_DIM // 2
    inv_freq = rope_base ** (-(jnp.arange(half, dtype=jnp.float32) * 2.0 / HEAD_DIM))
    angles = positions[:, None] * inv_freq
    cosine = jnp.cos(angles)
    sine = jnp.sin(angles)
    first_norm_factor = lax.rsqrt(
        jnp.mean(layer_input_rows * layer_input_rows, axis=1, keepdims=True) + norm_eps
    )
    first_standardized = layer_input_rows * first_norm_factor
    gain_fragment = lax.all_gather(attn_gain, "shard", axis=0, tiled=True)
    query_piece = lax.all_gather(w_query, "shard", axis=0, tiled=True)
    key_piece = lax.all_gather(w_key, "shard", axis=0, tiled=True)
    value_piece = lax.all_gather(w_value, "shard", axis=0, tiled=True)
    normalized_rows = (first_standardized * gain_fragment.astype(jnp.float32)).astype(jnp.bfloat16)
    joined = jnp.concatenate([query_piece, key_piece, value_piece], 1)
    result = (
        jnp.dot(normalized_rows, joined, preferred_element_type=jnp.float32),
        normalized_rows,
        gain_fragment.astype(jnp.float32),
    )
    folded = result
    projected, normed_one, first_norm_gain = (folded[0], folded[1], folded[2])
    queries = rotate(
        projected[:, :q_cols].reshape(rows, KV_HEADS, groups, HEAD_DIM),
        cosine[:, None, None, :],
        sine[:, None, None, :],
    ).astype(jnp.bfloat16)
    keys = rotate(
        projected[:, q_cols : q_cols + kv_cols].reshape(rows, KV_HEADS, HEAD_DIM),
        cosine[:, None, :],
        sine[:, None, :],
    ).astype(jnp.bfloat16)
    values = projected[:, q_cols + kv_cols :].reshape(rows, KV_HEADS, HEAD_DIM).astype(jnp.bfloat16)
    scores = scores_of(queries, keys, allowed)
    top = jnp.max(scores, axis=-1, keepdims=True)
    log_total = top + jnp.log(jnp.sum(jnp.exp(scores - top), axis=-1, keepdims=True))
    probs = jnp.exp(scores - log_total)
    probs_low = probs.astype(jnp.bfloat16)
    attn = (
        jnp.einsum("grqk,kgd->qgrd", probs_low, values, preferred_element_type=jnp.float32)
        .reshape(rows, q_cols)
        .astype(jnp.bfloat16)
    )
    part = attn
    result = (
        jnp.dot(
            part,
            lax.all_gather(w_out, "shard", axis=0, tiled=True),
            preferred_element_type=jnp.float32,
        ),
    )
    folded_out = result
    residual_hidden_state = layer_input_rows + folded_out[0]
    second_norm_factor = lax.rsqrt(
        jnp.mean(residual_hidden_state * residual_hidden_state, axis=1, keepdims=True) + norm_eps
    )
    second_standardized = residual_hidden_state * second_norm_factor
    gain_fragment = lax.all_gather(mlp_gain, "shard", axis=0, tiled=True)
    gate_piece = lax.all_gather(w_gate, "shard", axis=0, tiled=True)
    up_piece = lax.all_gather(w_up, "shard", axis=0, tiled=True)
    normalized_rows = (second_standardized * gain_fragment.astype(jnp.float32)).astype(jnp.bfloat16)
    joined = jnp.concatenate([gate_piece, up_piece], 1)
    result = (
        jnp.dot(normalized_rows, joined, preferred_element_type=jnp.float32),
        normalized_rows,
        gain_fragment.astype(jnp.float32),
    )
    folded_mlp = result
    gate = folded_mlp[0][:, :FF]
    up_value = folded_mlp[0][:, FF:]
    normed_two = folded_mlp[1]
    second_norm_gain = folded_mlp[2]
    sigma = jax.nn.sigmoid(gate)
    swish = gate * sigma
    inner = (swish * up_value).astype(jnp.bfloat16)
    part = inner
    result = (
        jnp.dot(
            part,
            lax.all_gather(w_down, "shard", axis=0, tiled=True),
            preferred_element_type=jnp.float32,
        ),
    )
    output = (residual_hidden_state + result[0]).astype(jnp.bfloat16).reshape(1, rows, width)
    grad_out = cotangent.reshape(rows, width)
    grad_down = lax.psum_scatter(
        contract_rows(inner, grad_out).astype(jnp.bfloat16),
        "shard",
        scatter_dimension=0,
        tiled=True,
    )
    down_full, gate_full, up_full = (
        lax.all_gather(w_down, "shard", axis=0, tiled=True),
        lax.all_gather(w_gate, "shard", axis=0, tiled=True),
        lax.all_gather(w_up, "shard", axis=0, tiled=True),
    )
    grad_inner = contract_cols(grad_out, down_full)
    grad_gate = (grad_inner * up_value * sigma * (1.0 + gate * (1.0 - sigma))).astype(jnp.bfloat16)
    grad_up = (grad_inner * swish).astype(jnp.bfloat16)
    grad_mlp = jnp.concatenate([grad_gate, grad_up], 1)
    mlp_shards = lax.psum_scatter(
        contract_rows(normed_two, grad_mlp).astype(jnp.bfloat16),
        "shard",
        scatter_dimension=0,
        tiled=True,
    ).astype(jnp.float32)
    second_norm_gradient = contract_cols(grad_gate, gate_full) + contract_cols(grad_up, up_full)
    second_gain_products = jnp.sum(second_norm_gradient * second_standardized, axis=0)
    hidden_gradient = grad_out.astype(jnp.float32) + norm_backward_step(
        second_norm_gradient * second_norm_gain, second_standardized, second_norm_factor
    )
    grad_hidden_low = hidden_gradient.astype(jnp.bfloat16)
    grad_out_proj = lax.psum_scatter(
        contract_rows(attn, grad_hidden_low).astype(jnp.bfloat16),
        "shard",
        scatter_dimension=0,
        tiled=True,
    )
    grad_attn = contract_cols(grad_hidden_low, lax.all_gather(w_out, "shard", axis=0, tiled=True))
    grad_attn = grad_attn.astype(jnp.bfloat16).reshape(rows, KV_HEADS, groups, HEAD_DIM)
    scores_again = scores_of(queries, keys, allowed)
    probs_again = jnp.exp(scores_again - log_total)
    probs_again_low = probs_again.astype(jnp.bfloat16)
    grad_probs = jnp.einsum("qgrd,kgd->grqk", grad_attn, values, preferred_element_type=jnp.float32)
    grad_values = jnp.einsum(
        "grqk,qgrd->kgd", probs_again_low, grad_attn, preferred_element_type=jnp.float32
    )
    grad_scores = (
        probs_again * (grad_probs - jnp.sum(grad_probs * probs_again, axis=-1, keepdims=True))
    ).astype(jnp.bfloat16)
    grad_queries = jnp.einsum(
        "grqk,kgd->qgrd", grad_scores, keys, preferred_element_type=jnp.float32
    ) * HEAD_DIM ** (-0.5)
    grad_keys = jnp.einsum(
        "grqk,qgrd->kgd", grad_scores, queries, preferred_element_type=jnp.float32
    ) * HEAD_DIM ** (-0.5)
    grad_queries = rotate(grad_queries, cosine[:, None, None, :], -sine[:, None, None, :]).reshape(
        rows, q_cols
    )
    grad_keys = rotate(grad_keys, cosine[:, None, :], -sine[:, None, :]).reshape(rows, kv_cols)
    grad_joined = jnp.concatenate(
        [
            grad_queries.astype(jnp.bfloat16),
            grad_keys.astype(jnp.bfloat16),
            grad_values.reshape(rows, kv_cols).astype(jnp.bfloat16),
        ],
        1,
    )
    qkv_shards = lax.psum_scatter(
        contract_rows(normed_one, grad_joined).astype(jnp.bfloat16),
        "shard",
        scatter_dimension=0,
        tiled=True,
    ).astype(jnp.float32)
    local_qkv = jnp.concatenate([w_query, w_key, w_value], 1)
    first_norm_gradient = contract_cols(
        grad_joined, lax.all_gather(local_qkv, "shard", axis=0, tiled=True)
    )
    first_gain_products = jnp.sum(first_norm_gradient * first_standardized, axis=0)
    input_gradient_rows = hidden_gradient + norm_backward_step(
        first_norm_gradient * first_norm_gain, first_standardized, first_norm_factor
    )
    input_grad = input_gradient_rows.astype(jnp.bfloat16).reshape(1, rows, width)
    gain_one_grad, gain_two_grad = (
        lax.psum_scatter(first_gain_products, "shard", scatter_dimension=0, tiled=True),
        lax.psum_scatter(second_gain_products, "shard", scatter_dimension=0, tiled=True),
    )
    summed = (
        lax.psum(gain_one_grad.astype(jnp.bfloat16), "rep").astype(jnp.float32),
        lax.psum(qkv_shards[:, :q_cols].astype(jnp.bfloat16), "rep").astype(jnp.float32),
        lax.psum(qkv_shards[:, q_cols : q_cols + kv_cols].astype(jnp.bfloat16), "rep").astype(
            jnp.float32
        ),
        lax.psum(qkv_shards[:, q_cols + kv_cols :].astype(jnp.bfloat16), "rep").astype(jnp.float32),
        lax.psum(grad_out_proj, "rep").astype(jnp.float32),
        lax.psum(gain_two_grad.astype(jnp.bfloat16), "rep").astype(jnp.float32),
        lax.psum(mlp_shards[:, :FF].astype(jnp.bfloat16), "rep").astype(jnp.float32),
        lax.psum(mlp_shards[:, FF:].astype(jnp.bfloat16), "rep").astype(jnp.float32),
        lax.psum(grad_down, "rep").astype(jnp.float32),
    )
    return (
        output,
        input_grad,
        summed[0],
        summed[1],
        summed[2],
        summed[3],
        summed[4],
        summed[5],
        summed[6],
        summed[7],
        summed[8],
    )


def solution(mesh):
    rep, shard = mesh.devices.shape
    if shard == KV_HEADS and rep % 2 == 0:
        fine = Mesh(np.asarray(mesh.devices).reshape(rep // 2, 2, shard), ("z", "core", "shard"))
        body, every = pieces, ("z", "core", "shard")
    else:
        fine, body, every = mesh, general, ("rep", "shard")
    seqs, vec, mat = P(every, None, None), P("shard"), P("shard", None)
    in_specs = (seqs, P(every, None), vec, mat, mat, mat, mat, vec, mat, mat, mat, seqs)
    out_specs = (seqs, seqs, vec, mat, mat, mat, mat, vec, mat, mat, mat)
    return jax.shard_map(body, mesh=fine, in_specs=in_specs, out_specs=out_specs, check_vma=False)
```

```python
import functools

import jax
import jax.numpy as jnp
import numpy as np
from jax import lax
from jax.experimental import pallas as pl
from jax.experimental.pallas import tpu as pltpu
from jax.sharding import Mesh
from jax.sharding import PartitionSpec as P

HEADS = 8
KV_HEADS = 4
HEAD_DIM = 256
FF = 8192

rope_base = 1000042.0
norm_eps = 1e-06
mask_fill = -1e30

BF = jnp.bfloat16
F32 = jnp.float32
MESH = pl.DeviceIdType.MESH
ANY = pl.BlockSpec(memory_space=pl.ANY)
VM = pl.BlockSpec(memory_space=pltpu.VMEM)
DMA = pltpu.SemaphoreType.DMA


def mm(a, b):
    return jnp.dot(a, b, preferred_element_type=F32)


def mm_tn(a, b):
    return lax.dot_general(a, b, (((0,), (0,)), ((), ())), preferred_element_type=F32)


def mm_nt(a, b):
    return lax.dot_general(a, b, (((1,), (1,)), ((), ())), preferred_element_type=F32)


def rotate(values, cosine, sine):
    half = values.shape[-1] // 2
    first = values[..., :half]
    second = values[..., half:]
    return jnp.concatenate([first * cosine - second * sine, second * cosine + first * sine], -1)


def norm_backward_step(grad_hat, normalized_rows, factor):
    return factor * (
        grad_hat - normalized_rows * jnp.mean(grad_hat * normalized_rows, axis=1, keepdims=True)
    )


class Place:
    def __init__(self):
        self.z = lax.axis_index("z")
        self.c = lax.axis_index("core")
        self.s = lax.axis_index("shard")

    def shard(self, d):
        s = self.s
        if d == 0:
            return s
        if d == 1:
            return s + 1 - 2 * lax.rem(s, 2)
        if d == 2:
            return lax.rem(s + 2, 4)
        return 3 - s

    def shard_at(self, d):
        s = self.s
        one = s + 1 - 2 * lax.rem(s, 2)
        two = lax.rem(s + 2, 4)
        return jnp.where(d == 0, s, jnp.where(d == 1, one, jnp.where(d == 2, two, 3 - s)))

    def to(self, d):
        return {"shard": self.shard(d)}

    def sibling(self):
        return {"core": 1 - self.c}


def greet(ids):
    barrier = pltpu.get_barrier_semaphore()
    for d in ids:
        pl.semaphore_signal(barrier, inc=1, device_id=d, device_id_type=MESH)
    pl.semaphore_wait(barrier, len(ids))


def rcopy(src, dst, send, recv, dev):
    return pltpu.make_async_remote_copy(
        src_ref=src, dst_ref=dst, send_sem=send, recv_sem=recv, device_id=dev, device_id_type=MESH
    )


GATHER_SEMS = [DMA((6,)), DMA((6,)), DMA((7,)), DMA((7,)), DMA((1,))]


class Gather:
    def __init__(self, p, src, out, sems):
        self.p, self.src, self.out = p, src, out
        self.send, self.recv, self.csend, self.crecv, self.lsem = sems
        self.rows = src.shape[0]
        self.half = self.rows // 2

    def at(self, d, h, core=None):
        core = self.p.c if core is None else core
        row = (core * 4 + self.p.shard(d)) * self.rows
        if h is None:
            return self.out.at[pl.ds(row, self.rows)]
        return self.out.at[pl.ds(row + h * self.half, self.half)]

    def move(self, k):
        d, h, to = [(0, 0, 1), (0, 1, 2), (0, 1, 1), (0, 0, 2), (1, 0, 2), (2, 1, 1)][k]
        dst = self.at(d, h)
        src = self.src.at[pl.ds(h * self.half, self.half)] if d == 0 else dst
        return rcopy(src, dst, self.send.at[k], self.recv.at[k], self.p.to(to))

    def landed(self, k):
        d, h = [(1, 0), (2, 1), (1, 1), (2, 0), (3, 0), (3, 1)][k]
        return self.at(d, h)

    def pass_on(self, k):
        here = self.src if k == 6 else self.landed(k)
        there = self.at(0, None) if k == 6 else self.landed(k)
        return rcopy(here, there, self.csend.at[k], self.crecv.at[k], self.p.sibling())

    def arrived(self, k):
        ref = self.landed(k)
        rcopy(ref, ref, self.send.at[k], self.recv.at[k], self.p.to(1)).wait_recv()
        self.pass_on(k).start()

    def start(self):
        for k in range(4):
            self.move(k).start()
        self.pass_on(6).start()
        pltpu.make_async_copy(self.src, self.at(0, None), self.lsem.at[0]).start()

    def relay(self):
        for k in (0, 1):
            self.arrived(k)
            self.move(4 + k).start()

    def early(self):
        for k in (2, 3):
            self.arrived(k)

    def late(self):
        for k in (4, 5):
            self.arrived(k)

    def both(self, ks):
        for k in ks:
            self.pass_on(k).wait_recv()

    def home(self):
        self.both((6,))
        pltpu.make_async_copy(self.src, self.at(0, None), self.lsem.at[0]).wait()

    def close(self):
        for k in range(6):
            self.move(k).wait_send()
        for k in range(7):
            self.pass_on(k).wait_send()

    def finish(self, early=False):
        if not early:
            self.early()
        self.late()
        self.both(range(7))
        pltpu.make_async_copy(self.src, self.at(0, None), self.lsem.at[0]).wait()
        self.close()


SCATTER_SEMS = [DMA((4,)), DMA((4,)), DMA((4,)), DMA((6,)), DMA((6,))]
ORDER = (3, 1, 2, 0)


def scatter_scratch(rows, width):
    half = rows // 2
    return [
        pltpu.VMEM((4, rows, width), BF),
        pltpu.VMEM((4, rows, width), BF),
        pltpu.VMEM((6, half, width), BF),
    ] + SCATTER_SEMS


class Scatter:
    def __init__(self, p, part, scratch):
        self.p, self.part = p, part
        self.own, self.got, self.slot, self.lsem, self.csend, self.crecv, self.send, self.recv = scratch
        self.rows = self.own.shape[1]
        self.half = self.rows // 2

    def block(self, core, d):
        return self.part.at[pl.ds((core * 4 + self.p.shard(d)) * self.rows, self.rows)]

    def local(self, d):
        return pltpu.make_async_copy(self.block(self.p.c, d), self.own.at[d], self.lsem.at[d])

    def swap(self, d):
        src = self.block(1 - self.p.c, d)
        return rcopy(src, self.got.at[d], self.csend.at[d], self.crecv.at[d], self.p.sibling())

    def rowsof(self, h):
        return pl.ds(h * self.half, self.half)

    def move(self, k):
        d, h, to = [(3, 0, 1), (3, 1, 2), (1, 0, 1), (2, 1, 2), (2, 0, 2), (1, 1, 1)][k]
        return rcopy(
            self.own.at[d, self.rowsof(h)], self.slot.at[k], self.send.at[k], self.recv.at[k], self.p.to(to)
        )

    def start(self):
        for d in ORDER:
            self.swap(d).start()
            self.local(d).start()

    def pair(self, d):
        self.swap(d).wait_recv()
        self.local(d).wait()
        self.own[d] = (self.own[d].astype(F32) + self.got[d].astype(F32)).astype(BF)

    def first(self, k):
        self.pair(ORDER[k])
        for m in ((0, 1), (2,), (3,), ())[k]:
            self.move(m).start()

    def relay(self):
        for k, d, h in ((0, 2, 0), (1, 1, 1)):
            self.move(k).wait_recv()
            r = self.rowsof(h)
            self.own[d, r] = (self.own[d, r].astype(F32) + self.slot[k].astype(F32)).astype(BF)
            self.move(4 + k).start()

    def total(self, h):
        near, far = (2, 4) if h == 0 else (3, 5)
        self.move(near).wait_recv()
        self.move(far).wait_recv()
        return (
            self.own[0, self.rowsof(h)].astype(F32)
            + self.slot[near].astype(F32)
            + self.slot[far].astype(F32)
        )

    def drain(self):
        for k in range(6):
            self.move(k).wait_send()
        for d in range(4):
            self.swap(d).wait_send()


def params(cid, mb):
    return pltpu.CompilerParams(
        collective_id=cid, has_side_effects=True, vmem_limit_bytes=mb * 2**20
    )


def plane_ids(p):
    return [p.to(1), p.to(2), p.to(3), p.sibling()]


class Columns:
    def __init__(self, p, sems):
        self.p = p
        self.send, self.recv, self.lsem = sems

    def cols(self, j, d, src, width):
        return src.at[:, pl.ds(pl.multiple_of(j * width, width), width)]

    def copy(self, k, d, src, dst):
        if d == 0:
            return pltpu.make_async_copy(src, dst, self.lsem.at[k])
        return rcopy(src, dst, self.send.at[k, d - 1], self.recv.at[k, d - 1], self.p.to(d))


def rows_at(ref, r, n, c0, width):
    return ref.at[pl.ds(r, n), pl.ds(c0, width)]


def greet_line(p, ids):
    barrier = pltpu.get_barrier_semaphore()
    nz = lax.axis_size("z")
    for d in ids:
        pl.semaphore_signal(barrier, inc=1, device_id=d, device_id_type=MESH)

    @pl.when(p.z > 0)
    def _():
        pl.semaphore_signal(barrier, inc=1, device_id={"z": p.z - 1}, device_id_type=MESH)

    @pl.when(p.z < nz - 1)
    def _():
        pl.semaphore_signal(barrier, inc=1, device_id={"z": p.z + 1}, device_id_type=MESH)

    ends = jnp.where(p.z == 0, 1, 0) + jnp.where(p.z == nz - 1, 1, 0)
    pl.semaphore_wait(barrier, len(ids) + 2 - ends)


def relay_sems(nz):
    return [DMA((3,)), DMA((3,)), DMA((1,)), DMA((2, nz, 3)), DMA((nz, 3))]


class Relay:
    def __init__(self, p, w, dst, c0, sems):
        self.p, self.w, self.dst, self.c0 = p, w, dst, c0
        self.xs, self.xr, self.ls, self.zs, self.zr = sems
        self.nz = lax.axis_size("z")
        self.part = w.shape[0]
        self.n = self.part // self.nz
        self.fb = w.shape[1] // 8

    def cols(self, d):
        return pl.ds(pl.multiple_of((self.p.shard(d) * 2 + self.p.c) * self.fb, self.fb), self.fb)

    def rows(self, d, q):
        return self.dst.at[pl.ds(self.p.shard(d) * self.part + q * self.n, self.n), pl.ds(self.c0, self.fb)]

    def fetch(self, d):
        src = self.w.at[pl.ds(self.p.z * self.n, self.n), self.cols(d)]
        return rcopy(src, self.rows(0, self.p.z), self.xs.at[d - 1], self.xr.at[d - 1], self.p.to(d))

    def local(self):
        dst = self.dst.at[pl.ds(self.p.s * self.part, self.part), pl.ds(self.c0, self.fb)]
        return pltpu.make_async_copy(self.w.at[:, self.cols(0)], dst, self.ls.at[0])

    def along(self, way, q, d):
        ref = self.rows(d, q)
        to = {"z": self.p.z + (1 if way else -1)}
        return rcopy(ref, ref, self.zs.at[way, q, d - 1], self.zr.at[q, d - 1], to)

    def start(self):
        for d in (3, 1, 2):
            self.fetch(d).start()
        self.local().start()

    def can(self, way):
        return self.p.z < self.nz - 1 if way else self.p.z > 0

    def own(self):
        for d in (1, 2, 3):
            self.fetch(d).wait_recv()
        for way in (0, 1):

            @pl.when(self.can(way))
            def _():
                for d in (1, 2, 3):
                    self.along(way, self.p.z, d).start()

    def hop(self, k):
        for way in (0, 1):
            q = self.p.z - k if way else self.p.z + k
            there = q >= 0 if way else q < self.nz

            @pl.when(there)
            def _():
                for d in (1, 2, 3):
                    self.along(way, q, d).wait_recv()

            @pl.when(jnp.logical_and(there, self.can(way)))
            def _():
                for d in (1, 2, 3):
                    self.along(way, q, d).start()

    def finish(self):
        for d in (1, 2, 3):
            self.fetch(d).wait_send()
        for k in range(self.nz):
            for way in (0, 1):
                q = self.p.z - k if way else self.p.z + k
                there = q >= 0 if way else q < self.nz

                @pl.when(jnp.logical_and(there, self.can(way)))
                def _():
                    for d in (1, 2, 3):
                        self.along(way, q, d).wait_send()


class Forward:
    def __init__(self, p, xa, xn1, wqkv, wo, seg, gain, freq, sc, ob, bufs, sems):
        self.p, self.xa, self.xn1 = p, xa, xn1
        self.wqkv, self.wo, self.seg, self.gain, self.freq = wqkv, wo, seg, gain, freq
        self.sc, self.ob = sc, ob
        self.xb, self.nb, self.q, self.k, self.v, self.attn, self.probs, self.turn, self.kept, self.came = bufs
        self.xsem, self.nsem, self.send, self.recv = sems
        self.n = self.xb.shape[1]

    def block(self, i):
        return lax.rem(i, 2) * 4 + self.p.shard_at(i // 2)

    def rows(self, ref, i):
        return ref.at[pl.ds(self.block(i) * self.n, self.n)]

    def load(self, i):
        b = lax.rem(i, 2)
        return pltpu.make_async_copy(self.rows(self.xa, i), self.xb.at[b], self.xsem.at[b])

    def store(self, i):
        b = lax.rem(i, 2)
        return pltpu.make_async_copy(self.nb.at[b], self.rows(self.xn1, i), self.nsem.at[b])

    def swap(self, i):
        return rcopy(self.kept.at[i], self.came.at[i], self.send.at[i], self.recv.at[i], self.p.sibling())

    def seg_of(self, i):
        row = self.seg[self.block(i)]
        return row[0:1], row.T[:, 0:1]

    def first(self, i):
        b, k = lax.rem(i, 2), self.block(i)
        self.load(i).wait()

        @pl.when(i >= 2)
        def _():
            self.store(i - 2).wait()

        x = self.xb[b].astype(F32)
        f = lax.rsqrt(jnp.mean(x * x, axis=1, keepdims=True) + norm_eps)
        xn = (x * f * self.gain).astype(BF)
        self.nb[b] = xn
        self.store(i).start()
        lin = mm(xn, self.wqkv[...])
        row, col = self.seg_of(i)
        start = jnp.sum((row < col).astype(F32), axis=1, keepdims=True)
        at = lax.broadcasted_iota(jnp.int32, (self.n, 1), 0).astype(F32)
        angle = (at - start) * self.freq
        cosine, sine = jnp.cos(angle), jnp.sin(angle)
        self.turn[k] = jnp.concatenate([cosine, sine], -1)
        hd = HEAD_DIM
        self.q[k] = rotate(lin[:, :hd], cosine, sine).astype(BF)
        kv = lin[:, hd:]
        self.kept[i] = jnp.where(self.p.c == 0, rotate(kv, cosine, sine), kv).astype(BF)
        self.swap(i).start()

    def second(self, i):
        n, k = self.n, self.block(i)
        self.swap(i).wait()
        mine, came = self.kept[i], self.came[i]
        key = jnp.where(self.p.c == 0, mine, came)
        value = jnp.where(self.p.c == 0, came, mine)
        self.k[k], self.v[k] = key, value
        row, col = self.seg_of(i)
        down = lax.broadcasted_iota(jnp.int32, (n, n), 0)
        over = lax.broadcasted_iota(jnp.int32, (n, n), 1)
        allowed = jnp.logical_and(row == col, down >= over)
        scores = jnp.where(allowed, mm_nt(self.q[k], key) * HEAD_DIM ** (-0.5), mask_fill)
        ex = jnp.exp(scores - jnp.max(scores, axis=-1, keepdims=True))
        probs = ex / jnp.sum(ex, axis=-1, keepdims=True)
        self.probs[k] = probs
        attn = mm(probs.astype(BF), value).astype(BF)
        self.attn[k] = attn
        term = mm(attn, self.wo[...]).astype(BF)
        d = i // 2
        mine_too = lax.rem(i, 2) == self.p.c

        @pl.when(mine_too)
        def _():
            self.sc.own[d] = term

        @pl.when(jnp.logical_not(mine_too))
        def _():
            self.ob[d] = term
            self.sc.swap(d).start()

    def finish(self):
        self.store(6).wait()
        self.store(7).wait()


class MadeScatter(Scatter):
    def __init__(self, p, made, scratch):
        super().__init__(p, None, scratch)
        self.made = made

    def swap(self, d):
        return rcopy(self.made.at[d], self.got.at[d], self.csend.at[d], self.crecv.at[d], self.p.sibling())

    def pair(self, d):
        self.swap(d).wait_recv()
        self.own[d] = (self.own[d].astype(F32) + self.got[d].astype(F32)).astype(BF)


class Feed:
    def __init__(self, p, block, xn2, g, wgu, wd, outs, bufs, sems):
        self.p, self.block = p, block
        self.xn2, self.g, self.wgu, self.wd, self.outs = xn2, g, wgu, wd, outs
        self.xb, self.gb, self.made, self.got = bufs
        self.xsem, self.gsem, self.osem = sems
        self.n = self.xb.shape[1]
        self.fb = wd.shape[0]

    def rows(self, ref, i):
        return ref.at[pl.ds(self.block(i) * self.n, self.n)]

    def loads(self, i):
        b = lax.rem(i, 2)
        return [
            pltpu.make_async_copy(self.rows(self.xn2, i), self.xb.at[b], self.xsem.at[b]),
            pltpu.make_async_copy(self.rows(self.g, i), self.gb.at[b], self.gsem.at[b]),
        ]

    def stores(self, i):
        b = lax.rem(i, 2)
        srcs = (self.got.at[2 + b, :, pl.ds(0, self.fb)], self.made.at[b], self.got.at[b])
        return [
            pltpu.make_async_copy(src, self.rows(out, i), self.osem.at[j, b])
            for j, (src, out) in enumerate(zip(srcs, self.outs, strict=True))
        ]

    def step(self, i):
        b, fb = lax.rem(i, 2), self.fb
        for cp in self.loads(i):
            cp.wait()

        @pl.when(i >= 2)
        def _():
            for cp in self.stores(i - 2):
                cp.wait()

        xn, g = self.xb[b], self.gb[b]
        gate, up = mm(xn, self.wgu[:, :fb]), mm(xn, self.wgu[:, fb:])
        sigma = jax.nn.sigmoid(gate)
        swish = gate * sigma
        hid = (swish * up).astype(BF)
        self.got[2 + b, :, :fb] = hid
        dhid = mm_nt(g, self.wd[...])
        dgate = (dhid * up * sigma * (1.0 + gate * (1.0 - sigma))).astype(BF)
        dup = (dhid * swish).astype(BF)
        self.made[b, :, :fb] = dgate
        self.made[b, :, fb:] = dup
        self.got[b] = mm_nt(self.made[b], self.wgu[...]).astype(BF)
        for cp in self.stores(i):
            cp.start()

    def finish(self):
        for i in (6, 7):
            for cp in self.stores(i):
                cp.wait()


def front_kernel(
    x_ref, seg_ref, gain_ref, freq_ref, wq_ref, wk_ref, wv_ref, wo_hbm, wg_ref, wu_ref, wd_hbm, g_ref,
    h_ref, xn2_ref, ga_ref, wgu_ref, gains_ref, xa_ref, wqkv_ref, xn1_ref, q_ref, k_ref, v_ref,
    attn_ref, probs_ref, turn_ref, hid_ref, dgu_ref, dx_ref, *scr
):
    p = Place()
    nz = lax.axis_size("z")
    others = [(0, 1)] + [(d, o) for d in (1, 2, 3) for o in (0, 1)]

    def dev(d, o):
        return {"core": 1 - p.c if o else p.c, "shard": p.shard(d)}

    scr = list(scr)

    def take(n):
        out = scr[:n]
        del scr[:n]
        return out

    ga = Gather(p, x_ref, xa_ref, take(5))
    gg = Gather(p, g_ref, ga_ref, take(5))
    [xnb] = take(1)
    gx = Gather(p, xnb, xn2_ref, take(5))
    co = Columns(p, take(3))
    tsend, trecv, tlocal = take(3)
    fb = wgu_ref.shape[1] // 2
    re = [Relay(p, wg_ref, wgu_ref, 0, take(5)), Relay(p, wu_ref, wgu_ref, fb, take(5))]
    [made] = take(1)
    sc = MadeScatter(p, made, take(8))
    wqkv, wo, seg, seg8, gaina_ref, lsem = take(6)
    bufs, sems = take(10), take(4)
    [osem] = take(1)
    wgu, wd, gsem, fsem = take(4)
    part, hd = wq_ref.shape[0], HEAD_DIM

    load_wo = pltpu.make_async_copy(wo_hbm.at[pl.ds(p.c * hd, hd)], wo, lsem.at[0])
    load_wqkv = pltpu.make_async_copy(wqkv_ref, wqkv, lsem.at[1])
    load_wd = pltpu.make_async_copy(wd_hbm.at[pl.ds(p.c * fb, fb)], wd, lsem.at[2])
    load_wgu = pltpu.make_async_copy(wgu_ref, wgu, lsem.at[3])
    load_wo.start()
    load_wd.start()
    seg8[...] = jnp.broadcast_to(seg_ref[...].astype(F32), seg8.shape)
    greet_line(p, [dev(d, o) for d, o in others])

    def q_copy(d):
        src = co.cols(p.shard(d) * 2 + p.c, d, wq_ref, hd)
        return co.copy(0, d, src, rows_at(wqkv_ref, p.s * part, part, 0, hd))

    def kv_copy(d, w):
        src = co.cols(p.shard(d), d, w, hd)
        return co.copy(1, d, src, rows_at(wqkv_ref, p.s * part, part, hd, hd))

    def small(k):
        d, o = others[k]
        yield rcopy(seg8, seg.at[p.c * 4 + p.s], tsend.at[k], trecv.at[k], dev(d, o))
        if d and not o:
            yield rcopy(gain_ref, gaina_ref.at[p.s], tsend.at[7 + d - 1], trecv.at[7 + d - 1], dev(d, o))

    smalls = [cp for k in range(7) for cp in small(k)] + [
        pltpu.make_async_copy(seg8, seg.at[p.c * 4 + p.s], tlocal.at[0]),
        pltpu.make_async_copy(gain_ref, gaina_ref.at[p.s], tlocal.at[1]),
    ]
    for cp in smalls:
        cp.start()
    for d in (3, 1, 2, 0):
        q_copy(d).start()

        @pl.when(p.c == 0)
        def _():
            kv_copy(d, wk_ref).start()

        @pl.when(p.c != 0)
        def _():
            kv_copy(d, wv_ref).start()

    ga.start()
    for cp in smalls:
        cp.wait()
    re[0].start()
    ga.relay()
    for d in (3, 1, 2, 0):
        q_copy(d).wait()
        kv_copy(d, wk_ref).wait()
    load_wqkv.start()
    ga.home()
    load_wo.wait()
    load_wqkv.wait()
    gain1 = jnp.concatenate([gaina_ref[j, 0:1] for j in range(4)], -1)
    gain2 = jnp.concatenate([gaina_ref[j, 1:2] for j in range(4)], -1)
    gains_ref[0:1], gains_ref[1:2] = gain1, gain2
    fw = Forward(p, xa_ref, xn1_ref, wqkv, wo, seg, gain1, freq_ref[...], sc, made, bufs, sems)

    def pair(d):
        sc.pair(d)
        if d == 3:
            sc.move(0).start()
            sc.move(1).start()
        elif d:
            sc.move(1 + d).start()

    def step(i):
        at_tick(i, 1, ga.early)
        at_tick(i, 1, re[1].start)
        at_tick(i, 2, lambda: ga.both((0, 2)))
        at_tick(i, 2, re[0].own)
        at_tick(i, 4, lambda: ga.both((1, 3)))
        at_tick(i, 4, re[1].own)
        at_tick(i, 5, ga.late)
        at_tick(i, 5, gg.start)
        at_tick(i, 6, lambda: ga.both((4, 5)))
        at_tick(i, 5, lambda: re[0].hop(1))
        at_tick(i, 7, lambda: re[1].hop(1))
        at_tick(i, 8, lambda: re[0].hop(2))

        @pl.when(jnp.logical_and(lax.rem(i, 2) == 0, i < 8))
        def _():
            fw.load(i).start()
            fw.load(i + 1).start()

        pl.when(i < 8)(lambda: fw.first(i))
        pl.when(i > 0)(lambda: fw.second(i - 1))
        for d in range(4):
            at_tick(i, 2 * d + 2, functools.partial(pair, d))

    loop(0, 9, step)
    saved = [
        pltpu.make_async_copy(a, b, osem.at[j])
        for j, (a, b) in enumerate(
            zip(bufs[2:8], (q_ref, k_ref, v_ref, attn_ref, probs_ref, turn_ref), strict=True)
        )
    ]
    for cp in saved:
        cp.start()
    gg.relay()
    sc.relay()
    re[1].hop(2)
    half = sc.half
    for h in (0, 1):
        r = pl.ds(h * half, half)
        res = x_ref[r].astype(F32) + sc.total(h)
        h_ref[r] = res
        f = lax.rsqrt(jnp.mean(res * res, axis=1, keepdims=True) + norm_eps)
        xnb[r] = (res * f * gain2).astype(BF)
    gx.start()
    re[0].hop(nz - 1)
    gg.early()
    gg.late()
    re[1].hop(nz - 1)
    for r in re:
        r.local().wait()
    load_wgu.start()
    fw.finish()
    sc.drain()
    load_wd.wait()
    gg.home()
    gx.home()
    gx.relay()
    fd = Feed(
        p, fw.block, xn2_ref, ga_ref, wgu, wd, (hid_ref, dgu_ref, dx_ref),
        (bufs[0], bufs[1], made, sc.got), (sems[0], gsem, fsem),
    )

    for cp in fd.loads(0):
        cp.start()
    load_wgu.wait()

    def feed(i):
        for ks, when in (((0, 2), 1), ((1, 3), 3), ((4, 5), 5)):
            at_tick(i, when, lambda ks=ks: (gx.both(ks), gg.both(ks)))

        @pl.when(i < 7)
        def _():
            for cp in fd.loads(i + 1):
                cp.start()

        fd.step(i)
        at_tick(i, 0, gx.early)
        at_tick(i, 3, gx.late)

    loop(0, 8, feed)
    fd.finish()
    for gather in (ga, gg, gx):
        gather.close()
    for r in re:
        r.finish()
    for cp in saved:
        cp.wait()


def front(x, seg, gains, freq, wq, wk, wv, wo, wg, wu, wd, g):
    rows, width = x.shape
    hd = HEAD_DIM
    fb = wg.shape[1] // 8
    nz = lax.axis_size("z")
    every = jax.ShapeDtypeStruct((8 * rows, width), BF)
    head = jax.ShapeDtypeStruct((8, rows, hd), BF)
    keep = pltpu.VMEM((8, rows, hd), BF)
    wide = pltpu.VMEM((2, rows, width), BF)
    return pl.pallas_call(
        front_kernel,
        out_shape=(
            jax.ShapeDtypeStruct((rows, width), F32),
            every,
            every,
            jax.ShapeDtypeStruct((width, wg.shape[1] // 4), BF),
            jax.ShapeDtypeStruct((2, width), F32),
            every,
            jax.ShapeDtypeStruct((width, 2 * hd), BF),
            every,
            head,
            head,
            head,
            head,
            jax.ShapeDtypeStruct((8, rows, rows), F32),
            jax.ShapeDtypeStruct((8, rows, hd), F32),
            jax.ShapeDtypeStruct((8 * rows, fb), BF),
            jax.ShapeDtypeStruct((8 * rows, 2 * fb), BF),
            every,
        ),
        in_specs=[VM] * 4 + [ANY] * 7 + [VM],
        out_specs=(VM, ANY, ANY, ANY, VM) + (ANY,) * 12,
        scratch_shapes=GATHER_SEMS * 2
        + [pltpu.VMEM((rows, width), BF)]
        + GATHER_SEMS
        + [DMA((2, 3)), DMA((2, 3)), DMA((2,)), DMA((10,)), DMA((10,)), DMA((2,))]
        + relay_sems(nz) * 2
        + [pltpu.VMEM((4, rows, width), BF)]
        + scatter_scratch(rows, width)
        + [
            pltpu.VMEM((width, 2 * hd), BF),
            pltpu.VMEM((hd, width), BF),
            pltpu.VMEM((8, 8, rows), F32),
            pltpu.VMEM((8, rows), F32),
            pltpu.VMEM((4, *gains.shape), F32),
            DMA((4,)),
        ]
        + [wide, wide, keep, keep, keep, keep]
        + [pltpu.VMEM((8, rows, rows), F32), pltpu.VMEM((8, rows, hd), F32), keep, keep]
        + [DMA((2,)), DMA((2,)), DMA((8,)), DMA((8,)), DMA((6,))]
        + [pltpu.VMEM((width, 2 * fb), BF), pltpu.VMEM((fb, width), BF), DMA((2,)), DMA((3, 2))],
        compiler_params=params(0, 63),
        name="front",
    )(x, seg, gains, freq, wq, wk, wv, wo, wg, wu, wd, g)


CH = 32
QR = 4 * CH
FINE = 64 // CH
DOWN, GU, OUT, QKV = range(4)
COUNT = {DOWN: 512 // CH, GU: 1024 // CH, OUT: 128 // CH, QKV: 1024 // QR}
N_TICKS = sum(COUNT.values())
EARLY = COUNT[DOWN] + COUNT[GU]
GJ = COUNT[GU] // 4
SLOTS, N_SLOTTED = 12, EARLY + COUNT[OUT]


class Chain:
    def __init__(self, p, h, ins, outs, bufs, sems):
        self.p, self.h = p, h
        self.ins = ins
        self.gate, self.up, self.down, self.out, self.wq, self.wk, self.wv = outs
        self.buf, self.bufq, self.ring, self.ring_sem, self.credit = bufs
        self.rs_send, self.rs_recv, self.ag_send, self.ag_recv, self.cp_send, self.cp_recv, self.tsend = sems
        nz = lax.axis_size("z")
        self.nz = nz
        self.pos = nz - 1 - p.z if h == 0 else p.z
        self.step = -1 if h == 0 else 1

    def dev(self, by):
        return {"z": self.p.z + by}

    BASE = {GU: 0, DOWN: COUNT[GU], OUT: EARLY, QKV: EARLY + COUNT[OUT]}

    def tick(self, kind, t):
        return self.BASE[kind] + t

    def dist(self, kind, t):
        return t // GJ if kind == GU else lax.rem(t, 4)

    def row(self, kind, t):
        return lax.rem(t, GJ) * CH if kind == GU else (t // 4) * QR

    def shard_of(self, kind, t):
        return self.p.shard_at(self.dist(kind, t))

    def mine(self, kind, t):
        h = self.h
        if kind == DOWN:
            return self.ins[DOWN].at[pl.ds(h * 512 + t * CH, CH)]
        if kind == OUT:
            return self.ins[OUT].at[pl.ds(h * 128 + t * CH, CH)]
        row = self.shard_of(kind, t) * 512 + h * 256 + self.row(kind, t)
        return self.ins[kind].at[pl.ds(row, QR if kind == QKV else CH)]

    def fetch(self, kind, t):
        r = lax.rem(self.tick(kind, t), RING)
        return pltpu.make_async_copy(self.mine(kind, t), self.ring.at[r], self.ring_sem.at[r])

    def ahead(self, kind, t):
        @pl.when(self.pos > 0)
        def _():
            self.fetch(kind, t).start()

    def slot(self, kind, t):
        return self.bufq.at[t] if kind == QKV else self.buf.at[lax.rem(self.tick(kind, t), SLOTS)]

    def may_send(self, kind, t):
        if kind != QKV:

            @pl.when(self.tick(kind, t) >= SLOTS)
            def _():
                pl.semaphore_wait(self.credit, 1)

    def retire(self, kind, t):
        self.gone(kind, t)
        if kind != QKV:

            @pl.when(jnp.logical_and(self.pos > 0, self.tick(kind, t) < N_SLOTTED - SLOTS))
            def _():
                pl.semaphore_signal(self.credit, inc=1, device_id=self.dev(-self.step), device_id_type=MESH)

    def rs_copy(self, kind, t, src):
        k = self.tick(kind, t)
        return rcopy(
            src, self.slot(kind, t), self.rs_send.at[k], self.rs_recv.at[k], self.dev(self.step)
        )

    def begin(self, kind, t):
        @pl.when(self.pos == 0)
        def _():
            self.may_send(kind, t)
            self.rs_copy(kind, t, self.mine(kind, t)).start()

    def reduce(self, kind, t):
        first, last = self.pos == 0, self.pos == self.nz - 1

        @pl.when(jnp.logical_not(first))
        def _():
            slot = self.slot(kind, t)
            if kind in (DOWN, GU):
                self.fetch(kind, t).wait()
                own = self.ring.at[lax.rem(self.tick(kind, t), RING)]
            else:
                own = self.mine(kind, t)
            self.rs_copy(kind, t, slot).wait_recv()
            slot[...] = (slot[...].astype(F32) + own[...].astype(F32)).astype(BF)

        @pl.when(jnp.logical_and(jnp.logical_not(first), jnp.logical_not(last)))
        def _():
            self.may_send(kind, t)
            self.rs_copy(kind, t, self.slot(kind, t)).start()

        @pl.when(last)
        def _():
            self.turn(kind, t)

    def pieces(self, kind, t, s, d_shard):
        h, c = self.h, self.p.c
        if kind == DOWN:
            return [(None, self.down.at[pl.ds(c * 1024 + h * 512 + t * CH, CH)])]
        if kind == OUT:
            return [(None, self.out.at[pl.ds(c * 256 + h * 128 + t * CH, CH)])]
        if kind == GU:
            r = h * 256 + self.row(kind, t)
            c0 = pl.multiple_of((s * 2 + c) * 1024, 1024)
            return [
                ((0, 1024), self.gate.at[pl.ds(r, CH), pl.ds(c0, 1024)]),
                ((1024, 1024), self.up.at[pl.ds(r, CH), pl.ds(c0, 1024)]),
            ]
        r = h * 256 + (t // 4) * QR
        cq = pl.multiple_of((s * 2 + c) * 256, 256)
        return [((0, 256), self.wq.at[pl.ds(r, QR), pl.ds(cq, 256)])]

    def kv_piece(self, t, s, w):
        r = self.h * 256 + (t // 4) * QR
        return w.at[pl.ds(r, QR), pl.ds(pl.multiple_of(s * 256, 256), 256)]

    def turn(self, kind, t):
        slot = self.slot(kind, t)
        k = self.tick(kind, t)
        to = self.p.s if kind in (DOWN, OUT) else self.shard_of(kind, t)

        def send(i, src, dst):
            if kind in (DOWN, OUT):
                pltpu.make_async_copy(src, dst, self.ag_recv.at[i, k]).start()
                return

            @pl.when(self.dist(kind, t) == 0)
            def _():
                pltpu.make_async_copy(src, dst, self.ag_recv.at[i, k]).start()

            @pl.when(self.dist(kind, t) != 0)
            def _():
                rcopy(src, dst, self.tsend.at[i, k], self.ag_recv.at[i, k], {"shard": to}).start()

        for i, (cols, dst) in enumerate(self.pieces(kind, t, self.p.s, to)):
            send(i, slot if cols is None else slot.at[:, pl.ds(*cols)], dst)
        if kind == QKV:
            src = slot.at[:, pl.ds(256, 256)]

            @pl.when(self.p.c == 0)
            def _():
                send(1, src, self.kv_piece(t, self.p.s, self.wk))

            @pl.when(self.p.c != 0)
            def _():
                send(1, src, self.kv_piece(t, self.p.s, self.wv))

    def spread_copy(self, i, k, ref):
        return rcopy(ref, ref, self.ag_send.at[i, k], self.ag_recv.at[i, k], self.dev(-self.step))

    def spread(self, kind, t):
        k = self.tick(kind, t)
        s = self.p.s if kind in (DOWN, OUT) else self.shard_of(kind, t)

        def go(i, ref, wait=True):
            if wait:
                self.spread_copy(i, k, ref).wait_recv()

            @pl.when(self.pos > 0)
            def _():
                self.spread_copy(i, k, ref).start()

            rcopy(ref, ref, self.cp_send.at[i, k], self.cp_recv.at[i, k], self.p.sibling()).start()

        for i, (_, ref) in enumerate(self.pieces(kind, t, s, None)):
            go(i, ref)
        if kind == QKV:
            self.spread_copy(1, k, self.kv_piece(t, s, self.wk)).wait_recv()

            @pl.when(self.p.c == 0)
            def _():
                go(1, self.kv_piece(t, s, self.wk), False)

            @pl.when(self.p.c != 0)
            def _():
                go(1, self.kv_piece(t, s, self.wv), False)

    def gone(self, kind, t):
        k = self.tick(kind, t)

        @pl.when(self.pos < self.nz - 1)
        def _():
            self.rs_copy(kind, t, self.slot(kind, t)).wait_send()

        if kind not in (GU, QKV):
            return

        @pl.when(jnp.logical_and(self.pos == self.nz - 1, self.dist(kind, t) != 0))
        def _():
            slot = self.slot(kind, t)
            for i, (cols, dst) in enumerate(self.pieces(kind, t, self.p.s, None)):
                src = slot.at[:, pl.ds(*cols)]
                rcopy(src, dst, self.tsend.at[i, k], self.ag_recv.at[i, k], self.p.to(1)).wait_send()
            if kind == QKV:
                src = slot.at[:, pl.ds(256, 256)]
                dst = self.kv_piece(t, self.p.s, self.wk)
                rcopy(src, dst, self.tsend.at[1, k], self.ag_recv.at[1, k], self.p.to(1)).wait_send()

    def drain_spread(self, kind, t):
        k = self.tick(kind, t)
        s = self.p.s if kind in (DOWN, OUT) else self.shard_of(kind, t)
        refs = [ref for _, ref in self.pieces(kind, t, s, None)]
        if kind == QKV:
            refs.append(self.kv_piece(t, s, self.wk))
        for i, ref in enumerate(refs):

            @pl.when(self.pos > 0)
            def _():
                self.spread_copy(i, k, ref).wait_send()

            rcopy(ref, ref, self.cp_send.at[i, k], self.cp_recv.at[i, k], self.p.sibling()).wait()


RING = 4
CHAIN_SEMS = [DMA((N_TICKS,))] * 2 + [DMA((2, N_TICKS))] * 5


def loop(lo, hi, body):
    def step(t, _):
        body(t)
        return 0

    lax.fori_loop(lo, hi, step, 0)


SKEW, TURN, RETIRE = 2, 3, 4


def between(i, lo, hi):
    return jnp.logical_and(i >= lo, i < hi)


def each(i, lo, hi, act):
    for kind, n in COUNT.items():
        base = Chain.BASE[kind]
        a, b = max(lo, base), min(hi, base + n)
        if isinstance(i, int):
            if a <= i < b:
                act(kind, i - base)
        elif a < b:

            @pl.when(between(i, a, b))
            def _():
                act(kind, i - base)


def at_tick(t, when, act):
    @pl.when(t == when)
    def _():
        act()


def all_greet(p):
    nz = lax.axis_size("z")
    greet(plane_ids(p) + [{"z": lax.rem(p.z + k, nz)} for k in range(1, nz)])


class GainSums:
    def __init__(self, p, tot, got, gz, send, recv):
        self.p, self.tot, self.got, self.gz, self.send, self.recv = p, tot, got, gz, send, recv
        self.nz = lax.axis_size("z")

    def copy(self, k):
        dev = (self.p.sibling(), self.p.to(1), self.p.to(2))[k]
        return rcopy(self.tot.at[k], self.got.at[k], self.send.at[k], self.recv.at[k], dev)

    def along(self, k):
        to = {"z": lax.rem(self.p.z + k, self.nz)}
        return rcopy(
            self.tot.at[3], self.gz.at[self.p.z], self.send.at[2 + k], self.recv.at[3 + self.p.z], to
        )

    def landed(self, k):
        src = lax.rem(self.p.z + self.nz - k, self.nz)
        ref = self.gz.at[src]
        return rcopy(ref, ref, self.send.at[2 + k], self.recv.at[3 + src], {"z": src})

    def add(self, k):
        self.copy(k).wait()
        self.tot[k + 1] = self.tot[k] + self.got[k]
        if k < 2:
            self.copy(k + 1).start()
        else:
            for j in range(1, self.nz):
                self.along(j).start()
            self.gz[self.p.z] = self.tot[3]

    def finish(self):
        for j in range(1, self.nz):
            self.along(j).wait_send()
            self.landed(j).wait_recv()
        total = self.gz[0]
        for j in range(1, self.nz):
            total = total + self.gz[j]
        return total


class Attention:
    def __init__(self, p, hbm, wo, wqkv, part, gout, gqkv, bufs, sems):
        self.p, self.hbm, self.wo, self.wqkv, self.part = p, hbm, wo, wqkv, part
        self.gout, self.gqkv = gout, gqkv
        self.bufs, self.other, self.came, self.kept, self.dq, self.rows_out = bufs[:8], *bufs[8:]
        self.sem, self.send, self.recv, self.psem = sems
        self.n = self.rows_out.shape[1]

    def load(self, i, j):
        src = self.hbm[i]
        ref = src.at[pl.ds(j * self.n, self.n)] if len(src.shape) == 2 else src.at[j]
        b = lax.rem(j, 2)
        return pltpu.make_async_copy(ref, self.bufs[i].at[b], self.sem.at[i, b])

    def fetch(self, j):
        for i in range(7):
            self.load(i, j).start()

    def swap(self, j):
        return rcopy(self.other.at[j], self.came.at[j], self.send.at[j], self.recv.at[j], self.p.sibling())

    def first(self, j):
        for i in range(7):
            self.load(i, j).wait()

        @pl.when(j < 7)
        def _():
            self.fetch(j + 1)

        b = lax.rem(j, 2)
        dhb, q, k, v, attn, probs, turn = (self.bufs[i][b] for i in range(7))
        scale = HEAD_DIM ** (-0.5)
        half = HEAD_DIM // 2
        cosine, sine = turn[:, :half], turn[:, half:]
        dattn = mm_nt(dhb, self.wo[...]).astype(BF)
        g = mm_tn(attn, dhb)
        self.gout[...] = jnp.where(j == 0, g, self.gout[...] + g)
        dp = mm_nt(dattn, v)
        dv = mm_tn(probs.astype(BF), dattn)
        ds = (probs * (dp - jnp.sum(dp * probs, axis=-1, keepdims=True))).astype(BF)
        dq = rotate(mm(ds, k) * scale, cosine, -sine)
        dk = rotate(mm_tn(ds, q) * scale, cosine, -sine)
        zero = self.p.c == 0
        self.dq[b] = dq.astype(BF)
        self.kept[b] = jnp.where(zero, dk, dv)
        self.other[j] = jnp.where(zero, dv, dk).astype(BF)
        self.swap(j).start()
        self.load(7, j).start()

    def out_copy(self, j):
        b = lax.rem(j, 2)
        return pltpu.make_async_copy(self.rows_out.at[b], self.part.at[pl.ds(j * self.n, self.n)], self.psem.at[b])

    def second(self, j):
        b = lax.rem(j, 2)
        self.swap(j).wait()
        self.load(7, j).wait()
        dkv = (self.kept[b] + self.came[j].astype(F32)).astype(BF)
        dqkv = jnp.concatenate([self.dq[b], dkv], -1)
        g = mm_tn(self.bufs[7][b], dqkv)
        self.gqkv[...] = jnp.where(j == 0, g, self.gqkv[...] + g)

        @pl.when(j >= 2)
        def _():
            self.out_copy(j - 2).wait()

        self.rows_out[b] = mm_nt(dqkv, self.wqkv[...]).astype(BF)
        self.out_copy(j).start()

    def finish(self):
        self.out_copy(6).wait()
        self.out_copy(7).wait()


class Outer:
    def __init__(self, p, left, right_hbm, right, xc, out, row, sems):
        self.p, self.left, self.right_hbm, self.right, self.xc, self.out = p, left, right_hbm, right, xc, out
        self.row = row
        self.dsem, self.xsem, self.osem = sems

    def whole(self):
        return pltpu.make_async_copy(self.right_hbm, self.right, self.dsem.at[0])

    def load(self, n):
        b = lax.rem(n, 2)
        cols = pl.ds(pl.multiple_of(self.row(n), 256), 256)
        return pltpu.make_async_copy(self.left.at[:, cols], self.xc.at[b], self.xsem.at[b])

    def store(self, n, made):
        rows = pl.ds(pl.multiple_of(self.row(n), 256), 256)
        return pltpu.make_async_copy(made, self.out.at[rows], self.osem.at[0])

    def step(self, n, last, made):
        @pl.when(n == 0)
        def _():
            self.whole().wait()

        @pl.when(n > 0)
        def _():
            self.store(n - 1, made).wait()

        self.block(n, last, made)

    def block(self, n, last, made):
        self.load(n).wait()

        @pl.when(n < last)
        def _():
            self.load(n + 1).start()

        made[...] = mm_tn(self.xc[lax.rem(n, 2)], self.right[...]).astype(BF)
        self.store(n, made).start()


class Product:
    def __init__(self, hid, wd_hbm, right, made, out, sems):
        self.hid, self.wd_hbm, self.right, self.made, self.out = hid, wd_hbm, right, made, out
        self.wsem, self.hsem, self.osem = sems
        self.n, self.fb = made.shape[1], hid.shape[1]

    def weights(self):
        return pltpu.make_async_copy(self.wd_hbm, self.right.at[pl.ds(0, self.fb)], self.wsem.at[0])

    def space(self, i):
        return pl.ds(self.fb + lax.rem(i, 2) * self.n, self.n)

    def load(self, i):
        dst = self.right.at[self.space(i), pl.ds(0, self.fb)]
        return pltpu.make_async_copy(self.hid.at[pl.ds(i * self.n, self.n)], dst, self.hsem.at[lax.rem(i, 2)])

    def store(self, i):
        b = lax.rem(i, 2)
        return pltpu.make_async_copy(self.made.at[b], self.out.at[pl.ds(i * self.n, self.n)], self.osem.at[b])

    def start(self):
        self.weights().start()
        self.load(0).start()

    def step(self, i):
        @pl.when(i == 0)
        def _():
            self.weights().wait()

        self.load(i).wait()

        @pl.when(i < 7)
        def _():
            self.load(i + 1).start()

        @pl.when(i >= 2)
        def _():
            self.store(i - 2).wait()

        h = self.right[self.space(i), : self.fb]
        self.made[lax.rem(i, 2)] = mm(h, self.right[: self.fb]).astype(BF)
        self.store(i).start()

    def finish(self):
        self.store(6).wait()
        self.store(7).wait()


def tail_kernel(
    part_ref, x_hbm, h_hbm, g_hbm, gain_ref, hid_ref, ga_ref, xn2_ref, dgu_hbm, wd_hbm, wo_hbm, wqkv_ref,
    q_ref, k_ref, v_ref, attn_ref, probs_ref, turn_ref, xn1_ref,
    out_hbm, grad_hbm, gains_ref, dhb_ref, p1_ref, ggu_ref, gd_ref, dpart_ref, gate, up, down, out, wq, wk, wv,
    bufa, bufb, qa, qb, ringa, ringb, ring_sem, credita, creditb, big, xc, dsem, xsem, osem, psem, hsem, psem2, tot, got, gz, gsend, grecv,
    low, xg, hb, dh, gout, gqkv, gout_low, gqkv_low, wo_ref, io_sem, free_sem, *scr
):
    p = Place()
    nz = lax.axis_size("z")
    s1 = Scatter(p, part_ref, scr[:8])
    s2 = Scatter(p, dpart_ref, scr[:8])
    s3 = Scatter(p, p1_ref, scr[:8])
    ga = Gather(p, low, dhb_ref, scr[8:13])
    sums = GainSums(p, tot, got, gz, gsend, grecv)
    hbm = (dhb_ref, q_ref, k_ref, v_ref, attn_ref, probs_ref, turn_ref, xn1_ref)
    at = Attention(p, hbm, wo_ref, wqkv_ref, p1_ref, gout, gqkv, scr[13:26], scr[26:30])
    gu = Outer(
        p, xn2_ref, dgu_hbm, big, xc, ggu_ref,
        lambda n: p.shard_at(n // 2) * 512 + lax.rem(n, 2) * 256,
        (dsem, xsem.at[0], osem.at[0]),
    )
    gd = Outer(
        p, hid_ref, ga_ref, big, xc, gd_ref,
        lambda n: lax.rem(n, 2) * 512 + (n // 2) * 256,
        (dsem.at[pl.ds(1, 1)], xsem.at[1], osem.at[1]),
    )
    made = at.rows_out.at[0]
    fb = hid_ref.shape[1]
    wd = wd_hbm.at[pl.ds(p.c * fb, fb)]
    pr = Product(hid_ref, wd, big, at.rows_out, dpart_ref, (psem.at[pl.ds(0, 1)], hsem, psem2))
    ins = (gd_ref, ggu_ref, gout_low, gqkv_low)
    outs = (gate, up, down, out, wq, wk, wv)
    n = len(CHAIN_SEMS)
    chains = [
        Chain(p, 0, ins, outs, (bufa, qa, ringa, ring_sem.at[0], credita), scr[30 : 30 + n]),
        Chain(p, 1, ins, outs, (bufb, qb, ringb, ring_sem.at[1], creditb), scr[30 + n : 30 + 2 * n]),
    ]
    line = SKEW * (nz - 1)
    half = s1.half

    def io(k):
        wo = wo_hbm.at[pl.ds(p.c * HEAD_DIM, HEAD_DIM)]
        src, dst = [(h_hbm, hb), (g_hbm, xg), (x_hbm, xg), (low, out_hbm), (low, grad_hbm), (wo, wo_ref)][k]
        return pltpu.make_async_copy(src, dst, io_sem.at[k])

    io(0).start()
    io(1).start()
    io(5).start()
    gu.whole().start()
    gu.load(0).start()
    tot[0] = jnp.zeros_like(tot[0])
    all_greet(p)
    s1.start()
    s1.first(0)
    gu.step(0, 7, made)
    s1.first(1)
    gu.step(1, 7, made)
    gu.store(1, made).wait()

    def norm2():
        for k in (0, 1, 5):
            io(k).wait()
        for h in (0, 1):
            r = pl.ds(h * half, half)
            dx = s1.total(h)
            res = hb[r]
            f = lax.rsqrt(jnp.mean(res * res, axis=1, keepdims=True) + norm_eps)
            hat = res * f
            term = jnp.sum(dx * hat, axis=0, keepdims=True)
            tot[0, 1:2] = term if h == 0 else tot[0, 1:2] + term
            d = xg[r].astype(F32) + norm_backward_step(dx * gain_ref[1:2], hat, f)
            dh[r] = d
            low[r] = d.astype(BF)
        ga.start()
        io(2).start()

    def gathered():
        ga.finish()
        s1.drain()
        at.fetch(0)
        s2.start()

    def output():
        for h in (0, 1):
            r = pl.ds(h * half, half)
            low[r] = (hb[r] + s2.total(h)).astype(BF)
        io(3).start()
        s2.drain()
        for d in (p.to(1), p.to(2), p.sibling()):
            pl.semaphore_signal(free_sem, inc=1, device_id=d, device_id_type=MESH)

    def attended():
        at.finish()
        gout_low[...] = gout[...].astype(BF)
        gqkv_low[...] = gqkv[...].astype(BF)
        pl.semaphore_wait(free_sem, 3)
        s3.start()

    def norm1():
        io(2).wait()
        io(3).wait()
        for h in (0, 1):
            r = pl.ds(h * half, half)
            dx = s3.total(h)
            xf = xg[r].astype(F32)
            f = lax.rsqrt(jnp.mean(xf * xf, axis=1, keepdims=True) + norm_eps)
            hat = xf * f
            term = jnp.sum(dx * hat, axis=0, keepdims=True)
            tot[0, 0:1] = term if h == 0 else tot[0, 0:1] + term
            low[r] = (dh[r] + norm_backward_step(dx * gain_ref[0:1], hat, f)).astype(BF)
        io(4).start()
        sums.copy(0).start()

    def gains():
        gains_ref[...] = sums.finish()

    def gate_up(n):
        @pl.when(n > 2)
        def _():
            gu.store(n - 1, made).wait()

        gu.block(n, 7, made)

    def products():
        gu.store(7, made).wait()
        pr.start()

    def two_products(i):
        pr.step(i)
        pr.step(i + 1)

    def downs():
        pr.finish()
        gd.whole().start()
        gd.load(0).start()

    def tick(t):
        for ch in chains:
            each(t + 1 - SKEW * ch.pos, 0, EARLY, ch.ahead)
            each(t, 0, N_TICKS, ch.begin)
            each(t - SKEW * ch.pos, 0, N_TICKS, ch.reduce)
        for ch in chains:
            each(t - TURN - 2 * line + SKEW * ch.pos, 0, N_TICKS, ch.spread)
            each(t - RETIRE - SKEW * ch.pos, 0, N_SLOTTED, ch.retire)
        u = t // FINE
        pl.when(jnp.logical_and(between(t, 2, 14), lax.rem(t, 2) == 0))(lambda: gate_up(t // 2 + 1))
        at_tick(t, 14, products)
        pl.when(between(t, 16, 20))(lambda: two_products(2 * (t - 16)))
        at_tick(t, 20, downs)
        pl.when(jnp.logical_and(between(t, 25, 33), lax.rem(t, 2) == 1))(
            lambda: gd.step((t - 25) // 2, 3, gout_low)
        )
        at_tick(t, 33, lambda: gd.store(3, gout_low).wait())
        for k in range(4):
            if k >= 2:
                at_tick(t, k - 2, functools.partial(s1.first, k))
            at_tick(t, FINE * A0 + k, functools.partial(s2.first, k))
            at_tick(t, FINE * (A0 + 9) + 1 + k, functools.partial(s3.first, k))

        @pl.when(lax.rem(t, FINE) == 0)
        def _():
            at_tick(u, 3, s1.relay)
            at_tick(u, 5, norm2)
            at_tick(u, 7, ga.relay)
            at_tick(u, A0 - 1, gathered)
            pl.when(between(u, A0 + 1, A0 + 9))(lambda: at.second(u - A0 - 1))
            pl.when(between(u, A0, A0 + 8))(lambda: at.first(u - A0))
            at_tick(u, A0 + 3, s2.relay)
            at_tick(u, A0 + 5, output)
            at_tick(u, A0 + 9, attended)
            at_tick(u, A0 + 12, s3.relay)
            at_tick(u, A0 + 14, norm1)
            for k in range(3):
                at_tick(u, A0 + 15 + k, functools.partial(sums.add, k))
            at_tick(u, A0 + 19, gains)

    loop(0, N_TICKS + TURN + 2 * line, tick)
    io(4).wait()
    s3.drain()

    def drain(i):
        for ch in chains:
            each(i, N_SLOTTED, N_TICKS, ch.gone)
            each(i, 0, N_TICKS, ch.drain_spread)

    loop(0, N_TICKS, drain)


A0 = 12


def tail(part, x, h, g, gains, hid, g_all, xn2, dgu, wd, wo, wqkv, heads, xn1, ff):
    rows, width = x.shape
    nz = lax.axis_size("z")
    hd, pr = HEAD_DIM, width // 4
    shapes = [(pr, ff), (pr, ff), (ff // 4, width), (pr, width), (pr, width), (pr, 1024), (pr, 1024)]
    sq = pltpu.VMEM((2, rows, hd), BF)
    wide = pltpu.VMEM((2, rows, width), BF)
    return pl.pallas_call(
        tail_kernel,
        out_shape=(
            jax.ShapeDtypeStruct((rows, width), BF),
            jax.ShapeDtypeStruct((rows, width), BF),
            jax.ShapeDtypeStruct((8, width), F32),
            jax.ShapeDtypeStruct((8 * rows, width), BF),
            jax.ShapeDtypeStruct((8 * rows, width), BF),
            jax.ShapeDtypeStruct((width, width), BF),
            jax.ShapeDtypeStruct((hid.shape[1], width), BF),
            jax.ShapeDtypeStruct((8 * rows, width), BF),
        )
        + tuple(jax.ShapeDtypeStruct(s, BF) for s in shapes),
        in_specs=[ANY] * 4 + [VM] + [ANY] * 6 + [VM] + [ANY] * 7,
        out_specs=(ANY, ANY, VM) + (ANY,) * 12,
        scratch_shapes=[
            pltpu.VMEM((SLOTS, CH, width), BF),
            pltpu.VMEM((SLOTS, CH, width), BF),
            pltpu.VMEM((COUNT[QKV], QR, 512), BF),
            pltpu.VMEM((COUNT[QKV], QR, 512), BF),
            pltpu.VMEM((RING, CH, width), BF),
            pltpu.VMEM((RING, CH, width), BF),
            DMA((2, RING)),
            pltpu.SemaphoreType.REGULAR,
            pltpu.SemaphoreType.REGULAR,
            pltpu.VMEM((8 * rows, width), BF),
            pltpu.VMEM((2, width, 256), BF),
            DMA((2,)),
            DMA((2, 2)),
            DMA((2, 1)),
            DMA((2,)),
            DMA((2,)),
            DMA((2,)),
            pltpu.VMEM((4, 8, width), F32),
            pltpu.VMEM((3, 8, width), F32),
            pltpu.VMEM((nz, 8, width), F32),
            DMA((nz + 3,)),
            DMA((nz + 3,)),
            pltpu.VMEM((rows, width), BF),
            pltpu.VMEM((rows, width), BF),
            pltpu.VMEM((rows, width), F32),
            pltpu.VMEM((rows, width), F32),
            pltpu.VMEM((hd, width), F32),
            pltpu.VMEM((width, 2 * hd), F32),
            pltpu.VMEM((hd, width), BF),
            pltpu.VMEM((width, 2 * hd), BF),
            pltpu.VMEM((hd, width), BF),
            DMA((6,)),
            pltpu.SemaphoreType.REGULAR,
        ]
        + scatter_scratch(rows, width)
        + GATHER_SEMS
        + [wide, sq, sq, sq, sq]
        + [pltpu.VMEM((2, rows, rows), F32), pltpu.VMEM((2, rows, hd), F32), wide]
        + [pltpu.VMEM((8, rows, hd), BF)] * 2
        + [pltpu.VMEM((2, rows, hd), F32), sq, wide]
        + [DMA((8, 2)), DMA((8,)), DMA((8,)), DMA((2,))]
        + CHAIN_SEMS * 2,
        compiler_params=params(2, 63),
        name="tail",
    )(part, x, h, g, gains, hid, g_all, xn2, dgu, wd, wo, wqkv, *heads, xn1)


def widen_kernel(*refs):
    n = len(refs) // 2
    for a, b in zip(refs[:n], refs[n:], strict=True):
        b[...] = a[...].astype(b.dtype)


def widen(arrays, kept):
    shapes = [jax.ShapeDtypeStruct(a.shape, F32) for a in arrays]
    shapes += [jax.ShapeDtypeStruct(a.shape, a.dtype) for a in kept]
    arrays = (*arrays, *kept)
    steps = 8

    def spec(a):
        return pl.BlockSpec((a.shape[0] // steps, a.shape[1]), lambda i: (i, 0))

    return pl.pallas_call(
        widen_kernel,
        grid=(steps,),
        out_shape=tuple(shapes),
        in_specs=[spec(a) for a in arrays],
        out_specs=tuple(spec(a) for a in arrays),
        compiler_params=pltpu.CompilerParams(vmem_limit_bytes=62 * 2**20),
        name="widen",
    )(*arrays)


def pieces(
    tokens,
    segment_ids,
    attn_gain,
    w_query,
    w_key,
    w_value,
    w_out,
    mlp_gain,
    w_gate,
    w_up,
    w_down,
    cotangent,
):
    rows, width = tokens.shape[1], tokens.shape[2]
    ns = lax.axis_size("shard")
    hd = HEAD_DIM
    ff = w_gate.shape[1]
    part = width // ns

    x = tokens.reshape(rows, width)
    g = cotangent.reshape(rows, width)
    gains = jnp.concatenate([attn_gain[None], mlp_gain[None], jnp.zeros((6, part), BF)], 0).astype(F32)
    half = np.arange(hd // 2, dtype=np.float64) * 2.0 / hd
    freq = jnp.asarray((rope_base ** -half).astype(np.float32)[None])
    h, xn2, g_all, _, gains, _, wqkv, xn1, q, k, v, attn, probs, turn, hid, dgu, dxpart = front(
        x, segment_ids, gains, freq, w_query, w_key, w_value, w_out, w_gate, w_up, w_down, g
    )
    heads = (q, k, v, attn, probs, turn)
    output, input_grad, gain_g, _, _, _, _, _, gate_g, up_g, down_g, out_g, wq_g, wk_g, wv_g = tail(
        dxpart,
        x,
        h,
        g,
        gains,
        hid,
        g_all,
        xn2,
        dgu,
        w_down,
        w_out,
        wqkv,
        heads,
        xn1,
        ff,
    )
    gain_g = lax.dynamic_slice_in_dim(gain_g, lax.axis_index("shard") * part, part, 1)
    wide = widen((wq_g, wk_g, wv_g, out_g, gate_g, up_g, down_g), (output, input_grad))
    output, input_grad = (a.reshape(1, rows, width) for a in wide[7:])
    return (output, input_grad, gain_g[0], *wide[:4], gain_g[1], *wide[4:7])


def contract_rows(left, right):
    return lax.dot_general(
        left, right, (((0,), (0,)), ((), ())), preferred_element_type=jnp.float32
    )


def contract_cols(left, right):
    return lax.dot_general(
        left, right, (((1,), (1,)), ((), ())), preferred_element_type=jnp.float32
    )


def scores_of(queries, keys, allowed):
    raw = jnp.einsum(
        "qgrd,kgd->grqk", queries, keys, preferred_element_type=jnp.float32
    ) * HEAD_DIM ** (-0.5)
    return jnp.where(allowed, raw, mask_fill)


def general(
    tokens,
    segment_ids,
    attn_gain,
    w_query,
    w_key,
    w_value,
    w_out,
    mlp_gain,
    w_gate,
    w_up,
    w_down,
    cotangent,
):
    rows = tokens.shape[1]
    width = tokens.shape[2]
    groups = HEADS // KV_HEADS
    q_cols = HEADS * HEAD_DIM
    kv_cols = KV_HEADS * HEAD_DIM
    layer_input_rows = tokens.reshape(rows, width).astype(jnp.float32)
    segments = segment_ids.reshape(rows)
    iota = jnp.arange(rows, dtype=jnp.int32)
    starts = jnp.sum((segments[None, :] < segments[:, None]).astype(jnp.int32), axis=1)
    positions = (iota - starts).astype(jnp.float32)
    allowed = (segments[:, None] == segments[None, :]) & (iota[:, None] >= iota[None, :])
    half = HEAD_DIM // 2
    inv_freq = rope_base ** (-(jnp.arange(half, dtype=jnp.float32) * 2.0 / HEAD_DIM))
    angles = positions[:, None] * inv_freq
    cosine = jnp.cos(angles)
    sine = jnp.sin(angles)
    first_norm_factor = lax.rsqrt(
        jnp.mean(layer_input_rows * layer_input_rows, axis=1, keepdims=True) + norm_eps
    )
    first_standardized = layer_input_rows * first_norm_factor
    gain_fragment = lax.all_gather(attn_gain, "shard", axis=0, tiled=True)
    query_piece = lax.all_gather(w_query, "shard", axis=0, tiled=True)
    key_piece = lax.all_gather(w_key, "shard", axis=0, tiled=True)
    value_piece = lax.all_gather(w_value, "shard", axis=0, tiled=True)
    normalized_rows = (first_standardized * gain_fragment.astype(jnp.float32)).astype(jnp.bfloat16)
    joined = jnp.concatenate([query_piece, key_piece, value_piece], 1)
    result = (
        jnp.dot(normalized_rows, joined, preferred_element_type=jnp.float32),
        normalized_rows,
        gain_fragment.astype(jnp.float32),
    )
    folded = result
    projected, normed_one, first_norm_gain = (folded[0], folded[1], folded[2])
    queries = rotate(
        projected[:, :q_cols].reshape(rows, KV_HEADS, groups, HEAD_DIM),
        cosine[:, None, None, :],
        sine[:, None, None, :],
    ).astype(jnp.bfloat16)
    keys = rotate(
        projected[:, q_cols : q_cols + kv_cols].reshape(rows, KV_HEADS, HEAD_DIM),
        cosine[:, None, :],
        sine[:, None, :],
    ).astype(jnp.bfloat16)
    values = projected[:, q_cols + kv_cols :].reshape(rows, KV_HEADS, HEAD_DIM).astype(jnp.bfloat16)
    scores = scores_of(queries, keys, allowed)
    top = jnp.max(scores, axis=-1, keepdims=True)
    log_total = top + jnp.log(jnp.sum(jnp.exp(scores - top), axis=-1, keepdims=True))
    probs = jnp.exp(scores - log_total)
    probs_low = probs.astype(jnp.bfloat16)
    attn = (
        jnp.einsum("grqk,kgd->qgrd", probs_low, values, preferred_element_type=jnp.float32)
        .reshape(rows, q_cols)
        .astype(jnp.bfloat16)
    )
    part = attn
    result = (
        jnp.dot(
            part,
            lax.all_gather(w_out, "shard", axis=0, tiled=True),
            preferred_element_type=jnp.float32,
        ),
    )
    folded_out = result
    residual_hidden_state = layer_input_rows + folded_out[0]
    second_norm_factor = lax.rsqrt(
        jnp.mean(residual_hidden_state * residual_hidden_state, axis=1, keepdims=True) + norm_eps
    )
    second_standardized = residual_hidden_state * second_norm_factor
    gain_fragment = lax.all_gather(mlp_gain, "shard", axis=0, tiled=True)
    gate_piece = lax.all_gather(w_gate, "shard", axis=0, tiled=True)
    up_piece = lax.all_gather(w_up, "shard", axis=0, tiled=True)
    normalized_rows = (second_standardized * gain_fragment.astype(jnp.float32)).astype(jnp.bfloat16)
    joined = jnp.concatenate([gate_piece, up_piece], 1)
    result = (
        jnp.dot(normalized_rows, joined, preferred_element_type=jnp.float32),
        normalized_rows,
        gain_fragment.astype(jnp.float32),
    )
    folded_mlp = result
    gate = folded_mlp[0][:, :FF]
    up_value = folded_mlp[0][:, FF:]
    normed_two = folded_mlp[1]
    second_norm_gain = folded_mlp[2]
    sigma = jax.nn.sigmoid(gate)
    swish = gate * sigma
    inner = (swish * up_value).astype(jnp.bfloat16)
    part = inner
    result = (
        jnp.dot(
            part,
            lax.all_gather(w_down, "shard", axis=0, tiled=True),
            preferred_element_type=jnp.float32,
        ),
    )
    output = (residual_hidden_state + result[0]).astype(jnp.bfloat16).reshape(1, rows, width)
    grad_out = cotangent.reshape(rows, width)
    grad_down = lax.psum_scatter(
        contract_rows(inner, grad_out).astype(jnp.bfloat16),
        "shard",
        scatter_dimension=0,
        tiled=True,
    )
    down_full, gate_full, up_full = (
        lax.all_gather(w_down, "shard", axis=0, tiled=True),
        lax.all_gather(w_gate, "shard", axis=0, tiled=True),
        lax.all_gather(w_up, "shard", axis=0, tiled=True),
    )
    grad_inner = contract_cols(grad_out, down_full)
    grad_gate = (grad_inner * up_value * sigma * (1.0 + gate * (1.0 - sigma))).astype(jnp.bfloat16)
    grad_up = (grad_inner * swish).astype(jnp.bfloat16)
    grad_mlp = jnp.concatenate([grad_gate, grad_up], 1)
    mlp_shards = lax.psum_scatter(
        contract_rows(normed_two, grad_mlp).astype(jnp.bfloat16),
        "shard",
        scatter_dimension=0,
        tiled=True,
    ).astype(jnp.float32)
    second_norm_gradient = contract_cols(grad_gate, gate_full) + contract_cols(grad_up, up_full)
    second_gain_products = jnp.sum(second_norm_gradient * second_standardized, axis=0)
    hidden_gradient = grad_out.astype(jnp.float32) + norm_backward_step(
        second_norm_gradient * second_norm_gain, second_standardized, second_norm_factor
    )
    grad_hidden_low = hidden_gradient.astype(jnp.bfloat16)
    grad_out_proj = lax.psum_scatter(
        contract_rows(attn, grad_hidden_low).astype(jnp.bfloat16),
        "shard",
        scatter_dimension=0,
        tiled=True,
    )
    grad_attn = contract_cols(grad_hidden_low, lax.all_gather(w_out, "shard", axis=0, tiled=True))
    grad_attn = grad_attn.astype(jnp.bfloat16).reshape(rows, KV_HEADS, groups, HEAD_DIM)
    scores_again = scores_of(queries, keys, allowed)
    probs_again = jnp.exp(scores_again - log_total)
    probs_again_low = probs_again.astype(jnp.bfloat16)
    grad_probs = jnp.einsum("qgrd,kgd->grqk", grad_attn, values, preferred_element_type=jnp.float32)
    grad_values = jnp.einsum(
        "grqk,qgrd->kgd", probs_again_low, grad_attn, preferred_element_type=jnp.float32
    )
    grad_scores = (
        probs_again * (grad_probs - jnp.sum(grad_probs * probs_again, axis=-1, keepdims=True))
    ).astype(jnp.bfloat16)
    grad_queries = jnp.einsum(
        "grqk,kgd->qgrd", grad_scores, keys, preferred_element_type=jnp.float32
    ) * HEAD_DIM ** (-0.5)
    grad_keys = jnp.einsum(
        "grqk,qgrd->kgd", grad_scores, queries, preferred_element_type=jnp.float32
    ) * HEAD_DIM ** (-0.5)
    grad_queries = rotate(grad_queries, cosine[:, None, None, :], -sine[:, None, None, :]).reshape(
        rows, q_cols
    )
    grad_keys = rotate(grad_keys, cosine[:, None, :], -sine[:, None, :]).reshape(rows, kv_cols)
    grad_joined = jnp.concatenate(
        [
            grad_queries.astype(jnp.bfloat16),
            grad_keys.astype(jnp.bfloat16),
            grad_values.reshape(rows, kv_cols).astype(jnp.bfloat16),
        ],
        1,
    )
    qkv_shards = lax.psum_scatter(
        contract_rows(normed_one, grad_joined).astype(jnp.bfloat16),
        "shard",
        scatter_dimension=0,
        tiled=True,
    ).astype(jnp.float32)
    local_qkv = jnp.concatenate([w_query, w_key, w_value], 1)
    first_norm_gradient = contract_cols(
        grad_joined, lax.all_gather(local_qkv, "shard", axis=0, tiled=True)
    )
    first_gain_products = jnp.sum(first_norm_gradient * first_standardized, axis=0)
    input_gradient_rows = hidden_gradient + norm_backward_step(
        first_norm_gradient * first_norm_gain, first_standardized, first_norm_factor
    )
    input_grad = input_gradient_rows.astype(jnp.bfloat16).reshape(1, rows, width)
    gain_one_grad, gain_two_grad = (
        lax.psum_scatter(first_gain_products, "shard", scatter_dimension=0, tiled=True),
        lax.psum_scatter(second_gain_products, "shard", scatter_dimension=0, tiled=True),
    )
    summed = (
        lax.psum(gain_one_grad.astype(jnp.bfloat16), "rep").astype(jnp.float32),
        lax.psum(qkv_shards[:, :q_cols].astype(jnp.bfloat16), "rep").astype(jnp.float32),
        lax.psum(qkv_shards[:, q_cols : q_cols + kv_cols].astype(jnp.bfloat16), "rep").astype(
            jnp.float32
        ),
        lax.psum(qkv_shards[:, q_cols + kv_cols :].astype(jnp.bfloat16), "rep").astype(jnp.float32),
        lax.psum(grad_out_proj, "rep").astype(jnp.float32),
        lax.psum(gain_two_grad.astype(jnp.bfloat16), "rep").astype(jnp.float32),
        lax.psum(mlp_shards[:, :FF].astype(jnp.bfloat16), "rep").astype(jnp.float32),
        lax.psum(mlp_shards[:, FF:].astype(jnp.bfloat16), "rep").astype(jnp.float32),
        lax.psum(grad_down, "rep").astype(jnp.float32),
    )
    return (
        output,
        input_grad,
        summed[0],
        summed[1],
        summed[2],
        summed[3],
        summed[4],
        summed[5],
        summed[6],
        summed[7],
        summed[8],
    )


def solution(mesh):
    rep, shard = mesh.devices.shape
    if shard == KV_HEADS and rep % 2 == 0:
        fine = Mesh(np.asarray(mesh.devices).reshape(rep // 2, 2, shard), ("z", "core", "shard"))
        body, every = pieces, ("z", "core", "shard")
    else:
        fine, body, every = mesh, general, ("rep", "shard")
    seqs, vec, mat = P(every, None, None), P("shard"), P("shard", None)
    in_specs = (seqs, P(every, None), vec, mat, mat, mat, mat, vec, mat, mat, mat, seqs)
    out_specs = (seqs, seqs, vec, mat, mat, mat, mat, vec, mat, mat, mat)
    return jax.shard_map(body, mesh=fine, in_specs=in_specs, out_specs=out_specs, check_vma=False)
```

```python
import functools

import jax
import jax.numpy as jnp
import numpy as np
from jax import lax
from jax.experimental import pallas as pl
from jax.experimental.pallas import tpu as pltpu
from jax.sharding import Mesh
from jax.sharding import PartitionSpec as P

HEADS = 8
KV_HEADS = 4
HEAD_DIM = 256
FF = 8192

rope_base = 1000042.0
norm_eps = 1e-06
mask_fill = -1e30

BF = jnp.bfloat16
F32 = jnp.float32
MESH = pl.DeviceIdType.MESH
ANY = pl.BlockSpec(memory_space=pl.ANY)
VM = pl.BlockSpec(memory_space=pltpu.VMEM)
DMA = pltpu.SemaphoreType.DMA


def mm(a, b):
    return jnp.dot(a, b, preferred_element_type=F32)


def mm_tn(a, b):
    return lax.dot_general(a, b, (((0,), (0,)), ((), ())), preferred_element_type=F32)


def mm_nt(a, b):
    return lax.dot_general(a, b, (((1,), (1,)), ((), ())), preferred_element_type=F32)


def rotate(values, cosine, sine):
    half = values.shape[-1] // 2
    first = values[..., :half]
    second = values[..., half:]
    return jnp.concatenate([first * cosine - second * sine, second * cosine + first * sine], -1)


def norm_backward_step(grad_hat, normalized_rows, factor):
    return factor * (
        grad_hat - normalized_rows * jnp.mean(grad_hat * normalized_rows, axis=1, keepdims=True)
    )


class Place:
    def __init__(self):
        self.z = lax.axis_index("z")
        self.c = lax.axis_index("core")
        self.s = lax.axis_index("shard")

    def shard(self, d):
        s = self.s
        if d == 0:
            return s
        if d == 1:
            return s + 1 - 2 * lax.rem(s, 2)
        if d == 2:
            return lax.rem(s + 2, 4)
        return 3 - s

    def shard_at(self, d):
        s = self.s
        one = s + 1 - 2 * lax.rem(s, 2)
        two = lax.rem(s + 2, 4)
        return jnp.where(d == 0, s, jnp.where(d == 1, one, jnp.where(d == 2, two, 3 - s)))

    def to(self, d):
        return {"shard": self.shard(d)}

    def sibling(self):
        return {"core": 1 - self.c}


def greet(ids):
    barrier = pltpu.get_barrier_semaphore()
    for d in ids:
        pl.semaphore_signal(barrier, inc=1, device_id=d, device_id_type=MESH)
    pl.semaphore_wait(barrier, len(ids))


def rcopy(src, dst, send, recv, dev):
    return pltpu.make_async_remote_copy(
        src_ref=src, dst_ref=dst, send_sem=send, recv_sem=recv, device_id=dev, device_id_type=MESH
    )


GATHER_SEMS = [DMA((6,)), DMA((6,)), DMA((7,)), DMA((7,)), DMA((1,))]


class Gather:
    def __init__(self, p, src, out, sems):
        self.p, self.src, self.out = p, src, out
        self.send, self.recv, self.csend, self.crecv, self.lsem = sems
        self.rows = src.shape[0]
        self.half = self.rows // 2

    def at(self, d, h, core=None):
        core = self.p.c if core is None else core
        row = (core * 4 + self.p.shard(d)) * self.rows
        if h is None:
            return self.out.at[pl.ds(row, self.rows)]
        return self.out.at[pl.ds(row + h * self.half, self.half)]

    def move(self, k):
        d, h, to = [(0, 0, 1), (0, 1, 2), (0, 1, 1), (0, 0, 2), (1, 0, 2), (2, 1, 1)][k]
        dst = self.at(d, h)
        src = self.src.at[pl.ds(h * self.half, self.half)] if d == 0 else dst
        return rcopy(src, dst, self.send.at[k], self.recv.at[k], self.p.to(to))

    def landed(self, k):
        d, h = [(1, 0), (2, 1), (1, 1), (2, 0), (3, 0), (3, 1)][k]
        return self.at(d, h)

    def pass_on(self, k):
        here = self.src if k == 6 else self.landed(k)
        there = self.at(0, None) if k == 6 else self.landed(k)
        return rcopy(here, there, self.csend.at[k], self.crecv.at[k], self.p.sibling())

    def arrived(self, k):
        ref = self.landed(k)
        rcopy(ref, ref, self.send.at[k], self.recv.at[k], self.p.to(1)).wait_recv()
        self.pass_on(k).start()

    def start(self):
        for k in range(4):
            self.move(k).start()
        self.pass_on(6).start()
        pltpu.make_async_copy(self.src, self.at(0, None), self.lsem.at[0]).start()

    def relay(self):
        for k in (0, 1):
            self.arrived(k)
            self.move(4 + k).start()

    def early(self):
        for k in (2, 3):
            self.arrived(k)

    def late(self):
        for k in (4, 5):
            self.arrived(k)

    def both(self, ks):
        for k in ks:
            self.pass_on(k).wait_recv()

    def home(self):
        self.both((6,))
        pltpu.make_async_copy(self.src, self.at(0, None), self.lsem.at[0]).wait()

    def close(self):
        for k in range(6):
            self.move(k).wait_send()
        for k in range(7):
            self.pass_on(k).wait_send()

    def finish(self, early=False):
        if not early:
            self.early()
        self.late()
        self.both(range(7))
        pltpu.make_async_copy(self.src, self.at(0, None), self.lsem.at[0]).wait()
        self.close()


SCATTER_SEMS = [DMA((4,)), DMA((4,)), DMA((4,)), DMA((6,)), DMA((6,))]
ORDER = (3, 1, 2, 0)


def scatter_scratch(rows, width):
    half = rows // 2
    return [
        pltpu.VMEM((4, rows, width), BF),
        pltpu.VMEM((4, rows, width), BF),
        pltpu.VMEM((6, half, width), BF),
    ] + SCATTER_SEMS


class Scatter:
    def __init__(self, p, part, scratch):
        self.p, self.part = p, part
        self.own, self.got, self.slot, self.lsem, self.csend, self.crecv, self.send, self.recv = scratch
        self.rows = self.own.shape[1]
        self.half = self.rows // 2

    def block(self, core, d):
        return self.part.at[pl.ds((core * 4 + self.p.shard(d)) * self.rows, self.rows)]

    def local(self, d):
        return pltpu.make_async_copy(self.block(self.p.c, d), self.own.at[d], self.lsem.at[d])

    def swap(self, d):
        src = self.block(1 - self.p.c, d)
        return rcopy(src, self.got.at[d], self.csend.at[d], self.crecv.at[d], self.p.sibling())

    def rowsof(self, h):
        return pl.ds(h * self.half, self.half)

    def move(self, k):
        d, h, to = [(3, 0, 1), (3, 1, 2), (1, 0, 1), (2, 1, 2), (2, 0, 2), (1, 1, 1)][k]
        return rcopy(
            self.own.at[d, self.rowsof(h)], self.slot.at[k], self.send.at[k], self.recv.at[k], self.p.to(to)
        )

    def start(self):
        for d in ORDER:
            self.swap(d).start()
            self.local(d).start()

    def pair(self, d):
        self.swap(d).wait_recv()
        self.local(d).wait()
        self.own[d] = (self.own[d].astype(F32) + self.got[d].astype(F32)).astype(BF)

    def first(self, k):
        self.pair(ORDER[k])
        for m in ((0, 1), (2,), (3,), ())[k]:
            self.move(m).start()

    def relay(self):
        for k, d, h in ((0, 2, 0), (1, 1, 1)):
            self.move(k).wait_recv()
            r = self.rowsof(h)
            self.own[d, r] = (self.own[d, r].astype(F32) + self.slot[k].astype(F32)).astype(BF)
            self.move(4 + k).start()

    def total(self, h):
        near, far = (2, 4) if h == 0 else (3, 5)
        self.move(near).wait_recv()
        self.move(far).wait_recv()
        return (
            self.own[0, self.rowsof(h)].astype(F32)
            + self.slot[near].astype(F32)
            + self.slot[far].astype(F32)
        )

    def drain(self):
        for k in range(6):
            self.move(k).wait_send()
        for d in range(4):
            self.swap(d).wait_send()


def params(cid, mb):
    return pltpu.CompilerParams(
        collective_id=cid, has_side_effects=True, vmem_limit_bytes=mb * 2**20
    )


def plane_ids(p):
    return [p.to(1), p.to(2), p.to(3), p.sibling()]


class Columns:
    def __init__(self, p, sems):
        self.p = p
        self.send, self.recv, self.lsem = sems

    def cols(self, j, d, src, width):
        return src.at[:, pl.ds(pl.multiple_of(j * width, width), width)]

    def copy(self, k, d, src, dst):
        if d == 0:
            return pltpu.make_async_copy(src, dst, self.lsem.at[k])
        return rcopy(src, dst, self.send.at[k, d - 1], self.recv.at[k, d - 1], self.p.to(d))


def rows_at(ref, r, n, c0, width):
    return ref.at[pl.ds(r, n), pl.ds(c0, width)]


def greet_line(p, ids):
    barrier = pltpu.get_barrier_semaphore()
    nz = lax.axis_size("z")
    for d in ids:
        pl.semaphore_signal(barrier, inc=1, device_id=d, device_id_type=MESH)

    @pl.when(p.z > 0)
    def _():
        pl.semaphore_signal(barrier, inc=1, device_id={"z": p.z - 1}, device_id_type=MESH)

    @pl.when(p.z < nz - 1)
    def _():
        pl.semaphore_signal(barrier, inc=1, device_id={"z": p.z + 1}, device_id_type=MESH)

    ends = jnp.where(p.z == 0, 1, 0) + jnp.where(p.z == nz - 1, 1, 0)
    pl.semaphore_wait(barrier, len(ids) + 2 - ends)


def relay_sems(nz):
    return [DMA((3,)), DMA((3,)), DMA((1,)), DMA((2, nz, 3)), DMA((nz, 3))]


class Relay:
    def __init__(self, p, w, dst, c0, sems):
        self.p, self.w, self.dst, self.c0 = p, w, dst, c0
        self.xs, self.xr, self.ls, self.zs, self.zr = sems
        self.nz = lax.axis_size("z")
        self.part = w.shape[0]
        self.n = self.part // self.nz
        self.fb = w.shape[1] // 8

    def cols(self, d):
        return pl.ds(pl.multiple_of((self.p.shard(d) * 2 + self.p.c) * self.fb, self.fb), self.fb)

    def rows(self, d, q):
        return self.dst.at[pl.ds(self.p.shard(d) * self.part + q * self.n, self.n), pl.ds(self.c0, self.fb)]

    def fetch(self, d):
        src = self.w.at[pl.ds(self.p.z * self.n, self.n), self.cols(d)]
        return rcopy(src, self.rows(0, self.p.z), self.xs.at[d - 1], self.xr.at[d - 1], self.p.to(d))

    def local(self):
        dst = self.dst.at[pl.ds(self.p.s * self.part, self.part), pl.ds(self.c0, self.fb)]
        return pltpu.make_async_copy(self.w.at[:, self.cols(0)], dst, self.ls.at[0])

    def along(self, way, q, d):
        ref = self.rows(d, q)
        to = {"z": self.p.z + (1 if way else -1)}
        return rcopy(ref, ref, self.zs.at[way, q, d - 1], self.zr.at[q, d - 1], to)

    def start(self):
        for d in (3, 1, 2):
            self.fetch(d).start()
        self.local().start()

    def can(self, way):
        return self.p.z < self.nz - 1 if way else self.p.z > 0

    def own(self):
        for d in (1, 2, 3):
            self.fetch(d).wait_recv()
        for way in (0, 1):

            @pl.when(self.can(way))
            def _():
                for d in (1, 2, 3):
                    self.along(way, self.p.z, d).start()

    def hop(self, k):
        for way in (0, 1):
            q = self.p.z - k if way else self.p.z + k
            there = q >= 0 if way else q < self.nz

            @pl.when(there)
            def _():
                for d in (1, 2, 3):
                    self.along(way, q, d).wait_recv()

            @pl.when(jnp.logical_and(there, self.can(way)))
            def _():
                for d in (1, 2, 3):
                    self.along(way, q, d).start()

    def finish(self):
        for d in (1, 2, 3):
            self.fetch(d).wait_send()
        for k in range(self.nz):
            for way in (0, 1):
                q = self.p.z - k if way else self.p.z + k
                there = q >= 0 if way else q < self.nz

                @pl.when(jnp.logical_and(there, self.can(way)))
                def _():
                    for d in (1, 2, 3):
                        self.along(way, q, d).wait_send()


class Forward:
    def __init__(self, p, xa, xn1, wqkv, wo, seg, gain, freq, sc, ob, bufs, sems):
        self.p, self.xa, self.xn1 = p, xa, xn1
        self.wqkv, self.wo, self.seg, self.gain, self.freq = wqkv, wo, seg, gain, freq
        self.sc, self.ob = sc, ob
        self.xb, self.nb, self.q, self.k, self.v, self.attn, self.probs, self.turn, self.kept, self.came = bufs
        self.xsem, self.nsem, self.send, self.recv = sems
        self.n = self.xb.shape[1]

    def block(self, i):
        return lax.rem(i, 2) * 4 + self.p.shard_at(i // 2)

    def rows(self, ref, i):
        return ref.at[pl.ds(self.block(i) * self.n, self.n)]

    def load(self, i):
        b = lax.rem(i, 2)
        return pltpu.make_async_copy(self.rows(self.xa, i), self.xb.at[b], self.xsem.at[b])

    def store(self, i):
        b = lax.rem(i, 2)
        return pltpu.make_async_copy(self.nb.at[b], self.rows(self.xn1, i), self.nsem.at[b])

    def swap(self, i):
        return rcopy(self.kept.at[i], self.came.at[i], self.send.at[i], self.recv.at[i], self.p.sibling())

    def seg_of(self, i):
        row = self.seg[self.block(i)]
        return row[0:1], row.T[:, 0:1]

    def first(self, i):
        b, k = lax.rem(i, 2), self.block(i)
        self.load(i).wait()

        @pl.when(i >= 2)
        def _():
            self.store(i - 2).wait()

        x = self.xb[b].astype(F32)
        f = lax.rsqrt(jnp.mean(x * x, axis=1, keepdims=True) + norm_eps)
        xn = (x * f * self.gain).astype(BF)
        self.nb[b] = xn
        self.store(i).start()
        lin = mm(xn, self.wqkv[...])
        row, col = self.seg_of(i)
        start = jnp.sum((row < col).astype(F32), axis=1, keepdims=True)
        at = lax.broadcasted_iota(jnp.int32, (self.n, 1), 0).astype(F32)
        angle = (at - start) * self.freq
        cosine, sine = jnp.cos(angle), jnp.sin(angle)
        self.turn[k] = jnp.concatenate([cosine, sine], -1)
        hd = HEAD_DIM
        self.q[k] = rotate(lin[:, :hd], cosine, sine).astype(BF)
        kv = lin[:, hd:]
        self.kept[i] = jnp.where(self.p.c == 0, rotate(kv, cosine, sine), kv).astype(BF)
        self.swap(i).start()

    def second(self, i):
        n, k = self.n, self.block(i)
        self.swap(i).wait()
        mine, came = self.kept[i], self.came[i]
        key = jnp.where(self.p.c == 0, mine, came)
        value = jnp.where(self.p.c == 0, came, mine)
        self.k[k], self.v[k] = key, value
        row, col = self.seg_of(i)
        down = lax.broadcasted_iota(jnp.int32, (n, n), 0)
        over = lax.broadcasted_iota(jnp.int32, (n, n), 1)
        allowed = jnp.logical_and(row == col, down >= over)
        scores = jnp.where(allowed, mm_nt(self.q[k], key) * HEAD_DIM ** (-0.5), mask_fill)
        ex = jnp.exp(scores - jnp.max(scores, axis=-1, keepdims=True))
        probs = ex / jnp.sum(ex, axis=-1, keepdims=True)
        self.probs[k] = probs
        attn = mm(probs.astype(BF), value).astype(BF)
        self.attn[k] = attn
        term = mm(attn, self.wo[...]).astype(BF)
        d = i // 2
        mine_too = lax.rem(i, 2) == self.p.c

        @pl.when(mine_too)
        def _():
            self.sc.own[d] = term

        @pl.when(jnp.logical_not(mine_too))
        def _():
            self.ob[d] = term
            self.sc.swap(d).start()

    def finish(self):
        self.store(6).wait()
        self.store(7).wait()


class MadeScatter(Scatter):
    def __init__(self, p, made, scratch):
        super().__init__(p, None, scratch)
        self.made = made

    def swap(self, d):
        return rcopy(self.made.at[d], self.got.at[d], self.csend.at[d], self.crecv.at[d], self.p.sibling())

    def pair(self, d):
        self.swap(d).wait_recv()
        self.own[d] = (self.own[d].astype(F32) + self.got[d].astype(F32)).astype(BF)


class Feed:
    def __init__(self, p, block, xn2, g, wgu, wd, outs, bufs, sems):
        self.p, self.block = p, block
        self.xn2, self.g, self.wgu, self.wd, self.outs = xn2, g, wgu, wd, outs
        self.xb, self.gb, self.made, self.got = bufs
        self.xsem, self.gsem, self.osem = sems
        self.n = self.xb.shape[1]
        self.fb = wd.shape[0]

    def rows(self, ref, i):
        return ref.at[pl.ds(self.block(i) * self.n, self.n)]

    def loads(self, i):
        b = lax.rem(i, 2)
        return [
            pltpu.make_async_copy(self.rows(self.xn2, i), self.xb.at[b], self.xsem.at[b]),
            pltpu.make_async_copy(self.rows(self.g, i), self.gb.at[b], self.gsem.at[b]),
        ]

    def stores(self, i):
        b = lax.rem(i, 2)
        srcs = (self.got.at[2 + b, :, pl.ds(0, self.fb)], self.made.at[b], self.got.at[b])
        return [
            pltpu.make_async_copy(src, self.rows(out, i), self.osem.at[j, b])
            for j, (src, out) in enumerate(zip(srcs, self.outs, strict=True))
        ]

    def step(self, i):
        b, fb = lax.rem(i, 2), self.fb
        for cp in self.loads(i):
            cp.wait()

        @pl.when(i >= 2)
        def _():
            for cp in self.stores(i - 2):
                cp.wait()

        xn, g = self.xb[b], self.gb[b]
        gate, up = mm(xn, self.wgu[:, :fb]), mm(xn, self.wgu[:, fb:])
        sigma = jax.nn.sigmoid(gate)
        swish = gate * sigma
        hid = (swish * up).astype(BF)
        self.got[2 + b, :, :fb] = hid
        dhid = mm_nt(g, self.wd[...])
        dgate = (dhid * up * sigma * (1.0 + gate * (1.0 - sigma))).astype(BF)
        dup = (dhid * swish).astype(BF)
        self.made[b, :, :fb] = dgate
        self.made[b, :, fb:] = dup
        self.got[b] = mm_nt(self.made[b], self.wgu[...]).astype(BF)
        for cp in self.stores(i):
            cp.start()

    def finish(self):
        for i in (6, 7):
            for cp in self.stores(i):
                cp.wait()


def front_kernel(
    x_ref, seg_ref, gain_ref, freq_ref, wq_ref, wk_ref, wv_ref, wo_hbm, wg_ref, wu_ref, wd_hbm, g_ref,
    h_ref, xn2_ref, ga_ref, wgu_ref, gains_ref, xa_ref, wqkv_ref, xn1_ref, q_ref, k_ref, v_ref,
    attn_ref, probs_ref, turn_ref, hid_ref, dgu_ref, dx_ref, *scr
):
    p = Place()
    nz = lax.axis_size("z")
    others = [(0, 1)] + [(d, o) for d in (1, 2, 3) for o in (0, 1)]

    def dev(d, o):
        return {"core": 1 - p.c if o else p.c, "shard": p.shard(d)}

    scr = list(scr)

    def take(n):
        out = scr[:n]
        del scr[:n]
        return out

    ga = Gather(p, x_ref, xa_ref, take(5))
    gg = Gather(p, g_ref, ga_ref, take(5))
    [xnb] = take(1)
    gx = Gather(p, xnb, xn2_ref, take(5))
    co = Columns(p, take(3))
    tsend, trecv, tlocal = take(3)
    fb = wgu_ref.shape[1] // 2
    re = [Relay(p, wg_ref, wgu_ref, 0, take(5)), Relay(p, wu_ref, wgu_ref, fb, take(5))]
    [made] = take(1)
    sc = MadeScatter(p, made, take(8))
    wqkv, wo, seg, seg8, gaina_ref, lsem = take(6)
    bufs, sems = take(10), take(4)
    [osem] = take(1)
    wgu, wd, gsem, fsem = take(4)
    part, hd = wq_ref.shape[0], HEAD_DIM

    load_wo = pltpu.make_async_copy(wo_hbm.at[pl.ds(p.c * hd, hd)], wo, lsem.at[0])
    load_wqkv = pltpu.make_async_copy(wqkv_ref, wqkv, lsem.at[1])
    load_wd = pltpu.make_async_copy(wd_hbm.at[pl.ds(p.c * fb, fb)], wd, lsem.at[2])
    load_wgu = pltpu.make_async_copy(wgu_ref, wgu, lsem.at[3])
    load_wo.start()
    load_wd.start()
    seg8[...] = jnp.broadcast_to(seg_ref[...].astype(F32), seg8.shape)
    greet_line(p, [dev(d, o) for d, o in others])

    def q_copy(d):
        src = co.cols(p.shard(d) * 2 + p.c, d, wq_ref, hd)
        return co.copy(0, d, src, rows_at(wqkv_ref, p.s * part, part, 0, hd))

    def kv_copy(d, w):
        src = co.cols(p.shard(d), d, w, hd)
        return co.copy(1, d, src, rows_at(wqkv_ref, p.s * part, part, hd, hd))

    def small(k):
        d, o = others[k]
        yield rcopy(seg8, seg.at[p.c * 4 + p.s], tsend.at[k], trecv.at[k], dev(d, o))
        if d and not o:
            yield rcopy(gain_ref, gaina_ref.at[p.s], tsend.at[7 + d - 1], trecv.at[7 + d - 1], dev(d, o))

    smalls = [cp for k in range(7) for cp in small(k)] + [
        pltpu.make_async_copy(seg8, seg.at[p.c * 4 + p.s], tlocal.at[0]),
        pltpu.make_async_copy(gain_ref, gaina_ref.at[p.s], tlocal.at[1]),
    ]
    for cp in smalls:
        cp.start()
    for d in (3, 1, 2, 0):
        q_copy(d).start()

        @pl.when(p.c == 0)
        def _():
            kv_copy(d, wk_ref).start()

        @pl.when(p.c != 0)
        def _():
            kv_copy(d, wv_ref).start()

    ga.start()
    for cp in smalls:
        cp.wait()
    re[0].start()
    ga.relay()
    for d in (3, 1, 2, 0):
        q_copy(d).wait()
        kv_copy(d, wk_ref).wait()
    load_wqkv.start()
    ga.home()
    load_wo.wait()
    load_wqkv.wait()
    gain1 = jnp.concatenate([gaina_ref[j, 0:1] for j in range(4)], -1)
    gain2 = jnp.concatenate([gaina_ref[j, 1:2] for j in range(4)], -1)
    gains_ref[0:1], gains_ref[1:2] = gain1, gain2
    fw = Forward(p, xa_ref, xn1_ref, wqkv, wo, seg, gain1, freq_ref[...], sc, made, bufs, sems)

    def pair(d):
        sc.pair(d)
        if d == 3:
            sc.move(0).start()
            sc.move(1).start()
        elif d:
            sc.move(1 + d).start()

    def step(i):
        at_tick(i, 1, ga.early)
        at_tick(i, 1, re[1].start)
        at_tick(i, 2, lambda: ga.both((0, 2)))
        at_tick(i, 2, re[0].own)
        at_tick(i, 4, lambda: ga.both((1, 3)))
        at_tick(i, 4, re[1].own)
        at_tick(i, 5, ga.late)
        at_tick(i, 5, gg.start)
        at_tick(i, 6, lambda: ga.both((4, 5)))
        at_tick(i, 5, lambda: re[0].hop(1))
        at_tick(i, 7, lambda: re[1].hop(1))
        at_tick(i, 8, lambda: re[0].hop(2))

        @pl.when(jnp.logical_and(lax.rem(i, 2) == 0, i < 8))
        def _():
            fw.load(i).start()
            fw.load(i + 1).start()

        pl.when(i < 8)(lambda: fw.first(i))
        pl.when(i > 0)(lambda: fw.second(i - 1))
        for d in range(4):
            at_tick(i, 2 * d + 2, functools.partial(pair, d))

    loop(0, 9, step)
    saved = [
        pltpu.make_async_copy(a, b, osem.at[j])
        for j, (a, b) in enumerate(
            zip(bufs[2:8], (q_ref, k_ref, v_ref, attn_ref, probs_ref, turn_ref), strict=True)
        )
    ]
    for cp in saved:
        cp.start()
    gg.relay()
    sc.relay()
    re[1].hop(2)
    half = sc.half
    for h in (0, 1):
        r = pl.ds(h * half, half)
        res = x_ref[r].astype(F32) + sc.total(h)
        h_ref[r] = res
        f = lax.rsqrt(jnp.mean(res * res, axis=1, keepdims=True) + norm_eps)
        xnb[r] = (res * f * gain2).astype(BF)
    gx.start()
    re[0].hop(nz - 1)
    gg.early()
    gg.late()
    re[1].hop(nz - 1)
    for r in re:
        r.local().wait()
    load_wgu.start()
    fw.finish()
    sc.drain()
    load_wd.wait()
    gg.home()
    gx.home()
    gx.relay()
    fd = Feed(
        p, fw.block, xn2_ref, ga_ref, wgu, wd, (hid_ref, dgu_ref, dx_ref),
        (bufs[0], bufs[1], made, sc.got), (sems[0], gsem, fsem),
    )

    for cp in fd.loads(0):
        cp.start()
    load_wgu.wait()

    def feed(i):
        for ks, when in (((0, 2), 1), ((1, 3), 3), ((4, 5), 5)):
            at_tick(i, when, lambda ks=ks: (gx.both(ks), gg.both(ks)))

        @pl.when(i < 7)
        def _():
            for cp in fd.loads(i + 1):
                cp.start()

        fd.step(i)
        at_tick(i, 0, gx.early)
        at_tick(i, 3, gx.late)

    loop(0, 8, feed)
    fd.finish()
    for gather in (ga, gg, gx):
        gather.close()
    for r in re:
        r.finish()
    for cp in saved:
        cp.wait()


def front(x, seg, gains, freq, wq, wk, wv, wo, wg, wu, wd, g):
    rows, width = x.shape
    hd = HEAD_DIM
    fb = wg.shape[1] // 8
    nz = lax.axis_size("z")
    every = jax.ShapeDtypeStruct((8 * rows, width), BF)
    head = jax.ShapeDtypeStruct((8, rows, hd), BF)
    keep = pltpu.VMEM((8, rows, hd), BF)
    wide = pltpu.VMEM((2, rows, width), BF)
    return pl.pallas_call(
        front_kernel,
        out_shape=(
            jax.ShapeDtypeStruct((rows, width), F32),
            every,
            every,
            jax.ShapeDtypeStruct((width, wg.shape[1] // 4), BF),
            jax.ShapeDtypeStruct((2, width), F32),
            every,
            jax.ShapeDtypeStruct((width, 2 * hd), BF),
            every,
            head,
            head,
            head,
            head,
            jax.ShapeDtypeStruct((8, rows, rows), F32),
            jax.ShapeDtypeStruct((8, rows, hd), F32),
            jax.ShapeDtypeStruct((8 * rows, fb), BF),
            jax.ShapeDtypeStruct((8 * rows, 2 * fb), BF),
            every,
        ),
        in_specs=[VM] * 4 + [ANY] * 7 + [VM],
        out_specs=(VM, ANY, ANY, ANY, VM) + (ANY,) * 12,
        scratch_shapes=GATHER_SEMS * 2
        + [pltpu.VMEM((rows, width), BF)]
        + GATHER_SEMS
        + [DMA((2, 3)), DMA((2, 3)), DMA((2,)), DMA((10,)), DMA((10,)), DMA((2,))]
        + relay_sems(nz) * 2
        + [pltpu.VMEM((4, rows, width), BF)]
        + scatter_scratch(rows, width)
        + [
            pltpu.VMEM((width, 2 * hd), BF),
            pltpu.VMEM((hd, width), BF),
            pltpu.VMEM((8, 8, rows), F32),
            pltpu.VMEM((8, rows), F32),
            pltpu.VMEM((4, *gains.shape), F32),
            DMA((4,)),
        ]
        + [wide, wide, keep, keep, keep, keep]
        + [pltpu.VMEM((8, rows, rows), F32), pltpu.VMEM((8, rows, hd), F32), keep, keep]
        + [DMA((2,)), DMA((2,)), DMA((8,)), DMA((8,)), DMA((6,))]
        + [pltpu.VMEM((width, 2 * fb), BF), pltpu.VMEM((fb, width), BF), DMA((2,)), DMA((3, 2))],
        compiler_params=params(0, 63),
        name="front",
    )(x, seg, gains, freq, wq, wk, wv, wo, wg, wu, wd, g)


CH = 32
QR = 4 * CH
FINE = 64 // CH
DOWN, GU, OUT, QKV = range(4)
COUNT = {DOWN: 512 // CH, GU: 1024 // CH, OUT: 128 // CH, QKV: 1024 // QR}
N_TICKS = sum(COUNT.values())
EARLY = COUNT[DOWN] + COUNT[GU]
GJ = COUNT[GU] // 4
SLOTS, N_SLOTTED = 12, EARLY + COUNT[OUT]


class Chain:
    def __init__(self, p, h, ins, outs, bufs, sems):
        self.p, self.h = p, h
        self.ins = ins
        self.gate, self.up, self.down, self.out, self.wq, self.wk, self.wv = outs
        self.buf, self.bufq, self.ring, self.ring_sem, self.credit = bufs
        self.rs_send, self.rs_recv, self.ag_send, self.ag_recv, self.cp_send, self.cp_recv, self.tsend = sems
        nz = lax.axis_size("z")
        self.nz = nz
        self.pos = nz - 1 - p.z if h == 0 else p.z
        self.step = -1 if h == 0 else 1

    def dev(self, by):
        return {"z": self.p.z + by}

    BASE = {GU: 0, DOWN: COUNT[GU], OUT: EARLY, QKV: EARLY + COUNT[OUT]}

    def tick(self, kind, t):
        return self.BASE[kind] + t

    def dist(self, kind, t):
        return t // GJ if kind == GU else lax.rem(t, 4)

    def row(self, kind, t):
        return lax.rem(t, GJ) * CH if kind == GU else (t // 4) * QR

    def shard_of(self, kind, t):
        return self.p.shard_at(self.dist(kind, t))

    def mine(self, kind, t):
        h = self.h
        if kind == DOWN:
            return self.ins[DOWN].at[pl.ds(h * 512 + t * CH, CH)]
        if kind == OUT:
            return self.ins[OUT].at[pl.ds(h * 128 + t * CH, CH)]
        row = self.shard_of(kind, t) * 512 + h * 256 + self.row(kind, t)
        return self.ins[kind].at[pl.ds(row, QR if kind == QKV else CH)]

    def fetch(self, kind, t):
        r = lax.rem(self.tick(kind, t), RING)
        return pltpu.make_async_copy(self.mine(kind, t), self.ring.at[r], self.ring_sem.at[r])

    def ahead(self, kind, t):
        @pl.when(self.pos > 0)
        def _():
            self.fetch(kind, t).start()

    def slot(self, kind, t):
        return self.bufq.at[t] if kind == QKV else self.buf.at[lax.rem(self.tick(kind, t), SLOTS)]

    def may_send(self, kind, t):
        if kind != QKV:

            @pl.when(self.tick(kind, t) >= SLOTS)
            def _():
                pl.semaphore_wait(self.credit, 1)

    def retire(self, kind, t):
        self.gone(kind, t)
        if kind != QKV:

            @pl.when(jnp.logical_and(self.pos > 0, self.tick(kind, t) < N_SLOTTED - SLOTS))
            def _():
                pl.semaphore_signal(self.credit, inc=1, device_id=self.dev(-self.step), device_id_type=MESH)

    def rs_copy(self, kind, t, src):
        k = self.tick(kind, t)
        return rcopy(
            src, self.slot(kind, t), self.rs_send.at[k], self.rs_recv.at[k], self.dev(self.step)
        )

    def begin(self, kind, t):
        @pl.when(self.pos == 0)
        def _():
            self.may_send(kind, t)
            self.rs_copy(kind, t, self.mine(kind, t)).start()

    def reduce(self, kind, t):
        first, last = self.pos == 0, self.pos == self.nz - 1

        @pl.when(jnp.logical_not(first))
        def _():
            slot = self.slot(kind, t)
            if kind in (DOWN, GU):
                self.fetch(kind, t).wait()
                own = self.ring.at[lax.rem(self.tick(kind, t), RING)]
            else:
                own = self.mine(kind, t)
            self.rs_copy(kind, t, slot).wait_recv()
            slot[...] = (slot[...].astype(F32) + own[...].astype(F32)).astype(BF)

        @pl.when(jnp.logical_and(jnp.logical_not(first), jnp.logical_not(last)))
        def _():
            self.may_send(kind, t)
            self.rs_copy(kind, t, self.slot(kind, t)).start()

        @pl.when(last)
        def _():
            self.turn(kind, t)

    def pieces(self, kind, t, s, d_shard):
        h, c = self.h, self.p.c
        if kind == DOWN:
            return [(None, self.down.at[pl.ds(c * 1024 + h * 512 + t * CH, CH)])]
        if kind == OUT:
            return [(None, self.out.at[pl.ds(c * 256 + h * 128 + t * CH, CH)])]
        if kind == GU:
            r = h * 256 + self.row(kind, t)
            c0 = pl.multiple_of((s * 2 + c) * 1024, 1024)
            return [
                ((0, 1024), self.gate.at[pl.ds(r, CH), pl.ds(c0, 1024)]),
                ((1024, 1024), self.up.at[pl.ds(r, CH), pl.ds(c0, 1024)]),
            ]
        r = h * 256 + (t // 4) * QR
        cq = pl.multiple_of((s * 2 + c) * 256, 256)
        return [((0, 256), self.wq.at[pl.ds(r, QR), pl.ds(cq, 256)])]

    def kv_piece(self, t, s, w):
        r = self.h * 256 + (t // 4) * QR
        return w.at[pl.ds(r, QR), pl.ds(pl.multiple_of(s * 256, 256), 256)]

    def turn(self, kind, t):
        slot = self.slot(kind, t)
        k = self.tick(kind, t)
        to = self.p.s if kind in (DOWN, OUT) else self.shard_of(kind, t)

        def send(i, src, dst):
            if kind in (DOWN, OUT):
                pltpu.make_async_copy(src, dst, self.ag_recv.at[i, k]).start()
                return

            @pl.when(self.dist(kind, t) == 0)
            def _():
                pltpu.make_async_copy(src, dst, self.ag_recv.at[i, k]).start()

            @pl.when(self.dist(kind, t) != 0)
            def _():
                rcopy(src, dst, self.tsend.at[i, k], self.ag_recv.at[i, k], {"shard": to}).start()

        for i, (cols, dst) in enumerate(self.pieces(kind, t, self.p.s, to)):
            send(i, slot if cols is None else slot.at[:, pl.ds(*cols)], dst)
        if kind == QKV:
            src = slot.at[:, pl.ds(256, 256)]

            @pl.when(self.p.c == 0)
            def _():
                send(1, src, self.kv_piece(t, self.p.s, self.wk))

            @pl.when(self.p.c != 0)
            def _():
                send(1, src, self.kv_piece(t, self.p.s, self.wv))

    def spread_copy(self, i, k, ref):
        return rcopy(ref, ref, self.ag_send.at[i, k], self.ag_recv.at[i, k], self.dev(-self.step))

    def spread(self, kind, t):
        k = self.tick(kind, t)
        s = self.p.s if kind in (DOWN, OUT) else self.shard_of(kind, t)

        def go(i, ref, wait=True):
            if wait:
                self.spread_copy(i, k, ref).wait_recv()

            @pl.when(self.pos > 0)
            def _():
                self.spread_copy(i, k, ref).start()

            rcopy(ref, ref, self.cp_send.at[i, k], self.cp_recv.at[i, k], self.p.sibling()).start()

        for i, (_, ref) in enumerate(self.pieces(kind, t, s, None)):
            go(i, ref)
        if kind == QKV:
            self.spread_copy(1, k, self.kv_piece(t, s, self.wk)).wait_recv()

            @pl.when(self.p.c == 0)
            def _():
                go(1, self.kv_piece(t, s, self.wk), False)

            @pl.when(self.p.c != 0)
            def _():
                go(1, self.kv_piece(t, s, self.wv), False)

    def gone(self, kind, t):
        k = self.tick(kind, t)

        @pl.when(self.pos < self.nz - 1)
        def _():
            self.rs_copy(kind, t, self.slot(kind, t)).wait_send()

        if kind not in (GU, QKV):
            return

        @pl.when(jnp.logical_and(self.pos == self.nz - 1, self.dist(kind, t) != 0))
        def _():
            slot = self.slot(kind, t)
            for i, (cols, dst) in enumerate(self.pieces(kind, t, self.p.s, None)):
                src = slot.at[:, pl.ds(*cols)]
                rcopy(src, dst, self.tsend.at[i, k], self.ag_recv.at[i, k], self.p.to(1)).wait_send()
            if kind == QKV:
                src = slot.at[:, pl.ds(256, 256)]
                dst = self.kv_piece(t, self.p.s, self.wk)
                rcopy(src, dst, self.tsend.at[1, k], self.ag_recv.at[1, k], self.p.to(1)).wait_send()

    def drain_spread(self, kind, t):
        k = self.tick(kind, t)
        s = self.p.s if kind in (DOWN, OUT) else self.shard_of(kind, t)
        refs = [ref for _, ref in self.pieces(kind, t, s, None)]
        if kind == QKV:
            refs.append(self.kv_piece(t, s, self.wk))
        for i, ref in enumerate(refs):

            @pl.when(self.pos > 0)
            def _():
                self.spread_copy(i, k, ref).wait_send()

            rcopy(ref, ref, self.cp_send.at[i, k], self.cp_recv.at[i, k], self.p.sibling()).wait()


RING = 4
CHAIN_SEMS = [DMA((N_TICKS,))] * 2 + [DMA((2, N_TICKS))] * 5


def loop(lo, hi, body):
    def step(t, _):
        body(t)
        return 0

    lax.fori_loop(lo, hi, step, 0)


SKEW, TURN, RETIRE = 2, 3, 4


def between(i, lo, hi):
    return jnp.logical_and(i >= lo, i < hi)


def each(i, lo, hi, act):
    for kind, n in COUNT.items():
        base = Chain.BASE[kind]
        a, b = max(lo, base), min(hi, base + n)
        if isinstance(i, int):
            if a <= i < b:
                act(kind, i - base)
        elif a < b:

            @pl.when(between(i, a, b))
            def _():
                act(kind, i - base)


def at_tick(t, when, act):
    @pl.when(t == when)
    def _():
        act()


def all_greet(p):
    nz = lax.axis_size("z")
    greet(plane_ids(p) + [{"z": lax.rem(p.z + k, nz)} for k in range(1, nz)])


class GainSums:
    def __init__(self, p, tot, got, gz, send, recv):
        self.p, self.tot, self.got, self.gz, self.send, self.recv = p, tot, got, gz, send, recv
        self.nz = lax.axis_size("z")

    def copy(self, k):
        dev = (self.p.sibling(), self.p.to(1), self.p.to(2))[k]
        return rcopy(self.tot.at[k], self.got.at[k], self.send.at[k], self.recv.at[k], dev)

    def along(self, k):
        to = {"z": lax.rem(self.p.z + k, self.nz)}
        return rcopy(
            self.tot.at[3], self.gz.at[self.p.z], self.send.at[2 + k], self.recv.at[3 + self.p.z], to
        )

    def landed(self, k):
        src = lax.rem(self.p.z + self.nz - k, self.nz)
        ref = self.gz.at[src]
        return rcopy(ref, ref, self.send.at[2 + k], self.recv.at[3 + src], {"z": src})

    def add(self, k):
        self.copy(k).wait()
        self.tot[k + 1] = self.tot[k] + self.got[k]
        if k < 2:
            self.copy(k + 1).start()
        else:
            for j in range(1, self.nz):
                self.along(j).start()
            self.gz[self.p.z] = self.tot[3]

    def finish(self):
        for j in range(1, self.nz):
            self.along(j).wait_send()
            self.landed(j).wait_recv()
        total = self.gz[0]
        for j in range(1, self.nz):
            total = total + self.gz[j]
        return total


class Attention:
    def __init__(self, p, hbm, wo, wqkv, part, gout, gqkv, bufs, sems):
        self.p, self.hbm, self.wo, self.wqkv, self.part = p, hbm, wo, wqkv, part
        self.gout, self.gqkv = gout, gqkv
        self.bufs, self.other, self.came, self.kept, self.dq, self.rows_out = bufs[:8], *bufs[8:]
        self.sem, self.send, self.recv, self.psem = sems
        self.n = self.rows_out.shape[1]

    def load(self, i, j):
        src = self.hbm[i]
        ref = src.at[pl.ds(j * self.n, self.n)] if len(src.shape) == 2 else src.at[j]
        b = lax.rem(j, 2)
        return pltpu.make_async_copy(ref, self.bufs[i].at[b], self.sem.at[i, b])

    def fetch(self, j):
        for i in range(7):
            self.load(i, j).start()

    def swap(self, j):
        return rcopy(self.other.at[j], self.came.at[j], self.send.at[j], self.recv.at[j], self.p.sibling())

    def first(self, j):
        for i in range(7):
            self.load(i, j).wait()

        @pl.when(j < 7)
        def _():
            self.fetch(j + 1)

        b = lax.rem(j, 2)
        dhb, q, k, v, attn, probs, turn = (self.bufs[i][b] for i in range(7))
        scale = HEAD_DIM ** (-0.5)
        half = HEAD_DIM // 2
        cosine, sine = turn[:, :half], turn[:, half:]
        dattn = mm_nt(dhb, self.wo[...]).astype(BF)
        g = mm_tn(attn, dhb)
        self.gout[...] = jnp.where(j == 0, g, self.gout[...] + g)
        dp = mm_nt(dattn, v)
        dv = mm_tn(probs.astype(BF), dattn)
        ds = (probs * (dp - jnp.sum(dp * probs, axis=-1, keepdims=True))).astype(BF)
        dq = rotate(mm(ds, k) * scale, cosine, -sine)
        dk = rotate(mm_tn(ds, q) * scale, cosine, -sine)
        zero = self.p.c == 0
        self.dq[b] = dq.astype(BF)
        self.kept[b] = jnp.where(zero, dk, dv)
        self.other[j] = jnp.where(zero, dv, dk).astype(BF)
        self.swap(j).start()
        self.load(7, j).start()

    def out_copy(self, j):
        b = lax.rem(j, 2)
        return pltpu.make_async_copy(self.rows_out.at[b], self.part.at[pl.ds(j * self.n, self.n)], self.psem.at[b])

    def second(self, j):
        b = lax.rem(j, 2)
        self.swap(j).wait()
        self.load(7, j).wait()
        dkv = (self.kept[b] + self.came[j].astype(F32)).astype(BF)
        dqkv = jnp.concatenate([self.dq[b], dkv], -1)
        g = mm_tn(self.bufs[7][b], dqkv)
        self.gqkv[...] = jnp.where(j == 0, g, self.gqkv[...] + g)

        @pl.when(j >= 2)
        def _():
            self.out_copy(j - 2).wait()

        self.rows_out[b] = mm_nt(dqkv, self.wqkv[...]).astype(BF)
        self.out_copy(j).start()

    def finish(self):
        self.out_copy(6).wait()
        self.out_copy(7).wait()


class Outer:
    def __init__(self, p, left, right_hbm, right, xc, out, row, sems):
        self.p, self.left, self.right_hbm, self.right, self.xc, self.out = p, left, right_hbm, right, xc, out
        self.row = row
        self.dsem, self.xsem, self.osem = sems

    def whole(self):
        return pltpu.make_async_copy(self.right_hbm, self.right, self.dsem.at[0])

    def load(self, n):
        b = lax.rem(n, 2)
        cols = pl.ds(pl.multiple_of(self.row(n), 256), 256)
        return pltpu.make_async_copy(self.left.at[:, cols], self.xc.at[b], self.xsem.at[b])

    def store(self, n, made):
        rows = pl.ds(pl.multiple_of(self.row(n), 256), 256)
        return pltpu.make_async_copy(made, self.out.at[rows], self.osem.at[0])

    def step(self, n, last, made):
        @pl.when(n == 0)
        def _():
            self.whole().wait()

        @pl.when(n > 0)
        def _():
            self.store(n - 1, made).wait()

        self.block(n, last, made)

    def block(self, n, last, made):
        self.load(n).wait()

        @pl.when(n < last)
        def _():
            self.load(n + 1).start()

        made[...] = mm_tn(self.xc[lax.rem(n, 2)], self.right[...]).astype(BF)
        self.store(n, made).start()


class Product:
    def __init__(self, hid, wd_hbm, right, made, out, sems):
        self.hid, self.wd_hbm, self.right, self.made, self.out = hid, wd_hbm, right, made, out
        self.wsem, self.hsem, self.osem = sems
        self.n, self.fb = made.shape[1], hid.shape[1]

    def weights(self):
        return pltpu.make_async_copy(self.wd_hbm, self.right.at[pl.ds(0, self.fb)], self.wsem.at[0])

    def space(self, i):
        return pl.ds(self.fb + lax.rem(i, 2) * self.n, self.n)

    def load(self, i):
        dst = self.right.at[self.space(i), pl.ds(0, self.fb)]
        return pltpu.make_async_copy(self.hid.at[pl.ds(i * self.n, self.n)], dst, self.hsem.at[lax.rem(i, 2)])

    def store(self, i):
        b = lax.rem(i, 2)
        return pltpu.make_async_copy(self.made.at[b], self.out.at[pl.ds(i * self.n, self.n)], self.osem.at[b])

    def start(self):
        self.weights().start()
        self.load(0).start()

    def step(self, i):
        @pl.when(i == 0)
        def _():
            self.weights().wait()

        self.load(i).wait()

        @pl.when(i < 7)
        def _():
            self.load(i + 1).start()

        @pl.when(i >= 2)
        def _():
            self.store(i - 2).wait()

        h = self.right[self.space(i), : self.fb]
        self.made[lax.rem(i, 2)] = mm(h, self.right[: self.fb]).astype(BF)
        self.store(i).start()

    def finish(self):
        self.store(6).wait()
        self.store(7).wait()


def tail_kernel(
    part_ref, x_hbm, h_hbm, g_hbm, gain_ref, hid_ref, ga_ref, xn2_ref, dgu_hbm, wd_hbm, wo_hbm, wqkv_ref,
    q_ref, k_ref, v_ref, attn_ref, probs_ref, turn_ref, xn1_ref,
    out_hbm, grad_hbm, gains_ref, dhb_ref, p1_ref, ggu_ref, gd_ref, dpart_ref, gate, up, down, out, wq, wk, wv,
    bufa, bufb, qa, qb, ringa, ringb, ring_sem, credita, creditb, big, xc, dsem, xsem, osem, psem, hsem, psem2, tot, got, gz, gsend, grecv,
    low, xg, hb, dh, gout, gqkv, gout_low, gqkv_low, wo_ref, io_sem, free_sem, *scr
):
    p = Place()
    nz = lax.axis_size("z")
    s1 = Scatter(p, part_ref, scr[:8])
    s2 = Scatter(p, dpart_ref, scr[:8])
    s3 = Scatter(p, p1_ref, scr[:8])
    ga = Gather(p, low, dhb_ref, scr[8:13])
    sums = GainSums(p, tot, got, gz, gsend, grecv)
    hbm = (dhb_ref, q_ref, k_ref, v_ref, attn_ref, probs_ref, turn_ref, xn1_ref)
    at = Attention(p, hbm, wo_ref, wqkv_ref, p1_ref, gout, gqkv, scr[13:26], scr[26:30])
    gu = Outer(
        p, xn2_ref, dgu_hbm, big, xc, ggu_ref,
        lambda n: p.shard_at(n // 2) * 512 + lax.rem(n, 2) * 256,
        (dsem, xsem.at[0], osem.at[0]),
    )
    gd = Outer(
        p, hid_ref, ga_ref, big, xc, gd_ref,
        lambda n: lax.rem(n, 2) * 512 + (n // 2) * 256,
        (dsem.at[pl.ds(1, 1)], xsem.at[1], osem.at[1]),
    )
    made = at.rows_out.at[0]
    fb = hid_ref.shape[1]
    wd = wd_hbm.at[pl.ds(p.c * fb, fb)]
    pr = Product(hid_ref, wd, big, at.rows_out, dpart_ref, (psem.at[pl.ds(0, 1)], hsem, psem2))
    ins = (gd_ref, ggu_ref, gout_low, gqkv_low)
    outs = (gate, up, down, out, wq, wk, wv)
    n = len(CHAIN_SEMS)
    chains = [
        Chain(p, 0, ins, outs, (bufa, qa, ringa, ring_sem.at[0], credita), scr[30 : 30 + n]),
        Chain(p, 1, ins, outs, (bufb, qb, ringb, ring_sem.at[1], creditb), scr[30 + n : 30 + 2 * n]),
    ]
    line = SKEW * (nz - 1)
    half = s1.half

    def io(k):
        wo = wo_hbm.at[pl.ds(p.c * HEAD_DIM, HEAD_DIM)]
        src, dst = [(h_hbm, hb), (g_hbm, xg), (x_hbm, xg), (low, out_hbm), (low, grad_hbm), (wo, wo_ref)][k]
        return pltpu.make_async_copy(src, dst, io_sem.at[k])

    io(0).start()
    io(1).start()
    io(5).start()
    gu.whole().start()
    gu.load(0).start()
    tot[0] = jnp.zeros_like(tot[0])
    all_greet(p)
    s1.start()
    s1.first(0)
    gu.step(0, 7, made)
    s1.first(1)
    gu.step(1, 7, made)
    gu.store(1, made).wait()

    def norm2():
        for k in (0, 1, 5):
            io(k).wait()
        for h in (0, 1):
            r = pl.ds(h * half, half)
            dx = s1.total(h)
            res = hb[r]
            f = lax.rsqrt(jnp.mean(res * res, axis=1, keepdims=True) + norm_eps)
            hat = res * f
            term = jnp.sum(dx * hat, axis=0, keepdims=True)
            tot[0, 1:2] = term if h == 0 else tot[0, 1:2] + term
            d = xg[r].astype(F32) + norm_backward_step(dx * gain_ref[1:2], hat, f)
            dh[r] = d
            low[r] = d.astype(BF)
        ga.start()
        io(2).start()

    def gathered():
        ga.finish()
        s1.drain()
        at.fetch(0)
        s2.start()

    def output():
        for h in (0, 1):
            r = pl.ds(h * half, half)
            low[r] = (hb[r] + s2.total(h)).astype(BF)
        io(3).start()
        s2.drain()
        for d in (p.to(1), p.to(2), p.sibling()):
            pl.semaphore_signal(free_sem, inc=1, device_id=d, device_id_type=MESH)

    def attended():
        at.finish()
        gout_low[...] = gout[...].astype(BF)
        gqkv_low[...] = gqkv[...].astype(BF)
        pl.semaphore_wait(free_sem, 3)
        s3.start()

    def norm1():
        io(2).wait()
        io(3).wait()
        for h in (0, 1):
            r = pl.ds(h * half, half)
            dx = s3.total(h)
            xf = xg[r].astype(F32)
            f = lax.rsqrt(jnp.mean(xf * xf, axis=1, keepdims=True) + norm_eps)
            hat = xf * f
            term = jnp.sum(dx * hat, axis=0, keepdims=True)
            tot[0, 0:1] = term if h == 0 else tot[0, 0:1] + term
            low[r] = (dh[r] + norm_backward_step(dx * gain_ref[0:1], hat, f)).astype(BF)
        io(4).start()
        sums.copy(0).start()

    def gains():
        gains_ref[...] = sums.finish()

    def gate_up(n):
        @pl.when(n > 2)
        def _():
            gu.store(n - 1, made).wait()

        gu.block(n, 7, made)

    def products():
        gu.store(7, made).wait()
        pr.start()

    def two_products(i):
        pr.step(i)
        pr.step(i + 1)

    def downs():
        pr.finish()
        gd.whole().start()
        gd.load(0).start()

    def tick(t):
        for ch in chains:
            each(t + 1 - SKEW * ch.pos, 0, EARLY, ch.ahead)
            each(t, 0, N_TICKS, ch.begin)
            each(t - SKEW * ch.pos, 0, N_TICKS, ch.reduce)
        for ch in chains:
            each(t - TURN - 2 * line + SKEW * ch.pos, 0, N_TICKS, ch.spread)
            each(t - RETIRE - SKEW * ch.pos, 0, N_SLOTTED, ch.retire)
        u = t // FINE
        pl.when(jnp.logical_and(between(t, 2, 14), lax.rem(t, 2) == 0))(lambda: gate_up(t // 2 + 1))
        at_tick(t, 14, products)
        pl.when(between(t, 16, 20))(lambda: two_products(2 * (t - 16)))
        at_tick(t, 20, downs)
        pl.when(jnp.logical_and(between(t, 25, 33), lax.rem(t, 2) == 1))(
            lambda: gd.step((t - 25) // 2, 3, gout_low)
        )
        at_tick(t, 33, lambda: gd.store(3, gout_low).wait())
        for k in range(4):
            if k >= 2:
                at_tick(t, k - 2, functools.partial(s1.first, k))
            at_tick(t, FINE * A0 + k, functools.partial(s2.first, k))
            at_tick(t, FINE * (A0 + 9) + 1 + k, functools.partial(s3.first, k))

        @pl.when(lax.rem(t, FINE) == 0)
        def _():
            at_tick(u, 3, s1.relay)
            at_tick(u, 5, norm2)
            at_tick(u, 7, ga.relay)
            at_tick(u, A0 - 1, gathered)
            pl.when(between(u, A0 + 1, A0 + 9))(lambda: at.second(u - A0 - 1))
            pl.when(between(u, A0, A0 + 8))(lambda: at.first(u - A0))
            at_tick(u, A0 + 3, s2.relay)
            at_tick(u, A0 + 5, output)
            at_tick(u, A0 + 9, attended)
            at_tick(u, A0 + 12, s3.relay)
            at_tick(u, A0 + 14, norm1)
            for k in range(3):
                at_tick(u, A0 + 15 + k, functools.partial(sums.add, k))
            at_tick(u, A0 + 19, gains)

    loop(0, N_TICKS + TURN + 2 * line, tick)
    io(4).wait()
    s3.drain()

    def drain(i):
        for ch in chains:
            each(i, N_SLOTTED, N_TICKS, ch.gone)
            each(i, 0, N_TICKS, ch.drain_spread)

    loop(0, N_TICKS, drain)


A0 = 12


def tail(part, x, h, g, gains, hid, g_all, xn2, dgu, wd, wo, wqkv, heads, xn1, ff):
    rows, width = x.shape
    nz = lax.axis_size("z")
    hd, pr = HEAD_DIM, width // 4
    shapes = [(pr, ff), (pr, ff), (ff // 4, width), (pr, width), (pr, width), (pr, 1024), (pr, 1024)]
    sq = pltpu.VMEM((2, rows, hd), BF)
    wide = pltpu.VMEM((2, rows, width), BF)
    return pl.pallas_call(
        tail_kernel,
        out_shape=(
            jax.ShapeDtypeStruct((rows, width), BF),
            jax.ShapeDtypeStruct((rows, width), BF),
            jax.ShapeDtypeStruct((8, width), F32),
            jax.ShapeDtypeStruct((8 * rows, width), BF),
            jax.ShapeDtypeStruct((8 * rows, width), BF),
            jax.ShapeDtypeStruct((width, width), BF),
            jax.ShapeDtypeStruct((hid.shape[1], width), BF),
            jax.ShapeDtypeStruct((8 * rows, width), BF),
        )
        + tuple(jax.ShapeDtypeStruct(s, BF) for s in shapes),
        in_specs=[ANY] * 4 + [VM] + [ANY] * 6 + [VM] + [ANY] * 7,
        out_specs=(ANY, ANY, VM) + (ANY,) * 12,
        scratch_shapes=[
            pltpu.VMEM((SLOTS, CH, width), BF),
            pltpu.VMEM((SLOTS, CH, width), BF),
            pltpu.VMEM((COUNT[QKV], QR, 512), BF),
            pltpu.VMEM((COUNT[QKV], QR, 512), BF),
            pltpu.VMEM((RING, CH, width), BF),
            pltpu.VMEM((RING, CH, width), BF),
            DMA((2, RING)),
            pltpu.SemaphoreType.REGULAR,
            pltpu.SemaphoreType.REGULAR,
            pltpu.VMEM((8 * rows, width), BF),
            pltpu.VMEM((2, width, 256), BF),
            DMA((2,)),
            DMA((2, 2)),
            DMA((2, 1)),
            DMA((2,)),
            DMA((2,)),
            DMA((2,)),
            pltpu.VMEM((4, 8, width), F32),
            pltpu.VMEM((3, 8, width), F32),
            pltpu.VMEM((nz, 8, width), F32),
            DMA((nz + 3,)),
            DMA((nz + 3,)),
            pltpu.VMEM((rows, width), BF),
            pltpu.VMEM((rows, width), BF),
            pltpu.VMEM((rows, width), F32),
            pltpu.VMEM((rows, width), F32),
            pltpu.VMEM((hd, width), F32),
            pltpu.VMEM((width, 2 * hd), F32),
            pltpu.VMEM((hd, width), BF),
            pltpu.VMEM((width, 2 * hd), BF),
            pltpu.VMEM((hd, width), BF),
            DMA((6,)),
            pltpu.SemaphoreType.REGULAR,
        ]
        + scatter_scratch(rows, width)
        + GATHER_SEMS
        + [wide, sq, sq, sq, sq]
        + [pltpu.VMEM((2, rows, rows), F32), pltpu.VMEM((2, rows, hd), F32), wide]
        + [pltpu.VMEM((8, rows, hd), BF)] * 2
        + [pltpu.VMEM((2, rows, hd), F32), sq, wide]
        + [DMA((8, 2)), DMA((8,)), DMA((8,)), DMA((2,))]
        + CHAIN_SEMS * 2,
        compiler_params=params(2, 63),
        name="tail",
    )(part, x, h, g, gains, hid, g_all, xn2, dgu, wd, wo, wqkv, *heads, xn1)


def widen_kernel(*refs):
    n = len(refs) // 2
    for a, b in zip(refs[:n], refs[n:], strict=True):
        b[...] = a[...].astype(b.dtype)


def widen(arrays, kept):
    shapes = [jax.ShapeDtypeStruct(a.shape, F32) for a in arrays]
    shapes += [jax.ShapeDtypeStruct(a.shape, a.dtype) for a in kept]
    arrays = (*arrays, *kept)
    steps = 4

    def spec(a):
        return pl.BlockSpec((a.shape[0] // steps, a.shape[1]), lambda i: (i, 0))

    return pl.pallas_call(
        widen_kernel,
        grid=(steps,),
        out_shape=tuple(shapes),
        in_specs=[spec(a) for a in arrays],
        out_specs=tuple(spec(a) for a in arrays),
        compiler_params=pltpu.CompilerParams(vmem_limit_bytes=62 * 2**20),
        name="widen",
    )(*arrays)


def pieces(
    tokens,
    segment_ids,
    attn_gain,
    w_query,
    w_key,
    w_value,
    w_out,
    mlp_gain,
    w_gate,
    w_up,
    w_down,
    cotangent,
):
    rows, width = tokens.shape[1], tokens.shape[2]
    ns = lax.axis_size("shard")
    hd = HEAD_DIM
    ff = w_gate.shape[1]
    part = width // ns

    x = tokens.reshape(rows, width)
    g = cotangent.reshape(rows, width)
    gains = jnp.concatenate([attn_gain[None], mlp_gain[None], jnp.zeros((6, part), BF)], 0).astype(F32)
    half = np.arange(hd // 2, dtype=np.float64) * 2.0 / hd
    freq = jnp.asarray((rope_base ** -half).astype(np.float32)[None])
    h, xn2, g_all, _, gains, _, wqkv, xn1, q, k, v, attn, probs, turn, hid, dgu, dxpart = front(
        x, segment_ids, gains, freq, w_query, w_key, w_value, w_out, w_gate, w_up, w_down, g
    )
    heads = (q, k, v, attn, probs, turn)
    output, input_grad, gain_g, _, _, _, _, _, gate_g, up_g, down_g, out_g, wq_g, wk_g, wv_g = tail(
        dxpart,
        x,
        h,
        g,
        gains,
        hid,
        g_all,
        xn2,
        dgu,
        w_down,
        w_out,
        wqkv,
        heads,
        xn1,
        ff,
    )
    gain_g = lax.dynamic_slice_in_dim(gain_g, lax.axis_index("shard") * part, part, 1)
    wide = widen((wq_g, wk_g, wv_g, out_g, gate_g, up_g, down_g), (output, input_grad))
    output, input_grad = (a.reshape(1, rows, width) for a in wide[7:])
    return (output, input_grad, gain_g[0], *wide[:4], gain_g[1], *wide[4:7])


def contract_rows(left, right):
    return lax.dot_general(
        left, right, (((0,), (0,)), ((), ())), preferred_element_type=jnp.float32
    )


def contract_cols(left, right):
    return lax.dot_general(
        left, right, (((1,), (1,)), ((), ())), preferred_element_type=jnp.float32
    )


def scores_of(queries, keys, allowed):
    raw = jnp.einsum(
        "qgrd,kgd->grqk", queries, keys, preferred_element_type=jnp.float32
    ) * HEAD_DIM ** (-0.5)
    return jnp.where(allowed, raw, mask_fill)


def general(
    tokens,
    segment_ids,
    attn_gain,
    w_query,
    w_key,
    w_value,
    w_out,
    mlp_gain,
    w_gate,
    w_up,
    w_down,
    cotangent,
):
    rows = tokens.shape[1]
    width = tokens.shape[2]
    groups = HEADS // KV_HEADS
    q_cols = HEADS * HEAD_DIM
    kv_cols = KV_HEADS * HEAD_DIM
    layer_input_rows = tokens.reshape(rows, width).astype(jnp.float32)
    segments = segment_ids.reshape(rows)
    iota = jnp.arange(rows, dtype=jnp.int32)
    starts = jnp.sum((segments[None, :] < segments[:, None]).astype(jnp.int32), axis=1)
    positions = (iota - starts).astype(jnp.float32)
    allowed = (segments[:, None] == segments[None, :]) & (iota[:, None] >= iota[None, :])
    half = HEAD_DIM // 2
    inv_freq = rope_base ** (-(jnp.arange(half, dtype=jnp.float32) * 2.0 / HEAD_DIM))
    angles = positions[:, None] * inv_freq
    cosine = jnp.cos(angles)
    sine = jnp.sin(angles)
    first_norm_factor = lax.rsqrt(
        jnp.mean(layer_input_rows * layer_input_rows, axis=1, keepdims=True) + norm_eps
    )
    first_standardized = layer_input_rows * first_norm_factor
    gain_fragment = lax.all_gather(attn_gain, "shard", axis=0, tiled=True)
    query_piece = lax.all_gather(w_query, "shard", axis=0, tiled=True)
    key_piece = lax.all_gather(w_key, "shard", axis=0, tiled=True)
    value_piece = lax.all_gather(w_value, "shard", axis=0, tiled=True)
    normalized_rows = (first_standardized * gain_fragment.astype(jnp.float32)).astype(jnp.bfloat16)
    joined = jnp.concatenate([query_piece, key_piece, value_piece], 1)
    result = (
        jnp.dot(normalized_rows, joined, preferred_element_type=jnp.float32),
        normalized_rows,
        gain_fragment.astype(jnp.float32),
    )
    folded = result
    projected, normed_one, first_norm_gain = (folded[0], folded[1], folded[2])
    queries = rotate(
        projected[:, :q_cols].reshape(rows, KV_HEADS, groups, HEAD_DIM),
        cosine[:, None, None, :],
        sine[:, None, None, :],
    ).astype(jnp.bfloat16)
    keys = rotate(
        projected[:, q_cols : q_cols + kv_cols].reshape(rows, KV_HEADS, HEAD_DIM),
        cosine[:, None, :],
        sine[:, None, :],
    ).astype(jnp.bfloat16)
    values = projected[:, q_cols + kv_cols :].reshape(rows, KV_HEADS, HEAD_DIM).astype(jnp.bfloat16)
    scores = scores_of(queries, keys, allowed)
    top = jnp.max(scores, axis=-1, keepdims=True)
    log_total = top + jnp.log(jnp.sum(jnp.exp(scores - top), axis=-1, keepdims=True))
    probs = jnp.exp(scores - log_total)
    probs_low = probs.astype(jnp.bfloat16)
    attn = (
        jnp.einsum("grqk,kgd->qgrd", probs_low, values, preferred_element_type=jnp.float32)
        .reshape(rows, q_cols)
        .astype(jnp.bfloat16)
    )
    part = attn
    result = (
        jnp.dot(
            part,
            lax.all_gather(w_out, "shard", axis=0, tiled=True),
            preferred_element_type=jnp.float32,
        ),
    )
    folded_out = result
    residual_hidden_state = layer_input_rows + folded_out[0]
    second_norm_factor = lax.rsqrt(
        jnp.mean(residual_hidden_state * residual_hidden_state, axis=1, keepdims=True) + norm_eps
    )
    second_standardized = residual_hidden_state * second_norm_factor
    gain_fragment = lax.all_gather(mlp_gain, "shard", axis=0, tiled=True)
    gate_piece = lax.all_gather(w_gate, "shard", axis=0, tiled=True)
    up_piece = lax.all_gather(w_up, "shard", axis=0, tiled=True)
    normalized_rows = (second_standardized * gain_fragment.astype(jnp.float32)).astype(jnp.bfloat16)
    joined = jnp.concatenate([gate_piece, up_piece], 1)
    result = (
        jnp.dot(normalized_rows, joined, preferred_element_type=jnp.float32),
        normalized_rows,
        gain_fragment.astype(jnp.float32),
    )
    folded_mlp = result
    gate = folded_mlp[0][:, :FF]
    up_value = folded_mlp[0][:, FF:]
    normed_two = folded_mlp[1]
    second_norm_gain = folded_mlp[2]
    sigma = jax.nn.sigmoid(gate)
    swish = gate * sigma
    inner = (swish * up_value).astype(jnp.bfloat16)
    part = inner
    result = (
        jnp.dot(
            part,
            lax.all_gather(w_down, "shard", axis=0, tiled=True),
            preferred_element_type=jnp.float32,
        ),
    )
    output = (residual_hidden_state + result[0]).astype(jnp.bfloat16).reshape(1, rows, width)
    grad_out = cotangent.reshape(rows, width)
    grad_down = lax.psum_scatter(
        contract_rows(inner, grad_out).astype(jnp.bfloat16),
        "shard",
        scatter_dimension=0,
        tiled=True,
    )
    down_full, gate_full, up_full = (
        lax.all_gather(w_down, "shard", axis=0, tiled=True),
        lax.all_gather(w_gate, "shard", axis=0, tiled=True),
        lax.all_gather(w_up, "shard", axis=0, tiled=True),
    )
    grad_inner = contract_cols(grad_out, down_full)
    grad_gate = (grad_inner * up_value * sigma * (1.0 + gate * (1.0 - sigma))).astype(jnp.bfloat16)
    grad_up = (grad_inner * swish).astype(jnp.bfloat16)
    grad_mlp = jnp.concatenate([grad_gate, grad_up], 1)
    mlp_shards = lax.psum_scatter(
        contract_rows(normed_two, grad_mlp).astype(jnp.bfloat16),
        "shard",
        scatter_dimension=0,
        tiled=True,
    ).astype(jnp.float32)
    second_norm_gradient = contract_cols(grad_gate, gate_full) + contract_cols(grad_up, up_full)
    second_gain_products = jnp.sum(second_norm_gradient * second_standardized, axis=0)
    hidden_gradient = grad_out.astype(jnp.float32) + norm_backward_step(
        second_norm_gradient * second_norm_gain, second_standardized, second_norm_factor
    )
    grad_hidden_low = hidden_gradient.astype(jnp.bfloat16)
    grad_out_proj = lax.psum_scatter(
        contract_rows(attn, grad_hidden_low).astype(jnp.bfloat16),
        "shard",
        scatter_dimension=0,
        tiled=True,
    )
    grad_attn = contract_cols(grad_hidden_low, lax.all_gather(w_out, "shard", axis=0, tiled=True))
    grad_attn = grad_attn.astype(jnp.bfloat16).reshape(rows, KV_HEADS, groups, HEAD_DIM)
    scores_again = scores_of(queries, keys, allowed)
    probs_again = jnp.exp(scores_again - log_total)
    probs_again_low = probs_again.astype(jnp.bfloat16)
    grad_probs = jnp.einsum("qgrd,kgd->grqk", grad_attn, values, preferred_element_type=jnp.float32)
    grad_values = jnp.einsum(
        "grqk,qgrd->kgd", probs_again_low, grad_attn, preferred_element_type=jnp.float32
    )
    grad_scores = (
        probs_again * (grad_probs - jnp.sum(grad_probs * probs_again, axis=-1, keepdims=True))
    ).astype(jnp.bfloat16)
    grad_queries = jnp.einsum(
        "grqk,kgd->qgrd", grad_scores, keys, preferred_element_type=jnp.float32
    ) * HEAD_DIM ** (-0.5)
    grad_keys = jnp.einsum(
        "grqk,qgrd->kgd", grad_scores, queries, preferred_element_type=jnp.float32
    ) * HEAD_DIM ** (-0.5)
    grad_queries = rotate(grad_queries, cosine[:, None, None, :], -sine[:, None, None, :]).reshape(
        rows, q_cols
    )
    grad_keys = rotate(grad_keys, cosine[:, None, :], -sine[:, None, :]).reshape(rows, kv_cols)
    grad_joined = jnp.concatenate(
        [
            grad_queries.astype(jnp.bfloat16),
            grad_keys.astype(jnp.bfloat16),
            grad_values.reshape(rows, kv_cols).astype(jnp.bfloat16),
        ],
        1,
    )
    qkv_shards = lax.psum_scatter(
        contract_rows(normed_one, grad_joined).astype(jnp.bfloat16),
        "shard",
        scatter_dimension=0,
        tiled=True,
    ).astype(jnp.float32)
    local_qkv = jnp.concatenate([w_query, w_key, w_value], 1)
    first_norm_gradient = contract_cols(
        grad_joined, lax.all_gather(local_qkv, "shard", axis=0, tiled=True)
    )
    first_gain_products = jnp.sum(first_norm_gradient * first_standardized, axis=0)
    input_gradient_rows = hidden_gradient + norm_backward_step(
        first_norm_gradient * first_norm_gain, first_standardized, first_norm_factor
    )
    input_grad = input_gradient_rows.astype(jnp.bfloat16).reshape(1, rows, width)
    gain_one_grad, gain_two_grad = (
        lax.psum_scatter(first_gain_products, "shard", scatter_dimension=0, tiled=True),
        lax.psum_scatter(second_gain_products, "shard", scatter_dimension=0, tiled=True),
    )
    summed = (
        lax.psum(gain_one_grad.astype(jnp.bfloat16), "rep").astype(jnp.float32),
        lax.psum(qkv_shards[:, :q_cols].astype(jnp.bfloat16), "rep").astype(jnp.float32),
        lax.psum(qkv_shards[:, q_cols : q_cols + kv_cols].astype(jnp.bfloat16), "rep").astype(
            jnp.float32
        ),
        lax.psum(qkv_shards[:, q_cols + kv_cols :].astype(jnp.bfloat16), "rep").astype(jnp.float32),
        lax.psum(grad_out_proj, "rep").astype(jnp.float32),
        lax.psum(gain_two_grad.astype(jnp.bfloat16), "rep").astype(jnp.float32),
        lax.psum(mlp_shards[:, :FF].astype(jnp.bfloat16), "rep").astype(jnp.float32),
        lax.psum(mlp_shards[:, FF:].astype(jnp.bfloat16), "rep").astype(jnp.float32),
        lax.psum(grad_down, "rep").astype(jnp.float32),
    )
    return (
        output,
        input_grad,
        summed[0],
        summed[1],
        summed[2],
        summed[3],
        summed[4],
        summed[5],
        summed[6],
        summed[7],
        summed[8],
    )


def solution(mesh):
    rep, shard = mesh.devices.shape
    if shard == KV_HEADS and rep % 2 == 0:
        fine = Mesh(np.asarray(mesh.devices).reshape(rep // 2, 2, shard), ("z", "core", "shard"))
        body, every = pieces, ("z", "core", "shard")
    else:
        fine, body, every = mesh, general, ("rep", "shard")
    seqs, vec, mat = P(every, None, None), P("shard"), P("shard", None)
    in_specs = (seqs, P(every, None), vec, mat, mat, mat, mat, vec, mat, mat, mat, seqs)
    out_specs = (seqs, seqs, vec, mat, mat, mat, mat, vec, mat, mat, mat)
    return jax.shard_map(body, mesh=fine, in_specs=in_specs, out_specs=out_specs, check_vma=False)
```
